32 devices in a mesh: seq: 8 (over z, y), row: 2 (over core), col: 2 (over x).
Axes of the slice: x: 2, y: 2, z: 4, core: 2. Of those that a mesh axis runs over, the one named last changes fastest.
Arguments:
- tokens_in: bfloat16 [4096, 1024], P('seq'), may hold values from -6 to 6
- teacher: bfloat16 [4096, 1024], P('seq', 'col'), may hold values from -6 to 6
- norm_gain: bfloat16 [1024], P('col'), may hold values from 0.5 to 1.5
- in_weight: bfloat16 [1024, 2, 2048], P('col', None, 'row'), may hold values from -0.1875 to 0.1875
- conv_weight: bfloat16 [4, 2048], P(None, ('row', 'col')), may hold values from -3 to 3
- conv_bias: bfloat16 [2048], P(('row', 'col')), may hold values from -3 to 3
- select_weight: bfloat16 [2048, 96], P(('row', 'col')), may hold values from -0.125 to 0.125
- step_weight: bfloat16 [64, 2048], P(None, ('row', 'col')), may hold values from -0.75 to 0.75
- step_bias: bfloat16 [2048], P(('row', 'col')), may hold values from -9 to -2.5
- decay_log: float32 [16, 2048], P(None, ('row', 'col')), may hold values from -4 to 2.5
- skip_gain: bfloat16 [2048], P(('row', 'col')), may hold values from 0.5 to 1.5
- out_weight: bfloat16 [2048, 1024], P('row', 'col'), may hold values from -0.25 to 0.25
- parents: int32 [8], replicated, may hold values from -1 to 5, as said below
- lengths: int32 [8], replicated, may hold values from 256 to 512, as said below
- valid_rows: int32 [8], replicated, may hold values from 1 to 512, as said below
Outputs:
- output: bfloat16 [4096, 1024], P(('seq', 'row'), 'col')
- tokens_grad: float32 [4096, 1024], P(('seq', 'row'), 'col')
- gain_grad: float32 [1024], P('col')
- in_grad: float32 [1024, 2, 2048], P('col', None, 'row')
- conv_grad: float32 [4, 2048], P(None, ('row', 'col'))
- conv_bias_grad: float32 [2048], P(('row', 'col'))
- select_grad: float32 [2048, 96], P(('row', 'col'))
- step_grad: float32 [64, 2048], P(None, ('row', 'col'))
- step_bias_grad: float32 [2048], P(('row', 'col'))
- decay_grad: float32 [16, 2048], P(None, ('row', 'col'))
- skip_grad: float32 [2048], P(('row', 'col'))
- out_grad: float32 [2048, 1024], P('row', 'col')
The draws below stay inside these ranges and needn't reach their ends.
Inputs may be any that keep to these rules, and one draw needn't show every extreme that they name: parents[0] = -1 and is the only root; for i >= 1, 0 <= parents[i] < i; the last segment's parent is the root. `lengths`: one segment has exactly 512 live slots and another exactly 256. valid_rows[i] <= lengths[i]; one segment has 512 and another 1.
All inputs are finite; a program needn't handle non-finite values.
Results may differ from the reference program's by a relative error of at most 0.014.
Values may be sent and summed in bfloat16 or wider, within the bound.
A program may use at most 192 MiB of HBM per device.

```python
import jax
import jax.numpy as jnp
from jax import lax

DMODEL = 1024
DINNER = 2048
STATE = 16
DTRANK = 64
KCONV = 4
SEG = 512
SEGS = 8
TOKENS = 4096


def draw_parents(key, part):
    picks = jax.random.randint(jax.random.fold_in(key, 17), (SEGS,), 0, 1 << 20)
    indices = jnp.arange(SEGS, dtype=jnp.int32)
    chosen = picks % jnp.maximum(indices, 1)
    chosen = jnp.where(indices == SEGS - 2, jnp.maximum(indices - 1, 0), chosen)
    chosen = jnp.where(indices == SEGS - 1, 0, chosen)
    return jnp.where(indices == 0, -1, chosen).astype(jnp.int32)


def length_tables(key):
    base = jax.random.fold_in(key, 29)
    order = jax.random.permutation(jax.random.fold_in(base, 1), SEGS)
    drawn = jax.random.randint(jax.random.fold_in(base, 2), (SEGS,), SEG // 2, SEG + 1)
    drawn = drawn.at[order[0]].set(SEG).at[order[1]].set(SEG // 2)
    picks = jax.random.randint(jax.random.fold_in(base, 3), (SEGS,), 0, 1 << 20)
    counted = 1 + picks % drawn
    counted = counted.at[order[0]].set(SEG).at[order[1]].set(1)
    return (drawn.astype(jnp.int32), counted.astype(jnp.int32))


def draw_lengths(key, part):
    return length_tables(key)[0]


def draw_valid_rows(key, part):
    return length_tables(key)[1]


def block_levels(key, extent, shards, low, high):
    factor_of, own = 1.0, jax.random.fold_in(key, 6)
    for dim, shards_of in shards:
        steps = jnp.exp(jax.random.uniform(jax.random.fold_in(own, dim), (shards_of,), jnp.float32, low / len(shards), high / len(shards)))
        factor_of = factor_of * jnp.repeat(steps, extent[dim] // shards_of).reshape([-1 if axis == dim else 1 for axis in range(len(extent))])
    return factor_of


def bell_draw(rng, shape, deviation, most, pieces=(), held_as=jnp.bfloat16):
    gain = block_levels(rng, shape, pieces, -0.22, 0.18) if pieces else 1.0
    values = jax.random.normal(rng, shape, jnp.float32) * deviation * gain
    return jnp.minimum(jnp.maximum(values, -most), most).astype(held_as)


def setup_inputs(seed: int = 0) -> dict:
    splits = jax.random.split(jax.random.key(seed), 16)
    return {
        "tokens_in": bell_draw(splits[0], (TOKENS, DMODEL), 1.0, 6.0, ((0, 8),)),
        "teacher": bell_draw(splits[1], (TOKENS, DMODEL), 1.0, 6.0, ((0, 8), (1, 2))),
        "norm_gain": jnp.clip(1.0 + 0.1 * jax.random.normal(splits[2], (DMODEL,), jnp.float32), 0.5, 1.5).astype(jnp.bfloat16),
        "in_weight": bell_draw(splits[3], (DMODEL, 2, DINNER), DMODEL ** -0.5, 0.1875, ((0, 2), (2, 2))),
        "conv_weight": bell_draw(splits[4], (KCONV, DINNER), KCONV ** -0.5, 3.0, ((1, 4),)),
        "conv_bias": bell_draw(splits[5], (DINNER,), 0.5, 3.0, ((0, 4),)),
        "select_weight": bell_draw(splits[6], (DINNER, DTRANK + 2 * STATE), DINNER ** -0.5, 0.125, ((0, 4),)),
        "step_weight": bell_draw(splits[7], (DTRANK, DINNER), DTRANK ** -0.5, 0.75, ((1, 4),)),
        "step_bias": jnp.clip(-9.0 + 6.5 * jax.random.uniform(splits[8], (DINNER,), jnp.float32) ** block_levels(splits[8], (DINNER,), ((0, 4),), -0.2, 0.2), -9.0, -2.5).astype(jnp.bfloat16),
        "decay_log": jnp.clip(-4.0 + 6.5 * jax.random.uniform(splits[9], (STATE, DINNER), jnp.float32) ** block_levels(splits[9], (STATE, DINNER), ((1, 4),), -0.2, 0.2), -4.0, 2.5),
        "skip_gain": jnp.clip(0.5 + 1.0 * jax.random.uniform(splits[10], (DINNER,), jnp.float32) ** block_levels(splits[10], (DINNER,), ((0, 4),), -0.2, 0.2), 0.5, 1.5).astype(jnp.bfloat16),
        "out_weight": bell_draw(splits[11], (DINNER, DMODEL), (DINNER // 4) ** -0.5, 0.25, ((0, 2), (1, 2))),
        "parents": draw_parents(jax.random.fold_in(splits[15], 71), 0),
        "lengths": draw_lengths(jax.random.fold_in(splits[15], 71), 0),
        "valid_rows": draw_valid_rows(jax.random.fold_in(splits[15], 71), 0),
    }


exact_mode = lax.Precision.HIGHEST
norm_epsilon = 1e-05
scan_rows = 64

@jax.custom_vjp
def low(v):
    return lax.optimization_barrier(v.astype(jnp.bfloat16)).astype(jnp.float32)

@jax.custom_vjp
def low_back(v):
    return v

def low_keep(v):
    return (low(v), None)

def low_pass(kept, grad):
    return (grad,)

def back_keep(v):
    return (v, None)

def back_low(kept, grad):
    return (low(grad),)
low.defvjp(low_keep, low_pass)
low_back.defvjp(back_keep, back_low)

def block_scan(carry, inputs, neg_decay):

    def advance(current, values):
        delta, active, gate_b, gate_c = values
        current = jnp.exp(delta[None, :] * neg_decay) * current + gate_b[:, None] * (delta * active)[None, :]
        return (current, lax.optimization_barrier(jnp.sum(gate_c[:, None] * current, axis=0)))
    return lax.scan(advance, carry, inputs)

def segment_forward(tokens_seg, tail_in, start, live, weights):
    norm_gain, in_weight, conv_weight, conv_bias, select_weight, step_weight, step_bias, decay_log, skip_gain, out_weight = weights
    inv_rms = lax.rsqrt(lax.optimization_barrier(jnp.mean(tokens_seg * tokens_seg, axis=1)) + norm_epsilon)
    hidden_in = low(tokens_seg * inv_rms[:, None] * norm_gain[None, :])
    joined = jnp.dot(hidden_in, in_weight.reshape(DMODEL, 2 * DINNER), precision=exact_mode).reshape(SEG, 2, DINNER)
    joined = low_back(joined)
    inner = joined[:, 0]
    gate_in = joined[:, 1]
    extended = jnp.concatenate([tail_in, inner], axis=0)
    pre_act = jnp.zeros((SEG, DINNER), jnp.float32) + conv_bias[None, :]
    for tap_index in range(KCONV):
        pre_act = pre_act + conv_weight[tap_index][None, :] * extended[tap_index:tap_index + SEG]
    active = low(jax.nn.silu(pre_act))
    selected = jnp.dot(active, select_weight, precision=exact_mode)
    step_low = low(selected[:, :DTRANK])
    gate_b = selected[:, DTRANK:DTRANK + STATE]
    gate_c = selected[:, DTRANK + STATE:]
    step_pre = jnp.dot(step_low, step_weight, precision=exact_mode) + step_bias[None, :]
    delta = jax.nn.softplus(step_pre) * live[:, None]
    neg_decay = -jnp.exp(decay_log)
    scanner = jax.checkpoint(block_scan)
    blocks = SEG // scan_rows

    def split_rows(values):
        return values.reshape(blocks, scan_rows, values.shape[1])
    final_state, scanned = lax.scan(lambda carry, inputs: scanner(carry, inputs, neg_decay), start, (split_rows(delta), split_rows(active), split_rows(gate_b), split_rows(gate_c)))
    mixed_pre = scanned.reshape(SEG, DINNER) + skip_gain[None, :] * active
    mixed = low(mixed_pre * jax.nn.silu(gate_in))
    branch = low_back(jnp.dot(mixed, out_weight, precision=exact_mode))
    return (tokens_seg + branch, final_state, inner)

def all_segments(tokens_f, weights, parents, lengths):
    run_segment = jax.checkpoint(segment_forward)
    rows = jnp.arange(SEG, dtype=jnp.int32)

    def visit(tables, index):
        finals, tails = tables
        above = parents[index]
        slot = jnp.maximum(above, 0).astype(jnp.int32)
        present = (above >= 0).astype(jnp.float32)
        start = lax.dynamic_index_in_dim(finals, slot, 0, keepdims=False) * present
        tail_in = lax.dynamic_index_in_dim(tails, slot, 0, keepdims=False) * present
        tokens_seg = lax.dynamic_slice_in_dim(tokens_f, (index * SEG).astype(jnp.int32), SEG, 0)
        live = (rows < lengths[index]).astype(jnp.float32)
        result, final_state, inner = run_segment(tokens_seg, tail_in, start, live, weights)
        own_tail = lax.dynamic_slice_in_dim(inner, (lengths[index] - (KCONV - 1)).astype(jnp.int32), KCONV - 1, 0)
        finals = lax.dynamic_update_index_in_dim(finals, final_state, index, 0)
        tails = lax.dynamic_update_index_in_dim(tails, own_tail, index, 0)
        return ((finals, tails), result)
    empty = (jnp.zeros((SEGS, STATE, DINNER), jnp.float32), jnp.zeros((SEGS, KCONV - 1, DINNER), jnp.float32))
    return lax.scan(visit, empty, jnp.arange(SEGS, dtype=jnp.int32))[1].reshape(TOKENS, DMODEL)

def reference(tokens_in, teacher, norm_gain, in_weight, conv_weight, conv_bias, select_weight, step_weight, step_bias, decay_log, skip_gain, out_weight, parents, lengths, valid_rows):
    weights = tuple((value.astype(jnp.float32) for value in (norm_gain, in_weight, conv_weight, conv_bias, select_weight, step_weight, step_bias, decay_log, skip_gain, out_weight)))

    def forward(tokens_f, *params):
        return all_segments(tokens_f, params, parents, lengths)
    result, pullback = jax.vjp(forward, tokens_in.astype(jnp.float32), *weights)
    rows = jnp.arange(SEG, dtype=jnp.int32)
    counted = (rows[None, :] < valid_rows[:, None]).astype(jnp.float32).reshape(TOKENS)
    scale = TOKENS / jnp.sum(valid_rows).astype(jnp.float32)
    cotangent = scale * (result - teacher.astype(jnp.float32)) * counted[:, None]
    grads = pullback(cotangent)
    return (result.astype(jnp.bfloat16), grads[0], grads[1], grads[2], grads[3], grads[4], grads[5], grads[6], grads[7], grads[8], grads[9], grads[10])
```

```python
import functools

import jax
import jax.numpy as jnp
from jax import lax
from jax.experimental import pallas as pl
from jax.experimental.pallas import tpu as pltpu
from jax.sharding import PartitionSpec as P

MESH = pl.DeviceIdType.MESH
F32 = jnp.float32
BF16 = jnp.bfloat16
norm_epsilon = 1e-05
spans = 8
lanes = 128
log2e = 1.4426950408889634
vmem_bytes = 60 * 1024 * 1024


def vmem_spec():
    return pl.BlockSpec(memory_space=pltpu.VMEM)


def smem_spec():
    return pl.BlockSpec(memory_space=pltpu.SMEM)


def struct(shape, dtype):
    return jax.ShapeDtypeStruct(shape, dtype)


def dot(a, b):
    return jnp.dot(a, b, preferred_element_type=F32)


def dot_tn(a, b):
    return lax.dot_general(a, b, (((0,), (0,)), ((), ())), preferred_element_type=F32)


def dot_nt(a, b):
    return lax.dot_general(a, b, (((1,), (1,)), ((), ())), preferred_element_type=F32)


def sigmoid(v):
    return 1.0 / (1.0 + jnp.exp(-v))


def slope_of(v, sigma):
    return sigma * (1.0 + v * (1.0 - sigma))


def to_steps(rows, steps):
    place = lax.broadcasted_iota(jnp.int32, (rows, rows), 0)
    token = lax.broadcasted_iota(jnp.int32, (rows, rows), 1)
    return (token == (place % spans) * steps + place // spans).astype(F32).astype(BF16)


def to_tokens(rows, steps):
    token = lax.broadcasted_iota(jnp.int32, (rows, rows), 0)
    place = lax.broadcasted_iota(jnp.int32, (rows, rows), 1)
    return (token == (place % spans) * steps + place // spans).astype(F32).astype(BF16)


def step_tokens(rows, steps):
    place = lax.broadcasted_iota(jnp.int32, (rows, 1), 0)
    return (place % spans) * steps + place // spans


def spread_matrix(states):
    row = lax.broadcasted_iota(jnp.int32, (2 * states, states * lanes), 0)
    col = lax.broadcasted_iota(jnp.int32, (2 * states, states * lanes), 1)
    return (row % states == col // lanes).astype(F32).astype(BF16)


def gather_matrix(states):
    row = lax.broadcasted_iota(jnp.int32, (states * lanes, states), 0)
    col = lax.broadcasted_iota(jnp.int32, (states * lanes, states), 1)
    return (row // lanes == col).astype(F32).astype(BF16)


def spread(values, states):
    high = values.astype(BF16)
    rest = (values - high.astype(F32)).astype(BF16)
    return dot(jnp.concatenate([high, rest], axis=1), spread_matrix(states))


def shift_spans(values, amount):
    return jnp.roll(values, amount, axis=values.ndim - 2)


def span_index(shape):
    return lax.broadcasted_iota(jnp.int32, shape, len(shape) - 2)


def run_kernel(kernel, outs, args, name, scratch=(), specs=None, flops=0, collective=None):
    params = dict(vmem_limit_bytes=vmem_bytes)
    if collective is not None:
        params.update(collective_id=collective, has_side_effects=True)
    return pl.pallas_call(
        kernel,
        out_shape=outs,
        in_specs=[
            smem_spec() if a.dtype == jnp.int32 else vmem_spec() for a in args
        ],
        out_specs=jax.tree.map(lambda _: vmem_spec(), outs),
        scratch_shapes=list(scratch),
        compiler_params=pltpu.CompilerParams(**params),
        cost_estimate=pl.CostEstimate(
            flops=int(flops),
            transcendentals=0,
            bytes_accessed=int(sum(a.size * a.dtype.itemsize for a in args)),
        ),
        name=name,
    )(*args)


def barrier_with(peers):
    barrier = pltpu.get_barrier_semaphore()
    for peer in peers:
        pl.semaphore_signal(barrier, inc=1, device_id=peer, device_id_type=MESH)
    pl.semaphore_wait(barrier, len(peers))


def remote(src, dst, send, recv, peer):
    return pltpu.make_async_remote_copy(
        src_ref=src, dst_ref=dst, send_sem=send, recv_sem=recv, device_id=peer, device_id_type=MESH
    )


def row_peer():
    return {"row": 1 - lax.axis_index("row")}


def col_peer():
    return {"col": 1 - lax.axis_index("col")}


def entry_kernel(tail_ref, wi_ref, gain_ref, tails_ref, wo_ref, gain_o_ref, tsend, trecv, csend, crecv):
    count = tails_ref.shape[0]
    me = lax.axis_index("seq")
    peers = [{"seq": lax.rem(me + j, count)} for j in range(1, count)]
    barrier_with([col_peer()] + peers)
    copies = []
    for j, peer in enumerate(peers):
        copies.append(remote(tail_ref, tails_ref.at[me], tsend.at[j], trecv.at[j], peer))
    copies.append(remote(gain_ref, gain_o_ref, csend.at[0], crecv.at[0], col_peer()))
    copies.append(remote(wi_ref, wo_ref, csend.at[1], crecv.at[1], col_peer()))
    for copy in copies:
        copy.start()
    tails_ref[me] = tail_ref[...]
    for copy in copies:
        copy.wait()


def entry_exchange(tail, wi_send, gain_send, count):
    return run_kernel(
        entry_kernel,
        (
            struct((count,) + tail.shape, tail.dtype),
            struct(wi_send.shape, wi_send.dtype),
            struct(gain_send.shape, gain_send.dtype),
        ),
        (tail, wi_send, gain_send),
        "entry_exchange",
        scratch=[
            pltpu.SemaphoreType.DMA((count,)),
            pltpu.SemaphoreType.DMA((count,)),
            pltpu.SemaphoreType.DMA((2,)),
            pltpu.SemaphoreType.DMA((2,)),
        ],
        collective=0,
    )


def seq_gather_kernel(x_ref, o_ref, send, recv):
    count = o_ref.shape[0]
    me = lax.axis_index("seq")
    peers = [{"seq": lax.rem(me + j, count)} for j in range(1, count)]
    barrier_with(peers)
    copies = [
        remote(x_ref, o_ref.at[me], send.at[j], recv.at[j], peer) for j, peer in enumerate(peers)
    ]
    for copy in copies:
        copy.start()
    o_ref[me] = x_ref[...]
    for copy in copies:
        copy.wait()


def seq_gather(x, count, collective, name):
    return run_kernel(
        seq_gather_kernel,
        struct((count,) + x.shape, x.dtype),
        (x,),
        name,
        scratch=[pltpu.SemaphoreType.DMA((count,)), pltpu.SemaphoreType.DMA((count,))],
        collective=collective,
    )


def quad_sum_kernel(x_ref, o_ref, from_row, to_col, from_col, send, recv):
    barrier_with([row_peer(), col_peer()])
    first = remote(x_ref, from_row, send.at[0], recv.at[0], row_peer())
    first.start()
    first.wait()
    pair = x_ref[...] + from_row[...]
    to_col[...] = pair.astype(BF16)
    second = remote(to_col, from_col, send.at[1], recv.at[1], col_peer())
    second.start()
    o_ref[...] = pair
    second.wait()
    o_ref[...] += from_col[...].astype(F32)


def quad_sum(x, collective, name):
    return run_kernel(
        quad_sum_kernel,
        struct(x.shape, F32),
        (x,),
        name,
        scratch=[
            pltpu.VMEM(x.shape, F32),
            pltpu.VMEM(x.shape, BF16),
            pltpu.VMEM(x.shape, BF16),
            pltpu.SemaphoreType.DMA((2,)),
            pltpu.SemaphoreType.DMA((2,)),
        ],
        collective=collective,
    )


def middle_kernel(
    part_ref, tok_ref, teach_ref, ints_ref, scale_ref,
    out_ref, cot_ref, low_ref,
    from_row, to_col, from_col, send, recv,
):
    half = tok_ref.shape[0]
    row = lax.axis_index("row")
    mine = pl.multiple_of(row * half, half)
    other = pl.multiple_of((1 - row) * half, half)
    barrier_with([row_peer(), col_peer()])
    first = [
        remote(part_ref.at[h, pl.ds(other, half), :], from_row.at[h], send.at[h], recv.at[h], row_peer())
        for h in (1, 0)
    ]
    for copy in first:
        copy.start()
    first[0].wait()
    to_col[...] = (
        part_ref[1, pl.ds(mine, half), :].astype(F32) + from_row[1].astype(F32)
    ).astype(BF16)
    second = remote(to_col, from_col, send.at[2], recv.at[2], col_peer())
    second.start()
    first[1].wait()
    tile = part_ref[0, pl.ds(mine, half), :].astype(F32) + from_row[0].astype(F32)
    tile = tile + tok_ref[...].astype(F32)
    second.wait()
    result = tile + from_col[...].astype(F32)
    out_ref[...] = result.astype(BF16)
    positions = mine + lax.broadcasted_iota(jnp.int32, (half, 1), 0)
    counted = (positions < ints_ref[0]).astype(F32) * scale_ref[0:1, 0:1]
    cot = (result - teach_ref[...].astype(F32)) * counted
    cot_ref[...] = cot
    low_ref[0, pl.ds(mine, half), :] = cot.astype(BF16)
    third = [
        remote(low_ref.at[0, pl.ds(mine, half), :], low_ref.at[1, pl.ds(mine, half), :], send.at[3], recv.at[3], col_peer()),
        remote(low_ref.at[0, pl.ds(mine, half), :], low_ref.at[0, pl.ds(mine, half), :], send.at[4], recv.at[4], row_peer()),
    ]
    for copy in third:
        copy.start()
    third[0].wait()
    fourth = remote(low_ref.at[1, pl.ds(mine, half), :], low_ref.at[1, pl.ds(mine, half), :], send.at[5], recv.at[5], row_peer())
    fourth.start()
    third[1].wait()
    fourth.wait()


def middle_exchange(part, tok_tile, teach_tile, my_valid, scale):
    _, rows, width = part.shape
    half = rows // 2
    return run_kernel(
        middle_kernel,
        (struct((half, width), BF16), struct((half, width), F32), struct((2, rows, width), BF16)),
        (part, tok_tile, teach_tile, my_valid, scale),
        "middle_exchange",
        scratch=[
            pltpu.VMEM((2, half, width), BF16),
            pltpu.VMEM((half, width), BF16),
            pltpu.VMEM((half, width), BF16),
            pltpu.SemaphoreType.DMA((6,)),
            pltpu.SemaphoreType.DMA((6,)),
        ],
        collective=3,
    )


def hidden_kernel(part_ref, tail_ref, out_ref, tout_ref, from_row, trow, to_col, from_col, tcol, tfrom, send, recv):
    half = out_ref.shape[0]
    row = lax.axis_index("row")
    mine = pl.multiple_of(row * half, half)
    other = pl.multiple_of((1 - row) * half, half)
    barrier_with([row_peer(), col_peer()])
    first = [
        remote(part_ref.at[h, pl.ds(other, half), :], from_row.at[h], send.at[h], recv.at[h], row_peer())
        for h in (1, 0)
    ]
    first.append(remote(tail_ref, trow, send.at[2], recv.at[2], row_peer()))
    for copy in (first[2], first[0], first[1]):
        copy.start()
    first[2].wait()
    tails = tail_ref[...] + trow[...]
    tcol[...] = tails[1]
    last = remote(tcol, tfrom, send.at[3], recv.at[3], col_peer())
    last.start()
    first[0].wait()
    to_col[...] = (
        part_ref[1, pl.ds(mine, half), :].astype(F32) + from_row[1].astype(F32)
    ).astype(BF16)
    second = remote(to_col, from_col, send.at[4], recv.at[4], col_peer())
    second.start()
    first[1].wait()
    out_ref[...] = part_ref[0, pl.ds(mine, half), :].astype(F32) + from_row[0].astype(F32)
    last.wait()
    tout_ref[...] = tails[0] + tfrom[...]
    second.wait()
    out_ref[...] += from_col[...].astype(F32)


def hidden_exchange(part, tail):
    _, rows, width = part.shape
    half = rows // 2
    return run_kernel(
        hidden_kernel,
        (struct((half, width), F32), struct(tail.shape[1:], F32)),
        (part, tail),
        "hidden_exchange",
        scratch=[
            pltpu.VMEM((2, half, width), BF16),
            pltpu.VMEM(tail.shape, F32),
            pltpu.VMEM((half, width), BF16),
            pltpu.VMEM((half, width), BF16),
            pltpu.VMEM(tail.shape[1:], F32),
            pltpu.VMEM(tail.shape[1:], F32),
            pltpu.SemaphoreType.DMA((5,)),
            pltpu.SemaphoreType.DMA((5,)),
        ],
        collective=5,
    )


def finish_kernel(
    hid_ref, tails_ref, tok_ref, toko_ref, gain_ref, cot_ref, parents_ref, lengths_ref,
    tg_ref, gg_ref, mean_out, mean_in, gain_out, gain_in, send, recv, *, width
):
    half = tok_ref.shape[0]
    count, margin8 = tails_ref.shape[0], tails_ref.shape[1]
    row = lax.axis_index("row")
    me = lax.axis_index("seq")
    barrier_with([row_peer(), col_peer()])
    positions = row * half + lax.broadcasted_iota(jnp.int32, (half, margin8), 0)
    slot = lax.broadcasted_iota(jnp.int32, (half, margin8), 1)
    hidden = hid_ref[...]
    length = lengths_ref[me]
    own_tail = jnp.zeros(tails_ref.shape[1:], F32)
    for child in range(count):
        is_child = (parents_ref[child] == me).astype(F32)
        own_tail = own_tail + is_child * tails_ref[child].astype(F32)
    place = ((positions == length - 3 + slot) & (slot < 3)).astype(F32)
    hidden = hidden + jnp.dot(place, own_tail, preferred_element_type=F32, precision=lax.Precision.HIGHEST)
    tok = tok_ref[...].astype(F32)
    toko = toko_ref[...].astype(F32)
    total = jnp.sum(tok * tok, axis=1, keepdims=True) + jnp.sum(toko * toko, axis=1, keepdims=True)
    inv = lax.rsqrt(total / width + norm_epsilon)
    normed = tok * inv
    gain_out[...] = jnp.broadcast_to(jnp.sum(hidden * normed, axis=0, keepdims=True), gain_out.shape)
    scaled = hidden * gain_ref[0:1, :].astype(F32)
    mean = jnp.sum(scaled * normed, axis=1, keepdims=True)
    ones = jnp.ones((8, lanes), F32)
    mean_out[...] = lax.dot_general(
        ones, jnp.broadcast_to(mean / lanes, (half, lanes)), (((1,), (1,)), ((), ())),
        preferred_element_type=F32, precision=lax.Precision.HIGHEST,
    )
    copies = [
        remote(mean_out, mean_in, send.at[0], recv.at[0], col_peer()),
        remote(gain_out, gain_in, send.at[1], recv.at[1], row_peer()),
    ]
    for copy in copies:
        copy.start()
    for copy in copies:
        copy.wait()
    other = lax.dot_general(
        mean_in[...], jnp.full((8, lanes), 0.125, F32), (((0,), (0,)), ((), ())),
        preferred_element_type=F32, precision=lax.Precision.HIGHEST,
    )
    mean = (mean + other[:, 0:1]) / width
    tg_ref[...] = cot_ref[...] + inv * (scaled - normed * mean)
    gg_ref[...] = gain_out[...] + gain_in[...]


def finish_exchange(hid, tails, tok, toko, gain, cot, parents, lengths, width):
    half, cols = hid.shape
    return run_kernel(
        functools.partial(finish_kernel, width=width),
        (struct((half, cols), F32), struct((8, cols), F32)),
        (hid, tails, tok, toko, gain, cot, parents, lengths),
        "finish_exchange",
        scratch=[
            pltpu.VMEM((8, half), F32),
            pltpu.VMEM((8, half), F32),
            pltpu.VMEM((8, cols), F32),
            pltpu.VMEM((8, cols), F32),
            pltpu.SemaphoreType.DMA((2,)),
            pltpu.SemaphoreType.DMA((2,)),
        ],
        collective=6,
    )


def forward_in_kernel(
    tok_ref, toko_ref, tails_ref, tailso_ref, gain_ref, gaino_ref, wi_ref, wio_ref,
    cw_ref, cb_ref, sw_ref, ints_ref,
    hid_ref, hidt_ref, ext_ref, act_ref, sel_ref,
):
    rows, half = tok_ref.shape
    steps = rows // spans
    width = 2 * half
    parent = jnp.maximum(ints_ref[0], 0)
    present = (ints_ref[0] >= 0).astype(F32)
    gain = gain_ref[0:1, :].astype(F32)
    gaino = gaino_ref[0:1, :].astype(F32)

    def hidden_of(own, other):
        own = own.astype(F32)
        other = other.astype(F32)
        total = jnp.sum(own * own, axis=1, keepdims=True) + jnp.sum(other * other, axis=1, keepdims=True)
        inv = lax.rsqrt(total / width + norm_epsilon)
        return (own * inv * gain).astype(BF16), (other * inv * gaino).astype(BF16)

    hid, hido = hidden_of(tok_ref[...], toko_ref[...])
    order = to_steps(rows, steps)
    hid = dot(order, hid).astype(BF16)
    hido = dot(order, hido).astype(BF16)
    hid_ref[0] = hid
    hid_ref[1] = hido
    inner = dot(hid, wi_ref[...]) + dot(hido, wio_ref[...])
    tail, tailo = hidden_of(tails_ref[parent], tailso_ref[parent])
    hidt_ref[0] = tail
    hidt_ref[1] = tailo
    tail_inner = (dot(tail, wi_ref[...]) + dot(tailo, wio_ref[...])) * present
    last = inner[rows - 3 * spans :]
    first_span = lax.broadcasted_iota(jnp.int32, (spans, half), 0) == 0
    for j in range(3):
        block = jnp.roll(last[j * spans : (j + 1) * spans], 1, axis=0)
        ext_ref[j * spans : (j + 1) * spans, :] = jnp.where(
            first_span, jnp.broadcast_to(tail_inner[5 + j : 6 + j, :], (spans, half)), block
        )
    ext_ref[3 * spans :, :] = inner
    taps = cw_ref[...].astype(F32)
    pre = jnp.broadcast_to(cb_ref[0:1, :].astype(F32), (rows, half))
    for k in range(4):
        pre = pre + taps[k : k + 1, :] * ext_ref[k * spans : k * spans + rows, :]
    act = (pre * sigmoid(pre)).astype(BF16)
    act_ref[...] = act
    sel_ref[...] = dot(act, sw_ref[...])


def conv_pre(ext_ref, cw_ref, cb_ref, rows, half):
    taps = cw_ref[...].astype(F32)
    pre = jnp.broadcast_to(cb_ref[0:1, :].astype(F32), (rows, half))
    for k in range(4):
        pre = pre + taps[k : k + 1, :] * ext_ref[k * spans : k * spans + rows, :]
    return pre


def group_ds(group):
    return pl.ds(pl.multiple_of(group * lanes, lanes), lanes)


def step_ds(step):
    return pl.ds(pl.multiple_of(step * spans, spans), spans)


def decay_rows(decay_log_ref, decay_b, scale):
    states, width = decay_log_ref.shape
    rate = -jnp.exp(decay_log_ref[...]) * scale
    for n in range(states):
        decay_b[n] = jnp.broadcast_to(rate[n : n + 1, :], (spans, width))


def span_sum_kernel_part(delta_ref, steps):
    total = delta_ref[0:spans, :]
    for s in range(1, steps):
        total = total + delta_ref[s * spans : (s + 1) * spans, :]
    return total


def forward_ends_kernel(
    sel_ref, tw_ref, tb_ref, dl_ref, act_ref, ints_ref,
    delta_ref, pre_ref, reach_ref, cum_ref, send_ref,
    drive, b_ref, rate_ref,
):
    rows, width = act_ref.shape
    steps = rows // spans
    states = dl_ref.shape[0]
    rank = tw_ref.shape[0]
    length = ints_ref[0]
    sel = sel_ref[...]
    step_pre = dot(sel[:, :rank].astype(BF16), tw_ref[...]) + tb_ref[0:1, :].astype(F32)
    pre_ref[...] = step_pre
    live = (step_tokens(rows, steps) < length).astype(F32)
    delta = (jnp.maximum(step_pre, 0.0) + jnp.log1p(jnp.exp(-jnp.abs(step_pre)))) * live
    delta_ref[...] = delta
    drive[...] = delta * act_ref[...].astype(F32)
    b_ref[...] = spread(sel[:, rank : rank + states], states)
    decay_rows(dl_ref, rate_ref, log2e)

    for group in range(width // lanes):
        here = slice(group * lanes, (group + 1) * lanes)

        def advance(step, carry):
            d = delta_ref[step_ds(step), here]
            w = drive[step_ds(step), here]
            out = []
            for n in range(states):
                a = jnp.exp2(d * rate_ref[n, :, here])
                out.append(a * carry[n] + w * b_ref[step_ds(step), n * lanes : (n + 1) * lanes])
            return tuple(out)

        ends = lax.fori_loop(0, steps, advance, (jnp.zeros((spans, lanes), F32),) * states)
        for n in range(states):
            reach_ref[n, :, here] = ends[n]

    total = span_sum_kernel_part(delta_ref, steps)
    index2 = span_index((spans, width))
    part = total
    shift = 1
    while shift < spans:
        inside = index2 >= shift
        for n in range(states):
            own = reach_ref[n]
            earlier = jnp.where(inside, shift_spans(own, shift), 0.0)
            reach_ref[n] = own + jnp.exp2(part * rate_ref[n]) * earlier
        part = part + jnp.where(inside, shift_spans(part, shift), 0.0)
        shift *= 2
    cum_ref[...] = part
    sums = part[spans - 1 : spans, :]
    high = sums.astype(BF16)
    mid = (sums - high.astype(F32)).astype(BF16)
    low = (sums - high.astype(F32) - mid.astype(F32)).astype(BF16)
    ends = jnp.concatenate([reach_ref[n, spans - 1 : spans, :] for n in range(states)], axis=0)
    extra = jnp.concatenate(
        [high.astype(F32), mid.astype(F32), low.astype(F32), jnp.zeros((5, width), F32)], axis=0
    )
    send_ref[...] = jnp.concatenate([ends, extra], axis=0).astype(BF16)


def segment_sum(table_ref, index, states):
    block = table_ref[index].astype(F32)
    return block[:states], block[states : states + 1] + block[states + 1 : states + 2] + block[states + 2 : states + 3]


def forward_out_kernel(
    table_ref, parents_ref, me_ref, dl_ref, reach_ref, cum_ref, delta_ref, act_ref, sel_ref,
    hid_ref, wg_ref, wgo_ref, skip_ref, ow_ref, owo_ref,
    starts_ref, mpre_ref, gate_ref, mixed_ref, part_ref,
    finals, drive, b_ref, c_ref, rate_ref,
):
    rows, width = act_ref.shape
    steps = rows // spans
    states = dl_ref.shape[0]
    rank = sel_ref.shape[1] - 2 * states
    count = table_ref.shape[0]
    me = me_ref[0]
    decay_rows(dl_ref, rate_ref, log2e)
    rate = -jnp.exp(dl_ref[...]) * log2e

    def start_of(target):
        above = parents_ref[target]
        return finals[jnp.maximum(above, 0)] * (above >= 0).astype(F32)

    def visit(target, carry):
        end, total = segment_sum(table_ref, target, states)
        finals[target] = jnp.exp2(rate * total) * start_of(target) + end
        return carry

    finals[0] = jnp.zeros(finals.shape[1:], F32)
    lax.fori_loop(0, count, visit, 0)
    start = start_of(me)
    sel = sel_ref[...]
    drive[...] = delta_ref[...] * act_ref[...].astype(F32)
    b_ref[...] = spread(sel[:, rank : rank + states], states)
    c_ref[...] = spread(sel[:, rank + states :], states)
    index2 = span_index((spans, width))
    cum = jnp.where(index2 >= 1, shift_spans(cum_ref[...], 1), 0.0)
    for n in range(states):
        earlier = jnp.where(index2 >= 1, shift_spans(reach_ref[n], 1), 0.0)
        starts_ref[n] = jnp.exp2(cum * rate_ref[n]) * start[n : n + 1, :] + earlier

    for group in range(width // lanes):
        here = slice(group * lanes, (group + 1) * lanes)

        def advance(step, carry):
            d = delta_ref[step_ds(step), here]
            w = drive[step_ds(step), here]
            out = []
            reads = [None] * 4
            for n in range(states):
                a = jnp.exp2(d * rate_ref[n, :, here])
                now = a * carry[n] + w * b_ref[step_ds(step), n * lanes : (n + 1) * lanes]
                out.append(now)
                term = c_ref[step_ds(step), n * lanes : (n + 1) * lanes] * now
                reads[n % 4] = term if reads[n % 4] is None else reads[n % 4] + term
            mpre_ref[step_ds(step), here] = (reads[0] + reads[1]) + (reads[2] + reads[3])
            return tuple(out)

        lax.fori_loop(0, steps, advance, tuple(starts_ref[n, :, here] for n in range(states)))

    gate = dot(hid_ref[0], wg_ref[...]) + dot(hid_ref[1], wgo_ref[...])
    gate_ref[...] = gate
    mixed_pre = mpre_ref[...] + skip_ref[0:1, :].astype(F32) * act_ref[...].astype(F32)
    mpre_ref[...] = mixed_pre
    mixed = (mixed_pre * (gate * sigmoid(gate))).astype(BF16)
    mixed_ref[...] = mixed
    natural = dot(to_tokens(rows, steps), mixed).astype(BF16)
    part_ref[0] = dot(natural, ow_ref[...]).astype(BF16)
    part_ref[1] = dot(natural, owo_ref[...]).astype(BF16)


def backward_in_kernel(
    cot_ref, mixed_ref, ow_ref, owo_ref, gate_ref, mpre_ref, act_ref, skip_ref, sel_ref,
    delta_ref, dl_ref, cum_ref, hid_ref,
    og_ref, ggrad_ref, ig_ref, pgrad_ref, sgrad_ref, back_ref, flow_ref,
    c_ref, rate_ref,
):
    rows, width = act_ref.shape
    steps = rows // spans
    states = dl_ref.shape[0]
    rank = sel_ref.shape[1] - 2 * states
    order = to_steps(rows, steps)
    cot = dot(order, cot_ref[0]).astype(BF16)
    coto = dot(order, cot_ref[1]).astype(BF16)
    mixed_grad = dot_nt(cot, ow_ref[...]) + dot_nt(coto, owo_ref[...])
    gate = gate_ref[...]
    sigma = sigmoid(gate)
    pre_grad = mixed_grad * (gate * sigma)
    pgrad_ref[...] = pre_grad
    gate_grad = (mixed_grad * mpre_ref[...] * slope_of(gate, sigma)).astype(BF16)
    ggrad_ref[...] = gate_grad
    sgrad_ref[...] = jnp.broadcast_to(
        jnp.sum(pre_grad * act_ref[...].astype(F32), axis=0, keepdims=True), sgrad_ref.shape
    )
    c_ref[...] = spread(sel_ref[:, rank + states :], states)
    decay_rows(dl_ref, rate_ref, log2e)

    for group in range(width // lanes):
        here = slice(group * lanes, (group + 1) * lanes)

        def retreat(back, carry):
            step = steps - 1 - back
            d = delta_ref[step_ds(step), here]
            p = pgrad_ref[step_ds(step), here]
            out = []
            for n in range(states):
                a = jnp.exp2(d * rate_ref[n, :, here])
                out.append(a * (c_ref[step_ds(step), n * lanes : (n + 1) * lanes] * p + carry[n]))
            return tuple(out)

        flows = lax.fori_loop(0, steps, retreat, (jnp.zeros((spans, lanes), F32),) * states)
        for n in range(states):
            back_ref[n, :, here] = flows[n]

    index2 = span_index((spans, width))
    cum = cum_ref[...]
    part = cum - jnp.where(index2 >= 1, shift_spans(cum, 1), 0.0)
    shift = 1
    while shift < spans:
        inside = index2 < spans - shift
        for n in range(states):
            own = back_ref[n]
            later = jnp.where(inside, shift_spans(own, -shift), 0.0)
            back_ref[n] = own + jnp.exp2(part * rate_ref[n]) * later
        part = part + jnp.where(inside, shift_spans(part, -shift), 0.0)
        shift *= 2
    flow_ref[...] = jnp.concatenate(
        [back_ref[n, 0:1, :] for n in range(states)], axis=0
    ).astype(BF16)
    og_ref[0] = dot_tn(mixed_ref[...], cot).astype(BF16)
    og_ref[1] = dot_tn(mixed_ref[...], coto).astype(BF16)
    ig_ref[0] = dot_tn(hid_ref[0], gate_grad).astype(BF16)
    ig_ref[1] = dot_tn(hid_ref[1], gate_grad).astype(BF16)


def backward_scan_kernel(
    table_ref, flows_ref, parents_ref, me_ref, length_ref, dl_ref, starts_ref, back_ref, cum_ref,
    delta_ref, act_ref, sel_ref, pgrad_ref, pre_ref, tw_ref,
    selg_ref, agrad_ref, small_ref, stepg_ref, dgrad_ref,
    grads, drive, b_ref, c_ref, rate_ref, decay_buf, state_buf, b_sum, c_sum, dg_ref,
):
    rows, width = act_ref.shape
    steps = rows // spans
    states = dl_ref.shape[0]
    rank = tw_ref.shape[0]
    count = table_ref.shape[0]
    me = me_ref[0]
    rate = -jnp.exp(dl_ref[...]) * log2e
    decay_rows(dl_ref, rate_ref, log2e)
    grads[...] = jnp.zeros(grads.shape, F32)

    def visit(visited, carry):
        target = count - 1 - visited
        _, total = segment_sum(table_ref, target, states)
        flow = flows_ref[target].astype(F32) + jnp.exp2(rate * total) * grads[target]
        above = parents_ref[target]
        slot = jnp.maximum(above, 0)
        grads[slot] = grads[slot] + flow * (above >= 0).astype(F32)
        return carry

    lax.fori_loop(0, count - 1, visit, 0)
    end_grad = grads[me]
    sel = sel_ref[...]
    drive[...] = delta_ref[...] * act_ref[...].astype(F32)
    b_ref[...] = spread(sel[:, rank : rank + states], states)
    c_ref[...] = spread(sel[:, rank + states :], states)
    index2 = span_index((spans, width))
    cum = cum_ref[...]
    after = cum[spans - 1 : spans, :] - cum
    inside = index2 < spans - 1

    for group in range(width // lanes):
        here = slice(group * lanes, (group + 1) * lanes)

        def advance(step, carry):
            d = delta_ref[step_ds(step), here]
            w = drive[step_ds(step), here]
            out = []
            for n in range(states):
                state_buf[n, step_ds(step), :] = carry[n]
                a = jnp.exp2(d * rate_ref[n, :, here])
                decay_buf[n, step_ds(step), :] = a
                out.append(a * carry[n] + w * b_ref[step_ds(step), n * lanes : (n + 1) * lanes])
            return tuple(out)

        finals = lax.fori_loop(0, steps, advance, tuple(starts_ref[n, :, here] for n in range(states)))
        for n in range(states):
            state_buf[n, rows : rows + spans, :] = finals[n]

        later = []
        for n in range(states):
            flow = jnp.where(inside[:, here], shift_spans(back_ref[n, :, here], -1), 0.0)
            later.append(flow + jnp.exp2(after[:, here] * rate_ref[n, :, here]) * end_grad[n : n + 1, here])

        def retreat(back, carry):
            step = steps - 1 - back
            at = step_ds(step)
            d = delta_ref[at, here]
            p = pgrad_ref[at, here]
            w = drive[at, here]
            flows, sums = carry
            new_flows, new_sums = [], []
            weighted = [None, None]
            decayed = [None, None]
            for n in range(states):
                cols = slice(n * lanes, (n + 1) * lanes)
                a = decay_buf[n, at, :]
                adjoint = c_ref[at, cols] * p + flows[n]
                moved = a * adjoint
                growth = moved * state_buf[n, at, :]
                new_flows.append(moved)
                new_sums.append(sums[n] + growth * d)
                term = adjoint * b_ref[at, cols]
                weighted[n % 2] = term if weighted[n % 2] is None else weighted[n % 2] + term
                term = growth * rate_ref[n, :, here]
                decayed[n % 2] = term if decayed[n % 2] is None else decayed[n % 2] + term
                b_term = adjoint * w
                c_term = state_buf[n, step_ds(step + 1), :] * p
                if group == 0:
                    b_sum[at, cols] = b_term
                    c_sum[at, cols] = c_term
                else:
                    b_sum[at, cols] += b_term
                    c_sum[at, cols] += c_term
            bw = weighted[0] + weighted[1]
            dg_ref[at, here] = (decayed[0] + decayed[1]) * (1.0 / log2e) + act_ref[at, here].astype(F32) * bw
            agrad_ref[at, here] = bw * d
            return (tuple(new_flows), tuple(new_sums))

        zero = jnp.zeros((spans, lanes), F32)
        _, sums = lax.fori_loop(0, steps, retreat, (tuple(later), (zero,) * states))
        for n in range(states):
            dgrad_ref[n : n + 1, here] = (
                jnp.sum(sums[n], axis=0, keepdims=True) * rate[n : n + 1, here] * (1.0 / log2e)
            )

    live = (step_tokens(rows, steps) < length_ref[0]).astype(F32)
    step_pre_grad = dg_ref[...] * live * sigmoid(pre_ref[...])
    small_ref[...] = jnp.broadcast_to(jnp.sum(step_pre_grad, axis=0, keepdims=True), small_ref.shape)
    low = step_pre_grad.astype(BF16)
    stepg_ref[...] = dot_tn(sel[:, :rank].astype(BF16), low)
    gather = gather_matrix(states)
    selg_ref[...] = jnp.concatenate(
        [dot_nt(low, tw_ref[...]), dot(b_sum[...].astype(BF16), gather), dot(c_sum[...].astype(BF16), gather)],
        axis=1,
    )


def backward_out_kernel(
    selg_ref, act_ref, sw_ref, agrad_ref, skip_ref, pgrad_ref, ext_ref, cw_ref, cb_ref,
    hid_ref, hidt_ref, wi_ref, wio_ref, wg_ref, wgo_ref, ggrad_ref,
    ig_ref, part_ref, tpart_ref, selw_ref, cgrad_ref,
    cig_ref,
):
    rows, width = act_ref.shape
    steps = rows // spans
    selg = selg_ref[...].astype(BF16)
    selw_ref[...] = dot_tn(selg, act_ref[...])
    active_grad = (
        agrad_ref[...] + skip_ref[0:1, :].astype(F32) * pgrad_ref[...] + dot_nt(selg, sw_ref[...])
    )
    pre = conv_pre(ext_ref, cw_ref, cb_ref, rows, width)
    conv_in = active_grad * slope_of(pre, sigmoid(pre))
    cig_ref[0:rows, :] = conv_in
    last_span = lax.broadcasted_iota(jnp.int32, (spans, width), 0) == spans - 1
    for j in range(3):
        block = jnp.roll(conv_in[j * spans : (j + 1) * spans], -1, axis=0)
        cig_ref[rows + j * spans : rows + (j + 1) * spans, :] = jnp.where(last_span, 0.0, block)
    taps = cw_ref[...].astype(F32)
    sums = [
        jnp.sum(conv_in * ext_ref[k * spans : k * spans + rows, :], axis=0, keepdims=True)
        for k in range(4)
    ]
    sums.append(jnp.sum(conv_in, axis=0, keepdims=True))
    sums.append(jnp.zeros((3, width), F32))
    cgrad_ref[...] = jnp.concatenate(sums, axis=0)
    inner_grad = jnp.zeros((rows, width), F32)
    for k in range(4):
        inner_grad = inner_grad + taps[k : k + 1, :] * cig_ref[(3 - k) * spans : (3 - k) * spans + rows, :]
    inner_low = inner_grad.astype(BF16)
    tails = [jnp.zeros((5, width), F32)]
    for i in range(3):
        row = jnp.zeros((1, width), F32)
        for k in range(i + 1):
            row = row + taps[k : k + 1, :] * conv_in[(i - k) * spans : (i - k) * spans + 1, :]
        tails.append(row)
    tail_low = jnp.concatenate(tails, axis=0).astype(BF16)
    order = to_tokens(rows, steps)
    natural = dot(order, inner_low).astype(BF16)
    naturalg = dot(order, ggrad_ref[...]).astype(BF16)
    for h, (wi, wg) in enumerate(((wi_ref, wg_ref), (wio_ref, wgo_ref))):
        part_ref[h] = (dot_nt(natural, wi[...]) + dot_nt(naturalg, wg[...])).astype(BF16)
        tpart_ref[h] = dot_nt(tail_low, wi[...])
        ig_ref[h] = (dot_tn(hid_ref[h], inner_low) + dot_tn(hidt_ref[h], tail_low)).astype(BF16)


def seq_bits(count):
    bits = []
    mask = 1
    while mask < count:
        bits.append(mask)
        mask *= 2
    return bits


def sum_scatter(value, count):
    me = lax.axis_index("seq")
    for mask in seq_bits(count):
        half = value.shape[0] // 2
        mine = (me // mask) % 2
        keep = lax.dynamic_slice_in_dim(value, mine * half, half, 0)
        give = lax.dynamic_slice_in_dim(value, (1 - mine) * half, half, 0)
        got = lax.ppermute(give, "seq", [(i, i ^ mask) for i in range(count)])
        value = (keep.astype(F32) + got.astype(F32)).astype(value.dtype)
    return value


def gather_back(value, count):
    me = lax.axis_index("seq")
    for mask in reversed(seq_bits(count)):
        mine = (me // mask) % 2
        got = lax.ppermute(value, "seq", [(i, i ^ mask) for i in range(count)])
        low = jnp.where(mine == 0, value, got)
        high = jnp.where(mine == 0, got, value)
        value = jnp.concatenate([low, high], axis=0)
    return value


def on_device(
    tokens_in, teacher, norm_gain, in_weight, conv_weight, conv_bias, select_weight, step_weight,
    step_bias, decay_log, skip_gain, out_weight, parents, lengths, valid_rows,
):
    rows, width = tokens_in.shape
    half = norm_gain.shape[0]
    inner = decay_log.shape[1]
    states = decay_log.shape[0]
    rank = step_weight.shape[0]
    selects = rank + 2 * states
    steps = rows // spans
    count = lax.axis_size("seq")
    row_len = rows // lax.axis_size("row")
    row = lax.axis_index("row")
    col = lax.axis_index("col")
    me = lax.axis_index("seq")
    my_len = lengths[me][None]
    my_parent = parents[me][None]
    my_valid = valid_rows[me][None]
    me1 = me.astype(jnp.int32)[None]
    scale = jnp.full((8, lanes), 1.0, F32) * (rows * count / jnp.sum(valid_rows).astype(F32))

    def halves(value, axis):
        size = value.shape[axis] // 2
        own = lax.dynamic_slice_in_dim(value, col * size, size, axis)
        other = lax.dynamic_slice_in_dim(value, (1 - col) * size, size, axis)
        return own, other

    def rows8(value):
        return jnp.broadcast_to(value[None, :], (8, value.shape[0]))

    swap = [(0, 1), (1, 0)]
    tok, toko = halves(tokens_in, 1)
    tail = lax.dynamic_slice_in_dim(tokens_in, my_len[0] - 8, 8, 0)
    w_own, w_send = halves(in_weight, 2)
    wi, wg = w_own[:, 0], w_own[:, 1]
    wi_send, wg_send = w_send[:, 0], w_send[:, 1]
    ow, ow_send = halves(out_weight, 0)
    gain = rows8(norm_gain)
    skip = rows8(skip_gain)
    conv_b = rows8(conv_bias)
    step_b = rows8(step_bias)

    tails, wio, gaino = entry_exchange(tail, wi_send, gain, count)
    wg_send, ow_send, wio = lax.optimization_barrier((wg_send, ow_send, wio))
    wgo = lax.ppermute(wg_send, "col", swap)
    owo = lax.ppermute(ow_send, "col", swap)
    tails_own, tails_oth = halves(tails, 2)

    hid, hid_tail, ext, act, sel_part = run_kernel(
        forward_in_kernel,
        (
            struct((2, rows, half), BF16),
            struct((2, 8, half), BF16),
            struct((rows + 3 * spans, inner), F32),
            struct((rows, inner), BF16),
            struct((rows, selects), F32),
        ),
        (tok, toko, tails_own, tails_oth, gain, gaino, wi, wio, conv_weight, conv_b, select_weight, my_parent),
        "forward_in",
        flops=2e9,
    )
    sel = quad_sum(sel_part, 1, "select_sum")
    delta, step_pre, reach, cum, seg_map = run_kernel(
        forward_ends_kernel,
        (
            struct((rows, inner), F32),
            struct((rows, inner), F32),
            struct((states, spans, inner), F32),
            struct((spans, inner), F32),
            struct((states + 8, inner), BF16),
        ),
        (sel, step_weight, step_b, decay_log, act, my_len),
        "forward_ends",
        scratch=[
            pltpu.VMEM((rows, inner), F32),
            pltpu.VMEM((rows, states * lanes), F32),
            pltpu.VMEM((states, spans, inner), F32),
        ],
        flops=2e9,
    )
    table = seq_gather(seg_map, count, 2, "state_gather")
    starts, mixed_pre, gate, mixed, part = run_kernel(
        forward_out_kernel,
        (
            struct((states, spans, inner), F32),
            struct((rows, inner), F32),
            struct((rows, inner), F32),
            struct((rows, inner), BF16),
            struct((2, rows, half), BF16),
        ),
        (
            table, parents, me1, decay_log, reach, cum, delta, act, sel, hid, wg, wgo, skip, ow, owo,
        ),
        "forward_out",
        scratch=[
            pltpu.VMEM((count, states, inner), F32),
            pltpu.VMEM((rows, inner), F32),
            pltpu.VMEM((rows, states * lanes), F32),
            pltpu.VMEM((rows, states * lanes), F32),
            pltpu.VMEM((states, spans, inner), F32),
        ],
        flops=4e9,
    )
    tok_tile = lax.dynamic_slice_in_dim(tok, row * row_len, row_len, 0)
    toko_tile = lax.dynamic_slice_in_dim(toko, row * row_len, row_len, 0)
    teach_tile = lax.dynamic_slice_in_dim(teacher, row * row_len, row_len, 0)
    output, cot_tile, cot = middle_exchange(part, tok_tile, teach_tile, my_valid, scale)
    out_part, gate_grad, ig_gate, pre_grad, skip_part, back, flow = run_kernel(
        backward_in_kernel,
        (
            struct((2, inner, half), BF16),
            struct((rows, inner), BF16),
            struct((2, half, inner), BF16),
            struct((rows, inner), F32),
            struct((8, inner), F32),
            struct((states, spans, inner), F32),
            struct((states, inner), BF16),
        ),
        (cot, mixed, ow, owo, gate, mixed_pre, act, skip, sel, delta, decay_log, cum, hid),
        "backward_in",
        scratch=[
            pltpu.VMEM((rows, states * lanes), F32),
            pltpu.VMEM((states, spans, inner), F32),
        ],
        flops=4e9,
    )
    flows = seq_gather(flow, count, 4, "flow_gather")
    selg_part, active_grad, step_bias_part, step_part, decay_part = run_kernel(
        backward_scan_kernel,
        (
            struct((rows, selects), F32),
            struct((rows, inner), F32),
            struct((8, inner), F32),
            struct((rank, inner), F32),
            struct((states, inner), F32),
        ),
        (
            table, flows, parents, me1, my_len, decay_log, starts, back, cum, delta, act, sel,
            pre_grad, step_pre, step_weight,
        ),
        "backward_scan",
        scratch=[
            pltpu.VMEM((count, states, inner), F32),
            pltpu.VMEM((rows, inner), F32),
            pltpu.VMEM((rows, states * lanes), F32),
            pltpu.VMEM((rows, states * lanes), F32),
            pltpu.VMEM((states, spans, inner), F32),
            pltpu.VMEM((states, rows, lanes), F32),
            pltpu.VMEM((states, rows + spans, lanes), F32),
            pltpu.VMEM((rows, states * lanes), F32),
            pltpu.VMEM((rows, states * lanes), F32),
            pltpu.VMEM((rows, inner), F32),
        ],
        flops=8e9,
    )
    selg = quad_sum(selg_part, 7, "select_grad_sum")
    ig_inner, hid_part, tail_part, select_part, conv_part = run_kernel(
        backward_out_kernel,
        (
            struct((2, half, inner), BF16),
            struct((2, rows, half), BF16),
            struct((2, 8, half), F32),
            struct((selects, inner), F32),
            struct((8, inner), F32),
        ),
        (
            selg, act, select_weight, active_grad, skip, pre_grad, ext, conv_weight, conv_b,
            hid, hid_tail, wi, wio, wg, wgo, gate_grad,
        ),
        "backward_out",
        scratch=[pltpu.VMEM((rows + 3 * spans, inner), F32)],
        flops=6e9,
    )
    hid_tile, tail_tile = hidden_exchange(hid_part, tail_part)
    tail_table = seq_gather(
        jnp.concatenate([tail_tile[5:8], tail_tile[:5]], axis=0), count, 8, "tail_gather"
    )
    tokens_grad, gain_part = finish_exchange(
        hid_tile, tail_table, tok_tile, toko_tile, gain, cot_tile, parents, lengths, width
    )

    def flat(pair):
        return pair.reshape(-1, pair.shape[-1])

    small = jnp.concatenate(
        [
            step_part, decay_part, select_part, conv_part[:5], skip_part[:1], step_bias_part[:1],
            gain_part[:1],
        ],
        axis=0,
    )
    pad = -small.shape[0] % (8 * count)
    small = jnp.pad(small, ((0, pad), (0, 0)))
    first = jnp.concatenate([flat(out_part), flat(ig_gate)], axis=0)
    first = gather_back(sum_scatter(first, count), count)
    second = gather_back(sum_scatter(flat(ig_inner), count), count)
    small = gather_back(sum_scatter(small, count), count)
    og = first[: 2 * inner].reshape(2, inner, half)
    igg = first[2 * inner :].reshape(2, half, inner)
    igi = second.reshape(2, half, inner)
    from_pair = lax.ppermute(jnp.stack([og[1], igg[1], igi[1]]), "col", swap)
    left = col == 0

    def beside(own, other, axis):
        return jnp.concatenate(
            [jnp.where(left, own, other), jnp.where(left, other, own)], axis=axis
        ).astype(F32)

    out_grad = beside(og[0], from_pair[0], 0)
    in_grad = jnp.stack([beside(igi[0], from_pair[2], 1), beside(igg[0], from_pair[1], 1)], axis=1)
    at = 0
    pieces = []
    for size in (rank, states, selects, 4, 1, 1, 1, 1):
        pieces.append(small[at : at + size])
        at += size
    step_grad, decay_grad, select_grad, conv_grad, conv_bias_grad, skip_grad, step_bias_grad, gain_grad = pieces
    return (
        output,
        tokens_grad,
        gain_grad[0],
        in_grad,
        conv_grad,
        conv_bias_grad[0],
        select_grad.T,
        step_grad,
        step_bias_grad[0],
        decay_grad,
        skip_grad[0],
        out_grad,
    )


def solution(mesh):
    placed = (
        P("seq", None),
        P("seq", "col"),
        P("col"),
        P("col", None, "row"),
        P(None, ("row", "col")),
        P(("row", "col")),
        P(("row", "col"), None),
        P(None, ("row", "col")),
        P(("row", "col")),
        P(None, ("row", "col")),
        P(("row", "col")),
        P("row", "col"),
        P(),
        P(),
        P(),
    )
    return jax.shard_map(
        on_device,
        mesh=mesh,
        in_specs=placed,
        out_specs=(
            P(("seq", "row"), "col"),
            P(("seq", "row"), "col"),
            P("col"),
            P("col", None, "row"),
            P(None, ("row", "col")),
            P(("row", "col")),
            P(("row", "col"), None),
            P(None, ("row", "col")),
            P(("row", "col")),
            P(None, ("row", "col")),
            P(("row", "col")),
            P("row", "col"),
        ),
        check_vma=False,
    )
```

```python
import functools

import jax
import jax.numpy as jnp
from jax import lax
from jax.experimental import pallas as pl
from jax.experimental.pallas import tpu as pltpu
from jax.sharding import PartitionSpec as P

MESH = pl.DeviceIdType.MESH
F32 = jnp.float32
BF16 = jnp.bfloat16
norm_epsilon = 1e-05
spans = 8
lanes = 128
log2e = 1.4426950408889634
vmem_bytes = 60 * 1024 * 1024


def vmem_spec():
    return pl.BlockSpec(memory_space=pltpu.VMEM)


def smem_spec():
    return pl.BlockSpec(memory_space=pltpu.SMEM)


def struct(shape, dtype):
    return jax.ShapeDtypeStruct(shape, dtype)


def dot(a, b):
    return jnp.dot(a, b, preferred_element_type=F32)


def dot_tn(a, b):
    return lax.dot_general(a, b, (((0,), (0,)), ((), ())), preferred_element_type=F32)


def dot_nt(a, b):
    return lax.dot_general(a, b, (((1,), (1,)), ((), ())), preferred_element_type=F32)


def sigmoid(v):
    return 1.0 / (1.0 + jnp.exp(-v))


def slope_of(v, sigma):
    return sigma * (1.0 + v * (1.0 - sigma))


def to_steps(rows, steps):
    place = lax.broadcasted_iota(jnp.int32, (rows, rows), 0)
    token = lax.broadcasted_iota(jnp.int32, (rows, rows), 1)
    return (token == (place % spans) * steps + place // spans).astype(F32).astype(BF16)


def to_tokens(rows, steps):
    token = lax.broadcasted_iota(jnp.int32, (rows, rows), 0)
    place = lax.broadcasted_iota(jnp.int32, (rows, rows), 1)
    return (token == (place % spans) * steps + place // spans).astype(F32).astype(BF16)


def step_tokens(rows, steps):
    place = lax.broadcasted_iota(jnp.int32, (rows, 1), 0)
    return (place % spans) * steps + place // spans


def spread_matrix(states):
    row = lax.broadcasted_iota(jnp.int32, (2 * states, states * lanes), 0)
    col = lax.broadcasted_iota(jnp.int32, (2 * states, states * lanes), 1)
    return (row % states == col // lanes).astype(F32).astype(BF16)


def gather_matrix(states):
    row = lax.broadcasted_iota(jnp.int32, (states * lanes, states), 0)
    col = lax.broadcasted_iota(jnp.int32, (states * lanes, states), 1)
    return (row // lanes == col).astype(F32).astype(BF16)


def spread(values, states):
    high = values.astype(BF16)
    rest = (values - high.astype(F32)).astype(BF16)
    return dot(jnp.concatenate([high, rest], axis=1), spread_matrix(states))


def shift_spans(values, amount):
    return jnp.roll(values, amount, axis=values.ndim - 2)


def span_index(shape):
    return lax.broadcasted_iota(jnp.int32, shape, len(shape) - 2)


def run_kernel(kernel, outs, args, name, scratch=(), specs=None, flops=0, collective=None):
    params = dict(vmem_limit_bytes=vmem_bytes)
    if collective is not None:
        params.update(collective_id=collective, has_side_effects=True)
    return pl.pallas_call(
        kernel,
        out_shape=outs,
        in_specs=[
            smem_spec() if a.dtype == jnp.int32 else vmem_spec() for a in args
        ],
        out_specs=jax.tree.map(lambda _: vmem_spec(), outs),
        scratch_shapes=list(scratch),
        compiler_params=pltpu.CompilerParams(**params),
        cost_estimate=pl.CostEstimate(
            flops=int(flops),
            transcendentals=0,
            bytes_accessed=int(sum(a.size * a.dtype.itemsize for a in args)),
        ),
        name=name,
    )(*args)


def barrier_with(peers):
    barrier = pltpu.get_barrier_semaphore()
    for peer in peers:
        pl.semaphore_signal(barrier, inc=1, device_id=peer, device_id_type=MESH)
    pl.semaphore_wait(barrier, len(peers))


def remote(src, dst, send, recv, peer):
    return pltpu.make_async_remote_copy(
        src_ref=src, dst_ref=dst, send_sem=send, recv_sem=recv, device_id=peer, device_id_type=MESH
    )


def row_peer():
    return {"row": 1 - lax.axis_index("row")}


def col_peer():
    return {"col": 1 - lax.axis_index("col")}


def entry_kernel(tail_ref, wi_ref, gain_ref, tails_ref, wo_ref, gain_o_ref, tsend, trecv, csend, crecv):
    count = tails_ref.shape[0]
    me = lax.axis_index("seq")
    peers = [{"seq": lax.rem(me + j, count)} for j in range(1, count)]
    barrier_with([col_peer()] + peers)
    copies = []
    for j, peer in enumerate(peers):
        copies.append(remote(tail_ref, tails_ref.at[me], tsend.at[j], trecv.at[j], peer))
    copies.append(remote(gain_ref, gain_o_ref, csend.at[0], crecv.at[0], col_peer()))
    copies.append(remote(wi_ref, wo_ref, csend.at[1], crecv.at[1], col_peer()))
    for copy in copies:
        copy.start()
    tails_ref[me] = tail_ref[...]
    for copy in copies:
        copy.wait()


def entry_exchange(tail, wi_send, gain_send, count):
    return run_kernel(
        entry_kernel,
        (
            struct((count,) + tail.shape, tail.dtype),
            struct(wi_send.shape, wi_send.dtype),
            struct(gain_send.shape, gain_send.dtype),
        ),
        (tail, wi_send, gain_send),
        "entry_exchange",
        scratch=[
            pltpu.SemaphoreType.DMA((count,)),
            pltpu.SemaphoreType.DMA((count,)),
            pltpu.SemaphoreType.DMA((2,)),
            pltpu.SemaphoreType.DMA((2,)),
        ],
        collective=0,
    )


def seq_gather_kernel(x_ref, o_ref, send, recv):
    count = o_ref.shape[0]
    me = lax.axis_index("seq")
    peers = [{"seq": lax.rem(me + j, count)} for j in range(1, count)]
    barrier_with(peers)
    copies = [
        remote(x_ref, o_ref.at[me], send.at[j], recv.at[j], peer) for j, peer in enumerate(peers)
    ]
    for copy in copies:
        copy.start()
    o_ref[me] = x_ref[...]
    for copy in copies:
        copy.wait()


def seq_gather(x, count, collective, name):
    return run_kernel(
        seq_gather_kernel,
        struct((count,) + x.shape, x.dtype),
        (x,),
        name,
        scratch=[pltpu.SemaphoreType.DMA((count,)), pltpu.SemaphoreType.DMA((count,))],
        collective=collective,
    )


def quad_sum_kernel(x_ref, o_ref, from_row, to_col, from_col, send, recv):
    barrier_with([row_peer(), col_peer()])
    first = remote(x_ref, from_row, send.at[0], recv.at[0], row_peer())
    first.start()
    first.wait()
    pair = x_ref[...] + from_row[...]
    to_col[...] = pair.astype(BF16)
    second = remote(to_col, from_col, send.at[1], recv.at[1], col_peer())
    second.start()
    o_ref[...] = pair
    second.wait()
    o_ref[...] += from_col[...].astype(F32)


def quad_sum(x, collective, name):
    return run_kernel(
        quad_sum_kernel,
        struct(x.shape, F32),
        (x,),
        name,
        scratch=[
            pltpu.VMEM(x.shape, F32),
            pltpu.VMEM(x.shape, BF16),
            pltpu.VMEM(x.shape, BF16),
            pltpu.SemaphoreType.DMA((2,)),
            pltpu.SemaphoreType.DMA((2,)),
        ],
        collective=collective,
    )


def middle_kernel(
    part_ref, tok_ref, teach_ref, ints_ref, scale_ref,
    out_ref, cot_ref, low_ref,
    from_row, to_col, from_col, send, recv,
):
    half = tok_ref.shape[0]
    row = lax.axis_index("row")
    mine = pl.multiple_of(row * half, half)
    other = pl.multiple_of((1 - row) * half, half)
    barrier_with([row_peer(), col_peer()])
    first = [
        remote(part_ref.at[h, pl.ds(other, half), :], from_row.at[h], send.at[h], recv.at[h], row_peer())
        for h in (1, 0)
    ]
    for copy in first:
        copy.start()
    first[0].wait()
    to_col[...] = (
        part_ref[1, pl.ds(mine, half), :].astype(F32) + from_row[1].astype(F32)
    ).astype(BF16)
    second = remote(to_col, from_col, send.at[2], recv.at[2], col_peer())
    second.start()
    first[1].wait()
    tile = part_ref[0, pl.ds(mine, half), :].astype(F32) + from_row[0].astype(F32)
    tile = tile + tok_ref[...].astype(F32)
    second.wait()
    result = tile + from_col[...].astype(F32)
    out_ref[...] = result.astype(BF16)
    positions = mine + lax.broadcasted_iota(jnp.int32, (half, 1), 0)
    counted = (positions < ints_ref[0]).astype(F32) * scale_ref[0:1, 0:1]
    cot = (result - teach_ref[...].astype(F32)) * counted
    cot_ref[...] = cot
    low_ref[0, pl.ds(mine, half), :] = cot.astype(BF16)
    third = [
        remote(low_ref.at[0, pl.ds(mine, half), :], low_ref.at[1, pl.ds(mine, half), :], send.at[3], recv.at[3], col_peer()),
        remote(low_ref.at[0, pl.ds(mine, half), :], low_ref.at[0, pl.ds(mine, half), :], send.at[4], recv.at[4], row_peer()),
    ]
    for copy in third:
        copy.start()
    third[0].wait()
    fourth = remote(low_ref.at[1, pl.ds(mine, half), :], low_ref.at[1, pl.ds(mine, half), :], send.at[5], recv.at[5], row_peer())
    fourth.start()
    third[1].wait()
    fourth.wait()


def middle_exchange(part, tok_tile, teach_tile, my_valid, scale):
    _, rows, width = part.shape
    half = rows // 2
    return run_kernel(
        middle_kernel,
        (struct((half, width), BF16), struct((half, width), F32), struct((2, rows, width), BF16)),
        (part, tok_tile, teach_tile, my_valid, scale),
        "middle_exchange",
        scratch=[
            pltpu.VMEM((2, half, width), BF16),
            pltpu.VMEM((half, width), BF16),
            pltpu.VMEM((half, width), BF16),
            pltpu.SemaphoreType.DMA((6,)),
            pltpu.SemaphoreType.DMA((6,)),
        ],
        collective=3,
    )


def hidden_kernel(part_ref, tail_ref, out_ref, tout_ref, from_row, trow, to_col, from_col, tcol, tfrom, send, recv):
    half = out_ref.shape[0]
    row = lax.axis_index("row")
    mine = pl.multiple_of(row * half, half)
    other = pl.multiple_of((1 - row) * half, half)
    barrier_with([row_peer(), col_peer()])
    first = [
        remote(part_ref.at[h, pl.ds(other, half), :], from_row.at[h], send.at[h], recv.at[h], row_peer())
        for h in (1, 0)
    ]
    first.append(remote(tail_ref, trow, send.at[2], recv.at[2], row_peer()))
    for copy in (first[2], first[0], first[1]):
        copy.start()
    first[2].wait()
    tails = tail_ref[...] + trow[...]
    tcol[...] = tails[1]
    last = remote(tcol, tfrom, send.at[3], recv.at[3], col_peer())
    last.start()
    first[0].wait()
    to_col[...] = (
        part_ref[1, pl.ds(mine, half), :].astype(F32) + from_row[1].astype(F32)
    ).astype(BF16)
    second = remote(to_col, from_col, send.at[4], recv.at[4], col_peer())
    second.start()
    first[1].wait()
    out_ref[...] = part_ref[0, pl.ds(mine, half), :].astype(F32) + from_row[0].astype(F32)
    last.wait()
    tout_ref[...] = tails[0] + tfrom[...]
    second.wait()
    out_ref[...] += from_col[...].astype(F32)


def hidden_exchange(part, tail):
    _, rows, width = part.shape
    half = rows // 2
    return run_kernel(
        hidden_kernel,
        (struct((half, width), F32), struct(tail.shape[1:], F32)),
        (part, tail),
        "hidden_exchange",
        scratch=[
            pltpu.VMEM((2, half, width), BF16),
            pltpu.VMEM(tail.shape, F32),
            pltpu.VMEM((half, width), BF16),
            pltpu.VMEM((half, width), BF16),
            pltpu.VMEM(tail.shape[1:], F32),
            pltpu.VMEM(tail.shape[1:], F32),
            pltpu.SemaphoreType.DMA((5,)),
            pltpu.SemaphoreType.DMA((5,)),
        ],
        collective=5,
    )


def finish_kernel(
    hid_ref, tails_ref, tok_ref, toko_ref, gain_ref, cot_ref, parents_ref, lengths_ref,
    tg_ref, gg_ref, mean_out, mean_in, gain_out, gain_in, send, recv, *, width
):
    half = tok_ref.shape[0]
    count, margin8 = tails_ref.shape[0], tails_ref.shape[1]
    row = lax.axis_index("row")
    me = lax.axis_index("seq")
    barrier_with([row_peer(), col_peer()])
    positions = row * half + lax.broadcasted_iota(jnp.int32, (half, margin8), 0)
    slot = lax.broadcasted_iota(jnp.int32, (half, margin8), 1)
    hidden = hid_ref[...]
    length = lengths_ref[me]
    own_tail = jnp.zeros(tails_ref.shape[1:], F32)
    for child in range(count):
        is_child = (parents_ref[child] == me).astype(F32)
        own_tail = own_tail + is_child * tails_ref[child].astype(F32)
    place = ((positions == length - 3 + slot) & (slot < 3)).astype(F32)
    hidden = hidden + jnp.dot(place, own_tail, preferred_element_type=F32, precision=lax.Precision.HIGHEST)
    tok = tok_ref[...].astype(F32)
    toko = toko_ref[...].astype(F32)
    total = jnp.sum(tok * tok, axis=1, keepdims=True) + jnp.sum(toko * toko, axis=1, keepdims=True)
    inv = lax.rsqrt(total / width + norm_epsilon)
    normed = tok * inv
    gain_out[...] = jnp.broadcast_to(jnp.sum(hidden * normed, axis=0, keepdims=True), gain_out.shape)
    scaled = hidden * gain_ref[0:1, :].astype(F32)
    mean = jnp.sum(scaled * normed, axis=1, keepdims=True)
    ones = jnp.ones((8, lanes), F32)
    mean_out[...] = lax.dot_general(
        ones, jnp.broadcast_to(mean / lanes, (half, lanes)), (((1,), (1,)), ((), ())),
        preferred_element_type=F32, precision=lax.Precision.HIGHEST,
    )
    copies = [
        remote(mean_out, mean_in, send.at[0], recv.at[0], col_peer()),
        remote(gain_out, gain_in, send.at[1], recv.at[1], row_peer()),
    ]
    for copy in copies:
        copy.start()
    for copy in copies:
        copy.wait()
    other = lax.dot_general(
        mean_in[...], jnp.full((8, lanes), 0.125, F32), (((0,), (0,)), ((), ())),
        preferred_element_type=F32, precision=lax.Precision.HIGHEST,
    )
    mean = (mean + other[:, 0:1]) / width
    tg_ref[...] = cot_ref[...] + inv * (scaled - normed * mean)
    gg_ref[...] = gain_out[...] + gain_in[...]


def finish_exchange(hid, tails, tok, toko, gain, cot, parents, lengths, width):
    half, cols = hid.shape
    return run_kernel(
        functools.partial(finish_kernel, width=width),
        (struct((half, cols), F32), struct((8, cols), F32)),
        (hid, tails, tok, toko, gain, cot, parents, lengths),
        "finish_exchange",
        scratch=[
            pltpu.VMEM((8, half), F32),
            pltpu.VMEM((8, half), F32),
            pltpu.VMEM((8, cols), F32),
            pltpu.VMEM((8, cols), F32),
            pltpu.SemaphoreType.DMA((2,)),
            pltpu.SemaphoreType.DMA((2,)),
        ],
        collective=6,
    )


def forward_in_kernel(
    tok_ref, toko_ref, tails_ref, tailso_ref, gain_ref, gaino_ref, wi_ref, wio_ref,
    cw_ref, cb_ref, sw_ref, ints_ref,
    hid_ref, hidt_ref, ext_ref, act_ref, sel_ref,
):
    rows, half = tok_ref.shape
    steps = rows // spans
    width = 2 * half
    parent = jnp.maximum(ints_ref[0], 0)
    present = (ints_ref[0] >= 0).astype(F32)
    gain = gain_ref[0:1, :].astype(F32)
    gaino = gaino_ref[0:1, :].astype(F32)

    def hidden_of(own, other):
        own = own.astype(F32)
        other = other.astype(F32)
        total = jnp.sum(own * own, axis=1, keepdims=True) + jnp.sum(other * other, axis=1, keepdims=True)
        inv = lax.rsqrt(total / width + norm_epsilon)
        return (own * inv * gain).astype(BF16), (other * inv * gaino).astype(BF16)

    hid, hido = hidden_of(tok_ref[...], toko_ref[...])
    order = to_steps(rows, steps)
    hid = dot(order, hid).astype(BF16)
    hido = dot(order, hido).astype(BF16)
    hid_ref[0] = hid
    hid_ref[1] = hido
    inner = dot(hid, wi_ref[...]) + dot(hido, wio_ref[...])
    tail, tailo = hidden_of(tails_ref[parent], tailso_ref[parent])
    hidt_ref[0] = tail
    hidt_ref[1] = tailo
    tail_inner = (dot(tail, wi_ref[...]) + dot(tailo, wio_ref[...])) * present
    last = inner[rows - 3 * spans :]
    first_span = lax.broadcasted_iota(jnp.int32, (spans, half), 0) == 0
    for j in range(3):
        block = jnp.roll(last[j * spans : (j + 1) * spans], 1, axis=0)
        ext_ref[j * spans : (j + 1) * spans, :] = jnp.where(
            first_span, jnp.broadcast_to(tail_inner[5 + j : 6 + j, :], (spans, half)), block
        )
    ext_ref[3 * spans :, :] = inner
    taps = cw_ref[...].astype(F32)
    pre = jnp.broadcast_to(cb_ref[0:1, :].astype(F32), (rows, half))
    for k in range(4):
        pre = pre + taps[k : k + 1, :] * ext_ref[k * spans : k * spans + rows, :]
    act = (pre * sigmoid(pre)).astype(BF16)
    act_ref[...] = act
    sel_ref[...] = dot(act, sw_ref[...])


def conv_pre(ext_ref, cw_ref, cb_ref, rows, half):
    taps = cw_ref[...].astype(F32)
    pre = jnp.broadcast_to(cb_ref[0:1, :].astype(F32), (rows, half))
    for k in range(4):
        pre = pre + taps[k : k + 1, :] * ext_ref[k * spans : k * spans + rows, :]
    return pre


def group_ds(group):
    return pl.ds(pl.multiple_of(group * lanes, lanes), lanes)


def step_ds(step):
    return pl.ds(pl.multiple_of(step * spans, spans), spans)


def decay_rows(decay_log_ref, decay_b, scale):
    states, width = decay_log_ref.shape
    rate = -jnp.exp(decay_log_ref[...]) * scale
    for n in range(states):
        decay_b[n] = jnp.broadcast_to(rate[n : n + 1, :], (spans, width))


def span_sum_kernel_part(delta_ref, steps):
    total = delta_ref[0:spans, :]
    for s in range(1, steps):
        total = total + delta_ref[s * spans : (s + 1) * spans, :]
    return total


def forward_ends_kernel(
    sel_ref, tw_ref, tb_ref, dl_ref, act_ref, ints_ref,
    delta_ref, pre_ref, reach_ref, cum_ref, send_ref,
    drive, b_ref, rate_ref,
):
    rows, width = act_ref.shape
    steps = rows // spans
    states = dl_ref.shape[0]
    rank = tw_ref.shape[0]
    length = ints_ref[0]
    sel = sel_ref[...]
    step_pre = dot(sel[:, :rank].astype(BF16), tw_ref[...]) + tb_ref[0:1, :].astype(F32)
    pre_ref[...] = step_pre
    live = (step_tokens(rows, steps) < length).astype(F32)
    delta = (jnp.maximum(step_pre, 0.0) + jnp.log1p(jnp.exp(-jnp.abs(step_pre)))) * live
    delta_ref[...] = delta
    drive[...] = delta * act_ref[...].astype(F32)
    b_ref[...] = spread(sel[:, rank : rank + states], states)
    decay_rows(dl_ref, rate_ref, log2e)

    for group in range(width // lanes):
        here = slice(group * lanes, (group + 1) * lanes)

        def advance(step, carry):
            d = delta_ref[step_ds(step), here]
            w = drive[step_ds(step), here]
            out = []
            for n in range(states):
                a = jnp.exp2(d * rate_ref[n, :, here])
                out.append(a * carry[n] + w * b_ref[step_ds(step), n * lanes : (n + 1) * lanes])
            return tuple(out)

        ends = lax.fori_loop(0, steps, advance, (jnp.zeros((spans, lanes), F32),) * states)
        for n in range(states):
            reach_ref[n, :, here] = ends[n]

    total = span_sum_kernel_part(delta_ref, steps)
    index2 = span_index((spans, width))
    part = total
    shift = 1
    while shift < spans:
        inside = index2 >= shift
        for n in range(states):
            own = reach_ref[n]
            earlier = jnp.where(inside, shift_spans(own, shift), 0.0)
            reach_ref[n] = own + jnp.exp2(part * rate_ref[n]) * earlier
        part = part + jnp.where(inside, shift_spans(part, shift), 0.0)
        shift *= 2
    cum_ref[...] = part
    sums = part[spans - 1 : spans, :]
    high = sums.astype(BF16)
    mid = (sums - high.astype(F32)).astype(BF16)
    low = (sums - high.astype(F32) - mid.astype(F32)).astype(BF16)
    ends = jnp.concatenate([reach_ref[n, spans - 1 : spans, :] for n in range(states)], axis=0)
    extra = jnp.concatenate(
        [high.astype(F32), mid.astype(F32), low.astype(F32), jnp.zeros((5, width), F32)], axis=0
    )
    send_ref[...] = jnp.concatenate([ends, extra], axis=0).astype(BF16)


def segment_sum(table_ref, index, states):
    block = table_ref[index].astype(F32)
    return block[:states], block[states : states + 1] + block[states + 1 : states + 2] + block[states + 2 : states + 3]


def forward_out_kernel(
    table_ref, parents_ref, me_ref, dl_ref, reach_ref, cum_ref, delta_ref, act_ref, sel_ref,
    hid_ref, wg_ref, wgo_ref, skip_ref, ow_ref, owo_ref,
    starts_ref, mpre_ref, gate_ref, mixed_ref, part_ref,
    finals, drive, b_ref, c_ref, rate_ref,
):
    rows, width = act_ref.shape
    steps = rows // spans
    states = dl_ref.shape[0]
    rank = sel_ref.shape[1] - 2 * states
    count = table_ref.shape[0]
    me = me_ref[0]
    decay_rows(dl_ref, rate_ref, log2e)
    rate = -jnp.exp(dl_ref[...]) * log2e

    def start_of(target):
        above = parents_ref[target]
        return finals[jnp.maximum(above, 0)] * (above >= 0).astype(F32)

    def visit(target, carry):
        end, total = segment_sum(table_ref, target, states)
        finals[target] = jnp.exp2(rate * total) * start_of(target) + end
        return carry

    finals[0] = jnp.zeros(finals.shape[1:], F32)
    lax.fori_loop(0, count, visit, 0)
    start = start_of(me)
    sel = sel_ref[...]
    drive[...] = delta_ref[...] * act_ref[...].astype(F32)
    b_ref[...] = spread(sel[:, rank : rank + states], states)
    c_ref[...] = spread(sel[:, rank + states :], states)
    index2 = span_index((spans, width))
    cum = jnp.where(index2 >= 1, shift_spans(cum_ref[...], 1), 0.0)
    for n in range(states):
        earlier = jnp.where(index2 >= 1, shift_spans(reach_ref[n], 1), 0.0)
        starts_ref[n] = jnp.exp2(cum * rate_ref[n]) * start[n : n + 1, :] + earlier

    for group in range(width // lanes):
        here = slice(group * lanes, (group + 1) * lanes)

        def advance(step, carry):
            d = delta_ref[step_ds(step), here]
            w = drive[step_ds(step), here]
            out = []
            reads = [None] * 4
            for n in range(states):
                a = jnp.exp2(d * rate_ref[n, :, here])
                now = a * carry[n] + w * b_ref[step_ds(step), n * lanes : (n + 1) * lanes]
                out.append(now)
                term = c_ref[step_ds(step), n * lanes : (n + 1) * lanes] * now
                reads[n % 4] = term if reads[n % 4] is None else reads[n % 4] + term
            mpre_ref[step_ds(step), here] = (reads[0] + reads[1]) + (reads[2] + reads[3])
            return tuple(out)

        lax.fori_loop(0, steps, advance, tuple(starts_ref[n, :, here] for n in range(states)))

    gate = dot(hid_ref[0], wg_ref[...]) + dot(hid_ref[1], wgo_ref[...])
    gate_ref[...] = gate
    mixed_pre = mpre_ref[...] + skip_ref[0:1, :].astype(F32) * act_ref[...].astype(F32)
    mpre_ref[...] = mixed_pre
    mixed = (mixed_pre * (gate * sigmoid(gate))).astype(BF16)
    mixed_ref[...] = mixed
    natural = dot(to_tokens(rows, steps), mixed).astype(BF16)
    part_ref[0] = dot(natural, ow_ref[...]).astype(BF16)
    part_ref[1] = dot(natural, owo_ref[...]).astype(BF16)


def backward_in_kernel(
    cot_ref, mixed_ref, ow_ref, owo_ref, gate_ref, mpre_ref, act_ref, skip_ref, sel_ref,
    delta_ref, dl_ref, cum_ref, hid_ref,
    og_ref, ggrad_ref, ig_ref, pgrad_ref, sgrad_ref, back_ref, flow_ref,
    c_ref, rate_ref,
):
    rows, width = act_ref.shape
    steps = rows // spans
    states = dl_ref.shape[0]
    rank = sel_ref.shape[1] - 2 * states
    order = to_steps(rows, steps)
    cot = dot(order, cot_ref[0]).astype(BF16)
    coto = dot(order, cot_ref[1]).astype(BF16)
    mixed_grad = dot_nt(cot, ow_ref[...]) + dot_nt(coto, owo_ref[...])
    gate = gate_ref[...]
    sigma = sigmoid(gate)
    pre_grad = mixed_grad * (gate * sigma)
    pgrad_ref[...] = pre_grad
    gate_grad = (mixed_grad * mpre_ref[...] * slope_of(gate, sigma)).astype(BF16)
    ggrad_ref[...] = gate_grad
    sgrad_ref[...] = jnp.broadcast_to(
        jnp.sum(pre_grad * act_ref[...].astype(F32), axis=0, keepdims=True), sgrad_ref.shape
    )
    c_ref[...] = spread(sel_ref[:, rank + states :], states)
    decay_rows(dl_ref, rate_ref, log2e)

    for group in range(width // lanes):
        here = slice(group * lanes, (group + 1) * lanes)

        def retreat(back, carry):
            step = steps - 1 - back
            d = delta_ref[step_ds(step), here]
            p = pgrad_ref[step_ds(step), here]
            out = []
            for n in range(states):
                a = jnp.exp2(d * rate_ref[n, :, here])
                out.append(a * (c_ref[step_ds(step), n * lanes : (n + 1) * lanes] * p + carry[n]))
            return tuple(out)

        flows = lax.fori_loop(0, steps, retreat, (jnp.zeros((spans, lanes), F32),) * states)
        for n in range(states):
            back_ref[n, :, here] = flows[n]

    index2 = span_index((spans, width))
    cum = cum_ref[...]
    part = cum - jnp.where(index2 >= 1, shift_spans(cum, 1), 0.0)
    shift = 1
    while shift < spans:
        inside = index2 < spans - shift
        for n in range(states):
            own = back_ref[n]
            later = jnp.where(inside, shift_spans(own, -shift), 0.0)
            back_ref[n] = own + jnp.exp2(part * rate_ref[n]) * later
        part = part + jnp.where(inside, shift_spans(part, -shift), 0.0)
        shift *= 2
    flow_ref[...] = jnp.concatenate(
        [back_ref[n, 0:1, :] for n in range(states)], axis=0
    ).astype(BF16)
    og_ref[0] = dot_tn(mixed_ref[...], cot).astype(BF16)
    og_ref[1] = dot_tn(mixed_ref[...], coto).astype(BF16)
    ig_ref[0] = dot_tn(hid_ref[0], gate_grad).astype(BF16)
    ig_ref[1] = dot_tn(hid_ref[1], gate_grad).astype(BF16)


def backward_scan_kernel(
    table_ref, flows_ref, parents_ref, me_ref, length_ref, dl_ref, starts_ref, back_ref, cum_ref,
    delta_ref, act_ref, sel_ref, pgrad_ref, pre_ref, tw_ref,
    selg_ref, agrad_ref, small_ref, stepg_ref, dgrad_ref,
    grads, drive, b_ref, c_ref, rate_ref, decay_buf, state_buf, b_sum, c_sum, dg_ref,
):
    rows, width = act_ref.shape
    steps = rows // spans
    states = dl_ref.shape[0]
    rank = tw_ref.shape[0]
    count = table_ref.shape[0]
    me = me_ref[0]
    rate = -jnp.exp(dl_ref[...]) * log2e
    decay_rows(dl_ref, rate_ref, log2e)
    grads[...] = jnp.zeros(grads.shape, F32)

    def visit(visited, carry):
        target = count - 1 - visited
        _, total = segment_sum(table_ref, target, states)
        flow = flows_ref[target].astype(F32) + jnp.exp2(rate * total) * grads[target]
        above = parents_ref[target]
        slot = jnp.maximum(above, 0)
        grads[slot] = grads[slot] + flow * (above >= 0).astype(F32)
        return carry

    lax.fori_loop(0, count - 1, visit, 0)
    end_grad = grads[me]
    sel = sel_ref[...]
    drive[...] = delta_ref[...] * act_ref[...].astype(F32)
    b_ref[...] = spread(sel[:, rank : rank + states], states)
    c_ref[...] = spread(sel[:, rank + states :], states)
    index2 = span_index((spans, width))
    cum = cum_ref[...]
    after = cum[spans - 1 : spans, :] - cum
    inside = index2 < spans - 1

    for group in range(width // lanes):
        here = slice(group * lanes, (group + 1) * lanes)

        def advance(step, carry):
            d = delta_ref[step_ds(step), here]
            w = drive[step_ds(step), here]
            out = []
            for n in range(states):
                state_buf[n, step_ds(step), :] = carry[n]
                a = jnp.exp2(d * rate_ref[n, :, here])
                decay_buf[n, step_ds(step), :] = a
                out.append(a * carry[n] + w * b_ref[step_ds(step), n * lanes : (n + 1) * lanes])
            return tuple(out)

        finals = lax.fori_loop(0, steps, advance, tuple(starts_ref[n, :, here] for n in range(states)))
        for n in range(states):
            state_buf[n, rows : rows + spans, :] = finals[n]

        later = []
        for n in range(states):
            flow = jnp.where(inside[:, here], shift_spans(back_ref[n, :, here], -1), 0.0)
            later.append(flow + jnp.exp2(after[:, here] * rate_ref[n, :, here]) * end_grad[n : n + 1, here])

        def retreat(back, carry):
            step = steps - 1 - back
            at = step_ds(step)
            d = delta_ref[at, here]
            p = pgrad_ref[at, here]
            w = drive[at, here]
            flows, sums = carry
            new_flows, new_sums = [], []
            weighted = [None, None]
            decayed = [None, None]
            for n in range(states):
                cols = slice(n * lanes, (n + 1) * lanes)
                a = decay_buf[n, at, :]
                adjoint = c_ref[at, cols] * p + flows[n]
                moved = a * adjoint
                growth = moved * state_buf[n, at, :]
                new_flows.append(moved)
                new_sums.append(sums[n] + growth * d)
                term = adjoint * b_ref[at, cols]
                weighted[n % 2] = term if weighted[n % 2] is None else weighted[n % 2] + term
                term = growth * rate_ref[n, :, here]
                decayed[n % 2] = term if decayed[n % 2] is None else decayed[n % 2] + term
                b_term = adjoint * w
                c_term = state_buf[n, step_ds(step + 1), :] * p
                if group == 0:
                    b_sum[at, cols] = b_term
                    c_sum[at, cols] = c_term
                else:
                    b_sum[at, cols] += b_term
                    c_sum[at, cols] += c_term
            bw = weighted[0] + weighted[1]
            dg_ref[at, here] = (decayed[0] + decayed[1]) * (1.0 / log2e) + act_ref[at, here].astype(F32) * bw
            agrad_ref[at, here] = bw * d
            return (tuple(new_flows), tuple(new_sums))

        zero = jnp.zeros((spans, lanes), F32)
        _, sums = lax.fori_loop(0, steps, retreat, (tuple(later), (zero,) * states))
        for n in range(states):
            dgrad_ref[n : n + 1, here] = (
                jnp.sum(sums[n], axis=0, keepdims=True) * rate[n : n + 1, here] * (1.0 / log2e)
            )

    live = (step_tokens(rows, steps) < length_ref[0]).astype(F32)
    step_pre_grad = dg_ref[...] * live * sigmoid(pre_ref[...])
    small_ref[...] = jnp.broadcast_to(jnp.sum(step_pre_grad, axis=0, keepdims=True), small_ref.shape)
    low = step_pre_grad.astype(BF16)
    stepg_ref[...] = dot_tn(sel[:, :rank].astype(BF16), low)
    gather = gather_matrix(states)
    selg_ref[...] = jnp.concatenate(
        [dot_nt(low, tw_ref[...]), dot(b_sum[...].astype(BF16), gather), dot(c_sum[...].astype(BF16), gather)],
        axis=1,
    )


def backward_out_kernel(
    selg_ref, act_ref, sw_ref, agrad_ref, skip_ref, pgrad_ref, ext_ref, cw_ref, cb_ref,
    hid_ref, hidt_ref, wi_ref, wio_ref, wg_ref, wgo_ref, ggrad_ref,
    ig_ref, part_ref, tpart_ref, selw_ref, cgrad_ref,
    cig_ref,
):
    rows, width = act_ref.shape
    steps = rows // spans
    selg = selg_ref[...].astype(BF16)
    selw_ref[...] = dot_tn(selg, act_ref[...])
    active_grad = (
        agrad_ref[...] + skip_ref[0:1, :].astype(F32) * pgrad_ref[...] + dot_nt(selg, sw_ref[...])
    )
    pre = conv_pre(ext_ref, cw_ref, cb_ref, rows, width)
    conv_in = active_grad * slope_of(pre, sigmoid(pre))
    cig_ref[0:rows, :] = conv_in
    last_span = lax.broadcasted_iota(jnp.int32, (spans, width), 0) == spans - 1
    for j in range(3):
        block = jnp.roll(conv_in[j * spans : (j + 1) * spans], -1, axis=0)
        cig_ref[rows + j * spans : rows + (j + 1) * spans, :] = jnp.where(last_span, 0.0, block)
    taps = cw_ref[...].astype(F32)
    sums = [
        jnp.sum(conv_in * ext_ref[k * spans : k * spans + rows, :], axis=0, keepdims=True)
        for k in range(4)
    ]
    sums.append(jnp.sum(conv_in, axis=0, keepdims=True))
    sums.append(jnp.zeros((3, width), F32))
    cgrad_ref[...] = jnp.concatenate(sums, axis=0)
    inner_grad = jnp.zeros((rows, width), F32)
    for k in range(4):
        inner_grad = inner_grad + taps[k : k + 1, :] * cig_ref[(3 - k) * spans : (3 - k) * spans + rows, :]
    inner_low = inner_grad.astype(BF16)
    tails = [jnp.zeros((5, width), F32)]
    for i in range(3):
        row = jnp.zeros((1, width), F32)
        for k in range(i + 1):
            row = row + taps[k : k + 1, :] * conv_in[(i - k) * spans : (i - k) * spans + 1, :]
        tails.append(row)
    tail_low = jnp.concatenate(tails, axis=0).astype(BF16)
    order = to_tokens(rows, steps)
    natural = dot(order, inner_low).astype(BF16)
    naturalg = dot(order, ggrad_ref[...]).astype(BF16)
    for h, (wi, wg) in enumerate(((wi_ref, wg_ref), (wio_ref, wgo_ref))):
        part_ref[h] = (dot_nt(natural, wi[...]) + dot_nt(naturalg, wg[...])).astype(BF16)
        tpart_ref[h] = dot_nt(tail_low, wi[...])
        ig_ref[h] = (dot_tn(hid_ref[h], inner_low) + dot_tn(hidt_ref[h], tail_low)).astype(BF16)


def seq_bits(count):
    bits = []
    mask = 1
    while mask < count:
        bits.append(mask)
        mask *= 2
    return bits


def mask_order(count, swapped):
    bits = seq_bits(count)
    if swapped and len(bits) > 1:
        bits = [bits[1], bits[0]] + bits[2:]
    return bits


def widen(values):
    return values.astype(F32)


class Chunk:
    def __init__(self, source, total, stages, send, recv, masks, crossed, emit):
        self.source, self.total, self.stages = source, total, stages
        self.send, self.recv, self.masks, self.crossed, self.emit = send, recv, masks, crossed, emit
        self.count = source.shape[0]
        self.me = lax.axis_index("seq")
        self.copies = []
        self.levels = len(masks)

    def bit(self, level):
        return (self.me // self.masks[level]) % 2

    def peer(self, level):
        mask = self.masks[level]
        return {"seq": self.me + mask - 2 * mask * self.bit(level)}

    def start(self, src, dst, peer):
        at = len(self.copies)
        copy = remote(src, dst, self.send.at[at], self.recv.at[at], peer)
        copy.start()
        self.copies.append(copy)

    def place(self, level):
        start = 0
        for j in range(level + 1):
            start = start + self.bit(j) * (self.count >> (j + 1))
        return start

    def held(self, level):
        return self.source if level == 0 else self.stages[level - 1]

    def halve(self, level):
        size = self.count >> (level + 1)
        away = self.held(level).at[pl.ds((1 - self.bit(level)) * size, size)]
        self.start(away, self.stages[level], self.peer(level))

    def add(self, level):
        size = self.count >> (level + 1)
        kept = self.held(level)[pl.ds(self.bit(level) * size, size)]
        got = self.stages[level]
        got[...] = (widen(kept) + widen(got[...])).astype(got.dtype)

    def double(self, level):
        size = self.count >> (level + 1)
        region = self.total.at[pl.ds(self.place(level), size)]
        self.start(region, region, self.peer(level))

    def step(self, index):
        last = self.levels
        if index > 0:
            if index > 2 * last + int(self.crossed):
                return False
            self.copies[index - 1].wait_recv()
        if index < last:
            if index > 0:
                self.add(index - 1)
            self.halve(index)
            return True
        at = index - last
        if at == 0:
            self.add(last - 1)
            piece = self.stages[last - 1]
            home = self.total.at[pl.ds(self.place(last - 1), 1)]
            if self.crossed:
                self.start(piece, home, col_peer())
                return True
            home[...] = piece[...]
        level = last - 1 - (at - int(self.crossed))
        if level >= 0:
            self.double(level)
        else:
            self.emit(self.total)
        return True

    def finish(self):
        for copy in self.copies:
            copy.wait_send()


def run_chunks(chunks):
    for chunk in chunks:
        chunk.step(0)
    begun = [1] * len(chunks)
    longest = max(2 * c.levels + int(c.crossed) for c in chunks)
    for tick in range(longest + len(chunks)):
        for i, chunk in enumerate(chunks):
            if tick >= i and begun[i] <= 2 * chunk.levels + int(chunk.crossed):
                chunk.step(begun[i])
                begun[i] += 1
    for chunk in chunks:
        chunk.finish()


def grad_kernel(og_ref, igg_ref, igi_ref, small_ref, og_out, ig_out, small_out, totals, *rest):
    count = og_ref.shape[1]
    levels = len(seq_bits(count))
    halves, smalls, send, recv = rest[:levels], rest[levels : 2 * levels], rest[-2], rest[-1]
    col = lax.axis_index("col")
    me = lax.axis_index("seq")
    rows, width = og_ref.shape[2], og_ref.shape[3]

    def rows_out(side):
        def emit(total):
            for i in range(count):
                at = pl.multiple_of(side * count * rows, count * rows) + i * rows
                og_out[pl.ds(pl.multiple_of(at, 8), rows), :] = widen(total[i])
        return emit

    def lanes_out(which, side):
        def emit(total):
            at = pl.multiple_of(side * width, width)
            for i in range(count):
                ig_out[which, i * rows : (i + 1) * rows, pl.ds(at, width)] = widen(total[i])
        return emit

    def small_emit(total):
        pass

    peers = [
        {"seq": me + mask - 2 * mask * ((me // mask) % 2)} for mask in seq_bits(count)
    ]
    barrier_with([col_peer()] + peers)
    chunks = []
    plan = [
        (og_ref, 0, rows_out(col), False),
        (og_ref, 1, rows_out(1 - col), False),
        (igg_ref, 0, lanes_out(1, col), True),
        (igg_ref, 1, lanes_out(1, 1 - col), True),
        (igi_ref, 0, lanes_out(0, col), False),
        (igi_ref, 1, lanes_out(0, 1 - col), False),
    ]
    for i, (source, h, emit, swapped) in enumerate(plan):
        chunks.append(
            Chunk(
                source.at[h], totals.at[i], [s.at[i] for s in halves], send.at[i], recv.at[i],
                mask_order(count, swapped), h == 1, emit,
            )
        )
    chunks.append(
        Chunk(
            small_ref, small_out, smalls, send.at[len(plan)], recv.at[len(plan)],
            mask_order(count, False), False, small_emit,
        )
    )
    run_chunks(chunks)


def grad_sum(og, igg, igi, small):
    _, count, rows, width = og.shape
    levels = len(seq_bits(count))
    scratch = [pltpu.VMEM((6, count, rows, width), BF16)]
    scratch += [pltpu.VMEM((6, count >> (k + 1), rows, width), BF16) for k in range(levels)]
    scratch += [pltpu.VMEM((count >> (k + 1),) + small.shape[1:], F32) for k in range(levels)]
    scratch += [pltpu.SemaphoreType.DMA((7, 2 * levels + 1))] * 2
    return run_kernel(
        grad_kernel,
        (
            struct((2 * count * rows, width), F32),
            struct((2, count * rows, 2 * width), F32),
            struct(small.shape, F32),
        ),
        (og, igg, igi, small),
        "grad_sum",
        scratch=scratch,
        collective=9,
    )


def on_device(
    tokens_in, teacher, norm_gain, in_weight, conv_weight, conv_bias, select_weight, step_weight,
    step_bias, decay_log, skip_gain, out_weight, parents, lengths, valid_rows,
):
    rows, width = tokens_in.shape
    half = norm_gain.shape[0]
    inner = decay_log.shape[1]
    states = decay_log.shape[0]
    rank = step_weight.shape[0]
    selects = rank + 2 * states
    steps = rows // spans
    count = lax.axis_size("seq")
    row_len = rows // lax.axis_size("row")
    row = lax.axis_index("row")
    col = lax.axis_index("col")
    me = lax.axis_index("seq")
    my_len = lengths[me][None]
    my_parent = parents[me][None]
    my_valid = valid_rows[me][None]
    me1 = me.astype(jnp.int32)[None]
    scale = jnp.full((8, lanes), 1.0, F32) * (rows * count / jnp.sum(valid_rows).astype(F32))

    def halves(value, axis):
        size = value.shape[axis] // 2
        own = lax.dynamic_slice_in_dim(value, col * size, size, axis)
        other = lax.dynamic_slice_in_dim(value, (1 - col) * size, size, axis)
        return own, other

    def rows8(value):
        return jnp.broadcast_to(value[None, :], (8, value.shape[0]))

    swap = [(0, 1), (1, 0)]
    tok, toko = halves(tokens_in, 1)
    tail = lax.dynamic_slice_in_dim(tokens_in, my_len[0] - 8, 8, 0)
    w_own, w_send = halves(in_weight, 2)
    wi, wg = w_own[:, 0], w_own[:, 1]
    wi_send, wg_send = w_send[:, 0], w_send[:, 1]
    ow, ow_send = halves(out_weight, 0)
    gain = rows8(norm_gain)
    skip = rows8(skip_gain)
    conv_b = rows8(conv_bias)
    step_b = rows8(step_bias)

    tails, wio, gaino = entry_exchange(tail, wi_send, gain, count)
    wg_send, ow_send, wio = lax.optimization_barrier((wg_send, ow_send, wio))
    wgo = lax.ppermute(wg_send, "col", swap)
    owo = lax.ppermute(ow_send, "col", swap)
    tails_own, tails_oth = halves(tails, 2)

    hid, hid_tail, ext, act, sel_part = run_kernel(
        forward_in_kernel,
        (
            struct((2, rows, half), BF16),
            struct((2, 8, half), BF16),
            struct((rows + 3 * spans, inner), F32),
            struct((rows, inner), BF16),
            struct((rows, selects), F32),
        ),
        (tok, toko, tails_own, tails_oth, gain, gaino, wi, wio, conv_weight, conv_b, select_weight, my_parent),
        "forward_in",
        flops=2e9,
    )
    sel = quad_sum(sel_part, 1, "select_sum")
    delta, step_pre, reach, cum, seg_map = run_kernel(
        forward_ends_kernel,
        (
            struct((rows, inner), F32),
            struct((rows, inner), F32),
            struct((states, spans, inner), F32),
            struct((spans, inner), F32),
            struct((states + 8, inner), BF16),
        ),
        (sel, step_weight, step_b, decay_log, act, my_len),
        "forward_ends",
        scratch=[
            pltpu.VMEM((rows, inner), F32),
            pltpu.VMEM((rows, states * lanes), F32),
            pltpu.VMEM((states, spans, inner), F32),
        ],
        flops=2e9,
    )
    table = seq_gather(seg_map, count, 2, "state_gather")
    starts, mixed_pre, gate, mixed, part = run_kernel(
        forward_out_kernel,
        (
            struct((states, spans, inner), F32),
            struct((rows, inner), F32),
            struct((rows, inner), F32),
            struct((rows, inner), BF16),
            struct((2, rows, half), BF16),
        ),
        (
            table, parents, me1, decay_log, reach, cum, delta, act, sel, hid, wg, wgo, skip, ow, owo,
        ),
        "forward_out",
        scratch=[
            pltpu.VMEM((count, states, inner), F32),
            pltpu.VMEM((rows, inner), F32),
            pltpu.VMEM((rows, states * lanes), F32),
            pltpu.VMEM((rows, states * lanes), F32),
            pltpu.VMEM((states, spans, inner), F32),
        ],
        flops=4e9,
    )
    tok_tile = lax.dynamic_slice_in_dim(tok, row * row_len, row_len, 0)
    toko_tile = lax.dynamic_slice_in_dim(toko, row * row_len, row_len, 0)
    teach_tile = lax.dynamic_slice_in_dim(teacher, row * row_len, row_len, 0)
    output, cot_tile, cot = middle_exchange(part, tok_tile, teach_tile, my_valid, scale)
    out_part, gate_grad, ig_gate, pre_grad, skip_part, back, flow = run_kernel(
        backward_in_kernel,
        (
            struct((2, inner, half), BF16),
            struct((rows, inner), BF16),
            struct((2, half, inner), BF16),
            struct((rows, inner), F32),
            struct((8, inner), F32),
            struct((states, spans, inner), F32),
            struct((states, inner), BF16),
        ),
        (cot, mixed, ow, owo, gate, mixed_pre, act, skip, sel, delta, decay_log, cum, hid),
        "backward_in",
        scratch=[
            pltpu.VMEM((rows, states * lanes), F32),
            pltpu.VMEM((states, spans, inner), F32),
        ],
        flops=4e9,
    )
    flows = seq_gather(flow, count, 4, "flow_gather")
    selg_part, active_grad, step_bias_part, step_part, decay_part = run_kernel(
        backward_scan_kernel,
        (
            struct((rows, selects), F32),
            struct((rows, inner), F32),
            struct((8, inner), F32),
            struct((rank, inner), F32),
            struct((states, inner), F32),
        ),
        (
            table, flows, parents, me1, my_len, decay_log, starts, back, cum, delta, act, sel,
            pre_grad, step_pre, step_weight,
        ),
        "backward_scan",
        scratch=[
            pltpu.VMEM((count, states, inner), F32),
            pltpu.VMEM((rows, inner), F32),
            pltpu.VMEM((rows, states * lanes), F32),
            pltpu.VMEM((rows, states * lanes), F32),
            pltpu.VMEM((states, spans, inner), F32),
            pltpu.VMEM((states, rows, lanes), F32),
            pltpu.VMEM((states, rows + spans, lanes), F32),
            pltpu.VMEM((rows, states * lanes), F32),
            pltpu.VMEM((rows, states * lanes), F32),
            pltpu.VMEM((rows, inner), F32),
        ],
        flops=8e9,
    )
    selg = quad_sum(selg_part, 7, "select_grad_sum")
    ig_inner, hid_part, tail_part, select_part, conv_part = run_kernel(
        backward_out_kernel,
        (
            struct((2, half, inner), BF16),
            struct((2, rows, half), BF16),
            struct((2, 8, half), F32),
            struct((selects, inner), F32),
            struct((8, inner), F32),
        ),
        (
            selg, act, select_weight, active_grad, skip, pre_grad, ext, conv_weight, conv_b,
            hid, hid_tail, wi, wio, wg, wgo, gate_grad,
        ),
        "backward_out",
        scratch=[pltpu.VMEM((rows + 3 * spans, inner), F32)],
        flops=6e9,
    )
    hid_tile, tail_tile = hidden_exchange(hid_part, tail_part)
    tail_table = seq_gather(
        jnp.concatenate([tail_tile[5:8], tail_tile[:5]], axis=0), count, 8, "tail_gather"
    )
    tokens_grad, gain_part = finish_exchange(
        hid_tile, tail_table, tok_tile, toko_tile, gain, cot_tile, parents, lengths, width
    )

    small = jnp.concatenate(
        [
            step_part, decay_part, select_part, conv_part[:5], skip_part[:1], step_bias_part[:1],
            gain_part[:1],
        ],
        axis=0,
    )
    pad = -small.shape[0] % (8 * count)
    small = jnp.pad(small, ((0, pad), (0, 0)))

    def split(value):
        return value.reshape(2, count, value.shape[1] // count, value.shape[2])

    out_grad, in_both, small = grad_sum(
        split(out_part), split(ig_gate), split(ig_inner), small.reshape(count, -1, inner)
    )
    small = small.reshape(-1, inner)
    in_grad = in_both.transpose(1, 0, 2)
    at = 0
    pieces = []
    for size in (rank, states, selects, 4, 1, 1, 1, 1):
        pieces.append(small[at : at + size])
        at += size
    step_grad, decay_grad, select_grad, conv_grad, conv_bias_grad, skip_grad, step_bias_grad, gain_grad = pieces
    return (
        output,
        tokens_grad,
        gain_grad[0],
        in_grad,
        conv_grad,
        conv_bias_grad[0],
        select_grad.T,
        step_grad,
        step_bias_grad[0],
        decay_grad,
        skip_grad[0],
        out_grad,
    )


def solution(mesh):
    placed = (
        P("seq", None),
        P("seq", "col"),
        P("col"),
        P("col", None, "row"),
        P(None, ("row", "col")),
        P(("row", "col")),
        P(("row", "col"), None),
        P(None, ("row", "col")),
        P(("row", "col")),
        P(None, ("row", "col")),
        P(("row", "col")),
        P("row", "col"),
        P(),
        P(),
        P(),
    )
    return jax.shard_map(
        on_device,
        mesh=mesh,
        in_specs=placed,
        out_specs=(
            P(("seq", "row"), "col"),
            P(("seq", "row"), "col"),
            P("col"),
            P("col", None, "row"),
            P(None, ("row", "col")),
            P(("row", "col")),
            P(("row", "col"), None),
            P(None, ("row", "col")),
            P(("row", "col")),
            P(None, ("row", "col")),
            P(("row", "col")),
            P("row", "col"),
        ),
        check_vma=False,
    )
```

```python
import functools

import jax
import jax.numpy as jnp
from jax import lax
from jax.experimental import pallas as pl
from jax.experimental.pallas import tpu as pltpu
from jax.sharding import PartitionSpec as P

MESH = pl.DeviceIdType.MESH
F32 = jnp.float32
BF16 = jnp.bfloat16
norm_epsilon = 1e-05
spans = 8
lanes = 128
log2e = 1.4426950408889634
vmem_bytes = 60 * 1024 * 1024
vmem_most = 67043328


def vmem_spec():
    return pl.BlockSpec(memory_space=pltpu.VMEM)


def smem_spec():
    return pl.BlockSpec(memory_space=pltpu.SMEM)


def struct(shape, dtype):
    return jax.ShapeDtypeStruct(shape, dtype)


def dot(a, b):
    return jnp.dot(a, b, preferred_element_type=F32)


def dot_tn(a, b):
    return lax.dot_general(a, b, (((0,), (0,)), ((), ())), preferred_element_type=F32)


def dot_nt(a, b):
    return lax.dot_general(a, b, (((1,), (1,)), ((), ())), preferred_element_type=F32)


def sigmoid(v):
    return 1.0 / (1.0 + jnp.exp(-v))


def slope_of(v, sigma):
    return sigma * (1.0 + v * (1.0 - sigma))


def to_steps(rows, steps):
    place = lax.broadcasted_iota(jnp.int32, (rows, rows), 0)
    token = lax.broadcasted_iota(jnp.int32, (rows, rows), 1)
    return (token == (place % spans) * steps + place // spans).astype(F32).astype(BF16)


def to_tokens(rows, steps):
    token = lax.broadcasted_iota(jnp.int32, (rows, rows), 0)
    place = lax.broadcasted_iota(jnp.int32, (rows, rows), 1)
    return (token == (place % spans) * steps + place // spans).astype(F32).astype(BF16)


def step_tokens(rows, steps):
    place = lax.broadcasted_iota(jnp.int32, (rows, 1), 0)
    return (place % spans) * steps + place // spans


def spread_matrix(states):
    row = lax.broadcasted_iota(jnp.int32, (2 * states, states * lanes), 0)
    col = lax.broadcasted_iota(jnp.int32, (2 * states, states * lanes), 1)
    return (row % states == col // lanes).astype(F32).astype(BF16)


def gather_matrix(states):
    row = lax.broadcasted_iota(jnp.int32, (states * lanes, states), 0)
    col = lax.broadcasted_iota(jnp.int32, (states * lanes, states), 1)
    return (row // lanes == col).astype(F32).astype(BF16)


def spread(values, states):
    high = values.astype(BF16)
    rest = (values - high.astype(F32)).astype(BF16)
    return dot(jnp.concatenate([high, rest], axis=1), spread_matrix(states))


def shift_spans(values, amount):
    return jnp.roll(values, amount, axis=values.ndim - 2)


def span_index(shape):
    return lax.broadcasted_iota(jnp.int32, shape, len(shape) - 2)


def run_kernel(kernel, outs, args, name, scratch=(), flops=0, collective=None, grant=vmem_bytes):
    params = dict(vmem_limit_bytes=grant)
    if collective is not None:
        params.update(collective_id=collective, has_side_effects=True)
    return pl.pallas_call(
        kernel,
        out_shape=outs,
        in_specs=[
            smem_spec() if a.dtype == jnp.int32 else vmem_spec() for a in args
        ],
        out_specs=jax.tree.map(lambda _: vmem_spec(), outs),
        scratch_shapes=list(scratch),
        compiler_params=pltpu.CompilerParams(**params),
        cost_estimate=pl.CostEstimate(
            flops=int(flops),
            transcendentals=0,
            bytes_accessed=int(sum(a.size * a.dtype.itemsize for a in args)),
        ),
        name=name,
    )(*args)


def barrier_with(peers):
    barrier = pltpu.get_barrier_semaphore()
    for peer in peers:
        pl.semaphore_signal(barrier, inc=1, device_id=peer, device_id_type=MESH)
    pl.semaphore_wait(barrier, len(peers))


def remote(src, dst, send, recv, peer):
    return pltpu.make_async_remote_copy(
        src_ref=src, dst_ref=dst, send_sem=send, recv_sem=recv, device_id=peer, device_id_type=MESH
    )


def row_peer():
    return {"row": 1 - lax.axis_index("row")}


def col_peer():
    return {"col": 1 - lax.axis_index("col")}


def entry_kernel(tail_ref, wi_ref, gain_ref, tails_ref, wo_ref, gain_o_ref, tsend, trecv, csend, crecv):
    count = tails_ref.shape[0]
    me = lax.axis_index("seq")
    peers = [{"seq": lax.rem(me + j, count)} for j in range(1, count)]
    barrier_with([col_peer()] + peers)
    copies = []
    for j, peer in enumerate(peers):
        copies.append(remote(tail_ref, tails_ref.at[me], tsend.at[j], trecv.at[j], peer))
    copies.append(remote(gain_ref, gain_o_ref, csend.at[0], crecv.at[0], col_peer()))
    copies.append(remote(wi_ref, wo_ref, csend.at[1], crecv.at[1], col_peer()))
    for copy in copies:
        copy.start()
    tails_ref[me] = tail_ref[...]
    for copy in copies:
        copy.wait()


def entry_exchange(tail, wi_send, gain_send, count):
    return run_kernel(
        entry_kernel,
        (
            struct((count,) + tail.shape, tail.dtype),
            struct(wi_send.shape, wi_send.dtype),
            struct(gain_send.shape, gain_send.dtype),
        ),
        (tail, wi_send, gain_send),
        "entry_exchange",
        scratch=[
            pltpu.SemaphoreType.DMA((count,)),
            pltpu.SemaphoreType.DMA((count,)),
            pltpu.SemaphoreType.DMA((2,)),
            pltpu.SemaphoreType.DMA((2,)),
        ],
        collective=0,
    )


def seq_gather_kernel(x_ref, o_ref, send, recv):
    count = o_ref.shape[0]
    me = lax.axis_index("seq")
    peers = [{"seq": lax.rem(me + j, count)} for j in range(1, count)]
    barrier_with(peers)
    copies = [
        remote(x_ref, o_ref.at[me], send.at[j], recv.at[j], peer) for j, peer in enumerate(peers)
    ]
    for copy in copies:
        copy.start()
    o_ref[me] = x_ref[...]
    for copy in copies:
        copy.wait()


def seq_gather(x, count, collective, name):
    return run_kernel(
        seq_gather_kernel,
        struct((count,) + x.shape, x.dtype),
        (x,),
        name,
        scratch=[pltpu.SemaphoreType.DMA((count,)), pltpu.SemaphoreType.DMA((count,))],
        collective=collective,
    )


def quad_sum_kernel(x_ref, o_ref, from_row, to_col, from_col, send, recv):
    barrier_with([row_peer(), col_peer()])
    first = remote(x_ref, from_row, send.at[0], recv.at[0], row_peer())
    first.start()
    first.wait()
    pair = x_ref[...] + from_row[...]
    to_col[...] = pair.astype(BF16)
    second = remote(to_col, from_col, send.at[1], recv.at[1], col_peer())
    second.start()
    o_ref[...] = pair
    second.wait()
    o_ref[...] += from_col[...].astype(F32)


def quad_sum(x, collective, name):
    return run_kernel(
        quad_sum_kernel,
        struct(x.shape, F32),
        (x,),
        name,
        scratch=[
            pltpu.VMEM(x.shape, F32),
            pltpu.VMEM(x.shape, BF16),
            pltpu.VMEM(x.shape, BF16),
            pltpu.SemaphoreType.DMA((2,)),
            pltpu.SemaphoreType.DMA((2,)),
        ],
        collective=collective,
    )


def middle_kernel(
    part_ref, tok_ref, teach_ref, ints_ref, scale_ref,
    out_ref, cot_ref, low_ref,
    from_row, to_col, from_col, send, recv,
):
    half = tok_ref.shape[0]
    row = lax.axis_index("row")
    mine = pl.multiple_of(row * half, half)
    other = pl.multiple_of((1 - row) * half, half)
    barrier_with([row_peer(), col_peer()])
    first = [
        remote(part_ref.at[h, pl.ds(other, half), :], from_row.at[h], send.at[h], recv.at[h], row_peer())
        for h in (1, 0)
    ]
    for copy in first:
        copy.start()
    first[0].wait()
    to_col[...] = (
        part_ref[1, pl.ds(mine, half), :].astype(F32) + from_row[1].astype(F32)
    ).astype(BF16)
    second = remote(to_col, from_col, send.at[2], recv.at[2], col_peer())
    second.start()
    first[1].wait()
    tile = part_ref[0, pl.ds(mine, half), :].astype(F32) + from_row[0].astype(F32)
    tile = tile + tok_ref[...].astype(F32)
    second.wait()
    result = tile + from_col[...].astype(F32)
    out_ref[...] = result.astype(BF16)
    positions = mine + lax.broadcasted_iota(jnp.int32, (half, 1), 0)
    counted = (positions < ints_ref[0]).astype(F32) * scale_ref[0:1, 0:1]
    cot = (result - teach_ref[...].astype(F32)) * counted
    cot_ref[...] = cot
    low_ref[0, pl.ds(mine, half), :] = cot.astype(BF16)
    third = [
        remote(low_ref.at[0, pl.ds(mine, half), :], low_ref.at[1, pl.ds(mine, half), :], send.at[3], recv.at[3], col_peer()),
        remote(low_ref.at[0, pl.ds(mine, half), :], low_ref.at[0, pl.ds(mine, half), :], send.at[4], recv.at[4], row_peer()),
    ]
    for copy in third:
        copy.start()
    third[0].wait()
    fourth = remote(low_ref.at[1, pl.ds(mine, half), :], low_ref.at[1, pl.ds(mine, half), :], send.at[5], recv.at[5], row_peer())
    fourth.start()
    third[1].wait()
    fourth.wait()


def middle_exchange(part, tok_tile, teach_tile, my_valid, scale):
    _, rows, width = part.shape
    half = rows // 2
    return run_kernel(
        middle_kernel,
        (struct((half, width), BF16), struct((half, width), F32), struct((2, rows, width), BF16)),
        (part, tok_tile, teach_tile, my_valid, scale),
        "middle_exchange",
        scratch=[
            pltpu.VMEM((2, half, width), BF16),
            pltpu.VMEM((half, width), BF16),
            pltpu.VMEM((half, width), BF16),
            pltpu.SemaphoreType.DMA((6,)),
            pltpu.SemaphoreType.DMA((6,)),
        ],
        collective=3,
    )


def forward_in_kernel(
    tok_ref, toko_ref, tails_ref, tailso_ref, gain_ref, gaino_ref, wi_ref, wio_ref,
    cw_ref, cb_ref, sw_ref, ints_ref,
    hid_ref, hidt_ref, ext_ref, act_ref, sel_ref,
):
    rows, half = tok_ref.shape
    steps = rows // spans
    width = 2 * half
    parent = jnp.maximum(ints_ref[0], 0)
    present = (ints_ref[0] >= 0).astype(F32)
    gain = gain_ref[0:1, :].astype(F32)
    gaino = gaino_ref[0:1, :].astype(F32)

    def hidden_of(own, other):
        own = own.astype(F32)
        other = other.astype(F32)
        total = jnp.sum(own * own, axis=1, keepdims=True) + jnp.sum(other * other, axis=1, keepdims=True)
        inv = lax.rsqrt(total / width + norm_epsilon)
        return (own * inv * gain).astype(BF16), (other * inv * gaino).astype(BF16)

    hid, hido = hidden_of(tok_ref[...], toko_ref[...])
    order = to_steps(rows, steps)
    hid = dot(order, hid).astype(BF16)
    hido = dot(order, hido).astype(BF16)
    hid_ref[0] = hid
    hid_ref[1] = hido
    inner = dot(hid, wi_ref[...]) + dot(hido, wio_ref[...])
    tail, tailo = hidden_of(tails_ref[parent], tailso_ref[parent])
    hidt_ref[0] = tail
    hidt_ref[1] = tailo
    tail_inner = (dot(tail, wi_ref[...]) + dot(tailo, wio_ref[...])) * present
    last = inner[rows - 3 * spans :]
    first_span = lax.broadcasted_iota(jnp.int32, (spans, half), 0) == 0
    for j in range(3):
        block = jnp.roll(last[j * spans : (j + 1) * spans], 1, axis=0)
        ext_ref[j * spans : (j + 1) * spans, :] = jnp.where(
            first_span, jnp.broadcast_to(tail_inner[5 + j : 6 + j, :], (spans, half)), block
        )
    ext_ref[3 * spans :, :] = inner
    taps = cw_ref[...].astype(F32)
    pre = jnp.broadcast_to(cb_ref[0:1, :].astype(F32), (rows, half))
    for k in range(4):
        pre = pre + taps[k : k + 1, :] * ext_ref[k * spans : k * spans + rows, :]
    act = (pre * sigmoid(pre)).astype(BF16)
    act_ref[...] = act
    sel_ref[...] = dot(act, sw_ref[...])


def conv_pre(ext_ref, cw_ref, cb_ref, rows, half):
    taps = cw_ref[...].astype(F32)
    pre = jnp.broadcast_to(cb_ref[0:1, :].astype(F32), (rows, half))
    for k in range(4):
        pre = pre + taps[k : k + 1, :] * ext_ref[k * spans : k * spans + rows, :]
    return pre


def group_ds(group):
    return pl.ds(pl.multiple_of(group * lanes, lanes), lanes)


def step_ds(step):
    return pl.ds(pl.multiple_of(step * spans, spans), spans)


def decay_rows(decay_log_ref, decay_b, scale):
    states, width = decay_log_ref.shape
    rate = -jnp.exp(decay_log_ref[...]) * scale
    for n in range(states):
        decay_b[n] = jnp.broadcast_to(rate[n : n + 1, :], (spans, width))


def span_sum_kernel_part(delta_ref, steps):
    total = delta_ref[0:spans, :]
    for s in range(1, steps):
        total = total + delta_ref[s * spans : (s + 1) * spans, :]
    return total


def forward_ends_kernel(
    sel_ref, tw_ref, tb_ref, dl_ref, act_ref, ints_ref,
    delta_ref, pre_ref, reach_ref, cum_ref, send_ref,
    drive, b_ref, rate_ref,
):
    rows, width = act_ref.shape
    steps = rows // spans
    states = dl_ref.shape[0]
    rank = tw_ref.shape[0]
    length = ints_ref[0]
    sel = sel_ref[...]
    step_pre = dot(sel[:, :rank].astype(BF16), tw_ref[...]) + tb_ref[0:1, :].astype(F32)
    pre_ref[...] = step_pre
    live = (step_tokens(rows, steps) < length).astype(F32)
    delta = (jnp.maximum(step_pre, 0.0) + jnp.log1p(jnp.exp(-jnp.abs(step_pre)))) * live
    delta_ref[...] = delta
    drive[...] = delta * act_ref[...].astype(F32)
    b_ref[...] = spread(sel[:, rank : rank + states], states)
    decay_rows(dl_ref, rate_ref, log2e)

    for group in range(width // lanes):
        here = slice(group * lanes, (group + 1) * lanes)

        def advance(step, carry):
            d = delta_ref[step_ds(step), here]
            w = drive[step_ds(step), here]
            out = []
            for n in range(states):
                a = jnp.exp2(d * rate_ref[n, :, here])
                out.append(a * carry[n] + w * b_ref[step_ds(step), n * lanes : (n + 1) * lanes])
            return tuple(out)

        ends = lax.fori_loop(0, steps, advance, (jnp.zeros((spans, lanes), F32),) * states)
        for n in range(states):
            reach_ref[n, :, here] = ends[n]

    total = span_sum_kernel_part(delta_ref, steps)
    index2 = span_index((spans, width))
    part = total
    shift = 1
    while shift < spans:
        inside = index2 >= shift
        for n in range(states):
            own = reach_ref[n]
            earlier = jnp.where(inside, shift_spans(own, shift), 0.0)
            reach_ref[n] = own + jnp.exp2(part * rate_ref[n]) * earlier
        part = part + jnp.where(inside, shift_spans(part, shift), 0.0)
        shift *= 2
    cum_ref[...] = part
    sums = part[spans - 1 : spans, :]
    high = sums.astype(BF16)
    mid = (sums - high.astype(F32)).astype(BF16)
    low = (sums - high.astype(F32) - mid.astype(F32)).astype(BF16)
    ends = jnp.concatenate([reach_ref[n, spans - 1 : spans, :] for n in range(states)], axis=0)
    extra = jnp.concatenate(
        [high.astype(F32), mid.astype(F32), low.astype(F32), jnp.zeros((5, width), F32)], axis=0
    )
    send_ref[...] = jnp.concatenate([ends, extra], axis=0).astype(BF16)


def segment_sum(table_ref, index, states):
    block = table_ref[index].astype(F32)
    return block[:states], block[states : states + 1] + block[states + 1 : states + 2] + block[states + 2 : states + 3]


def forward_out_kernel(
    table_ref, parents_ref, me_ref, dl_ref, reach_ref, cum_ref, delta_ref, act_ref, sel_ref,
    hid_ref, wg_ref, wgo_ref, skip_ref, ow_ref, owo_ref,
    starts_ref, mpre_ref, gate_ref, mixed_ref, part_ref,
    finals, drive, b_ref, c_ref, rate_ref,
):
    rows, width = act_ref.shape
    steps = rows // spans
    states = dl_ref.shape[0]
    rank = sel_ref.shape[1] - 2 * states
    count = table_ref.shape[0]
    me = me_ref[0]
    decay_rows(dl_ref, rate_ref, log2e)
    rate = -jnp.exp(dl_ref[...]) * log2e

    def start_of(target):
        above = parents_ref[target]
        return finals[jnp.maximum(above, 0)] * (above >= 0).astype(F32)

    def visit(target, carry):
        end, total = segment_sum(table_ref, target, states)
        finals[target] = jnp.exp2(rate * total) * start_of(target) + end
        return carry

    finals[0] = jnp.zeros(finals.shape[1:], F32)
    lax.fori_loop(0, count, visit, 0)
    start = start_of(me)
    sel = sel_ref[...]
    drive[...] = delta_ref[...] * act_ref[...].astype(F32)
    b_ref[...] = spread(sel[:, rank : rank + states], states)
    c_ref[...] = spread(sel[:, rank + states :], states)
    index2 = span_index((spans, width))
    cum = jnp.where(index2 >= 1, shift_spans(cum_ref[...], 1), 0.0)
    for n in range(states):
        earlier = jnp.where(index2 >= 1, shift_spans(reach_ref[n], 1), 0.0)
        starts_ref[n] = jnp.exp2(cum * rate_ref[n]) * start[n : n + 1, :] + earlier

    for group in range(width // lanes):
        here = slice(group * lanes, (group + 1) * lanes)

        def advance(step, carry):
            d = delta_ref[step_ds(step), here]
            w = drive[step_ds(step), here]
            out = []
            reads = [None] * 4
            for n in range(states):
                a = jnp.exp2(d * rate_ref[n, :, here])
                now = a * carry[n] + w * b_ref[step_ds(step), n * lanes : (n + 1) * lanes]
                out.append(now)
                term = c_ref[step_ds(step), n * lanes : (n + 1) * lanes] * now
                reads[n % 4] = term if reads[n % 4] is None else reads[n % 4] + term
            mpre_ref[step_ds(step), here] = (reads[0] + reads[1]) + (reads[2] + reads[3])
            return tuple(out)

        lax.fori_loop(0, steps, advance, tuple(starts_ref[n, :, here] for n in range(states)))

    gate = dot(hid_ref[0], wg_ref[...]) + dot(hid_ref[1], wgo_ref[...])
    gate_ref[...] = gate
    mixed_pre = mpre_ref[...] + skip_ref[0:1, :].astype(F32) * act_ref[...].astype(F32)
    mpre_ref[...] = mixed_pre
    mixed = (mixed_pre * (gate * sigmoid(gate))).astype(BF16)
    mixed_ref[...] = mixed
    natural = dot(to_tokens(rows, steps), mixed).astype(BF16)
    part_ref[0] = dot(natural, ow_ref[...]).astype(BF16)
    part_ref[1] = dot(natural, owo_ref[...]).astype(BF16)


def backward_in_kernel(
    cot_ref, mixed_ref, ow_ref, owo_ref, gate_ref, mpre_ref, act_ref, skip_ref, sel_ref,
    delta_ref, dl_ref, cum_ref, hid_ref,
    og_ref, ggrad_ref, ig_ref, pgrad_ref, sgrad_ref, back_ref, flow_ref,
    c_ref, rate_ref,
):
    rows, width = act_ref.shape
    steps = rows // spans
    states = dl_ref.shape[0]
    rank = sel_ref.shape[1] - 2 * states
    order = to_steps(rows, steps)
    cot = dot(order, cot_ref[0]).astype(BF16)
    coto = dot(order, cot_ref[1]).astype(BF16)
    mixed_grad = dot_nt(cot, ow_ref[...]) + dot_nt(coto, owo_ref[...])
    gate = gate_ref[...]
    sigma = sigmoid(gate)
    pre_grad = mixed_grad * (gate * sigma)
    pgrad_ref[...] = pre_grad
    gate_grad = (mixed_grad * mpre_ref[...] * slope_of(gate, sigma)).astype(BF16)
    ggrad_ref[...] = gate_grad
    sgrad_ref[...] = jnp.broadcast_to(
        jnp.sum(pre_grad * act_ref[...].astype(F32), axis=0, keepdims=True), sgrad_ref.shape
    )
    c_ref[...] = spread(sel_ref[:, rank + states :], states)
    decay_rows(dl_ref, rate_ref, log2e)

    for group in range(width // lanes):
        here = slice(group * lanes, (group + 1) * lanes)

        def retreat(back, carry):
            step = steps - 1 - back
            d = delta_ref[step_ds(step), here]
            p = pgrad_ref[step_ds(step), here]
            out = []
            for n in range(states):
                a = jnp.exp2(d * rate_ref[n, :, here])
                out.append(a * (c_ref[step_ds(step), n * lanes : (n + 1) * lanes] * p + carry[n]))
            return tuple(out)

        flows = lax.fori_loop(0, steps, retreat, (jnp.zeros((spans, lanes), F32),) * states)
        for n in range(states):
            back_ref[n, :, here] = flows[n]

    index2 = span_index((spans, width))
    cum = cum_ref[...]
    part = cum - jnp.where(index2 >= 1, shift_spans(cum, 1), 0.0)
    shift = 1
    while shift < spans:
        inside = index2 < spans - shift
        for n in range(states):
            own = back_ref[n]
            later = jnp.where(inside, shift_spans(own, -shift), 0.0)
            back_ref[n] = own + jnp.exp2(part * rate_ref[n]) * later
        part = part + jnp.where(inside, shift_spans(part, -shift), 0.0)
        shift *= 2
    flow_ref[...] = jnp.concatenate(
        [back_ref[n, 0:1, :] for n in range(states)], axis=0
    ).astype(BF16)
    store_split(og_ref.at[0], dot_tn(mixed_ref[...], cot))
    store_split(og_ref.at[1], dot_tn(mixed_ref[...], coto))
    store_split(ig_ref.at[0], dot_tn(hid_ref[0], gate_grad))
    store_split(ig_ref.at[1], dot_tn(hid_ref[1], gate_grad))


def seq_bits(count):
    bits = []
    mask = 1
    while mask < count:
        bits.append(mask)
        mask *= 2
    return bits


def mask_order(count, swapped):
    bits = seq_bits(count)
    if swapped and len(bits) > 1:
        bits = [bits[1], bits[0]] + bits[2:]
    return bits


def widen(values):
    return values.astype(F32)


class Chunk:
    def __init__(self, source, total, stages, send, recv, masks, crossed, emit):
        self.source, self.total, self.stages = source, total, stages
        self.send, self.recv, self.masks, self.crossed, self.emit = send, recv, masks, crossed, emit
        self.count = source.shape[0]
        self.me = lax.axis_index("seq")
        self.copies = []
        self.at = 0
        self.levels = len(masks)

    def bit(self, level):
        return (self.me // self.masks[level]) % 2

    def peer(self, level):
        mask = self.masks[level]
        return {"seq": self.me + mask - 2 * mask * self.bit(level)}

    def start(self, src, dst, peer):
        at = len(self.copies)
        copy = remote(src, dst, self.send.at[at], self.recv.at[at], peer)
        copy.start()
        self.copies.append(copy)

    def place(self, level):
        start = 0
        for j in range(level + 1):
            start = start + self.bit(j) * (self.count >> (j + 1))
        return start

    def held(self, level):
        return self.source if level == 0 else self.stages[level - 1]

    def halve(self, level):
        size = self.count >> (level + 1)
        away = self.held(level).at[pl.ds((1 - self.bit(level)) * size, size)]
        self.start(away, self.stages[level], self.peer(level))

    def add(self, level):
        size = self.count >> (level + 1)
        kept = self.held(level)[pl.ds(self.bit(level) * size, size)]
        got = self.stages[level]
        got[...] = (widen(kept) + widen(got[...])).astype(got.dtype)

    def double(self, level):
        size = self.count >> (level + 1)
        region = self.total.at[pl.ds(self.place(level), size)]
        self.start(region, region, self.peer(level))

    def step(self, index):
        last = self.levels
        if index > 0:
            self.copies[index - 1].wait_recv()
        if index < last:
            if index > 0:
                self.add(index - 1)
            self.halve(index)
            return
        at = index - last
        if at == 0:
            self.add(last - 1)
            piece = self.stages[last - 1]
            home = self.total.at[pl.ds(self.place(last - 1), 1)]
            if self.crossed:
                self.start(piece, home, col_peer())
                return
            home[...] = piece[...]
        level = last - 1 - (at - int(self.crossed))
        if level >= 0:
            self.double(level)
        else:
            self.emit(self.total)

    def done(self):
        return self.at > 2 * self.levels + int(self.crossed)

    def next(self):
        if not self.done():
            self.step(self.at)
            self.at += 1

    def finish(self):
        for copy in self.copies:
            copy.wait_send()


def store_split(ref, value):
    rows = ref.shape[1]
    for i in range(ref.shape[0]):
        ref[i] = value[i * rows : (i + 1) * rows].astype(ref.dtype)


def advance_all(chunks):
    for chunk in chunks:
        chunk.next()


def run_out(chunks):
    while any(not chunk.done() for chunk in chunks):
        advance_all(chunks)
    for chunk in chunks:
        chunk.finish()


def small_rows(count, rank, states, selects):
    total = rank + states + selects + 8
    total += -total % (8 * count)
    return total // count


def backward_kernel(
    table_ref, flow_ref, parents_ref, lengths_ref, dl_ref, starts_ref, back_ref, cum_ref,
    delta_ref, act_ref, sel_ref, pgrad_ref, pre_ref, tw_ref,
    sw_ref, skip_ref, ext_ref, cw_ref, cb_ref, hid_ref, hidt_ref, wi_ref, wio_ref, wg_ref, wgo_ref,
    ggrad_ref, tok_ref, toko_ref, gain_ref, cot_ref, og_ref, igg_ref, sgrad_ref,
    og_out, ig_out, tg_ref, gg_ref, stepg_out, decayg_out, selectg_out, smallg_out,
    flows_ref, grads, c_ref, rate_ref, decay_buf, state_buf, b_sum, c_sum, agrad_ref, dgrad_ref,
    sel_part, sel_row, sel_low, sel_col, cig_ref, part_ref, tpart_ref,
    hid_row, tail_row, hid_low, hid_col, tail_low_ref, tail_col, tail_own, tails_ref,
    mean_out, mean_in, gain_out, gain_in, gain_pair, gains_ref,
    igi_ref, small_ref, totals, small_total, *rest,
    width,
):
    count = table_ref.shape[0]
    levels = len(seq_bits(count))
    halves, smalls = rest[:levels], rest[levels : 2 * levels]
    send, recv, pair_send, pair_recv, flow_send, flow_recv, tail_send, tail_recv, gain_send, gain_recv = rest[2 * levels :]
    rows, inner = act_ref.shape
    half = rows // 2
    steps = rows // spans
    states = dl_ref.shape[0]
    rank = tw_ref.shape[0]
    selects = sel_ref.shape[1]
    me = lax.axis_index("seq")
    row = lax.axis_index("row")
    col = lax.axis_index("col")
    mine = pl.multiple_of(row * half, half)
    other = pl.multiple_of((1 - row) * half, half)
    length = lengths_ref[me]
    peers = [{"seq": lax.rem(me + j, count)} for j in range(1, count)]
    barrier_with([row_peer(), col_peer()] + peers)

    def pair_copy(at, src, dst, peer):
        copy = remote(src, dst, pair_send.at[at], pair_recv.at[at], peer)
        copy.start()
        return copy

    def to_all(src, dst, sends, recvs):
        copies = [
            remote(src, dst.at[me], sends.at[j], recvs.at[j], peer) for j, peer in enumerate(peers)
        ]
        for copy in copies:
            copy.start()
        dst[me] = src[...]
        return copies

    block_rows, block = og_ref.shape[2], og_ref.shape[3]

    def rows_out(side):
        def emit(total):
            base = pl.multiple_of(side * (count * block_rows), count * block_rows)
            for i in range(count):
                og_out[pl.ds(pl.multiple_of(base + i * block_rows, 8), block_rows), :] = widen(total[i])
        return emit

    def lanes_out(which, side):
        def emit(total):
            tiles = block // lanes
            for i in range(count):
                value = widen(total[i])
                for j in range(tiles):
                    first = i * block_rows * 4 * tiles + (side * tiles + j) * 2 + which
                    ig_out[pl.ds(first, block_rows, stride=4 * tiles), :] = value[:, j * lanes : (j + 1) * lanes]
        return emit

    def small_slabs():
        slab = small_ref.shape[1] // 8
        return lambda at: (at // slab, slice((at % slab) * 8, (at % slab) * 8 + 8))

    place_of = small_slabs()

    def small_store(first, value):
        for j in range(value.shape[0] // 8):
            a, b = place_of(first // 8 + j)
            small_ref[a, b, :] = value[j * 8 : (j + 1) * 8]

    def small_emit(total):
        def read(first, size):
            parts = []
            for j in range(size // 8):
                a, b = place_of(first // 8 + j)
                parts.append(total[a, b, :])
            return jnp.concatenate(parts, axis=0) if len(parts) > 1 else parts[0]
        stepg_out[...] = read(0, rank)
        decayg_out[...] = read(rank, states)
        selectg_out[...] = read(rank + states, selects)
        smallg_out[...] = read(rank + states + selects, 8)

    plan = [
        (og_ref, 0, rows_out(col), False),
        (og_ref, 1, rows_out(1 - col), True),
        (igg_ref, 0, lanes_out(1, col), False),
        (igg_ref, 1, lanes_out(1, 1 - col), False),
        (igi_ref, 0, lanes_out(0, col), False),
        (igi_ref, 1, lanes_out(0, 1 - col), True),
    ]
    chunks = [
        Chunk(
            source.at[h], totals.at[i], [s.at[i] for s in halves], send.at[i], recv.at[i],
            mask_order(count, swapped), h == 1, emit,
        )
        for i, (source, h, emit, swapped) in enumerate(plan)
    ]
    small_chunk = Chunk(
        small_ref, small_total, smalls, send.at[len(plan)], recv.at[len(plan)],
        mask_order(count, False), False, small_emit,
    )

    drive = og_out.at[0:rows]
    dg_ref = og_out.at[rows : 2 * rows]

    def b_at(n, step):
        return ig_out[pl.ds(pl.multiple_of(n * rows + step * spans, spans), spans), :]

    flow_copies = to_all(flow_ref, flows_ref, flow_send, flow_recv)
    advance_all(chunks[:4])
    decay_rows(dl_ref, rate_ref, log2e)
    rate = -jnp.exp(dl_ref[...]) * log2e
    sel = sel_ref[...]
    drive[...] = delta_ref[...] * act_ref[...].astype(F32)
    for n in range(states):
        ig_out[n * rows : (n + 1) * rows, :] = jnp.broadcast_to(
            sel[:, rank + n : rank + n + 1], (rows, lanes)
        )
    c_ref[...] = spread(sel[:, rank + states :], states)
    index2 = span_index((spans, inner))
    cum = cum_ref[...]
    after = cum[spans - 1 : spans, :] - cum
    inside = index2 < spans - 1
    slot = lax.broadcasted_iota(jnp.int32, (count, 1, 1), 0)

    def visit(visited, carry):
        target = count - 1 - visited
        _, total = segment_sum(table_ref, target, states)
        flow = flows_ref[target].astype(F32) + jnp.exp2(rate * total) * grads[target]
        grads[...] = grads[...] + jnp.where(slot == parents_ref[target], flow[None], 0.0)
        return carry

    groups = inner // lanes
    pumps = {(0, 1): (), (1, 0): chunks[:2], (1, 1): chunks[2:4], (2, 0): chunks[:2], (2, 1): (), (3, 0): chunks[2:4], (3, 1): chunks[:2]}
    for group in range(groups):
        here = slice(group * lanes, (group + 1) * lanes)

        def advance(step, carry):
            d = delta_ref[step_ds(step), here]
            w = drive[step_ds(step), here]
            out = []
            for n in range(states):
                state_buf[n, step_ds(step), :] = carry[n]
                a = jnp.exp2(d * rate_ref[n, :, here])
                decay_buf[n, step_ds(step), :] = a
                out.append(a * carry[n] + w * b_at(n, step))
            return tuple(out)

        advance_all(pumps.get((group, 0), ()))
        finals = lax.fori_loop(0, steps, advance, tuple(starts_ref[n, :, here] for n in range(states)))
        for n in range(states):
            state_buf[n, rows : rows + spans, :] = finals[n]
        if group == 0:
            for copy in flow_copies:
                copy.wait()
            grads[...] = jnp.zeros(grads.shape, F32)
            lax.fori_loop(0, count - 1, visit, 0)
        advance_all(pumps.get((group, 1), ()))
        end_grad = grads[me]

        later = []
        for n in range(states):
            flow = jnp.where(inside[:, here], shift_spans(back_ref[n, :, here], -1), 0.0)
            later.append(flow + jnp.exp2(after[:, here] * rate_ref[n, :, here]) * end_grad[n : n + 1, here])

        def retreat(back, carry):
            step = steps - 1 - back
            at = step_ds(step)
            d = delta_ref[at, here]
            p = pgrad_ref[at, here]
            w = drive[at, here]
            flows, sums = carry
            new_flows, new_sums = [], []
            weighted = [None, None]
            decayed = [None, None]
            for n in range(states):
                cols = slice(n * lanes, (n + 1) * lanes)
                a = decay_buf[n, at, :]
                adjoint = c_ref[at, cols] * p + flows[n]
                moved = a * adjoint
                growth = moved * state_buf[n, at, :]
                new_flows.append(moved)
                new_sums.append(sums[n] + growth * d)
                term = adjoint * b_at(n, step)
                weighted[n % 2] = term if weighted[n % 2] is None else weighted[n % 2] + term
                term = growth * rate_ref[n, :, here]
                decayed[n % 2] = term if decayed[n % 2] is None else decayed[n % 2] + term
                b_term = adjoint * w
                c_term = state_buf[n, step_ds(step + 1), :] * p
                if group == 0:
                    b_sum[at, cols] = b_term
                    c_sum[at, cols] = c_term
                else:
                    b_sum[at, cols] += b_term
                    c_sum[at, cols] += c_term
            bw = weighted[0] + weighted[1]
            dg_ref[at, here] = (decayed[0] + decayed[1]) * (1.0 / log2e) + act_ref[at, here].astype(F32) * bw
            agrad_ref[at, here] = bw * d
            return (tuple(new_flows), tuple(new_sums))

        zero = jnp.zeros((spans, lanes), F32)
        _, sums = lax.fori_loop(0, steps, retreat, (tuple(later), (zero,) * states))
        for n in range(states):
            dgrad_ref[n : n + 1, here] = (
                jnp.sum(sums[n], axis=0, keepdims=True) * rate[n : n + 1, here] * (1.0 / log2e)
            )

    live = (step_tokens(rows, steps) < length).astype(F32)
    step_pre_grad = dg_ref[...] * live * sigmoid(pre_ref[...])
    low = step_pre_grad.astype(BF16)
    gather = gather_matrix(states)
    sel_part[...] = jnp.concatenate(
        [dot_nt(low, tw_ref[...]), dot(b_sum[...].astype(BF16), gather), dot(c_sum[...].astype(BF16), gather)],
        axis=1,
    )
    first = pair_copy(0, sel_part, sel_row, row_peer())
    advance_all(chunks[2:4])
    bias_sum = jnp.sum(step_pre_grad, axis=0, keepdims=True)
    small_store(0, dot_tn(sel[:, :rank].astype(BF16), low))
    small_store(rank, dgrad_ref[...])
    first.wait()
    pair = sel_part[...] + sel_row[...]
    sel_low[...] = pair.astype(BF16)
    second = pair_copy(1, sel_low, sel_col, col_peer())
    sel_part[...] = pair
    order = to_tokens(rows, steps)
    naturalg = dot(order, ggrad_ref[...]).astype(BF16)
    gate_parts = [dot_nt(naturalg, wg[...]) for wg in (wg_ref, wgo_ref)]
    pre = conv_pre(ext_ref, cw_ref, cb_ref, rows, inner)
    slope = slope_of(pre, sigmoid(pre))
    base_grad = agrad_ref[...] + skip_ref[0:1, :].astype(F32) * pgrad_ref[...]
    advance_all(chunks[:2])
    second.wait()
    selg = (sel_part[...] + sel_col[...].astype(F32)).astype(BF16)
    conv_in = (base_grad + dot_nt(selg, sw_ref[...])) * slope
    cig_ref[0:rows, :] = conv_in
    taps = cw_ref[...].astype(F32)
    tails = [jnp.zeros((5, inner), F32)]
    for i in range(3):
        line = jnp.zeros((1, inner), F32)
        for k in range(i + 1):
            line = line + taps[k : k + 1, :] * conv_in[(i - k) * spans : (i - k) * spans + 1, :]
        tails.append(line * (parents_ref[me] >= 0).astype(F32))
    tail_low = jnp.concatenate(tails, axis=0).astype(BF16)
    for h, wi in enumerate((wi_ref, wio_ref)):
        tpart_ref[h] = dot_nt(tail_low, wi[...])
    tail_first = pair_copy(2, tpart_ref, tail_row, row_peer())
    last_span = lax.broadcasted_iota(jnp.int32, (spans, inner), 0) == spans - 1
    for j in range(3):
        slab = jnp.roll(conv_in[j * spans : (j + 1) * spans], -1, axis=0)
        cig_ref[rows + j * spans : rows + (j + 1) * spans, :] = jnp.where(last_span, 0.0, slab)
    inner_grad = jnp.zeros((rows, inner), F32)
    for k in range(4):
        inner_grad = inner_grad + taps[k : k + 1, :] * cig_ref[(3 - k) * spans : (3 - k) * spans + rows, :]
    inner_low = inner_grad.astype(BF16)
    natural = dot(order, inner_low).astype(BF16)
    hid_copies = []
    for h, wi in ((1, wio_ref), (0, wi_ref)):
        part_ref[h] = (dot_nt(natural, wi[...]) + gate_parts[h]).astype(BF16)
        hid_copies.append(
            pair_copy(3 + h, part_ref.at[h, pl.ds(other, half), :], hid_row.at[h], row_peer())
        )
    tail_first.wait()
    tail_sum = tpart_ref[...] + tail_row[...]
    tail_low_ref[...] = tail_sum[1]
    tail_second = pair_copy(5, tail_low_ref, tail_col, col_peer())
    hid_copies[0].wait()
    hid_low[...] = (
        part_ref[1, pl.ds(mine, half), :].astype(F32) + hid_row[1].astype(F32)
    ).astype(BF16)
    hid_second = pair_copy(6, hid_low, hid_col, col_peer())
    for h in range(2):
        store_split(igi_ref.at[h], dot_tn(hid_ref[h], inner_low) + dot_tn(hidt_ref[h], tail_low))
    advance_all(chunks[4:])
    tail_second.wait()
    tail_own[...] = tail_sum[0] + tail_col[...]
    tail_copies = to_all(tail_own, tails_ref, tail_send, tail_recv)
    small_store(rank + states, dot_tn(selg, act_ref[...]))
    sums = [
        jnp.sum(conv_in * ext_ref[k * spans : k * spans + rows, :], axis=0, keepdims=True)
        for k in range(4)
    ]
    sums.append(jnp.sum(conv_in, axis=0, keepdims=True))
    sums.append(sgrad_ref[0:1, :])
    sums.append(bias_sum)
    sums.append(jnp.zeros((1, inner), F32))
    small_store(rank + states + selects, jnp.concatenate(sums, axis=0))
    for at in range((rank + states + selects + 8) // 8, small_ref.shape[0] * small_ref.shape[1] // 8):
        a, b = place_of(at)
        small_ref[a, b, :] = jnp.zeros((8, inner), F32)
    small_chunk.next()
    hid_copies[1].wait()
    hidden = part_ref[0, pl.ds(mine, half), :].astype(F32) + hid_row[0].astype(F32)
    advance_all(chunks[2:4])
    advance_all(chunks[:2])

    tok = tok_ref[...].astype(F32)
    toko = toko_ref[...].astype(F32)
    power = jnp.sum(tok * tok, axis=1, keepdims=True) + jnp.sum(toko * toko, axis=1, keepdims=True)
    inv = lax.rsqrt(power / width + norm_epsilon)
    normed = tok * inv
    margin8 = tails_ref.shape[1]
    positions = row * half + lax.broadcasted_iota(jnp.int32, (half, margin8), 0)
    line_of = lax.broadcasted_iota(jnp.int32, (half, margin8), 1)
    place = ((positions == length - margin8 + line_of) & (line_of >= margin8 - 3)).astype(F32)
    for copy in tail_copies:
        copy.wait()
    own_tail = jnp.zeros(tails_ref.shape[1:], F32)
    for child in range(count):
        is_child = (parents_ref[child] == me).astype(F32)
        own_tail = own_tail + is_child * tails_ref[child]
    hidden = hidden + jnp.dot(place, own_tail, preferred_element_type=F32, precision=lax.Precision.HIGHEST)
    hid_second.wait()
    hidden = hidden + hid_col[...].astype(F32)
    scaled = hidden * gain_ref[0:1, :].astype(F32)
    mean = jnp.sum(scaled * normed, axis=1, keepdims=True)
    mean_out[...] = lax.dot_general(
        jnp.ones((8, lanes), F32), jnp.broadcast_to(mean / lanes, (half, lanes)), (((1,), (1,)), ((), ())),
        preferred_element_type=F32, precision=lax.Precision.HIGHEST,
    )
    mean_copy = pair_copy(7, mean_out, mean_in, col_peer())
    gain_out[...] = jnp.broadcast_to(jnp.sum(hidden * normed, axis=0, keepdims=True), gain_out.shape)
    gain_copy = pair_copy(8, gain_out, gain_in, row_peer())
    advance_all(chunks[4:] + [small_chunk])
    gain_copy.wait()
    gain_pair[...] = gain_out[...] + gain_in[...]
    gain_copies = to_all(gain_pair, gains_ref, gain_send, gain_recv)
    mean_copy.wait()
    apart = lax.dot_general(
        mean_in[...], jnp.full((8, lanes), 0.125, F32), (((0,), (0,)), ((), ())),
        preferred_element_type=F32, precision=lax.Precision.HIGHEST,
    )
    mean = (mean + apart[:, 0:1]) / width
    tg_ref[...] = cot_ref[...] + inv * (scaled - normed * mean)
    advance_all(chunks[:4])
    advance_all(chunks[4:] + [small_chunk])
    for copy in gain_copies:
        copy.wait()
    gain_total = gains_ref[0]
    for i in range(1, count):
        gain_total = gain_total + gains_ref[i]
    gg_ref[...] = gain_total
    run_out(chunks + [small_chunk])


def backward_call(args, count, rows, width, inner, states, rank, selects):
    half = width // 2
    tile = rows // 2
    block_rows = half // count
    levels = len(seq_bits(count))
    small = small_rows(count, rank, states, selects)
    f32, bf16 = F32, BF16
    vm = pltpu.VMEM
    scratch = [
        vm((count, states, inner), bf16), vm((count, states, inner), f32),
        vm((rows, states * lanes), f32), vm((states, spans, inner), f32),
        vm((states, rows, lanes), f32), vm((states, rows + spans, lanes), f32),
        vm((rows, states * lanes), f32), vm((rows, states * lanes), f32),
        vm((rows, inner), f32), vm((states, inner), f32),
        vm((rows, selects), f32), vm((rows, selects), f32), vm((rows, selects), bf16), vm((rows, selects), bf16),
        vm((rows + 3 * spans, inner), f32), vm((2, rows, half), bf16), vm((2, 8, half), f32),
        vm((2, tile, half), bf16), vm((2, 8, half), f32), vm((tile, half), bf16), vm((tile, half), bf16),
        vm((8, half), f32), vm((8, half), f32), vm((8, half), f32), vm((count, 8, half), f32),
        vm((8, tile), f32), vm((8, tile), f32), vm((8, half), f32), vm((8, half), f32), vm((8, half), f32),
        vm((count, 8, half), f32),
        vm((2, count, block_rows, inner), bf16), vm((count, small, inner), f32),
        vm((6, count, block_rows, inner), bf16), vm((count, small, inner), f32),
    ]
    scratch += [vm((6, count >> (k + 1), block_rows, inner), bf16) for k in range(levels)]
    scratch += [vm((count >> (k + 1), small, inner), f32) for k in range(levels)]
    dma = pltpu.SemaphoreType.DMA
    scratch += [dma((7, 2 * levels + 1))] * 2 + [dma((9,))] * 2 + [dma((count,))] * 6
    return run_kernel(
        functools.partial(backward_kernel, width=width),
        (
            struct((2 * inner, half), f32),
            struct((half * 4 * inner // lanes, lanes), f32),
            struct((tile, half), f32),
            struct((8, half), f32),
            struct((rank, inner), f32),
            struct((states, inner), f32),
            struct((selects, inner), f32),
            struct((8, inner), f32),
        ),
        args,
        "backward",
        scratch=scratch,
        flops=16e9,
        collective=4,
        grant=vmem_most,
    )


def on_device(
    tokens_in, teacher, norm_gain, in_weight, conv_weight, conv_bias, select_weight, step_weight,
    step_bias, decay_log, skip_gain, out_weight, parents, lengths, valid_rows,
):
    rows, width = tokens_in.shape
    half = norm_gain.shape[0]
    inner = decay_log.shape[1]
    states = decay_log.shape[0]
    rank = step_weight.shape[0]
    selects = rank + 2 * states
    steps = rows // spans
    count = lax.axis_size("seq")
    row_len = rows // lax.axis_size("row")
    row = lax.axis_index("row")
    col = lax.axis_index("col")
    me = lax.axis_index("seq")
    my_len = lengths[me][None]
    my_parent = parents[me][None]
    my_valid = valid_rows[me][None]
    me1 = me.astype(jnp.int32)[None]
    scale = jnp.full((8, lanes), 1.0, F32) * (rows * count / jnp.sum(valid_rows).astype(F32))

    def halves(value, axis):
        size = value.shape[axis] // 2
        own = lax.dynamic_slice_in_dim(value, col * size, size, axis)
        other = lax.dynamic_slice_in_dim(value, (1 - col) * size, size, axis)
        return own, other

    def rows8(value):
        return jnp.broadcast_to(value[None, :], (8, value.shape[0]))

    swap = [(0, 1), (1, 0)]
    tok, toko = halves(tokens_in, 1)
    tail = lax.dynamic_slice_in_dim(tokens_in, my_len[0] - 8, 8, 0)
    w_own, w_send = halves(in_weight, 2)
    wi, wg = w_own[:, 0], w_own[:, 1]
    wi_send, wg_send = w_send[:, 0], w_send[:, 1]
    ow, ow_send = halves(out_weight, 0)
    gain = rows8(norm_gain)
    skip = rows8(skip_gain)
    conv_b = rows8(conv_bias)
    step_b = rows8(step_bias)

    tails, wio, gaino = entry_exchange(tail, wi_send, gain, count)
    wg_send, ow_send, wio = lax.optimization_barrier((wg_send, ow_send, wio))
    wgo = lax.ppermute(wg_send, "col", swap)
    owo = lax.ppermute(ow_send, "col", swap)
    tails_own, tails_oth = halves(tails, 2)

    hid, hid_tail, ext, act, sel_part = run_kernel(
        forward_in_kernel,
        (
            struct((2, rows, half), BF16),
            struct((2, 8, half), BF16),
            struct((rows + 3 * spans, inner), F32),
            struct((rows, inner), BF16),
            struct((rows, selects), F32),
        ),
        (tok, toko, tails_own, tails_oth, gain, gaino, wi, wio, conv_weight, conv_b, select_weight, my_parent),
        "forward_in",
        flops=2e9,
    )
    sel = quad_sum(sel_part, 1, "select_sum")
    delta, step_pre, reach, cum, seg_map = run_kernel(
        forward_ends_kernel,
        (
            struct((rows, inner), F32),
            struct((rows, inner), F32),
            struct((states, spans, inner), F32),
            struct((spans, inner), F32),
            struct((states + 8, inner), BF16),
        ),
        (sel, step_weight, step_b, decay_log, act, my_len),
        "forward_ends",
        scratch=[
            pltpu.VMEM((rows, inner), F32),
            pltpu.VMEM((rows, states * lanes), F32),
            pltpu.VMEM((states, spans, inner), F32),
        ],
        flops=2e9,
    )
    table = seq_gather(seg_map, count, 2, "state_gather")
    starts, mixed_pre, gate, mixed, part = run_kernel(
        forward_out_kernel,
        (
            struct((states, spans, inner), F32),
            struct((rows, inner), F32),
            struct((rows, inner), F32),
            struct((rows, inner), BF16),
            struct((2, rows, half), BF16),
        ),
        (
            table, parents, me1, decay_log, reach, cum, delta, act, sel, hid, wg, wgo, skip, ow, owo,
        ),
        "forward_out",
        scratch=[
            pltpu.VMEM((count, states, inner), F32),
            pltpu.VMEM((rows, inner), F32),
            pltpu.VMEM((rows, states * lanes), F32),
            pltpu.VMEM((rows, states * lanes), F32),
            pltpu.VMEM((states, spans, inner), F32),
        ],
        flops=4e9,
    )
    tok_tile = lax.dynamic_slice_in_dim(tok, row * row_len, row_len, 0)
    toko_tile = lax.dynamic_slice_in_dim(toko, row * row_len, row_len, 0)
    teach_tile = lax.dynamic_slice_in_dim(teacher, row * row_len, row_len, 0)
    output, cot_tile, cot = middle_exchange(part, tok_tile, teach_tile, my_valid, scale)
    out_part, gate_grad, ig_gate, pre_grad, skip_part, back, flow = run_kernel(
        backward_in_kernel,
        (
            struct((2, count, inner // count, half), BF16),
            struct((rows, inner), BF16),
            struct((2, count, half // count, inner), BF16),
            struct((rows, inner), F32),
            struct((8, inner), F32),
            struct((states, spans, inner), F32),
            struct((states, inner), BF16),
        ),
        (cot, mixed, ow, owo, gate, mixed_pre, act, skip, sel, delta, decay_log, cum, hid),
        "backward_in",
        scratch=[
            pltpu.VMEM((rows, states * lanes), F32),
            pltpu.VMEM((states, spans, inner), F32),
        ],
        flops=4e9,
    )
    out_grad, in_both, tokens_grad, gain_grad, step_grad, decay_grad, select_grad, small = backward_call(
        (
            table, flow, parents, lengths, decay_log, starts, back, cum, delta, act, sel, pre_grad,
            step_pre, step_weight, select_weight, skip, ext, conv_weight, conv_b, hid, hid_tail,
            wi, wio, wg, wgo, gate_grad, tok_tile, toko_tile, gain, cot_tile, out_part, ig_gate, skip_part,
        ),
        count, rows, width, inner, states, rank, selects,
    )
    in_grad = in_both.reshape(half, -1, 2, lanes).transpose(0, 2, 1, 3).reshape(half, 2, -1)
    conv_grad, conv_bias_grad, skip_grad, step_bias_grad = small[:4], small[4:5], small[5:6], small[6:7]
    return (
        output,
        tokens_grad,
        gain_grad[0],
        in_grad,
        conv_grad,
        conv_bias_grad[0],
        select_grad.T,
        step_grad,
        step_bias_grad[0],
        decay_grad,
        skip_grad[0],
        out_grad,
    )


def solution(mesh):
    placed = (
        P("seq", None),
        P("seq", "col"),
        P("col"),
        P("col", None, "row"),
        P(None, ("row", "col")),
        P(("row", "col")),
        P(("row", "col"), None),
        P(None, ("row", "col")),
        P(("row", "col")),
        P(None, ("row", "col")),
        P(("row", "col")),
        P("row", "col"),
        P(),
        P(),
        P(),
    )
    return jax.shard_map(
        on_device,
        mesh=mesh,
        in_specs=placed,
        out_specs=(
            P(("seq", "row"), "col"),
            P(("seq", "row"), "col"),
            P("col"),
            P("col", None, "row"),
            P(None, ("row", "col")),
            P(("row", "col")),
            P(("row", "col"), None),
            P(None, ("row", "col")),
            P(("row", "col")),
            P(None, ("row", "col")),
            P(("row", "col")),
            P("row", "col"),
        ),
        check_vma=False,
    )
```

```python
import functools

import jax
import jax.numpy as jnp
from jax import lax
from jax.experimental import pallas as pl
from jax.experimental.pallas import tpu as pltpu
from jax.sharding import PartitionSpec as P

MESH = pl.DeviceIdType.MESH
F32 = jnp.float32
BF16 = jnp.bfloat16
norm_epsilon = 1e-05
spans = 8
lanes = 128
log2e = 1.4426950408889634
vmem_bytes = 60 * 1024 * 1024
vmem_most = 67043328
chunk_plan = (False, True, False, True, False, False)


def vmem_spec():
    return pl.BlockSpec(memory_space=pltpu.VMEM)


def smem_spec():
    return pl.BlockSpec(memory_space=pltpu.SMEM)


def struct(shape, dtype):
    return jax.ShapeDtypeStruct(shape, dtype)


def dot(a, b):
    return jnp.dot(a, b, preferred_element_type=F32)


def dot_tn(a, b):
    return lax.dot_general(a, b, (((0,), (0,)), ((), ())), preferred_element_type=F32)


def dot_nt(a, b):
    return lax.dot_general(a, b, (((1,), (1,)), ((), ())), preferred_element_type=F32)


def sigmoid(v):
    return 1.0 / (1.0 + jnp.exp(-v))


def slope_of(v, sigma):
    return sigma * (1.0 + v * (1.0 - sigma))


def to_steps(rows, steps):
    place = lax.broadcasted_iota(jnp.int32, (rows, rows), 0)
    token = lax.broadcasted_iota(jnp.int32, (rows, rows), 1)
    return (token == (place % spans) * steps + place // spans).astype(F32).astype(BF16)


def to_tokens(rows, steps):
    token = lax.broadcasted_iota(jnp.int32, (rows, rows), 0)
    place = lax.broadcasted_iota(jnp.int32, (rows, rows), 1)
    return (token == (place % spans) * steps + place // spans).astype(F32).astype(BF16)


def step_tokens(rows, steps):
    place = lax.broadcasted_iota(jnp.int32, (rows, 1), 0)
    return (place % spans) * steps + place // spans


def spread_matrix(states):
    row = lax.broadcasted_iota(jnp.int32, (2 * states, states * lanes), 0)
    col = lax.broadcasted_iota(jnp.int32, (2 * states, states * lanes), 1)
    return (row % states == col // lanes).astype(F32).astype(BF16)


def gather_matrix(states):
    row = lax.broadcasted_iota(jnp.int32, (states * lanes, states), 0)
    col = lax.broadcasted_iota(jnp.int32, (states * lanes, states), 1)
    return (row // lanes == col).astype(F32).astype(BF16)


def spread(values, states):
    high = values.astype(BF16)
    rest = (values - high.astype(F32)).astype(BF16)
    return dot(jnp.concatenate([high, rest], axis=1), spread_matrix(states))


def shift_spans(values, amount):
    return jnp.roll(values, amount, axis=values.ndim - 2)


def span_index(shape):
    return lax.broadcasted_iota(jnp.int32, shape, len(shape) - 2)


def run_kernel(kernel, outs, args, name, scratch=(), flops=0, collective=None, grant=vmem_bytes):
    params = dict(vmem_limit_bytes=grant)
    if collective is not None:
        params.update(collective_id=collective, has_side_effects=True)
    return pl.pallas_call(
        kernel,
        out_shape=outs,
        in_specs=[
            smem_spec() if a.dtype == jnp.int32 else vmem_spec() for a in args
        ],
        out_specs=jax.tree.map(lambda _: vmem_spec(), outs),
        scratch_shapes=list(scratch),
        compiler_params=pltpu.CompilerParams(**params),
        cost_estimate=pl.CostEstimate(
            flops=int(flops),
            transcendentals=0,
            bytes_accessed=int(sum(a.size * a.dtype.itemsize for a in args)),
        ),
        name=name,
    )(*args)


def barrier_with(peers):
    barrier = pltpu.get_barrier_semaphore()
    for peer in peers:
        pl.semaphore_signal(barrier, inc=1, device_id=peer, device_id_type=MESH)
    pl.semaphore_wait(barrier, len(peers))


def remote(src, dst, send, recv, peer):
    return pltpu.make_async_remote_copy(
        src_ref=src, dst_ref=dst, send_sem=send, recv_sem=recv, device_id=peer, device_id_type=MESH
    )


def row_peer():
    return {"row": 1 - lax.axis_index("row")}


def col_peer():
    return {"col": 1 - lax.axis_index("col")}


def entry_kernel(tail_ref, wi_ref, gain_ref, tails_ref, wo_ref, gain_o_ref, tsend, trecv, csend, crecv):
    count = tails_ref.shape[0]
    me = lax.axis_index("seq")
    peers = [{"seq": lax.rem(me + j, count)} for j in range(1, count)]
    barrier_with([col_peer()] + peers)
    copies = []
    for j, peer in enumerate(peers):
        copies.append(remote(tail_ref, tails_ref.at[me], tsend.at[j], trecv.at[j], peer))
    copies.append(remote(gain_ref, gain_o_ref, csend.at[0], crecv.at[0], col_peer()))
    copies.append(remote(wi_ref, wo_ref, csend.at[1], crecv.at[1], col_peer()))
    for copy in copies:
        copy.start()
    tails_ref[me] = tail_ref[...]
    for copy in copies:
        copy.wait()


def entry_exchange(tail, wi_send, gain_send, count):
    return run_kernel(
        entry_kernel,
        (
            struct((count,) + tail.shape, tail.dtype),
            struct(wi_send.shape, wi_send.dtype),
            struct(gain_send.shape, gain_send.dtype),
        ),
        (tail, wi_send, gain_send),
        "entry_exchange",
        scratch=[
            pltpu.SemaphoreType.DMA((count,)),
            pltpu.SemaphoreType.DMA((count,)),
            pltpu.SemaphoreType.DMA((2,)),
            pltpu.SemaphoreType.DMA((2,)),
        ],
        collective=0,
    )


def seq_gather_kernel(x_ref, o_ref, send, recv):
    count = o_ref.shape[0]
    me = lax.axis_index("seq")
    peers = [{"seq": lax.rem(me + j, count)} for j in range(1, count)]
    barrier_with(peers)
    copies = [
        remote(x_ref, o_ref.at[me], send.at[j], recv.at[j], peer) for j, peer in enumerate(peers)
    ]
    for copy in copies:
        copy.start()
    o_ref[me] = x_ref[...]
    for copy in copies:
        copy.wait()


def seq_gather(x, count, collective, name):
    return run_kernel(
        seq_gather_kernel,
        struct((count,) + x.shape, x.dtype),
        (x,),
        name,
        scratch=[pltpu.SemaphoreType.DMA((count,)), pltpu.SemaphoreType.DMA((count,))],
        collective=collective,
    )


def quad_sum_kernel(x_ref, o_ref, from_row, to_col, from_col, send, recv):
    barrier_with([row_peer(), col_peer()])
    first = remote(x_ref, from_row, send.at[0], recv.at[0], row_peer())
    first.start()
    first.wait()
    pair = x_ref[...] + from_row[...]
    to_col[...] = pair.astype(BF16)
    second = remote(to_col, from_col, send.at[1], recv.at[1], col_peer())
    second.start()
    o_ref[...] = pair
    second.wait()
    o_ref[...] += from_col[...].astype(F32)


def quad_sum(x, collective, name):
    return run_kernel(
        quad_sum_kernel,
        struct(x.shape, F32),
        (x,),
        name,
        scratch=[
            pltpu.VMEM(x.shape, F32),
            pltpu.VMEM(x.shape, BF16),
            pltpu.VMEM(x.shape, BF16),
            pltpu.SemaphoreType.DMA((2,)),
            pltpu.SemaphoreType.DMA((2,)),
        ],
        collective=collective,
    )


def middle_kernel(
    part_ref, tok_ref, teach_ref, ints_ref, scale_ref,
    out_ref, cot_ref, low_ref,
    from_row, to_col, from_col, send, recv,
):
    half = tok_ref.shape[0]
    row = lax.axis_index("row")
    mine = pl.multiple_of(row * half, half)
    other = pl.multiple_of((1 - row) * half, half)
    barrier_with([row_peer(), col_peer()])
    first = [
        remote(part_ref.at[h, pl.ds(other, half), :], from_row.at[h], send.at[h], recv.at[h], row_peer())
        for h in (1, 0)
    ]
    for copy in first:
        copy.start()
    first[0].wait()
    to_col[...] = (
        part_ref[1, pl.ds(mine, half), :].astype(F32) + from_row[1].astype(F32)
    ).astype(BF16)
    second = remote(to_col, from_col, send.at[2], recv.at[2], col_peer())
    second.start()
    first[1].wait()
    tile = part_ref[0, pl.ds(mine, half), :].astype(F32) + from_row[0].astype(F32)
    tile = tile + tok_ref[...].astype(F32)
    second.wait()
    result = tile + from_col[...].astype(F32)
    out_ref[...] = result.astype(BF16)
    positions = mine + lax.broadcasted_iota(jnp.int32, (half, 1), 0)
    counted = (positions < ints_ref[0]).astype(F32) * scale_ref[0:1, 0:1]
    cot = (result - teach_ref[...].astype(F32)) * counted
    cot_ref[...] = cot
    low_ref[0, pl.ds(mine, half), :] = cot.astype(BF16)
    third = [
        remote(low_ref.at[0, pl.ds(mine, half), :], low_ref.at[1, pl.ds(mine, half), :], send.at[3], recv.at[3], col_peer()),
        remote(low_ref.at[0, pl.ds(mine, half), :], low_ref.at[0, pl.ds(mine, half), :], send.at[4], recv.at[4], row_peer()),
    ]
    for copy in third:
        copy.start()
    third[0].wait()
    fourth = remote(low_ref.at[1, pl.ds(mine, half), :], low_ref.at[1, pl.ds(mine, half), :], send.at[5], recv.at[5], row_peer())
    fourth.start()
    third[1].wait()
    fourth.wait()


def middle_exchange(part, tok_tile, teach_tile, my_valid, scale):
    _, rows, width = part.shape
    half = rows // 2
    return run_kernel(
        middle_kernel,
        (struct((half, width), BF16), struct((half, width), F32), struct((2, rows, width), BF16)),
        (part, tok_tile, teach_tile, my_valid, scale),
        "middle_exchange",
        scratch=[
            pltpu.VMEM((2, half, width), BF16),
            pltpu.VMEM((half, width), BF16),
            pltpu.VMEM((half, width), BF16),
            pltpu.SemaphoreType.DMA((6,)),
            pltpu.SemaphoreType.DMA((6,)),
        ],
        collective=3,
    )


def forward_in_kernel(
    tok_ref, toko_ref, tails_ref, tailso_ref, gain_ref, gaino_ref, wi_ref, wio_ref,
    cw_ref, cb_ref, sw_ref, ints_ref,
    hid_ref, hidt_ref, ext_ref, act_ref, sel_ref,
):
    rows, half = tok_ref.shape
    steps = rows // spans
    width = 2 * half
    parent = jnp.maximum(ints_ref[0], 0)
    present = (ints_ref[0] >= 0).astype(F32)
    gain = gain_ref[0:1, :].astype(F32)
    gaino = gaino_ref[0:1, :].astype(F32)

    def hidden_of(own, other):
        own = own.astype(F32)
        other = other.astype(F32)
        total = jnp.sum(own * own, axis=1, keepdims=True) + jnp.sum(other * other, axis=1, keepdims=True)
        inv = lax.rsqrt(total / width + norm_epsilon)
        return (own * inv * gain).astype(BF16), (other * inv * gaino).astype(BF16)

    hid, hido = hidden_of(tok_ref[...], toko_ref[...])
    order = to_steps(rows, steps)
    hid = dot(order, hid).astype(BF16)
    hido = dot(order, hido).astype(BF16)
    hid_ref[0] = hid
    hid_ref[1] = hido
    inner = dot(hid, wi_ref[...]) + dot(hido, wio_ref[...])
    tail, tailo = hidden_of(tails_ref[parent], tailso_ref[parent])
    hidt_ref[0] = tail
    hidt_ref[1] = tailo
    tail_inner = (dot(tail, wi_ref[...]) + dot(tailo, wio_ref[...])) * present
    last = inner[rows - 3 * spans :]
    first_span = lax.broadcasted_iota(jnp.int32, (spans, half), 0) == 0
    for j in range(3):
        block = jnp.roll(last[j * spans : (j + 1) * spans], 1, axis=0)
        ext_ref[j * spans : (j + 1) * spans, :] = jnp.where(
            first_span, jnp.broadcast_to(tail_inner[5 + j : 6 + j, :], (spans, half)), block
        )
    ext_ref[3 * spans :, :] = inner
    taps = cw_ref[...].astype(F32)
    pre = jnp.broadcast_to(cb_ref[0:1, :].astype(F32), (rows, half))
    for k in range(4):
        pre = pre + taps[k : k + 1, :] * ext_ref[k * spans : k * spans + rows, :]
    act = (pre * sigmoid(pre)).astype(BF16)
    act_ref[...] = act
    sel_ref[...] = dot(act, sw_ref[...])


def conv_pre(ext_ref, cw_ref, cb_ref, rows, half):
    taps = cw_ref[...].astype(F32)
    pre = jnp.broadcast_to(cb_ref[0:1, :].astype(F32), (rows, half))
    for k in range(4):
        pre = pre + taps[k : k + 1, :] * ext_ref[k * spans : k * spans + rows, :]
    return pre


def group_ds(group):
    return pl.ds(pl.multiple_of(group * lanes, lanes), lanes)


def step_ds(step):
    return pl.ds(pl.multiple_of(step * spans, spans), spans)


def decay_rows(decay_log_ref, decay_b, scale):
    states, width = decay_log_ref.shape
    rate = -jnp.exp(decay_log_ref[...]) * scale
    for n in range(states):
        decay_b[n] = jnp.broadcast_to(rate[n : n + 1, :], (spans, width))


def span_sum_kernel_part(delta_ref, steps):
    total = delta_ref[0:spans, :]
    for s in range(1, steps):
        total = total + delta_ref[s * spans : (s + 1) * spans, :]
    return total


def forward_ends_kernel(
    sel_ref, tw_ref, tb_ref, dl_ref, act_ref, ints_ref,
    delta_ref, pre_ref, reach_ref, cum_ref, send_ref,
    drive, b_ref, rate_ref,
):
    rows, width = act_ref.shape
    steps = rows // spans
    states = dl_ref.shape[0]
    rank = tw_ref.shape[0]
    length = ints_ref[0]
    sel = sel_ref[...]
    step_pre = dot(sel[:, :rank].astype(BF16), tw_ref[...]) + tb_ref[0:1, :].astype(F32)
    pre_ref[...] = step_pre
    live = (step_tokens(rows, steps) < length).astype(F32)
    delta = (jnp.maximum(step_pre, 0.0) + jnp.log1p(jnp.exp(-jnp.abs(step_pre)))) * live
    delta_ref[...] = delta
    drive[...] = delta * act_ref[...].astype(F32)
    b_ref[...] = spread(sel[:, rank : rank + states], states)
    decay_rows(dl_ref, rate_ref, log2e)

    for group in range(width // lanes):
        here = slice(group * lanes, (group + 1) * lanes)

        def advance(step, carry):
            d = delta_ref[step_ds(step), here]
            w = drive[step_ds(step), here]
            out = []
            for n in range(states):
                a = jnp.exp2(d * rate_ref[n, :, here])
                out.append(a * carry[n] + w * b_ref[step_ds(step), n * lanes : (n + 1) * lanes])
            return tuple(out)

        ends = lax.fori_loop(0, steps, advance, (jnp.zeros((spans, lanes), F32),) * states)
        for n in range(states):
            reach_ref[n, :, here] = ends[n]

    total = span_sum_kernel_part(delta_ref, steps)
    index2 = span_index((spans, width))
    part = total
    shift = 1
    while shift < spans:
        inside = index2 >= shift
        for n in range(states):
            own = reach_ref[n]
            earlier = jnp.where(inside, shift_spans(own, shift), 0.0)
            reach_ref[n] = own + jnp.exp2(part * rate_ref[n]) * earlier
        part = part + jnp.where(inside, shift_spans(part, shift), 0.0)
        shift *= 2
    cum_ref[...] = part
    sums = part[spans - 1 : spans, :]
    high = sums.astype(BF16)
    mid = (sums - high.astype(F32)).astype(BF16)
    low = (sums - high.astype(F32) - mid.astype(F32)).astype(BF16)
    ends = jnp.concatenate([reach_ref[n, spans - 1 : spans, :] for n in range(states)], axis=0)
    extra = jnp.concatenate(
        [high.astype(F32), mid.astype(F32), low.astype(F32), jnp.zeros((5, width), F32)], axis=0
    )
    send_ref[...] = jnp.concatenate([ends, extra], axis=0).astype(BF16)


def segment_sum(table_ref, index, states):
    block = table_ref[index].astype(F32)
    return block[:states], block[states : states + 1] + block[states + 1 : states + 2] + block[states + 2 : states + 3]


def forward_out_kernel(
    table_ref, parents_ref, me_ref, dl_ref, reach_ref, cum_ref, delta_ref, act_ref, sel_ref,
    hid_ref, wg_ref, wgo_ref, skip_ref, ow_ref, owo_ref,
    starts_ref, mpre_ref, gate_ref, mixed_ref, part_ref,
    finals, drive, b_ref, c_ref, rate_ref,
):
    rows, width = act_ref.shape
    steps = rows // spans
    states = dl_ref.shape[0]
    rank = sel_ref.shape[1] - 2 * states
    count = table_ref.shape[0]
    me = me_ref[0]
    decay_rows(dl_ref, rate_ref, log2e)
    rate = -jnp.exp(dl_ref[...]) * log2e

    def start_of(target):
        above = parents_ref[target]
        return finals[jnp.maximum(above, 0)] * (above >= 0).astype(F32)

    def visit(target, carry):
        end, total = segment_sum(table_ref, target, states)
        finals[target] = jnp.exp2(rate * total) * start_of(target) + end
        return carry

    finals[0] = jnp.zeros(finals.shape[1:], F32)
    lax.fori_loop(0, count, visit, 0)
    start = start_of(me)
    sel = sel_ref[...]
    drive[...] = delta_ref[...] * act_ref[...].astype(F32)
    b_ref[...] = spread(sel[:, rank : rank + states], states)
    c_ref[...] = spread(sel[:, rank + states :], states)
    index2 = span_index((spans, width))
    cum = jnp.where(index2 >= 1, shift_spans(cum_ref[...], 1), 0.0)
    for n in range(states):
        earlier = jnp.where(index2 >= 1, shift_spans(reach_ref[n], 1), 0.0)
        starts_ref[n] = jnp.exp2(cum * rate_ref[n]) * start[n : n + 1, :] + earlier

    for group in range(width // lanes):
        here = slice(group * lanes, (group + 1) * lanes)

        def advance(step, carry):
            d = delta_ref[step_ds(step), here]
            w = drive[step_ds(step), here]
            out = []
            reads = [None] * 4
            for n in range(states):
                a = jnp.exp2(d * rate_ref[n, :, here])
                now = a * carry[n] + w * b_ref[step_ds(step), n * lanes : (n + 1) * lanes]
                out.append(now)
                term = c_ref[step_ds(step), n * lanes : (n + 1) * lanes] * now
                reads[n % 4] = term if reads[n % 4] is None else reads[n % 4] + term
            mpre_ref[step_ds(step), here] = (reads[0] + reads[1]) + (reads[2] + reads[3])
            return tuple(out)

        lax.fori_loop(0, steps, advance, tuple(starts_ref[n, :, here] for n in range(states)))

    gate = dot(hid_ref[0], wg_ref[...]) + dot(hid_ref[1], wgo_ref[...])
    gate_ref[...] = gate
    mixed_pre = mpre_ref[...] + skip_ref[0:1, :].astype(F32) * act_ref[...].astype(F32)
    mpre_ref[...] = mixed_pre
    mixed = (mixed_pre * (gate * sigmoid(gate))).astype(BF16)
    mixed_ref[...] = mixed
    natural = dot(to_tokens(rows, steps), mixed).astype(BF16)
    part_ref[0] = dot(natural, ow_ref[...]).astype(BF16)
    part_ref[1] = dot(natural, owo_ref[...]).astype(BF16)


def backward_in_kernel(
    cot_ref, mixed_ref, ow_ref, owo_ref, gate_ref, mpre_ref, act_ref, skip_ref, sel_ref,
    delta_ref, dl_ref, cum_ref, hid_ref,
    og_ref, ggrad_ref, ig_ref, pgrad_ref, sgrad_ref, back_ref, flow_ref,
    c_ref, rate_ref,
):
    rows, width = act_ref.shape
    steps = rows // spans
    states = dl_ref.shape[0]
    rank = sel_ref.shape[1] - 2 * states
    order = to_steps(rows, steps)
    cot = dot(order, cot_ref[0]).astype(BF16)
    coto = dot(order, cot_ref[1]).astype(BF16)
    mixed_grad = dot_nt(cot, ow_ref[...]) + dot_nt(coto, owo_ref[...])
    gate = gate_ref[...]
    sigma = sigmoid(gate)
    pre_grad = mixed_grad * (gate * sigma)
    pgrad_ref[...] = pre_grad
    gate_grad = (mixed_grad * mpre_ref[...] * slope_of(gate, sigma)).astype(BF16)
    ggrad_ref[...] = gate_grad
    sgrad_ref[...] = jnp.broadcast_to(
        jnp.sum(pre_grad * act_ref[...].astype(F32), axis=0, keepdims=True), sgrad_ref.shape
    )
    c_ref[...] = spread(sel_ref[:, rank + states :], states)
    decay_rows(dl_ref, rate_ref, log2e)

    for group in range(width // lanes):
        here = slice(group * lanes, (group + 1) * lanes)

        def retreat(back, carry):
            step = steps - 1 - back
            d = delta_ref[step_ds(step), here]
            p = pgrad_ref[step_ds(step), here]
            out = []
            for n in range(states):
                a = jnp.exp2(d * rate_ref[n, :, here])
                out.append(a * (c_ref[step_ds(step), n * lanes : (n + 1) * lanes] * p + carry[n]))
            return tuple(out)

        flows = lax.fori_loop(0, steps, retreat, (jnp.zeros((spans, lanes), F32),) * states)
        for n in range(states):
            back_ref[n, :, here] = flows[n]

    index2 = span_index((spans, width))
    cum = cum_ref[...]
    part = cum - jnp.where(index2 >= 1, shift_spans(cum, 1), 0.0)
    shift = 1
    while shift < spans:
        inside = index2 < spans - shift
        for n in range(states):
            own = back_ref[n]
            later = jnp.where(inside, shift_spans(own, -shift), 0.0)
            back_ref[n] = own + jnp.exp2(part * rate_ref[n]) * later
        part = part + jnp.where(inside, shift_spans(part, -shift), 0.0)
        shift *= 2
    flow_ref[...] = jnp.concatenate(
        [back_ref[n, 0:1, :] for n in range(states)], axis=0
    ).astype(BF16)
    store_split(og_ref.at[0], dot_tn(mixed_ref[...], cot))
    store_split(og_ref.at[1], dot_tn(mixed_ref[...], coto))
    store_split(ig_ref.at[0], dot_tn(hid_ref[0], gate_grad))
    store_split(ig_ref.at[1], dot_tn(hid_ref[1], gate_grad))


def seq_bits(count):
    bits = []
    mask = 1
    while mask < count:
        bits.append(mask)
        mask *= 2
    return bits


def stages_of(count, first_pair):
    bits = seq_bits(count)
    if len(bits) < 3:
        return [(mask,) for mask in bits]
    if first_pair:
        return [(bits[1],), (bits[0],)] + [(mask,) for mask in bits[2:]]
    return [(bits[0],), (bits[1], bits[2])] + [(mask,) for mask in bits[3:]]


def stage_sizes(stages, count, crossed):
    sizes, copies = [], 0
    for i, masks in enumerate(stages):
        radix = 2 ** len(masks)
        count //= radix
        got = radix if crossed and i == len(stages) - 1 else radix - 1
        sizes.append((got, count))
        copies += got + radix - 1
    return sizes, copies


def bit_of(me, mask):
    return (me // mask) % 2


def toward(me, masks, pick):
    device, part = me, 0
    for k, mask in enumerate(masks):
        bit = bit_of(me, mask)
        weight = 2 ** (len(masks) - 1 - k)
        if (pick // weight) % 2:
            device = device + mask - 2 * mask * bit
            bit = 1 - bit
        part = part + weight * bit
    return device, part


def widen(values):
    return values.astype(F32)


class Chunk:
    def __init__(self, source, total, landings, send, recv, stages, crossed, emit):
        self.source, self.total, self.landings = source, total, landings
        self.send, self.recv, self.stages, self.crossed, self.emit = send, recv, stages, crossed, emit
        self.count = source.shape[0]
        self.me = lax.axis_index("seq")
        self.copies = []
        self.flying = []
        self.at = 0
        self.levels = len(stages)
        self.sizes = stage_sizes(stages, self.count, crossed)[0]

    def start(self, src, dst, peer):
        at = len(self.copies)
        copy = remote(src, dst, self.send.at[at], self.recv.at[at], peer)
        copy.start()
        self.copies.append(copy)
        self.flying.append(copy)

    def land(self):
        for copy in self.flying:
            copy.wait_recv()
        self.flying = []

    def place(self, level):
        start = 0
        for j in range(level + 1):
            start = start + toward(self.me, self.stages[j], 0)[1] * self.sizes[j][1]
        return start

    def crossing(self, level):
        return self.crossed and level == self.levels - 1

    def scatter(self, level):
        held = self.source if level == 0 else self.landings[level - 1].at[0]
        masks, (_, size) = self.stages[level], self.sizes[level]
        for pick in range(0 if self.crossing(level) else 1, 2 ** len(masks)):
            device, part = toward(self.me, masks, pick)
            peer = {"seq": device}
            if self.crossing(level):
                peer["col"] = 1 - lax.axis_index("col")
            slot = pick if self.crossing(level) else pick - 1
            self.start(held.at[pl.ds(part * size, size)], self.landings[level].at[slot], peer)

    def add(self, level):
        held = self.source if level == 0 else self.landings[level - 1].at[0]
        masks, (got, size) = self.stages[level], self.sizes[level]
        landing = self.landings[level]
        if self.crossing(level):
            total = widen(landing[0])
        else:
            own = toward(self.me, masks, 0)[1]
            total = widen(held[pl.ds(own * size, size)]) + widen(landing[0])
        for slot in range(1, got):
            total = total + widen(landing[slot])
        return total.astype(landing.dtype)

    def gather(self, level):
        size = self.sizes[level][1]
        region = self.total.at[pl.ds(self.place(level), size)]
        masks = self.stages[level]
        for pick in range(1, 2 ** len(masks)):
            self.start(region, region, {"seq": toward(self.me, masks, pick)[0]})

    def done(self):
        return self.at > 2 * self.levels

    def next(self):
        if self.done():
            return
        self.land()
        at, last = self.at, self.levels
        self.at += 1
        if at < last:
            if at > 0:
                self.landings[at - 1][0] = self.add(at - 1)
            self.scatter(at)
            return
        if at == last:
            self.total[pl.ds(self.place(last - 1), 1)] = self.add(last - 1)
        level = 2 * last - 1 - at
        if level >= 0:
            self.gather(level)
        else:
            self.emit(self.total)

    def finish(self):
        for copy in self.copies:
            copy.wait_send()


def store_split(ref, value):
    rows = ref.shape[1]
    for i in range(ref.shape[0]):
        ref[i] = value[i * rows : (i + 1) * rows].astype(ref.dtype)


def advance_all(chunks):
    for chunk in chunks:
        chunk.next()


def run_out(chunks):
    while any(not chunk.done() for chunk in chunks):
        advance_all(chunks)
    for chunk in chunks:
        chunk.finish()


def small_rows(count, rank, states, selects):
    total = rank + states + selects + 8
    total += -total % (8 * count)
    return total // count


def backward_kernel(
    table_ref, flow_ref, parents_ref, lengths_ref, dl_ref, starts_ref, back_ref, cum_ref,
    delta_ref, act_ref, sel_ref, pgrad_ref, pre_ref, tw_ref,
    sw_ref, skip_ref, ext_ref, cw_ref, cb_ref, hid_ref, hidt_ref, wi_ref, wio_ref, wg_ref, wgo_ref,
    ggrad_ref, tok_ref, toko_ref, gain_ref, cot_ref, og_ref, igg_ref, sgrad_ref,
    og_out, ig_out, tg_ref, gg_ref, stepg_out, decayg_out, selectg_out, smallg_out,
    flows_ref, grads, c_ref, rate_ref, decay_buf, state_buf, b_sum, c_sum, agrad_ref, dgrad_ref,
    sel_part, sel_row, sel_low, sel_col, cig_ref, part_ref, tpart_ref,
    hid_row, tail_row, hid_low, hid_col, tail_low_ref, tail_col, tail_own, tails_ref,
    mean_out, mean_in, gain_out, gain_in, gain_pair, gains_ref,
    igi_ref, small_ref, totals, small_total, *rest,
    width,
):
    count = table_ref.shape[0]
    landings = []
    for paired in chunk_plan + (False,):
        size = len(stages_of(count, paired))
        landings.append(rest[:size])
        rest = rest[size:]
    send, recv, pair_send, pair_recv, flow_send, flow_recv, tail_send, tail_recv, gain_send, gain_recv = rest
    rows, inner = act_ref.shape
    half = rows // 2
    steps = rows // spans
    states = dl_ref.shape[0]
    rank = tw_ref.shape[0]
    selects = sel_ref.shape[1]
    me = lax.axis_index("seq")
    row = lax.axis_index("row")
    col = lax.axis_index("col")
    mine = pl.multiple_of(row * half, half)
    other = pl.multiple_of((1 - row) * half, half)
    length = lengths_ref[me]
    peers = [{"seq": lax.rem(me + j, count)} for j in range(1, count)]
    across = sorted(
        {(masks, pick) for masks in (stages_of(count, p)[-1] for p in chunk_plan) for pick in range(1, 2 ** len(masks))}
    )
    flips = sorted({sum(m for k, m in enumerate(masks) if (pick >> (len(masks) - 1 - k)) % 2) for masks, pick in across})
    crossers = []
    for flip in flips:
        masks = tuple(m for m in seq_bits(count) if (flip // m) % 2)
        crossers.append({"seq": toward(me, masks, 2 ** len(masks) - 1)[0], "col": 1 - col})
    barrier_with([row_peer(), col_peer()] + peers + crossers)

    def pair_copy(at, src, dst, peer):
        copy = remote(src, dst, pair_send.at[at], pair_recv.at[at], peer)
        copy.start()
        return copy

    def to_all(src, dst, sends, recvs):
        copies = [
            remote(src, dst.at[me], sends.at[j], recvs.at[j], peer) for j, peer in enumerate(peers)
        ]
        for copy in copies:
            copy.start()
        dst[me] = src[...]
        return copies

    block_rows, block = og_ref.shape[2], og_ref.shape[3]

    def rows_out(side):
        def emit(total):
            base = pl.multiple_of(side * (count * block_rows), count * block_rows)
            for i in range(count):
                og_out[pl.ds(pl.multiple_of(base + i * block_rows, 8), block_rows), :] = widen(total[i])
        return emit

    def lanes_out(which, side):
        def emit(total):
            tiles = block // lanes
            for i in range(count):
                value = widen(total[i])
                for j in range(tiles):
                    first = i * block_rows * 4 * tiles + (side * tiles + j) * 2 + which
                    ig_out[pl.ds(first, block_rows, stride=4 * tiles), :] = value[:, j * lanes : (j + 1) * lanes]
        return emit

    def small_slabs():
        slab = small_ref.shape[1] // 8
        return lambda at: (at // slab, slice((at % slab) * 8, (at % slab) * 8 + 8))

    place_of = small_slabs()

    def small_store(first, value):
        for j in range(value.shape[0] // 8):
            a, b = place_of(first // 8 + j)
            small_ref[a, b, :] = value[j * 8 : (j + 1) * 8]

    def small_emit(total):
        def read(first, size):
            parts = []
            for j in range(size // 8):
                a, b = place_of(first // 8 + j)
                parts.append(total[a, b, :])
            return jnp.concatenate(parts, axis=0) if len(parts) > 1 else parts[0]
        stepg_out[...] = read(0, rank)
        decayg_out[...] = read(rank, states)
        selectg_out[...] = read(rank + states, selects)
        smallg_out[...] = read(rank + states + selects, 8)

    plan = [
        (og_ref, 0, rows_out(col)),
        (og_ref, 1, rows_out(1 - col)),
        (igg_ref, 0, lanes_out(1, col)),
        (igg_ref, 1, lanes_out(1, 1 - col)),
        (igi_ref, 0, lanes_out(0, col)),
        (igi_ref, 1, lanes_out(0, 1 - col)),
    ]
    chunks = [
        Chunk(
            source.at[h], totals.at[i], landings[i], send.at[i], recv.at[i],
            stages_of(count, chunk_plan[i]), h == 1, emit,
        )
        for i, (source, h, emit) in enumerate(plan)
    ]
    small_chunk = Chunk(
        small_ref, small_total, landings[-1], send.at[len(plan)], recv.at[len(plan)],
        stages_of(count, False), False, small_emit,
    )

    drive = og_out.at[0:rows]
    dg_ref = og_out.at[rows : 2 * rows]

    def b_at(n, step):
        return ig_out[pl.ds(pl.multiple_of(n * rows + step * spans, spans), spans), :]

    c0, c1, c2, c3, c4, c5 = chunks
    flow_copies = to_all(flow_ref, flows_ref, flow_send, flow_recv)
    advance_all((c0, c1, c2, c3))
    decay_rows(dl_ref, rate_ref, log2e)
    rate = -jnp.exp(dl_ref[...]) * log2e
    sel = sel_ref[...]
    drive[...] = delta_ref[...] * act_ref[...].astype(F32)
    for n in range(states):
        ig_out[n * rows : (n + 1) * rows, :] = jnp.broadcast_to(
            sel[:, rank + n : rank + n + 1], (rows, lanes)
        )
    c_ref[...] = spread(sel[:, rank + states :], states)
    index2 = span_index((spans, inner))
    cum = cum_ref[...]
    after = cum[spans - 1 : spans, :] - cum
    inside = index2 < spans - 1
    slot = lax.broadcasted_iota(jnp.int32, (count, 1, 1), 0)

    def visit(visited, carry):
        target = count - 1 - visited
        _, total = segment_sum(table_ref, target, states)
        flow = flows_ref[target].astype(F32) + jnp.exp2(rate * total) * grads[target]
        grads[...] = grads[...] + jnp.where(slot == parents_ref[target], flow[None], 0.0)
        return carry

    groups = inner // lanes
    pumps = {
        (1, 0): (c0, c1), (2, 0): (c2, c3), (2, 1): (c1,), (3, 0): (c0, c3), (3, 1): (c1,),
    }
    for group in range(groups):
        here = slice(group * lanes, (group + 1) * lanes)

        def advance(step, carry):
            d = delta_ref[step_ds(step), here]
            w = drive[step_ds(step), here]
            out = []
            for n in range(states):
                state_buf[n, step_ds(step), :] = carry[n]
                a = jnp.exp2(d * rate_ref[n, :, here])
                decay_buf[n, step_ds(step), :] = a
                out.append(a * carry[n] + w * b_at(n, step))
            return tuple(out)

        advance_all(pumps.get((group, 0), ()))
        finals = lax.fori_loop(0, steps, advance, tuple(starts_ref[n, :, here] for n in range(states)))
        for n in range(states):
            state_buf[n, rows : rows + spans, :] = finals[n]
        if group == 0:
            for copy in flow_copies:
                copy.wait()
            grads[...] = jnp.zeros(grads.shape, F32)
            lax.fori_loop(0, count - 1, visit, 0)
        advance_all(pumps.get((group, 1), ()))
        end_grad = grads[me]

        later = []
        for n in range(states):
            flow = jnp.where(inside[:, here], shift_spans(back_ref[n, :, here], -1), 0.0)
            later.append(flow + jnp.exp2(after[:, here] * rate_ref[n, :, here]) * end_grad[n : n + 1, here])

        def retreat(back, carry):
            step = steps - 1 - back
            at = step_ds(step)
            d = delta_ref[at, here]
            p = pgrad_ref[at, here]
            w = drive[at, here]
            flows, sums = carry
            new_flows, new_sums = [], []
            weighted = [None, None]
            decayed = [None, None]
            for n in range(states):
                cols = slice(n * lanes, (n + 1) * lanes)
                a = decay_buf[n, at, :]
                adjoint = c_ref[at, cols] * p + flows[n]
                moved = a * adjoint
                growth = moved * state_buf[n, at, :]
                new_flows.append(moved)
                new_sums.append(sums[n] + growth * d)
                term = adjoint * b_at(n, step)
                weighted[n % 2] = term if weighted[n % 2] is None else weighted[n % 2] + term
                term = growth * rate_ref[n, :, here]
                decayed[n % 2] = term if decayed[n % 2] is None else decayed[n % 2] + term
                b_term = adjoint * w
                c_term = state_buf[n, step_ds(step + 1), :] * p
                if group == 0:
                    b_sum[at, cols] = b_term
                    c_sum[at, cols] = c_term
                else:
                    b_sum[at, cols] += b_term
                    c_sum[at, cols] += c_term
            bw = weighted[0] + weighted[1]
            dg_ref[at, here] = (decayed[0] + decayed[1]) * (1.0 / log2e) + act_ref[at, here].astype(F32) * bw
            agrad_ref[at, here] = bw * d
            return (tuple(new_flows), tuple(new_sums))

        zero = jnp.zeros((spans, lanes), F32)
        _, sums = lax.fori_loop(0, steps, retreat, (tuple(later), (zero,) * states))
        for n in range(states):
            dgrad_ref[n : n + 1, here] = (
                jnp.sum(sums[n], axis=0, keepdims=True) * rate[n : n + 1, here] * (1.0 / log2e)
            )

    live = (step_tokens(rows, steps) < length).astype(F32)
    step_pre_grad = dg_ref[...] * live * sigmoid(pre_ref[...])
    low = step_pre_grad.astype(BF16)
    gather = gather_matrix(states)
    sel_part[...] = jnp.concatenate(
        [dot_nt(low, tw_ref[...]), dot(b_sum[...].astype(BF16), gather), dot(c_sum[...].astype(BF16), gather)],
        axis=1,
    )
    first = pair_copy(0, sel_part, sel_row, row_peer())
    advance_all((c2, c3, c0, c1))
    bias_sum = jnp.sum(step_pre_grad, axis=0, keepdims=True)
    small_store(0, dot_tn(sel[:, :rank].astype(BF16), low))
    small_store(rank, dgrad_ref[...])
    first.wait()
    pair = sel_part[...] + sel_row[...]
    sel_low[...] = pair.astype(BF16)
    second = pair_copy(1, sel_low, sel_col, col_peer())
    sel_part[...] = pair
    order = to_tokens(rows, steps)
    naturalg = dot(order, ggrad_ref[...]).astype(BF16)
    gate_parts = [dot_nt(naturalg, wg[...]) for wg in (wg_ref, wgo_ref)]
    pre = conv_pre(ext_ref, cw_ref, cb_ref, rows, inner)
    slope = slope_of(pre, sigmoid(pre))
    base_grad = agrad_ref[...] + skip_ref[0:1, :].astype(F32) * pgrad_ref[...]
    advance_all((c3,))
    second.wait()
    selg = (sel_part[...] + sel_col[...].astype(F32)).astype(BF16)
    conv_in = (base_grad + dot_nt(selg, sw_ref[...])) * slope
    cig_ref[0:rows, :] = conv_in
    taps = cw_ref[...].astype(F32)
    tails = [jnp.zeros((5, inner), F32)]
    for i in range(3):
        line = jnp.zeros((1, inner), F32)
        for k in range(i + 1):
            line = line + taps[k : k + 1, :] * conv_in[(i - k) * spans : (i - k) * spans + 1, :]
        tails.append(line * (parents_ref[me] >= 0).astype(F32))
    tail_low = jnp.concatenate(tails, axis=0).astype(BF16)
    for h, wi in enumerate((wi_ref, wio_ref)):
        tpart_ref[h] = dot_nt(tail_low, wi[...])
    tail_first = pair_copy(2, tpart_ref, tail_row, row_peer())
    last_span = lax.broadcasted_iota(jnp.int32, (spans, inner), 0) == spans - 1
    for j in range(3):
        slab = jnp.roll(conv_in[j * spans : (j + 1) * spans], -1, axis=0)
        cig_ref[rows + j * spans : rows + (j + 1) * spans, :] = jnp.where(last_span, 0.0, slab)
    inner_grad = jnp.zeros((rows, inner), F32)
    for k in range(4):
        inner_grad = inner_grad + taps[k : k + 1, :] * cig_ref[(3 - k) * spans : (3 - k) * spans + rows, :]
    inner_low = inner_grad.astype(BF16)
    natural = dot(order, inner_low).astype(BF16)
    hid_copies = []
    for h, wi in ((1, wio_ref), (0, wi_ref)):
        part_ref[h] = (dot_nt(natural, wi[...]) + gate_parts[h]).astype(BF16)
        hid_copies.append(
            pair_copy(3 + h, part_ref.at[h, pl.ds(other, half), :], hid_row.at[h], row_peer())
        )
    tail_first.wait()
    tail_sum = tpart_ref[...] + tail_row[...]
    tail_low_ref[...] = tail_sum[1]
    tail_second = pair_copy(5, tail_low_ref, tail_col, col_peer())
    hid_copies[0].wait()
    hid_low[...] = (
        part_ref[1, pl.ds(mine, half), :].astype(F32) + hid_row[1].astype(F32)
    ).astype(BF16)
    hid_second = pair_copy(6, hid_low, hid_col, col_peer())
    for h in range(2):
        store_split(igi_ref.at[h], dot_tn(hid_ref[h], inner_low) + dot_tn(hidt_ref[h], tail_low))
    advance_all((c4, c5, c2, c1, c3))
    tail_second.wait()
    tail_own[...] = tail_sum[0] + tail_col[...]
    tail_copies = to_all(tail_own, tails_ref, tail_send, tail_recv)
    small_store(rank + states, dot_tn(selg, act_ref[...]))
    sums = [
        jnp.sum(conv_in * ext_ref[k * spans : k * spans + rows, :], axis=0, keepdims=True)
        for k in range(4)
    ]
    sums.append(jnp.sum(conv_in, axis=0, keepdims=True))
    sums.append(sgrad_ref[0:1, :])
    sums.append(bias_sum)
    sums.append(jnp.zeros((1, inner), F32))
    small_store(rank + states + selects, jnp.concatenate(sums, axis=0))
    for at in range((rank + states + selects + 8) // 8, small_ref.shape[0] * small_ref.shape[1] // 8):
        a, b = place_of(at)
        small_ref[a, b, :] = jnp.zeros((8, inner), F32)
    small_chunk.next()
    hid_copies[1].wait()
    hidden = part_ref[0, pl.ds(mine, half), :].astype(F32) + hid_row[0].astype(F32)
    advance_all((c0, c4))

    tok = tok_ref[...].astype(F32)
    toko = toko_ref[...].astype(F32)
    power = jnp.sum(tok * tok, axis=1, keepdims=True) + jnp.sum(toko * toko, axis=1, keepdims=True)
    inv = lax.rsqrt(power / width + norm_epsilon)
    normed = tok * inv
    margin8 = tails_ref.shape[1]
    positions = row * half + lax.broadcasted_iota(jnp.int32, (half, margin8), 0)
    line_of = lax.broadcasted_iota(jnp.int32, (half, margin8), 1)
    place = ((positions == length - margin8 + line_of) & (line_of >= margin8 - 3)).astype(F32)
    for copy in tail_copies:
        copy.wait()
    own_tail = jnp.zeros(tails_ref.shape[1:], F32)
    for child in range(count):
        is_child = (parents_ref[child] == me).astype(F32)
        own_tail = own_tail + is_child * tails_ref[child]
    hidden = hidden + jnp.dot(place, own_tail, preferred_element_type=F32, precision=lax.Precision.HIGHEST)
    hid_second.wait()
    hidden = hidden + hid_col[...].astype(F32)
    scaled = hidden * gain_ref[0:1, :].astype(F32)
    mean = jnp.sum(scaled * normed, axis=1, keepdims=True)
    mean_out[...] = lax.dot_general(
        jnp.ones((8, lanes), F32), jnp.broadcast_to(mean / lanes, (half, lanes)), (((1,), (1,)), ((), ())),
        preferred_element_type=F32, precision=lax.Precision.HIGHEST,
    )
    mean_copy = pair_copy(7, mean_out, mean_in, col_peer())
    gain_out[...] = jnp.broadcast_to(jnp.sum(hidden * normed, axis=0, keepdims=True), gain_out.shape)
    gain_copy = pair_copy(8, gain_out, gain_in, row_peer())
    advance_all((c5, small_chunk))
    gain_copy.wait()
    gain_pair[...] = gain_out[...] + gain_in[...]
    gain_copies = to_all(gain_pair, gains_ref, gain_send, gain_recv)
    mean_copy.wait()
    apart = lax.dot_general(
        mean_in[...], jnp.full((8, lanes), 0.125, F32), (((0,), (0,)), ((), ())),
        preferred_element_type=F32, precision=lax.Precision.HIGHEST,
    )
    mean = (mean + apart[:, 0:1]) / width
    tg_ref[...] = cot_ref[...] + inv * (scaled - normed * mean)
    advance_all((c4, small_chunk, c5))
    for copy in gain_copies:
        copy.wait()
    gain_total = gains_ref[0]
    for i in range(1, count):
        gain_total = gain_total + gains_ref[i]
    gg_ref[...] = gain_total
    run_out(chunks + [small_chunk])


def backward_call(args, count, rows, width, inner, states, rank, selects):
    half = width // 2
    tile = rows // 2
    block_rows = half // count
    small = small_rows(count, rank, states, selects)
    f32, bf16 = F32, BF16
    vm = pltpu.VMEM
    scratch = [
        vm((count, states, inner), bf16), vm((count, states, inner), f32),
        vm((rows, states * lanes), f32), vm((states, spans, inner), f32),
        vm((states, rows, lanes), f32), vm((states, rows + spans, lanes), f32),
        vm((rows, states * lanes), f32), vm((rows, states * lanes), f32),
        vm((rows, inner), f32), vm((states, inner), f32),
        vm((rows, selects), f32), vm((rows, selects), f32), vm((rows, selects), bf16), vm((rows, selects), bf16),
        vm((rows + 3 * spans, inner), f32), vm((2, rows, half), bf16), vm((2, 8, half), f32),
        vm((2, tile, half), bf16), vm((2, 8, half), f32), vm((tile, half), bf16), vm((tile, half), bf16),
        vm((8, half), f32), vm((8, half), f32), vm((8, half), f32), vm((count, 8, half), f32),
        vm((8, tile), f32), vm((8, tile), f32), vm((8, half), f32), vm((8, half), f32), vm((8, half), f32),
        vm((count, 8, half), f32),
        vm((2, count, block_rows, inner), bf16), vm((count, small, inner), f32),
        vm((6, count, block_rows, inner), bf16), vm((count, small, inner), f32),
    ]
    most = 0
    for i, paired in enumerate(chunk_plan + (False,)):
        last = i == len(chunk_plan)
        sizes, copies = stage_sizes(stages_of(count, paired), count, i % 2 == 1)
        most = max(most, copies)
        scratch += [
            vm(size + ((small, inner) if last else (block_rows, inner)), f32 if last else bf16) for size in sizes
        ]
    dma = pltpu.SemaphoreType.DMA
    scratch += [dma((7, most))] * 2 + [dma((9,))] * 2 + [dma((count,))] * 6
    return run_kernel(
        functools.partial(backward_kernel, width=width),
        (
            struct((2 * inner, half), f32),
            struct((half * 4 * inner // lanes, lanes), f32),
            struct((tile, half), f32),
            struct((8, half), f32),
            struct((rank, inner), f32),
            struct((states, inner), f32),
            struct((selects, inner), f32),
            struct((8, inner), f32),
        ),
        args,
        "backward",
        scratch=scratch,
        flops=16e9,
        collective=4,
        grant=vmem_most,
    )


def on_device(
    tokens_in, teacher, norm_gain, in_weight, conv_weight, conv_bias, select_weight, step_weight,
    step_bias, decay_log, skip_gain, out_weight, parents, lengths, valid_rows,
):
    rows, width = tokens_in.shape
    half = norm_gain.shape[0]
    inner = decay_log.shape[1]
    states = decay_log.shape[0]
    rank = step_weight.shape[0]
    selects = rank + 2 * states
    steps = rows // spans
    count = lax.axis_size("seq")
    row_len = rows // lax.axis_size("row")
    row = lax.axis_index("row")
    col = lax.axis_index("col")
    me = lax.axis_index("seq")
    my_len = lengths[me][None]
    my_parent = parents[me][None]
    my_valid = valid_rows[me][None]
    me1 = me.astype(jnp.int32)[None]
    scale = jnp.full((8, lanes), 1.0, F32) * (rows * count / jnp.sum(valid_rows).astype(F32))

    def halves(value, axis):
        size = value.shape[axis] // 2
        own = lax.dynamic_slice_in_dim(value, col * size, size, axis)
        other = lax.dynamic_slice_in_dim(value, (1 - col) * size, size, axis)
        return own, other

    def rows8(value):
        return jnp.broadcast_to(value[None, :], (8, value.shape[0]))

    swap = [(0, 1), (1, 0)]
    tok, toko = halves(tokens_in, 1)
    tail = lax.dynamic_slice_in_dim(tokens_in, my_len[0] - 8, 8, 0)
    w_own, w_send = halves(in_weight, 2)
    wi, wg = w_own[:, 0], w_own[:, 1]
    wi_send, wg_send = w_send[:, 0], w_send[:, 1]
    ow, ow_send = halves(out_weight, 0)
    gain = rows8(norm_gain)
    skip = rows8(skip_gain)
    conv_b = rows8(conv_bias)
    step_b = rows8(step_bias)

    tails, wio, gaino = entry_exchange(tail, wi_send, gain, count)
    wg_send, ow_send, wio = lax.optimization_barrier((wg_send, ow_send, wio))
    wgo = lax.ppermute(wg_send, "col", swap)
    owo = lax.ppermute(ow_send, "col", swap)
    tails_own, tails_oth = halves(tails, 2)

    hid, hid_tail, ext, act, sel_part = run_kernel(
        forward_in_kernel,
        (
            struct((2, rows, half), BF16),
            struct((2, 8, half), BF16),
            struct((rows + 3 * spans, inner), F32),
            struct((rows, inner), BF16),
            struct((rows, selects), F32),
        ),
        (tok, toko, tails_own, tails_oth, gain, gaino, wi, wio, conv_weight, conv_b, select_weight, my_parent),
        "forward_in",
        flops=2e9,
    )
    sel = quad_sum(sel_part, 1, "select_sum")
    delta, step_pre, reach, cum, seg_map = run_kernel(
        forward_ends_kernel,
        (
            struct((rows, inner), F32),
            struct((rows, inner), F32),
            struct((states, spans, inner), F32),
            struct((spans, inner), F32),
            struct((states + 8, inner), BF16),
        ),
        (sel, step_weight, step_b, decay_log, act, my_len),
        "forward_ends",
        scratch=[
            pltpu.VMEM((rows, inner), F32),
            pltpu.VMEM((rows, states * lanes), F32),
            pltpu.VMEM((states, spans, inner), F32),
        ],
        flops=2e9,
    )
    table = seq_gather(seg_map, count, 2, "state_gather")
    starts, mixed_pre, gate, mixed, part = run_kernel(
        forward_out_kernel,
        (
            struct((states, spans, inner), F32),
            struct((rows, inner), F32),
            struct((rows, inner), F32),
            struct((rows, inner), BF16),
            struct((2, rows, half), BF16),
        ),
        (
            table, parents, me1, decay_log, reach, cum, delta, act, sel, hid, wg, wgo, skip, ow, owo,
        ),
        "forward_out",
        scratch=[
            pltpu.VMEM((count, states, inner), F32),
            pltpu.VMEM((rows, inner), F32),
            pltpu.VMEM((rows, states * lanes), F32),
            pltpu.VMEM((rows, states * lanes), F32),
            pltpu.VMEM((states, spans, inner), F32),
        ],
        flops=4e9,
    )
    tok_tile = lax.dynamic_slice_in_dim(tok, row * row_len, row_len, 0)
    toko_tile = lax.dynamic_slice_in_dim(toko, row * row_len, row_len, 0)
    teach_tile = lax.dynamic_slice_in_dim(teacher, row * row_len, row_len, 0)
    output, cot_tile, cot = middle_exchange(part, tok_tile, teach_tile, my_valid, scale)
    out_part, gate_grad, ig_gate, pre_grad, skip_part, back, flow = run_kernel(
        backward_in_kernel,
        (
            struct((2, count, inner // count, half), BF16),
            struct((rows, inner), BF16),
            struct((2, count, half // count, inner), BF16),
            struct((rows, inner), F32),
            struct((8, inner), F32),
            struct((states, spans, inner), F32),
            struct((states, inner), BF16),
        ),
        (cot, mixed, ow, owo, gate, mixed_pre, act, skip, sel, delta, decay_log, cum, hid),
        "backward_in",
        scratch=[
            pltpu.VMEM((rows, states * lanes), F32),
            pltpu.VMEM((states, spans, inner), F32),
        ],
        flops=4e9,
    )
    out_grad, in_both, tokens_grad, gain_grad, step_grad, decay_grad, select_grad, small = backward_call(
        (
            table, flow, parents, lengths, decay_log, starts, back, cum, delta, act, sel, pre_grad,
            step_pre, step_weight, select_weight, skip, ext, conv_weight, conv_b, hid, hid_tail,
            wi, wio, wg, wgo, gate_grad, tok_tile, toko_tile, gain, cot_tile, out_part, ig_gate, skip_part,
        ),
        count, rows, width, inner, states, rank, selects,
    )
    in_grad = in_both.reshape(half, -1, 2, lanes).transpose(0, 2, 1, 3).reshape(half, 2, -1)
    conv_grad, conv_bias_grad, skip_grad, step_bias_grad = small[:4], small[4:5], small[5:6], small[6:7]
    return (
        output,
        tokens_grad,
        gain_grad[0],
        in_grad,
        conv_grad,
        conv_bias_grad[0],
        select_grad.T,
        step_grad,
        step_bias_grad[0],
        decay_grad,
        skip_grad[0],
        out_grad,
    )


def solution(mesh):
    placed = (
        P("seq", None),
        P("seq", "col"),
        P("col"),
        P("col", None, "row"),
        P(None, ("row", "col")),
        P(("row", "col")),
        P(("row", "col"), None),
        P(None, ("row", "col")),
        P(("row", "col")),
        P(None, ("row", "col")),
        P(("row", "col")),
        P("row", "col"),
        P(),
        P(),
        P(),
    )
    return jax.shard_map(
        on_device,
        mesh=mesh,
        in_specs=placed,
        out_specs=(
            P(("seq", "row"), "col"),
            P(("seq", "row"), "col"),
            P("col"),
            P("col", None, "row"),
            P(None, ("row", "col")),
            P(("row", "col")),
            P(("row", "col"), None),
            P(None, ("row", "col")),
            P(("row", "col")),
            P(None, ("row", "col")),
            P(("row", "col")),
            P("row", "col"),
        ),
        check_vma=False,
    )
```

```python
import functools

import jax
import jax.numpy as jnp
from jax import lax
from jax.experimental import pallas as pl
from jax.experimental.pallas import tpu as pltpu
from jax.sharding import PartitionSpec as P

MESH = pl.DeviceIdType.MESH
F32 = jnp.float32
BF16 = jnp.bfloat16
norm_epsilon = 1e-05
spans = 8
lanes = 128
log2e = 1.4426950408889634
vmem_bytes = 60 * 1024 * 1024
vmem_most = 67043328
chunk_plan = (False, True, False, True, False, False)


def vmem_spec():
    return pl.BlockSpec(memory_space=pltpu.VMEM)


def smem_spec():
    return pl.BlockSpec(memory_space=pltpu.SMEM)


def struct(shape, dtype):
    return jax.ShapeDtypeStruct(shape, dtype)


def dot(a, b):
    return jnp.dot(a, b, preferred_element_type=F32)


def dot_tn(a, b):
    return lax.dot_general(a, b, (((0,), (0,)), ((), ())), preferred_element_type=F32)


def dot_nt(a, b):
    return lax.dot_general(a, b, (((1,), (1,)), ((), ())), preferred_element_type=F32)


def sigmoid(v):
    return 1.0 / (1.0 + jnp.exp(-v))


def slope_of(v, sigma):
    return sigma * (1.0 + v * (1.0 - sigma))


def to_steps(rows, steps):
    place = lax.broadcasted_iota(jnp.int32, (rows, rows), 0)
    token = lax.broadcasted_iota(jnp.int32, (rows, rows), 1)
    return (token == (place % spans) * steps + place // spans).astype(F32).astype(BF16)


def to_tokens(rows, steps):
    token = lax.broadcasted_iota(jnp.int32, (rows, rows), 0)
    place = lax.broadcasted_iota(jnp.int32, (rows, rows), 1)
    return (token == (place % spans) * steps + place // spans).astype(F32).astype(BF16)


def step_tokens(rows, steps):
    place = lax.broadcasted_iota(jnp.int32, (rows, 1), 0)
    return (place % spans) * steps + place // spans


def spread_matrix(states):
    row = lax.broadcasted_iota(jnp.int32, (2 * states, states * lanes), 0)
    col = lax.broadcasted_iota(jnp.int32, (2 * states, states * lanes), 1)
    return (row % states == col // lanes).astype(F32).astype(BF16)


def gather_matrix(states):
    row = lax.broadcasted_iota(jnp.int32, (states * lanes, states), 0)
    col = lax.broadcasted_iota(jnp.int32, (states * lanes, states), 1)
    return (row // lanes == col).astype(F32).astype(BF16)


def spread(values, states):
    high = values.astype(BF16)
    rest = (values - high.astype(F32)).astype(BF16)
    return dot(jnp.concatenate([high, rest], axis=1), spread_matrix(states))


def shift_spans(values, amount):
    return jnp.roll(values, amount, axis=values.ndim - 2)


def span_index(shape):
    return lax.broadcasted_iota(jnp.int32, shape, len(shape) - 2)


def run_kernel(kernel, outs, args, name, scratch=(), flops=0, collective=None, grant=vmem_bytes):
    params = dict(vmem_limit_bytes=grant)
    if collective is not None:
        params.update(collective_id=collective, has_side_effects=True)
    return pl.pallas_call(
        kernel,
        out_shape=outs,
        in_specs=[
            smem_spec() if a.dtype == jnp.int32 else vmem_spec() for a in args
        ],
        out_specs=jax.tree.map(lambda _: vmem_spec(), outs),
        scratch_shapes=list(scratch),
        compiler_params=pltpu.CompilerParams(**params),
        cost_estimate=pl.CostEstimate(
            flops=int(flops),
            transcendentals=0,
            bytes_accessed=int(sum(a.size * a.dtype.itemsize for a in args)),
        ),
        name=name,
    )(*args)


def barrier_with(peers):
    barrier = pltpu.get_barrier_semaphore()
    for peer in peers:
        pl.semaphore_signal(barrier, inc=1, device_id=peer, device_id_type=MESH)
    pl.semaphore_wait(barrier, len(peers))


def remote(src, dst, send, recv, peer):
    return pltpu.make_async_remote_copy(
        src_ref=src, dst_ref=dst, send_sem=send, recv_sem=recv, device_id=peer, device_id_type=MESH
    )


def row_peer():
    return {"row": 1 - lax.axis_index("row")}


def col_peer():
    return {"col": 1 - lax.axis_index("col")}


def entry_kernel(tail_ref, wi_ref, gain_ref, tails_ref, wo_ref, gain_o_ref, tsend, trecv, csend, crecv):
    count = tails_ref.shape[0]
    me = lax.axis_index("seq")
    peers = [{"seq": lax.rem(me + j, count)} for j in range(1, count)]
    barrier_with([col_peer()] + peers)
    copies = []
    for j, peer in enumerate(peers):
        copies.append(remote(tail_ref, tails_ref.at[me], tsend.at[j], trecv.at[j], peer))
    copies.append(remote(gain_ref, gain_o_ref, csend.at[0], crecv.at[0], col_peer()))
    copies.append(remote(wi_ref, wo_ref, csend.at[1], crecv.at[1], col_peer()))
    for copy in copies:
        copy.start()
    tails_ref[me] = tail_ref[...]
    for copy in copies:
        copy.wait()


def entry_exchange(tail, wi_send, gain_send, count):
    return run_kernel(
        entry_kernel,
        (
            struct((count,) + tail.shape, tail.dtype),
            struct(wi_send.shape, wi_send.dtype),
            struct(gain_send.shape, gain_send.dtype),
        ),
        (tail, wi_send, gain_send),
        "entry_exchange",
        scratch=[
            pltpu.SemaphoreType.DMA((count,)),
            pltpu.SemaphoreType.DMA((count,)),
            pltpu.SemaphoreType.DMA((2,)),
            pltpu.SemaphoreType.DMA((2,)),
        ],
        collective=0,
    )


def seq_gather_kernel(x_ref, o_ref, send, recv):
    count = o_ref.shape[0]
    me = lax.axis_index("seq")
    peers = [{"seq": lax.rem(me + j, count)} for j in range(1, count)]
    barrier_with(peers)
    copies = [
        remote(x_ref, o_ref.at[me], send.at[j], recv.at[j], peer) for j, peer in enumerate(peers)
    ]
    for copy in copies:
        copy.start()
    o_ref[me] = x_ref[...]
    for copy in copies:
        copy.wait()


def seq_gather(x, count, collective, name):
    return run_kernel(
        seq_gather_kernel,
        struct((count,) + x.shape, x.dtype),
        (x,),
        name,
        scratch=[pltpu.SemaphoreType.DMA((count,)), pltpu.SemaphoreType.DMA((count,))],
        collective=collective,
    )


def quad_sum_kernel(x_ref, o_ref, from_row, to_col, from_col, send, recv):
    barrier_with([row_peer(), col_peer()])
    first = remote(x_ref, from_row, send.at[0], recv.at[0], row_peer())
    first.start()
    first.wait()
    pair = x_ref[...] + from_row[...]
    to_col[...] = pair.astype(BF16)
    second = remote(to_col, from_col, send.at[1], recv.at[1], col_peer())
    second.start()
    o_ref[...] = pair
    second.wait()
    o_ref[...] += from_col[...].astype(F32)


def quad_sum(x, collective, name):
    return run_kernel(
        quad_sum_kernel,
        struct(x.shape, F32),
        (x,),
        name,
        scratch=[
            pltpu.VMEM(x.shape, F32),
            pltpu.VMEM(x.shape, BF16),
            pltpu.VMEM(x.shape, BF16),
            pltpu.SemaphoreType.DMA((2,)),
            pltpu.SemaphoreType.DMA((2,)),
        ],
        collective=collective,
    )


def middle_kernel(
    part_ref, tok_ref, teach_ref, ints_ref,
    out_ref, cot_ref, low_ref,
    from_row, to_col, from_col, send, recv,
):
    half = tok_ref.shape[0]
    segments = ints_ref.shape[0]
    row = lax.axis_index("row")
    mine = pl.multiple_of(row * half, half)
    other = pl.multiple_of((1 - row) * half, half)
    barrier_with([row_peer(), col_peer()])
    first = [
        remote(part_ref.at[h, pl.ds(other, half), :], from_row.at[h], send.at[h], recv.at[h], row_peer())
        for h in (1, 0)
    ]
    for copy in first:
        copy.start()
    first[0].wait()
    to_col[...] = (
        part_ref[1, pl.ds(mine, half), :].astype(F32) + from_row[1].astype(F32)
    ).astype(BF16)
    second = remote(to_col, from_col, send.at[2], recv.at[2], col_peer())
    second.start()
    first[1].wait()
    tile = part_ref[0, pl.ds(mine, half), :].astype(F32) + from_row[0].astype(F32)
    tile = tile + tok_ref[...].astype(F32)
    second.wait()
    result = tile + from_col[...].astype(F32)
    out_ref[...] = result.astype(BF16)
    positions = mine + lax.broadcasted_iota(jnp.int32, (half, 1), 0)
    total = ints_ref[0]
    for i in range(1, segments):
        total = total + ints_ref[i]
    share = jnp.full((half, 1), total, jnp.int32).astype(F32)
    counted = (positions < ints_ref[lax.axis_index("seq")]).astype(F32) * ((2 * half * segments) / share)
    cot = (result - teach_ref[...].astype(F32)) * counted
    cot_ref[...] = cot
    low_ref[0, pl.ds(mine, half), :] = cot.astype(BF16)
    third = [
        remote(low_ref.at[0, pl.ds(mine, half), :], low_ref.at[1, pl.ds(mine, half), :], send.at[3], recv.at[3], col_peer()),
        remote(low_ref.at[0, pl.ds(mine, half), :], low_ref.at[0, pl.ds(mine, half), :], send.at[4], recv.at[4], row_peer()),
    ]
    for copy in third:
        copy.start()
    third[0].wait()
    fourth = remote(low_ref.at[1, pl.ds(mine, half), :], low_ref.at[1, pl.ds(mine, half), :], send.at[5], recv.at[5], row_peer())
    fourth.start()
    third[1].wait()
    fourth.wait()


def middle_exchange(part, tok_tile, teach_tile, valid_rows):
    _, rows, width = part.shape
    half = rows // 2
    return run_kernel(
        middle_kernel,
        (struct((half, width), BF16), struct((half, width), F32), struct((2, rows, width), BF16)),
        (part, tok_tile, teach_tile, valid_rows),
        "middle_exchange",
        scratch=[
            pltpu.VMEM((2, half, width), BF16),
            pltpu.VMEM((half, width), BF16),
            pltpu.VMEM((half, width), BF16),
            pltpu.SemaphoreType.DMA((6,)),
            pltpu.SemaphoreType.DMA((6,)),
        ],
        collective=3,
    )


def forward_in_kernel(
    tok_ref, toko_ref, tails_ref, tailso_ref, gain_ref, gaino_ref, wi_ref, wio_ref,
    cw_ref, cb_ref, sw_ref, ints_ref,
    hid_ref, hidt_ref, ext_ref, act_ref, sel_ref,
):
    rows, half = tok_ref.shape
    steps = rows // spans
    width = 2 * half
    above = ints_ref[lax.axis_index("seq")]
    parent = jnp.maximum(above, 0)
    present = (above >= 0).astype(F32)
    gain = gain_ref[0:1, :].astype(F32)
    gaino = gaino_ref[0:1, :].astype(F32)

    def hidden_of(own, other):
        own = own.astype(F32)
        other = other.astype(F32)
        total = jnp.sum(own * own, axis=1, keepdims=True) + jnp.sum(other * other, axis=1, keepdims=True)
        inv = lax.rsqrt(total / width + norm_epsilon)
        return (own * inv * gain).astype(BF16), (other * inv * gaino).astype(BF16)

    hid, hido = hidden_of(tok_ref[...], toko_ref[...])
    order = to_steps(rows, steps)
    hid = dot(order, hid).astype(BF16)
    hido = dot(order, hido).astype(BF16)
    hid_ref[0] = hid
    hid_ref[1] = hido
    inner = dot(hid, wi_ref[...]) + dot(hido, wio_ref[...])
    tail, tailo = hidden_of(tails_ref[parent], tailso_ref[parent])
    hidt_ref[0] = tail
    hidt_ref[1] = tailo
    tail_inner = (dot(tail, wi_ref[...]) + dot(tailo, wio_ref[...])) * present
    last = inner[rows - 3 * spans :]
    first_span = lax.broadcasted_iota(jnp.int32, (spans, half), 0) == 0
    for j in range(3):
        block = jnp.roll(last[j * spans : (j + 1) * spans], 1, axis=0)
        ext_ref[j * spans : (j + 1) * spans, :] = jnp.where(
            first_span, jnp.broadcast_to(tail_inner[5 + j : 6 + j, :], (spans, half)), block
        )
    ext_ref[3 * spans :, :] = inner
    taps = cw_ref[...].astype(F32)
    pre = jnp.broadcast_to(cb_ref[0:1, :].astype(F32), (rows, half))
    for k in range(4):
        pre = pre + taps[k : k + 1, :] * ext_ref[k * spans : k * spans + rows, :]
    act = (pre * sigmoid(pre)).astype(BF16)
    act_ref[...] = act
    chosen = dot(act, sw_ref[...])
    sel_ref[...] = jnp.concatenate(
        [chosen, jnp.zeros((rows, sel_ref.shape[1] - chosen.shape[1]), F32)], axis=1
    )


def conv_pre(ext_ref, cw_ref, cb_ref, rows, half):
    taps = cw_ref[...].astype(F32)
    pre = jnp.broadcast_to(cb_ref[0:1, :].astype(F32), (rows, half))
    for k in range(4):
        pre = pre + taps[k : k + 1, :] * ext_ref[k * spans : k * spans + rows, :]
    return pre


def group_ds(group):
    return pl.ds(pl.multiple_of(group * lanes, lanes), lanes)


def step_ds(step):
    return pl.ds(pl.multiple_of(step * spans, spans), spans)


def decay_rows(decay_log_ref, decay_b, scale):
    states, width = decay_log_ref.shape
    rate = -jnp.exp(decay_log_ref[...]) * scale
    for n in range(states):
        decay_b[n] = jnp.broadcast_to(rate[n : n + 1, :], (spans, width))


def span_sum_kernel_part(delta_ref, steps):
    total = delta_ref[0:spans, :]
    for s in range(1, steps):
        total = total + delta_ref[s * spans : (s + 1) * spans, :]
    return total


def forward_ends_kernel(
    sel_ref, tw_ref, tb_ref, dl_ref, act_ref, ints_ref,
    delta_ref, pre_ref, reach_ref, cum_ref, send_ref,
    drive, b_ref, rate_ref,
):
    rows, width = act_ref.shape
    steps = rows // spans
    states = dl_ref.shape[0]
    rank = tw_ref.shape[0]
    length = ints_ref[lax.axis_index("seq")]
    sel = sel_ref[...]
    step_pre = dot(sel[:, :rank].astype(BF16), tw_ref[...]) + tb_ref[0:1, :].astype(F32)
    pre_ref[...] = step_pre
    live = (step_tokens(rows, steps) < length).astype(F32)
    delta = (jnp.maximum(step_pre, 0.0) + jnp.log1p(jnp.exp(-jnp.abs(step_pre)))) * live
    delta_ref[...] = delta
    drive[...] = delta * act_ref[...].astype(F32)
    b_ref[...] = spread(sel[:, rank : rank + states], states)
    decay_rows(dl_ref, rate_ref, log2e)

    for group in range(width // lanes):
        here = slice(group * lanes, (group + 1) * lanes)

        def advance(step, carry):
            d = delta_ref[step_ds(step), here]
            w = drive[step_ds(step), here]
            out = []
            for n in range(states):
                a = jnp.exp2(d * rate_ref[n, :, here])
                out.append(a * carry[n] + w * b_ref[step_ds(step), n * lanes : (n + 1) * lanes])
            return tuple(out)

        ends = lax.fori_loop(0, steps, advance, (jnp.zeros((spans, lanes), F32),) * states)
        for n in range(states):
            reach_ref[n, :, here] = ends[n]

    total = span_sum_kernel_part(delta_ref, steps)
    index2 = span_index((spans, width))
    part = total
    shift = 1
    while shift < spans:
        inside = index2 >= shift
        for n in range(states):
            own = reach_ref[n]
            earlier = jnp.where(inside, shift_spans(own, shift), 0.0)
            reach_ref[n] = own + jnp.exp2(part * rate_ref[n]) * earlier
        part = part + jnp.where(inside, shift_spans(part, shift), 0.0)
        shift *= 2
    cum_ref[...] = part
    sums = part[spans - 1 : spans, :]
    high = sums.astype(BF16)
    mid = (sums - high.astype(F32)).astype(BF16)
    low = (sums - high.astype(F32) - mid.astype(F32)).astype(BF16)
    ends = jnp.concatenate([reach_ref[n, spans - 1 : spans, :] for n in range(states)], axis=0)
    extra = jnp.concatenate(
        [high.astype(F32), mid.astype(F32), low.astype(F32), jnp.zeros((5, width), F32)], axis=0
    )
    send_ref[...] = jnp.concatenate([ends, extra], axis=0).astype(BF16)


def segment_sum(table_ref, index, states):
    block = table_ref[index].astype(F32)
    return block[:states], block[states : states + 1] + block[states + 1 : states + 2] + block[states + 2 : states + 3]


def forward_out_kernel(
    table_ref, parents_ref, dl_ref, reach_ref, cum_ref, delta_ref, act_ref, sel_ref,
    hid_ref, wg_ref, wgo_ref, skip_ref, ow_ref, owo_ref,
    starts_ref, mpre_ref, gate_ref, mixed_ref, part_ref,
    finals, drive, b_ref, c_ref, rate_ref, *, rank
):
    rows, width = act_ref.shape
    steps = rows // spans
    states = dl_ref.shape[0]
    count = table_ref.shape[0]
    me = lax.axis_index("seq")
    decay_rows(dl_ref, rate_ref, log2e)
    rate = -jnp.exp(dl_ref[...]) * log2e

    def start_of(target):
        above = parents_ref[target]
        return finals[jnp.maximum(above, 0)] * (above >= 0).astype(F32)

    def visit(target, carry):
        end, total = segment_sum(table_ref, target, states)
        finals[target] = jnp.exp2(rate * total) * start_of(target) + end
        return carry

    finals[0] = jnp.zeros(finals.shape[1:], F32)
    lax.fori_loop(0, count, visit, 0)
    start = start_of(me)
    sel = sel_ref[...]
    drive[...] = delta_ref[...] * act_ref[...].astype(F32)
    b_ref[...] = spread(sel[:, rank : rank + states], states)
    c_ref[...] = spread(sel[:, rank + states : rank + 2 * states], states)
    index2 = span_index((spans, width))
    cum = jnp.where(index2 >= 1, shift_spans(cum_ref[...], 1), 0.0)
    for n in range(states):
        earlier = jnp.where(index2 >= 1, shift_spans(reach_ref[n], 1), 0.0)
        starts_ref[n] = jnp.exp2(cum * rate_ref[n]) * start[n : n + 1, :] + earlier

    for group in range(width // lanes):
        here = slice(group * lanes, (group + 1) * lanes)

        def advance(step, carry):
            d = delta_ref[step_ds(step), here]
            w = drive[step_ds(step), here]
            out = []
            reads = [None] * 4
            for n in range(states):
                a = jnp.exp2(d * rate_ref[n, :, here])
                now = a * carry[n] + w * b_ref[step_ds(step), n * lanes : (n + 1) * lanes]
                out.append(now)
                term = c_ref[step_ds(step), n * lanes : (n + 1) * lanes] * now
                reads[n % 4] = term if reads[n % 4] is None else reads[n % 4] + term
            mpre_ref[step_ds(step), here] = (reads[0] + reads[1]) + (reads[2] + reads[3])
            return tuple(out)

        lax.fori_loop(0, steps, advance, tuple(starts_ref[n, :, here] for n in range(states)))

    gate = dot(hid_ref[0], wg_ref[...]) + dot(hid_ref[1], wgo_ref[...])
    gate_ref[...] = gate
    mixed_pre = mpre_ref[...] + skip_ref[0:1, :].astype(F32) * act_ref[...].astype(F32)
    mpre_ref[...] = mixed_pre
    mixed = (mixed_pre * (gate * sigmoid(gate))).astype(BF16)
    mixed_ref[...] = mixed
    natural = dot(to_tokens(rows, steps), mixed).astype(BF16)
    part_ref[0] = dot(natural, ow_ref[...]).astype(BF16)
    part_ref[1] = dot(natural, owo_ref[...]).astype(BF16)


def seq_bits(count):
    bits = []
    mask = 1
    while mask < count:
        bits.append(mask)
        mask *= 2
    return bits


def stages_of(count, first_pair):
    bits = seq_bits(count)
    if len(bits) < 3:
        return [(mask,) for mask in bits]
    if first_pair:
        return [(bits[1],), (bits[0],)] + [(mask,) for mask in bits[2:]]
    return [(bits[0],), (bits[1], bits[2])] + [(mask,) for mask in bits[3:]]


def stage_sizes(stages, count, crossed):
    sizes, copies = [], 0
    for i, masks in enumerate(stages):
        radix = 2 ** len(masks)
        count //= radix
        got = radix if crossed and i == len(stages) - 1 else radix - 1
        sizes.append((got, count))
        copies += got + radix - 1
    return sizes, copies


def bit_of(me, mask):
    return (me // mask) % 2


def toward(me, masks, pick):
    device, part = me, 0
    for k, mask in enumerate(masks):
        bit = bit_of(me, mask)
        weight = 2 ** (len(masks) - 1 - k)
        if (pick // weight) % 2:
            device = device + mask - 2 * mask * bit
            bit = 1 - bit
        part = part + weight * bit
    return device, part


def widen(values):
    return values.astype(F32)


class Chunk:
    def __init__(self, source, total, landings, send, recv, stages, crossed):
        self.source, self.total, self.landings = source, total, landings
        self.send, self.recv, self.stages, self.crossed = send, recv, stages, crossed
        self.count = source.shape[0]
        self.me = lax.axis_index("seq")
        self.copies = []
        self.flying = []
        self.at = 0
        self.levels = len(stages)
        self.sizes = stage_sizes(stages, self.count, crossed)[0]

    def start(self, src, dst, peer):
        at = len(self.copies)
        copy = remote(src, dst, self.send.at[at], self.recv.at[at], peer)
        copy.start()
        self.copies.append(copy)
        self.flying.append(copy)

    def land(self):
        for copy in self.flying:
            copy.wait_recv()
        self.flying = []

    def place(self, level):
        start = 0
        for j in range(level + 1):
            start = start + toward(self.me, self.stages[j], 0)[1] * self.sizes[j][1]
        return start

    def crossing(self, level):
        return self.crossed and level == self.levels - 1

    def scatter(self, level):
        held = self.source if level == 0 else self.landings[level - 1].at[0]
        masks, (_, size) = self.stages[level], self.sizes[level]
        for pick in range(0 if self.crossing(level) else 1, 2 ** len(masks)):
            device, part = toward(self.me, masks, pick)
            peer = {"seq": device}
            if self.crossing(level):
                peer["col"] = 1 - lax.axis_index("col")
            slot = pick if self.crossing(level) else pick - 1
            self.start(held.at[pl.ds(part * size, size)], self.landings[level].at[slot], peer)

    def add(self, level):
        held = self.source if level == 0 else self.landings[level - 1].at[0]
        masks, (got, size) = self.stages[level], self.sizes[level]
        landing = self.landings[level]
        if self.crossing(level):
            total = widen(landing[0])
        else:
            own = toward(self.me, masks, 0)[1]
            total = widen(held[pl.ds(own * size, size)]) + widen(landing[0])
        for slot in range(1, got):
            total = total + widen(landing[slot])
        return total.astype(landing.dtype)

    def gather(self, level):
        size = self.sizes[level][1]
        region = self.total.at[pl.ds(self.place(level), size)]
        masks = self.stages[level]
        for pick in range(1, 2 ** len(masks)):
            self.start(region, region, {"seq": toward(self.me, masks, pick)[0]})

    def done(self):
        return self.at > 2 * self.levels

    def next(self):
        if self.done():
            return
        self.land()
        at, last = self.at, self.levels
        self.at += 1
        if at < last:
            if at > 0:
                self.landings[at - 1][0] = self.add(at - 1)
            self.scatter(at)
            return
        if at == last:
            self.total[pl.ds(self.place(last - 1), 1)] = self.add(last - 1)
        level = 2 * last - 1 - at
        if level >= 0:
            self.gather(level)

    def finish(self):
        for copy in self.copies:
            copy.wait_send()


def store_split(ref, value):
    rows = ref.shape[1]
    for i in range(ref.shape[0]):
        ref[i] = value[i * rows : (i + 1) * rows].astype(ref.dtype)


def advance_all(chunks):
    for chunk in chunks:
        chunk.next()


def run_out(chunks):
    while any(not chunk.done() for chunk in chunks):
        advance_all(chunks)
    for chunk in chunks:
        chunk.finish()


def small_rows(count, rank, states, selects):
    total = rank + states + selects + 8
    total += -total % (8 * count)
    return total // count


def backward_kernel(
    cotangent_ref, mixed_ref, ow_ref, owo_ref, gate_ref, mpre_ref,
    table_ref, parents_ref, lengths_ref, dl_ref, starts_ref, cum_ref,
    delta_ref, act_ref, sel_ref, pre_ref, tw_ref,
    sw_ref, skip_ref, ext_ref, cw_ref, cb_ref, hid_ref, hidt_ref, wi_ref, wio_ref, wg_ref, wgo_ref,
    tok_ref, toko_ref, gain_ref, cot_ref,
    totals, small_total, tg_ref, gg_ref,
    og_ref, igg_ref, ggrad_ref, pgrad_ref, back_ref, flow_ref,
    flows_ref, grads, c_ref, rate_ref, state_buf, b_sum, c_sum, agrad_ref, dgrad_ref,
    sel_part, sel_row, sel_low, sel_col, cig_ref, part_ref, tpart_ref,
    hid_row, tail_row, hid_low, hid_col, tail_low_ref, tail_col, tail_own, tails_ref,
    mean_out, mean_in, gain_out, gain_in, gains_ref,
    igi_ref, small_ref, og_out, ig_out, *rest,
    width,
):
    count = table_ref.shape[0]
    landings = []
    for paired in chunk_plan + (False,):
        size = len(stages_of(count, paired))
        landings.append(rest[:size])
        rest = rest[size:]
    send, recv, pair_send, pair_recv, flow_send, flow_recv, tail_send, tail_recv, gain_send, gain_recv = rest
    rows, inner = act_ref.shape
    half = rows // 2
    steps = rows // spans
    states = dl_ref.shape[0]
    rank = tw_ref.shape[0]
    selects = sw_ref.shape[1]
    me = lax.axis_index("seq")
    row = lax.axis_index("row")
    col = lax.axis_index("col")
    mine = pl.multiple_of(row * half, half)
    other = pl.multiple_of((1 - row) * half, half)
    length = lengths_ref[me]
    peers = [{"seq": lax.rem(me + j, count)} for j in range(1, count)]
    across = sorted(
        {(masks, pick) for masks in (stages_of(count, p)[-1] for p in chunk_plan) for pick in range(1, 2 ** len(masks))}
    )
    flips = sorted({sum(m for k, m in enumerate(masks) if (pick >> (len(masks) - 1 - k)) % 2) for masks, pick in across})
    crossers = []
    for flip in flips:
        masks = tuple(m for m in seq_bits(count) if (flip // m) % 2)
        crossers.append({"seq": toward(me, masks, 2 ** len(masks) - 1)[0], "col": 1 - col})
    barrier_with([row_peer(), col_peer()] + peers + crossers)

    def pair_copy(at, src, dst, peer):
        copy = remote(src, dst, pair_send.at[at], pair_recv.at[at], peer)
        copy.start()
        return copy

    def to_all(src, dst, sends, recvs):
        copies = [
            remote(src, dst.at[me], sends.at[j], recvs.at[j], peer) for j, peer in enumerate(peers)
        ]
        for copy in copies:
            copy.start()
        dst[me] = src[...]
        return copies

    def small_slabs():
        slab = small_ref.shape[1] // 8
        return lambda at: (at // slab, slice((at % slab) * 8, (at % slab) * 8 + 8))

    place_of = small_slabs()

    def small_store(first, value):
        for j in range(value.shape[0] // 8):
            a, b = place_of(first // 8 + j)
            small_ref[a, b, :] = value[j * 8 : (j + 1) * 8]

    sources = [og_ref.at[0], og_ref.at[1], igg_ref.at[0], igg_ref.at[1], igi_ref.at[0], igi_ref.at[1]]
    chunks = [
        Chunk(
            source, totals.at[i], landings[i], send.at[i], recv.at[i],
            stages_of(count, chunk_plan[i]), i % 2 == 1,
        )
        for i, source in enumerate(sources)
    ]
    small_chunk = Chunk(
        small_ref, small_total, landings[-1], send.at[len(sources)], recv.at[len(sources)],
        stages_of(count, False), False,
    )

    drive = og_out.at[0:rows]
    dg_ref = og_out.at[rows : 2 * rows]

    def b_at(n, step):
        return ig_out[pl.ds(pl.multiple_of(n * rows + step * spans, spans), spans), :]

    c0, c1, c2, c3, c4, c5 = chunks
    early = {2: (c0, c1), -1: (c2, c3)}
    pumps = {
        (1, 0): (c0, c1), (2, 0): (c2, c3), (2, 1): (c1,), (3, 0): (c0, c3), (3, 1): (c1,),
    }
    from_tokens = to_steps(rows, steps)
    cot = dot(from_tokens, cotangent_ref[0]).astype(BF16)
    coto = dot(from_tokens, cotangent_ref[1]).astype(BF16)
    store_split(og_ref.at[0], dot_tn(mixed_ref[...], cot))
    store_split(og_ref.at[1], dot_tn(mixed_ref[...], coto))
    advance_all((c0, c1))
    mixed_grad = dot_nt(cot, ow_ref[...]) + dot_nt(coto, owo_ref[...])
    gate = gate_ref[...]
    sigma = sigmoid(gate)
    pre_grad = mixed_grad * (gate * sigma)
    pgrad_ref[...] = pre_grad
    gate_grad = (mixed_grad * mpre_ref[...] * slope_of(gate, sigma)).astype(BF16)
    ggrad_ref[...] = gate_grad
    store_split(igg_ref.at[0], dot_tn(hid_ref[0], gate_grad))
    store_split(igg_ref.at[1], dot_tn(hid_ref[1], gate_grad))
    advance_all((c2, c3))
    skip_sum = jnp.sum(pre_grad * act_ref[...].astype(F32), axis=0, keepdims=True)
    decay_rows(dl_ref, rate_ref, log2e)
    c_ref[...] = spread(sel_ref[:, rank + states : rank + 2 * states], states)

    for group in range(inner // lanes):
        here = slice(group * lanes, (group + 1) * lanes)

        def fall(back, carry):
            step = steps - 1 - back
            d = delta_ref[step_ds(step), here]
            p = pgrad_ref[step_ds(step), here]
            out = []
            for n in range(states):
                a = jnp.exp2(d * rate_ref[n, :, here])
                out.append(a * (c_ref[step_ds(step), n * lanes : (n + 1) * lanes] * p + carry[n]))
            return tuple(out)

        advance_all(early.get(group, ()))
        ends = lax.fori_loop(0, steps, fall, (jnp.zeros((spans, lanes), F32),) * states)
        for n in range(states):
            back_ref[n, :, here] = ends[n]

    index2 = span_index((spans, inner))
    cum = cum_ref[...]
    part = cum - jnp.where(index2 >= 1, shift_spans(cum, 1), 0.0)
    shift = 1
    while shift < spans:
        inside = index2 < spans - shift
        for n in range(states):
            own = back_ref[n]
            later = jnp.where(inside, shift_spans(own, -shift), 0.0)
            back_ref[n] = own + jnp.exp2(part * rate_ref[n]) * later
        part = part + jnp.where(inside, shift_spans(part, -shift), 0.0)
        shift *= 2
    flow_ref[...] = jnp.concatenate(
        [back_ref[n, 0:1, :] for n in range(states)], axis=0
    ).astype(BF16)

    flow_copies = to_all(flow_ref, flows_ref, flow_send, flow_recv)
    advance_all(early.get(-1, ()))
    rate = -jnp.exp(dl_ref[...]) * log2e
    sel = sel_ref[...]
    drive[...] = delta_ref[...] * act_ref[...].astype(F32)
    for n in range(states):
        ig_out[n * rows : (n + 1) * rows, :] = jnp.broadcast_to(
            sel[:, rank + n : rank + n + 1], (rows, lanes)
        )
    after = cum[spans - 1 : spans, :] - cum
    inside = index2 < spans - 1
    slot = lax.broadcasted_iota(jnp.int32, (count, 1, 1), 0)

    def visit(visited, carry):
        target = count - 1 - visited
        _, total = segment_sum(table_ref, target, states)
        flow = flows_ref[target].astype(F32) + jnp.exp2(rate * total) * grads[target]
        grads[...] = grads[...] + jnp.where(slot == parents_ref[target], flow[None], 0.0)
        return carry

    groups = inner // lanes
    for group in range(groups):
        here = slice(group * lanes, (group + 1) * lanes)

        def advance(step, carry):
            d = delta_ref[step_ds(step), here]
            w = drive[step_ds(step), here]
            out = []
            for n in range(states):
                state_buf[n, step_ds(step), :] = carry[n]
                a = jnp.exp2(d * rate_ref[n, :, here])
                out.append(a * carry[n] + w * b_at(n, step))
            return tuple(out)

        advance_all(pumps.get((group, 0), ()))
        finals = lax.fori_loop(0, steps, advance, tuple(starts_ref[n, :, here] for n in range(states)))
        for n in range(states):
            state_buf[n, rows : rows + spans, :] = finals[n]
        if group == 0:
            for copy in flow_copies:
                copy.wait()
            grads[...] = jnp.zeros(grads.shape, F32)
            lax.fori_loop(0, count - 1, visit, 0)
        advance_all(pumps.get((group, 1), ()))
        end_grad = grads[me]

        later = []
        for n in range(states):
            flow = jnp.where(inside[:, here], shift_spans(back_ref[n, :, here], -1), 0.0)
            later.append(flow + jnp.exp2(after[:, here] * rate_ref[n, :, here]) * end_grad[n : n + 1, here])

        def retreat(back, carry):
            step = steps - 1 - back
            at = step_ds(step)
            d = delta_ref[at, here]
            p = pgrad_ref[at, here]
            w = drive[at, here]
            flows, sums = carry
            new_flows, new_sums = [], []
            weighted = [None, None]
            decayed = [None, None]
            for n in range(states):
                cols = slice(n * lanes, (n + 1) * lanes)
                a = jnp.exp2(d * rate_ref[n, :, here])
                adjoint = c_ref[at, cols] * p + flows[n]
                moved = a * adjoint
                growth = moved * state_buf[n, at, :]
                new_flows.append(moved)
                new_sums.append(sums[n] + growth * d)
                term = adjoint * b_at(n, step)
                weighted[n % 2] = term if weighted[n % 2] is None else weighted[n % 2] + term
                term = growth * rate_ref[n, :, here]
                decayed[n % 2] = term if decayed[n % 2] is None else decayed[n % 2] + term
                b_term = adjoint * w
                c_term = state_buf[n, step_ds(step + 1), :] * p
                if group == 0:
                    b_sum[at, cols] = b_term
                    c_sum[at, cols] = c_term
                else:
                    b_sum[at, cols] += b_term
                    c_sum[at, cols] += c_term
            bw = weighted[0] + weighted[1]
            dg_ref[at, here] = (decayed[0] + decayed[1]) * (1.0 / log2e) + act_ref[at, here].astype(F32) * bw
            agrad_ref[at, here] = bw * d
            return (tuple(new_flows), tuple(new_sums))

        zero = jnp.zeros((spans, lanes), F32)
        _, sums = lax.fori_loop(0, steps, retreat, (tuple(later), (zero,) * states))
        for n in range(states):
            dgrad_ref[n : n + 1, here] = (
                jnp.sum(sums[n], axis=0, keepdims=True) * rate[n : n + 1, here] * (1.0 / log2e)
            )

    live = (step_tokens(rows, steps) < length).astype(F32)
    step_pre_grad = dg_ref[...] * live * sigmoid(pre_ref[...])
    low = step_pre_grad.astype(BF16)
    gather = gather_matrix(states)
    sel_part[...] = jnp.concatenate(
        [
            dot_nt(low, tw_ref[...]), dot(b_sum[...].astype(BF16), gather),
            dot(c_sum[...].astype(BF16), gather), jnp.zeros((rows, sel_part.shape[1] - selects), F32),
        ],
        axis=1,
    )
    first = pair_copy(0, sel_part, sel_row, row_peer())
    advance_all((c2, c3, c0, c1))
    bias_sum = jnp.sum(step_pre_grad, axis=0, keepdims=True)
    small_store(0, dot_tn(sel[:, :rank].astype(BF16), low))
    small_store(rank, dgrad_ref[...])
    first.wait()
    pair = sel_part[...] + sel_row[...]
    sel_low[...] = pair.astype(BF16)
    second = pair_copy(1, sel_low, sel_col, col_peer())
    sel_part[...] = pair
    order = to_tokens(rows, steps)
    naturalg = dot(order, ggrad_ref[...]).astype(BF16)
    gate_parts = [dot_nt(naturalg, wg[...]) for wg in (wg_ref, wgo_ref)]
    pre = conv_pre(ext_ref, cw_ref, cb_ref, rows, inner)
    slope = slope_of(pre, sigmoid(pre))
    base_grad = agrad_ref[...] + skip_ref[0:1, :].astype(F32) * pgrad_ref[...]
    advance_all((c3,))
    second.wait()
    selg = (sel_part[...] + sel_col[...].astype(F32)).astype(BF16)[:, :selects]
    conv_in = (base_grad + dot_nt(selg, sw_ref[...])) * slope
    cig_ref[0:rows, :] = conv_in
    taps = cw_ref[...].astype(F32)
    tails = [jnp.zeros((5, inner), F32)]
    for i in range(3):
        line = jnp.zeros((1, inner), F32)
        for k in range(i + 1):
            line = line + taps[k : k + 1, :] * conv_in[(i - k) * spans : (i - k) * spans + 1, :]
        tails.append(line * (parents_ref[me] >= 0).astype(F32))
    tail_low = jnp.concatenate(tails, axis=0).astype(BF16)
    for h, wi in enumerate((wi_ref, wio_ref)):
        tpart_ref[h] = dot_nt(tail_low, wi[...])
    tail_first = pair_copy(2, tpart_ref, tail_row, row_peer())
    last_span = lax.broadcasted_iota(jnp.int32, (spans, inner), 0) == spans - 1
    for j in range(3):
        slab = jnp.roll(conv_in[j * spans : (j + 1) * spans], -1, axis=0)
        cig_ref[rows + j * spans : rows + (j + 1) * spans, :] = jnp.where(last_span, 0.0, slab)
    inner_grad = jnp.zeros((rows, inner), F32)
    for k in range(4):
        inner_grad = inner_grad + taps[k : k + 1, :] * cig_ref[(3 - k) * spans : (3 - k) * spans + rows, :]
    inner_low = inner_grad.astype(BF16)
    natural = dot(order, inner_low).astype(BF16)
    hid_copies = []
    for h, wi in ((1, wio_ref), (0, wi_ref)):
        part_ref[h] = (dot_nt(natural, wi[...]) + gate_parts[h]).astype(BF16)
        hid_copies.append(
            pair_copy(3 + h, part_ref.at[h, pl.ds(other, half), :], hid_row.at[h], row_peer())
        )
    tail_first.wait()
    tail_sum = tpart_ref[...] + tail_row[...]
    tail_low_ref[...] = tail_sum[1]
    tail_second = pair_copy(5, tail_low_ref, tail_col, col_peer())
    hid_copies[0].wait()
    hid_low[...] = (
        part_ref[1, pl.ds(mine, half), :].astype(F32) + hid_row[1].astype(F32)
    ).astype(BF16)
    hid_second = pair_copy(6, hid_low, hid_col, col_peer())
    for h in range(2):
        store_split(igi_ref.at[h], dot_tn(hid_ref[h], inner_low) + dot_tn(hidt_ref[h], tail_low))
    advance_all((c4, c5, c2, c1, c3))
    tail_second.wait()
    tail_own[...] = tail_sum[0] + tail_col[...]
    tail_copies = to_all(tail_own, tails_ref, tail_send, tail_recv)
    small_store(rank + states, dot_tn(selg, act_ref[...]))
    sums = [
        jnp.sum(conv_in * ext_ref[k * spans : k * spans + rows, :], axis=0, keepdims=True)
        for k in range(4)
    ]
    sums.append(jnp.sum(conv_in, axis=0, keepdims=True))
    sums.append(skip_sum)
    sums.append(bias_sum)
    sums.append(jnp.zeros((1, inner), F32))
    small_store(rank + states + selects, jnp.concatenate(sums, axis=0))
    for at in range((rank + states + selects + 8) // 8, small_ref.shape[0] * small_ref.shape[1] // 8):
        a, b = place_of(at)
        small_ref[a, b, :] = jnp.zeros((8, inner), F32)
    small_chunk.next()
    hid_copies[1].wait()
    hidden = part_ref[0, pl.ds(mine, half), :].astype(F32) + hid_row[0].astype(F32)
    advance_all((c0, c4))

    tok = tok_ref[...].astype(F32)
    toko = toko_ref[...].astype(F32)
    power = jnp.sum(tok * tok, axis=1, keepdims=True) + jnp.sum(toko * toko, axis=1, keepdims=True)
    inv = lax.rsqrt(power / width + norm_epsilon)
    normed = tok * inv
    margin8 = tails_ref.shape[1]
    positions = row * half + lax.broadcasted_iota(jnp.int32, (half, margin8), 0)
    line_of = lax.broadcasted_iota(jnp.int32, (half, margin8), 1)
    place = ((positions == length - margin8 + line_of) & (line_of >= margin8 - 3)).astype(F32)
    for copy in tail_copies:
        copy.wait()
    own_tail = jnp.zeros(tails_ref.shape[1:], F32)
    for child in range(count):
        is_child = (parents_ref[child] == me).astype(F32)
        own_tail = own_tail + is_child * tails_ref[child]
    hidden = hidden + jnp.dot(place, own_tail, preferred_element_type=F32, precision=lax.Precision.HIGHEST)
    hid_second.wait()
    hidden = hidden + hid_col[...].astype(F32)
    scaled = hidden * gain_ref[0:1, :].astype(F32)
    mean = jnp.sum(scaled * normed, axis=1, keepdims=True)
    mean_out[...] = lax.dot_general(
        jnp.ones((8, lanes), F32), jnp.broadcast_to(mean / lanes, (half, lanes)), (((1,), (1,)), ((), ())),
        preferred_element_type=F32, precision=lax.Precision.HIGHEST,
    )
    mean_copy = pair_copy(7, mean_out, mean_in, col_peer())
    gain_out[...] = jnp.broadcast_to(jnp.sum(hidden * normed, axis=0, keepdims=True), gain_out.shape)
    gain_copy = pair_copy(8, gain_out, gain_in, row_peer())
    advance_all((c5, small_chunk))
    gain_copy.wait()
    gain_out[...] = gain_out[...] + gain_in[...]
    gain_copies = to_all(gain_out, gains_ref, gain_send, gain_recv)
    mean_copy.wait()
    apart = lax.dot_general(
        mean_in[...], jnp.full((8, lanes), 0.125, F32), (((0,), (0,)), ((), ())),
        preferred_element_type=F32, precision=lax.Precision.HIGHEST,
    )
    mean = (mean + apart[:, 0:1]) / width
    tg_ref[...] = cot_ref[...] + inv * (scaled - normed * mean)
    advance_all((c4, small_chunk, c5))
    for copy in gain_copies:
        copy.wait()
    gain_total = gains_ref[0]
    for i in range(1, count):
        gain_total = gain_total + gains_ref[i]
    gg_ref[...] = gain_total
    run_out(chunks + [small_chunk])


def backward_call(args, count, rows, width, inner, states, rank, selects, padded):
    half = width // 2
    tile = rows // 2
    block_rows = half // count
    small = small_rows(count, rank, states, selects)
    f32, bf16 = F32, BF16
    vm = pltpu.VMEM
    scratch = [
        vm((2, count, inner // count, half), bf16), vm((2, count, block_rows, inner), bf16),
        vm((rows, inner), bf16), vm((rows, inner), f32), vm((states, spans, inner), f32), vm((states, inner), bf16),
        vm((count, states, inner), bf16), vm((count, states, inner), f32),
        vm((rows, states * lanes), f32), vm((states, spans, inner), f32),
        vm((states, rows + spans, lanes), f32),
        vm((rows, states * lanes), f32), vm((rows, states * lanes), f32),
        vm((rows, inner), f32), vm((states, inner), f32),
        vm((rows, padded), f32), vm((rows, padded), f32), vm((rows, padded), bf16), vm((rows, padded), bf16),
        vm((rows + 3 * spans, inner), f32), vm((2, rows, half), bf16), vm((2, 8, half), f32),
        vm((2, tile, half), bf16), vm((2, 8, half), f32), vm((tile, half), bf16), vm((tile, half), bf16),
        vm((8, half), f32), vm((8, half), f32), vm((8, half), f32), vm((count, 8, half), f32),
        vm((8, tile), f32), vm((8, tile), f32), vm((8, half), f32), vm((8, half), f32),
        vm((count, 8, half), f32),
        vm((2, count, block_rows, inner), bf16), vm((count, small, inner), f32),
        vm((2 * inner, half), f32), vm((half * 4 * inner // lanes, lanes), f32),
    ]
    most = 0
    for i, paired in enumerate(chunk_plan + (False,)):
        last = i == len(chunk_plan)
        sizes, copies = stage_sizes(stages_of(count, paired), count, i % 2 == 1)
        most = max(most, copies)
        scratch += [
            vm(size + ((small, inner) if last else (block_rows, inner)), f32 if last else bf16) for size in sizes
        ]
    dma = pltpu.SemaphoreType.DMA
    scratch += [dma((7, most))] * 2 + [dma((9,))] * 2 + [dma((count,))] * 6
    return run_kernel(
        functools.partial(backward_kernel, width=width),
        (
            struct((6, count, block_rows, inner), bf16),
            struct((count, small, inner), f32),
            struct((tile, half), f32),
            struct((8, half), f32),
        ),
        args,
        "backward",
        scratch=scratch,
        flops=16e9,
        collective=4,
        grant=vmem_most,
    )


def final_kernel(
    totals, small_ref, tg_ref, gg_ref, branch_ref,
    out_out, tg_out, gain_out, ig_out, conv_out, bias_out, select_out, step_out, step_bias_out, decay_out, skip_out, og_out,
):
    count, rows, width = totals.shape[1:]
    col = lax.axis_index("col")
    tiles = width // lanes
    for side in range(2):
        place = col if side == 0 else 1 - col
        base = pl.multiple_of(place * (count * rows), count * rows)
        for i in range(count):
            og_out[pl.ds(pl.multiple_of(base + i * rows, 8), rows), :] = widen(totals[side, i])
            for which in range(2):
                value = widen(totals[(4 if which == 0 else 2) + side, i])
                for j in range(tiles):
                    first = i * rows * 4 * tiles + (place * tiles + j) * 2 + which
                    ig_out[pl.ds(first, rows, stride=4 * tiles), :] = value[:, j * lanes : (j + 1) * lanes]
    slab = small_ref.shape[1] // 8

    def read(first, size):
        parts = []
        for j in range(first // 8, (first + size) // 8):
            parts.append(small_ref[j // slab, (j % slab) * 8 : (j % slab) * 8 + 8, :])
        return jnp.concatenate(parts, axis=0) if len(parts) > 1 else parts[0]

    rank, states, selects = step_out.shape[0], decay_out.shape[0], select_out.shape[1]
    step_out[...] = read(0, rank)
    decay_out[...] = read(rank, states)
    select_out[...] = read(rank + states, selects).T
    last = read(rank + states + selects, 8)
    conv_out[...] = last[0:4]
    bias_out[...] = last[4]
    skip_out[...] = last[5]
    step_bias_out[...] = last[6]
    gain_out[...] = gg_ref[0, :]
    tg_out[...] = tg_ref[...]
    out_out[...] = branch_ref[...]


def final_call(totals, small, tg, gg, output, rank, states, selects):
    inner = totals.shape[3]
    half = tg.shape[1]
    return run_kernel(
        final_kernel,
        (
            struct(output.shape, BF16), struct(tg.shape, F32), struct((half,), F32),
            struct((half * 4 * inner // lanes, lanes), F32), struct((4, inner), F32), struct((inner,), F32),
            struct((inner, selects), F32), struct((rank, inner), F32), struct((inner,), F32),
            struct((states, inner), F32), struct((inner,), F32), struct((2 * inner, half), F32),
        ),
        (totals, small, tg, gg, output),
        "final",
    )


def on_device(
    tokens_in, teacher, norm_gain, in_weight, conv_weight, conv_bias, select_weight, step_weight,
    step_bias, decay_log, skip_gain, out_weight, parents, lengths, valid_rows,
):
    rows, width = tokens_in.shape
    half = norm_gain.shape[0]
    inner = decay_log.shape[1]
    states = decay_log.shape[0]
    rank = step_weight.shape[0]
    selects = rank + 2 * states
    padded = selects + -selects % lanes
    steps = rows // spans
    count = lax.axis_size("seq")
    row_len = rows // lax.axis_size("row")
    row = lax.axis_index("row")
    col = lax.axis_index("col")
    me = lax.axis_index("seq")
    def halves(value, axis):
        size = value.shape[axis] // 2
        own = lax.dynamic_slice_in_dim(value, col * size, size, axis)
        other = lax.dynamic_slice_in_dim(value, (1 - col) * size, size, axis)
        return own, other

    def rows8(value):
        return jnp.broadcast_to(value[None, :], (8, value.shape[0]))

    swap = [(0, 1), (1, 0)]
    tok, toko = halves(tokens_in, 1)
    tail = lax.dynamic_slice_in_dim(tokens_in, lengths[me] - 8, 8, 0)
    w_own, w_send = halves(in_weight, 2)
    wi, wg = w_own[:, 0], w_own[:, 1]
    wi_send, wg_send = w_send[:, 0], w_send[:, 1]
    ow, ow_send = halves(out_weight, 0)
    gain = rows8(norm_gain)
    skip = rows8(skip_gain)
    conv_b = rows8(conv_bias)
    step_b = rows8(step_bias)

    tails, wio, gaino = entry_exchange(tail, wi_send, gain, count)
    wg_send, wio = lax.optimization_barrier((wg_send, wio))
    wgo = lax.ppermute(wg_send, "col", swap)
    tails_own, tails_oth = halves(tails, 2)

    hid, hid_tail, ext, act, sel_part = run_kernel(
        forward_in_kernel,
        (
            struct((2, rows, half), BF16),
            struct((2, 8, half), BF16),
            struct((rows + 3 * spans, inner), F32),
            struct((rows, inner), BF16),
            struct((rows, padded), F32),
        ),
        (tok, toko, tails_own, tails_oth, gain, gaino, wi, wio, conv_weight, conv_b, select_weight, parents),
        "forward_in",
        flops=2e9,
    )
    sel = quad_sum(sel_part, 1, "select_sum")
    ow_send, sel = lax.optimization_barrier((ow_send, sel))
    owo = lax.ppermute(ow_send, "col", swap)
    delta, step_pre, reach, cum, seg_map = run_kernel(
        forward_ends_kernel,
        (
            struct((rows, inner), F32),
            struct((rows, inner), F32),
            struct((states, spans, inner), F32),
            struct((spans, inner), F32),
            struct((states + 8, inner), BF16),
        ),
        (sel, step_weight, step_b, decay_log, act, lengths),
        "forward_ends",
        scratch=[
            pltpu.VMEM((rows, inner), F32),
            pltpu.VMEM((rows, states * lanes), F32),
            pltpu.VMEM((states, spans, inner), F32),
        ],
        flops=2e9,
    )
    table = seq_gather(seg_map, count, 2, "state_gather")
    starts, mixed_pre, gate, mixed, part = run_kernel(
        functools.partial(forward_out_kernel, rank=rank),
        (
            struct((states, spans, inner), F32),
            struct((rows, inner), F32),
            struct((rows, inner), F32),
            struct((rows, inner), BF16),
            struct((2, rows, half), BF16),
        ),
        (
            table, parents, decay_log, reach, cum, delta, act, sel, hid, wg, wgo, skip, ow, owo,
        ),
        "forward_out",
        scratch=[
            pltpu.VMEM((count, states, inner), F32),
            pltpu.VMEM((rows, inner), F32),
            pltpu.VMEM((rows, states * lanes), F32),
            pltpu.VMEM((rows, states * lanes), F32),
            pltpu.VMEM((states, spans, inner), F32),
        ],
        flops=4e9,
    )
    tok_tile = lax.dynamic_slice_in_dim(tok, row * row_len, row_len, 0)
    toko_tile = lax.dynamic_slice_in_dim(toko, row * row_len, row_len, 0)
    teach_tile = lax.dynamic_slice_in_dim(teacher, row * row_len, row_len, 0)
    output, cot_tile, cot = middle_exchange(part, tok_tile, teach_tile, valid_rows)
    totals, small, tokens_grad, gain_total = backward_call(
        (
            cot, mixed, ow, owo, gate, mixed_pre,
            table, parents, lengths, decay_log, starts, cum, delta, act, sel,
            step_pre, step_weight, select_weight, skip, ext, conv_weight, conv_b, hid, hid_tail,
            wi, wio, wg, wgo, tok_tile, toko_tile, gain, cot_tile,
        ),
        count, rows, width, inner, states, rank, selects, padded,
    )
    (
        output, tokens_grad, gain_grad, in_both, conv_grad, conv_bias_grad, select_grad, step_grad,
        step_bias_grad, decay_grad, skip_grad, out_grad,
    ) = final_call(totals, small, tokens_grad, gain_total, output, rank, states, selects)
    in_grad = in_both.reshape(half, -1, 2, lanes).transpose(0, 2, 1, 3).reshape(half, 2, -1)
    return (
        output,
        tokens_grad,
        gain_grad,
        in_grad,
        conv_grad,
        conv_bias_grad,
        select_grad,
        step_grad,
        step_bias_grad,
        decay_grad,
        skip_grad,
        out_grad,
    )


def solution(mesh):
    placed = (
        P("seq", None),
        P("seq", "col"),
        P("col"),
        P("col", None, "row"),
        P(None, ("row", "col")),
        P(("row", "col")),
        P(("row", "col"), None),
        P(None, ("row", "col")),
        P(("row", "col")),
        P(None, ("row", "col")),
        P(("row", "col")),
        P("row", "col"),
        P(),
        P(),
        P(),
    )
    return jax.shard_map(
        on_device,
        mesh=mesh,
        in_specs=placed,
        out_specs=(
            P(("seq", "row"), "col"),
            P(("seq", "row"), "col"),
            P("col"),
            P("col", None, "row"),
            P(None, ("row", "col")),
            P(("row", "col")),
            P(("row", "col"), None),
            P(None, ("row", "col")),
            P(("row", "col")),
            P(None, ("row", "col")),
            P(("row", "col")),
            P("row", "col"),
        ),
        check_vma=False,
    )
```

```python
import functools

import jax
import jax.numpy as jnp
from jax import lax
from jax.experimental import pallas as pl
from jax.experimental.pallas import tpu as pltpu
from jax.sharding import PartitionSpec as P

MESH = pl.DeviceIdType.MESH
F32 = jnp.float32
BF16 = jnp.bfloat16
norm_epsilon = 1e-05
spans = 8
lanes = 128
log2e = 1.4426950408889634
vmem_bytes = 60 * 1024 * 1024
vmem_most = 67043328
chunk_plan = (False, True, False, True, False, True, False, True)


def vmem_spec():
    return pl.BlockSpec(memory_space=pltpu.VMEM)


def smem_spec():
    return pl.BlockSpec(memory_space=pltpu.SMEM)


def struct(shape, dtype):
    return jax.ShapeDtypeStruct(shape, dtype)


def dot(a, b):
    return jnp.dot(a, b, preferred_element_type=F32)


def dot_tn(a, b):
    return lax.dot_general(a, b, (((0,), (0,)), ((), ())), preferred_element_type=F32)


def dot_nt(a, b):
    return lax.dot_general(a, b, (((1,), (1,)), ((), ())), preferred_element_type=F32)


def sigmoid(v):
    return 1.0 / (1.0 + jnp.exp(-v))


def slope_of(v, sigma):
    return sigma * (1.0 + v * (1.0 - sigma))


def to_steps(rows, steps):
    place = lax.broadcasted_iota(jnp.int32, (rows, rows), 0)
    token = lax.broadcasted_iota(jnp.int32, (rows, rows), 1)
    return (token == (place % spans) * steps + place // spans).astype(F32).astype(BF16)


def to_tokens(rows, steps):
    token = lax.broadcasted_iota(jnp.int32, (rows, rows), 0)
    place = lax.broadcasted_iota(jnp.int32, (rows, rows), 1)
    return (token == (place % spans) * steps + place // spans).astype(F32).astype(BF16)


def step_tokens(rows, steps):
    place = lax.broadcasted_iota(jnp.int32, (rows, 1), 0)
    return (place % spans) * steps + place // spans


def spread_matrix(states):
    row = lax.broadcasted_iota(jnp.int32, (2 * states, states * lanes), 0)
    col = lax.broadcasted_iota(jnp.int32, (2 * states, states * lanes), 1)
    return (row % states == col // lanes).astype(F32).astype(BF16)


def gather_matrix(states):
    row = lax.broadcasted_iota(jnp.int32, (states * lanes, states), 0)
    col = lax.broadcasted_iota(jnp.int32, (states * lanes, states), 1)
    return (row // lanes == col).astype(F32).astype(BF16)


def spread(values, states):
    high = values.astype(BF16)
    rest = (values - high.astype(F32)).astype(BF16)
    return dot(jnp.concatenate([high, rest], axis=1), spread_matrix(states))


def shift_spans(values, amount):
    return jnp.roll(values, amount, axis=values.ndim - 2)


def span_index(shape):
    return lax.broadcasted_iota(jnp.int32, shape, len(shape) - 2)


def run_kernel(kernel, outs, args, name, scratch=(), flops=0, collective=None, grant=vmem_bytes):
    params = dict(vmem_limit_bytes=grant)
    if collective is not None:
        params.update(collective_id=collective, has_side_effects=True)
    return pl.pallas_call(
        kernel,
        out_shape=outs,
        in_specs=[
            smem_spec() if a.dtype == jnp.int32 else vmem_spec() for a in args
        ],
        out_specs=jax.tree.map(lambda _: vmem_spec(), outs),
        scratch_shapes=list(scratch),
        compiler_params=pltpu.CompilerParams(**params),
        cost_estimate=pl.CostEstimate(
            flops=int(flops),
            transcendentals=0,
            bytes_accessed=int(sum(a.size * a.dtype.itemsize for a in args)),
        ),
        name=name,
    )(*args)


def barrier_with(peers):
    barrier = pltpu.get_barrier_semaphore()
    for peer in peers:
        pl.semaphore_signal(barrier, inc=1, device_id=peer, device_id_type=MESH)
    pl.semaphore_wait(barrier, len(peers))


def remote(src, dst, send, recv, peer):
    return pltpu.make_async_remote_copy(
        src_ref=src, dst_ref=dst, send_sem=send, recv_sem=recv, device_id=peer, device_id_type=MESH
    )


def row_peer():
    return {"row": 1 - lax.axis_index("row")}


def col_peer():
    return {"col": 1 - lax.axis_index("col")}


def entry_kernel(tail_ref, wi_ref, gain_ref, tails_ref, wo_ref, gain_o_ref, tsend, trecv, csend, crecv):
    count = tails_ref.shape[0]
    me = lax.axis_index("seq")
    peers = [{"seq": lax.rem(me + j, count)} for j in range(1, count)]
    barrier_with([col_peer()] + peers)
    copies = []
    for j, peer in enumerate(peers):
        copies.append(remote(tail_ref, tails_ref.at[me], tsend.at[j], trecv.at[j], peer))
    copies.append(remote(gain_ref, gain_o_ref, csend.at[0], crecv.at[0], col_peer()))
    copies.append(remote(wi_ref, wo_ref, csend.at[1], crecv.at[1], col_peer()))
    for copy in copies:
        copy.start()
    tails_ref[me] = tail_ref[...]
    for copy in copies:
        copy.wait()


def entry_exchange(tail, wi_send, gain_send, count):
    return run_kernel(
        entry_kernel,
        (
            struct((count,) + tail.shape, tail.dtype),
            struct(wi_send.shape, wi_send.dtype),
            struct(gain_send.shape, gain_send.dtype),
        ),
        (tail, wi_send, gain_send),
        "entry_exchange",
        scratch=[
            pltpu.SemaphoreType.DMA((count,)),
            pltpu.SemaphoreType.DMA((count,)),
            pltpu.SemaphoreType.DMA((2,)),
            pltpu.SemaphoreType.DMA((2,)),
        ],
        collective=0,
    )


def seq_gather_kernel(x_ref, o_ref, send, recv):
    count = o_ref.shape[0]
    me = lax.axis_index("seq")
    peers = [{"seq": lax.rem(me + j, count)} for j in range(1, count)]
    barrier_with(peers)
    copies = [
        remote(x_ref, o_ref.at[me], send.at[j], recv.at[j], peer) for j, peer in enumerate(peers)
    ]
    for copy in copies:
        copy.start()
    o_ref[me] = x_ref[...]
    for copy in copies:
        copy.wait()


def seq_gather(x, count, collective, name):
    return run_kernel(
        seq_gather_kernel,
        struct((count,) + x.shape, x.dtype),
        (x,),
        name,
        scratch=[pltpu.SemaphoreType.DMA((count,)), pltpu.SemaphoreType.DMA((count,))],
        collective=collective,
    )


def quad_sum_kernel(x_ref, o_ref, from_row, to_col, from_col, send, recv):
    barrier_with([row_peer(), col_peer()])
    first = remote(x_ref, from_row, send.at[0], recv.at[0], row_peer())
    first.start()
    first.wait()
    pair = x_ref[...] + from_row[...]
    to_col[...] = pair.astype(BF16)
    second = remote(to_col, from_col, send.at[1], recv.at[1], col_peer())
    second.start()
    o_ref[...] = pair
    second.wait()
    o_ref[...] += from_col[...].astype(F32)


def quad_sum(x, collective, name):
    return run_kernel(
        quad_sum_kernel,
        struct(x.shape, F32),
        (x,),
        name,
        scratch=[
            pltpu.VMEM(x.shape, F32),
            pltpu.VMEM(x.shape, BF16),
            pltpu.VMEM(x.shape, BF16),
            pltpu.SemaphoreType.DMA((2,)),
            pltpu.SemaphoreType.DMA((2,)),
        ],
        collective=collective,
    )


def middle_kernel(
    part_ref, tok_ref, teach_ref, ints_ref,
    out_ref, cot_ref, low_ref,
    from_row, to_col, from_col, send, recv,
):
    half = tok_ref.shape[0]
    segments = ints_ref.shape[0]
    row = lax.axis_index("row")
    mine = pl.multiple_of(row * half, half)
    other = pl.multiple_of((1 - row) * half, half)
    barrier_with([row_peer(), col_peer()])
    first = [
        remote(part_ref.at[h, pl.ds(other, half), :], from_row.at[h], send.at[h], recv.at[h], row_peer())
        for h in (1, 0)
    ]
    for copy in first:
        copy.start()
    first[0].wait()
    to_col[...] = (
        part_ref[1, pl.ds(mine, half), :].astype(F32) + from_row[1].astype(F32)
    ).astype(BF16)
    second = remote(to_col, from_col, send.at[2], recv.at[2], col_peer())
    second.start()
    first[1].wait()
    tile = part_ref[0, pl.ds(mine, half), :].astype(F32) + from_row[0].astype(F32)
    tile = tile + tok_ref[...].astype(F32)
    second.wait()
    result = tile + from_col[...].astype(F32)
    out_ref[...] = result.astype(BF16)
    positions = mine + lax.broadcasted_iota(jnp.int32, (half, 1), 0)
    total = ints_ref[0]
    for i in range(1, segments):
        total = total + ints_ref[i]
    share = jnp.full((half, 1), total, jnp.int32).astype(F32)
    counted = (positions < ints_ref[lax.axis_index("seq")]).astype(F32) * ((2 * half * segments) / share)
    cot = (result - teach_ref[...].astype(F32)) * counted
    cot_ref[...] = cot
    low_ref[0, pl.ds(mine, half), :] = cot.astype(BF16)
    third = [
        remote(low_ref.at[0, pl.ds(mine, half), :], low_ref.at[1, pl.ds(mine, half), :], send.at[3], recv.at[3], col_peer()),
        remote(low_ref.at[0, pl.ds(mine, half), :], low_ref.at[0, pl.ds(mine, half), :], send.at[4], recv.at[4], row_peer()),
    ]
    for copy in third:
        copy.start()
    third[0].wait()
    fourth = remote(low_ref.at[1, pl.ds(mine, half), :], low_ref.at[1, pl.ds(mine, half), :], send.at[5], recv.at[5], row_peer())
    fourth.start()
    third[1].wait()
    fourth.wait()


def middle_exchange(part, tok_tile, teach_tile, valid_rows):
    _, rows, width = part.shape
    half = rows // 2
    return run_kernel(
        middle_kernel,
        (struct((half, width), BF16), struct((half, width), F32), struct((2, rows, width), BF16)),
        (part, tok_tile, teach_tile, valid_rows),
        "middle_exchange",
        scratch=[
            pltpu.VMEM((2, half, width), BF16),
            pltpu.VMEM((half, width), BF16),
            pltpu.VMEM((half, width), BF16),
            pltpu.SemaphoreType.DMA((6,)),
            pltpu.SemaphoreType.DMA((6,)),
        ],
        collective=3,
    )


def forward_in_kernel(
    tok_ref, toko_ref, tails_ref, tailso_ref, gain_ref, gaino_ref, wi_ref, wio_ref,
    cw_ref, cb_ref, sw_ref, ints_ref,
    hid_ref, hidt_ref, ext_ref, act_ref, sel_ref,
):
    rows, half = tok_ref.shape
    steps = rows // spans
    width = 2 * half
    above = ints_ref[lax.axis_index("seq")]
    parent = jnp.maximum(above, 0)
    present = (above >= 0).astype(F32)
    gain = gain_ref[0:1, :].astype(F32)
    gaino = gaino_ref[0:1, :].astype(F32)

    def hidden_of(own, other):
        own = own.astype(F32)
        other = other.astype(F32)
        total = jnp.sum(own * own, axis=1, keepdims=True) + jnp.sum(other * other, axis=1, keepdims=True)
        inv = lax.rsqrt(total / width + norm_epsilon)
        return (own * inv * gain).astype(BF16), (other * inv * gaino).astype(BF16)

    hid, hido = hidden_of(tok_ref[...], toko_ref[...])
    order = to_steps(rows, steps)
    hid = dot(order, hid).astype(BF16)
    hido = dot(order, hido).astype(BF16)
    hid_ref[0] = hid
    hid_ref[1] = hido
    inner = dot(hid, wi_ref[...]) + dot(hido, wio_ref[...])
    tail, tailo = hidden_of(tails_ref[parent], tailso_ref[parent])
    hidt_ref[0] = tail
    hidt_ref[1] = tailo
    tail_inner = (dot(tail, wi_ref[...]) + dot(tailo, wio_ref[...])) * present
    last = inner[rows - 3 * spans :]
    first_span = lax.broadcasted_iota(jnp.int32, (spans, half), 0) == 0
    for j in range(3):
        block = jnp.roll(last[j * spans : (j + 1) * spans], 1, axis=0)
        ext_ref[j * spans : (j + 1) * spans, :] = jnp.where(
            first_span, jnp.broadcast_to(tail_inner[5 + j : 6 + j, :], (spans, half)), block
        )
    ext_ref[3 * spans :, :] = inner
    taps = cw_ref[...].astype(F32)
    pre = jnp.broadcast_to(cb_ref[0:1, :].astype(F32), (rows, half))
    for k in range(4):
        pre = pre + taps[k : k + 1, :] * ext_ref[k * spans : k * spans + rows, :]
    act = (pre * sigmoid(pre)).astype(BF16)
    act_ref[...] = act
    chosen = dot(act, sw_ref[...])
    sel_ref[...] = jnp.concatenate(
        [chosen, jnp.zeros((rows, sel_ref.shape[1] - chosen.shape[1]), F32)], axis=1
    )


def conv_pre(ext_ref, cw_ref, cb_ref, rows, half):
    taps = cw_ref[...].astype(F32)
    pre = jnp.broadcast_to(cb_ref[0:1, :].astype(F32), (rows, half))
    for k in range(4):
        pre = pre + taps[k : k + 1, :] * ext_ref[k * spans : k * spans + rows, :]
    return pre


def group_ds(group):
    return pl.ds(pl.multiple_of(group * lanes, lanes), lanes)


def step_ds(step):
    return pl.ds(pl.multiple_of(step * spans, spans), spans)


def decay_rows(decay_log_ref, decay_b, scale):
    states, width = decay_log_ref.shape
    rate = -jnp.exp(decay_log_ref[...]) * scale
    for n in range(states):
        decay_b[n] = jnp.broadcast_to(rate[n : n + 1, :], (spans, width))


def span_sum_kernel_part(delta_ref, steps):
    total = delta_ref[0:spans, :]
    for s in range(1, steps):
        total = total + delta_ref[s * spans : (s + 1) * spans, :]
    return total


def forward_ends_kernel(
    sel_ref, tw_ref, tb_ref, dl_ref, act_ref, ints_ref,
    delta_ref, pre_ref, reach_ref, cum_ref, send_ref,
    drive, b_ref, rate_ref,
):
    rows, width = act_ref.shape
    steps = rows // spans
    states = dl_ref.shape[0]
    rank = tw_ref.shape[0]
    length = ints_ref[lax.axis_index("seq")]
    sel = sel_ref[...]
    step_pre = dot(sel[:, :rank].astype(BF16), tw_ref[...]) + tb_ref[0:1, :].astype(F32)
    pre_ref[...] = step_pre
    live = (step_tokens(rows, steps) < length).astype(F32)
    delta = (jnp.maximum(step_pre, 0.0) + jnp.log1p(jnp.exp(-jnp.abs(step_pre)))) * live
    delta_ref[...] = delta
    drive[...] = delta * act_ref[...].astype(F32)
    b_ref[...] = spread(sel[:, rank : rank + states], states)
    decay_rows(dl_ref, rate_ref, log2e)

    for group in range(width // lanes):
        here = slice(group * lanes, (group + 1) * lanes)

        def advance(step, carry):
            d = delta_ref[step_ds(step), here]
            w = drive[step_ds(step), here]
            out = []
            for n in range(states):
                a = jnp.exp2(d * rate_ref[n, :, here])
                out.append(a * carry[n] + w * b_ref[step_ds(step), n * lanes : (n + 1) * lanes])
            return tuple(out)

        ends = lax.fori_loop(0, steps, advance, (jnp.zeros((spans, lanes), F32),) * states)
        for n in range(states):
            reach_ref[n, :, here] = ends[n]

    total = span_sum_kernel_part(delta_ref, steps)
    index2 = span_index((spans, width))
    part = total
    shift = 1
    while shift < spans:
        inside = index2 >= shift
        for n in range(states):
            own = reach_ref[n]
            earlier = jnp.where(inside, shift_spans(own, shift), 0.0)
            reach_ref[n] = own + jnp.exp2(part * rate_ref[n]) * earlier
        part = part + jnp.where(inside, shift_spans(part, shift), 0.0)
        shift *= 2
    cum_ref[...] = part
    sums = part[spans - 1 : spans, :]
    high = sums.astype(BF16)
    mid = (sums - high.astype(F32)).astype(BF16)
    low = (sums - high.astype(F32) - mid.astype(F32)).astype(BF16)
    ends = jnp.concatenate([reach_ref[n, spans - 1 : spans, :] for n in range(states)], axis=0)
    extra = jnp.concatenate(
        [high.astype(F32), mid.astype(F32), low.astype(F32), jnp.zeros((5, width), F32)], axis=0
    )
    send_ref[...] = jnp.concatenate([ends, extra], axis=0).astype(BF16)


def segment_sum(table_ref, index, states):
    block = table_ref[index].astype(F32)
    return block[:states], block[states : states + 1] + block[states + 1 : states + 2] + block[states + 2 : states + 3]


def forward_out_kernel(
    table_ref, parents_ref, dl_ref, reach_ref, cum_ref, delta_ref, act_ref, sel_ref,
    hid_ref, wg_ref, wgo_ref, skip_ref, ow_ref, owo_ref,
    starts_ref, mpre_ref, gate_ref, mixed_ref, part_ref,
    finals, drive, b_ref, c_ref, rate_ref, *, rank
):
    rows, width = act_ref.shape
    steps = rows // spans
    states = dl_ref.shape[0]
    count = table_ref.shape[0]
    me = lax.axis_index("seq")
    decay_rows(dl_ref, rate_ref, log2e)
    rate = -jnp.exp(dl_ref[...]) * log2e

    def start_of(target):
        above = parents_ref[target]
        return finals[jnp.maximum(above, 0)] * (above >= 0).astype(F32)

    def visit(target, carry):
        end, total = segment_sum(table_ref, target, states)
        finals[target] = jnp.exp2(rate * total) * start_of(target) + end
        return carry

    finals[0] = jnp.zeros(finals.shape[1:], F32)
    lax.fori_loop(0, count, visit, 0)
    start = start_of(me)
    sel = sel_ref[...]
    drive[...] = delta_ref[...] * act_ref[...].astype(F32)
    b_ref[...] = spread(sel[:, rank : rank + states], states)
    c_ref[...] = spread(sel[:, rank + states : rank + 2 * states], states)
    index2 = span_index((spans, width))
    cum = jnp.where(index2 >= 1, shift_spans(cum_ref[...], 1), 0.0)
    for n in range(states):
        earlier = jnp.where(index2 >= 1, shift_spans(reach_ref[n], 1), 0.0)
        starts_ref[n] = jnp.exp2(cum * rate_ref[n]) * start[n : n + 1, :] + earlier

    for group in range(width // lanes):
        here = slice(group * lanes, (group + 1) * lanes)

        def advance(step, carry):
            d = delta_ref[step_ds(step), here]
            w = drive[step_ds(step), here]
            out = []
            reads = [None] * 4
            for n in range(states):
                a = jnp.exp2(d * rate_ref[n, :, here])
                now = a * carry[n] + w * b_ref[step_ds(step), n * lanes : (n + 1) * lanes]
                out.append(now)
                term = c_ref[step_ds(step), n * lanes : (n + 1) * lanes] * now
                reads[n % 4] = term if reads[n % 4] is None else reads[n % 4] + term
            mpre_ref[step_ds(step), here] = (reads[0] + reads[1]) + (reads[2] + reads[3])
            return tuple(out)

        lax.fori_loop(0, steps, advance, tuple(starts_ref[n, :, here] for n in range(states)))

    gate = dot(hid_ref[0], wg_ref[...]) + dot(hid_ref[1], wgo_ref[...])
    gate_ref[...] = gate
    mixed_pre = mpre_ref[...] + skip_ref[0:1, :].astype(F32) * act_ref[...].astype(F32)
    mpre_ref[...] = mixed_pre
    mixed = (mixed_pre * (gate * sigmoid(gate))).astype(BF16)
    mixed_ref[...] = mixed
    natural = dot(to_tokens(rows, steps), mixed).astype(BF16)
    part_ref[0] = dot(natural, ow_ref[...]).astype(BF16)
    part_ref[1] = dot(natural, owo_ref[...]).astype(BF16)


def seq_bits(count):
    bits = []
    mask = 1
    while mask < count:
        bits.append(mask)
        mask *= 2
    return bits


def stages_of(count, first_pair):
    bits = seq_bits(count)
    if len(bits) < 3:
        return [(mask,) for mask in bits]
    if first_pair:
        return [(bits[1],), (bits[0],)] + [(mask,) for mask in bits[2:]]
    return [(bits[0],), (bits[1], bits[2])] + [(mask,) for mask in bits[3:]]


def stage_sizes(stages, count, crossed):
    sizes, copies = [], 0
    for i, masks in enumerate(stages):
        radix = 2 ** len(masks)
        count //= radix
        got = radix if crossed and i == len(stages) - 1 else radix - 1
        sizes.append((got, count))
        copies += got + radix - 1
    return sizes, copies


def bit_of(me, mask):
    return (me // mask) % 2


def toward(me, masks, pick):
    device, part = me, 0
    for k, mask in enumerate(masks):
        bit = bit_of(me, mask)
        weight = 2 ** (len(masks) - 1 - k)
        if (pick // weight) % 2:
            device = device + mask - 2 * mask * bit
            bit = 1 - bit
        part = part + weight * bit
    return device, part


def widen(values):
    return values.astype(F32)


class Chunk:
    def __init__(self, source, total, landings, send, recv, stages, crossed):
        self.source, self.total, self.landings = source, total, landings
        self.send, self.recv, self.stages, self.crossed = send, recv, stages, crossed
        self.count = source.shape[0]
        self.me = lax.axis_index("seq")
        self.copies = []
        self.flying = []
        self.at = 0
        self.levels = len(stages)
        self.sizes = stage_sizes(stages, self.count, crossed)[0]

    def start(self, src, dst, peer):
        at = len(self.copies)
        copy = remote(src, dst, self.send.at[at], self.recv.at[at], peer)
        copy.start()
        self.copies.append(copy)
        self.flying.append(copy)

    def land(self):
        for copy in self.flying:
            copy.wait_recv()
        self.flying = []

    def place(self, level):
        start = 0
        for j in range(level + 1):
            start = start + toward(self.me, self.stages[j], 0)[1] * self.sizes[j][1]
        return start

    def crossing(self, level):
        return self.crossed and level == self.levels - 1

    def scatter(self, level):
        held = self.source if level == 0 else self.landings[level - 1].at[0]
        masks, (_, size) = self.stages[level], self.sizes[level]
        for pick in range(0 if self.crossing(level) else 1, 2 ** len(masks)):
            device, part = toward(self.me, masks, pick)
            peer = {"seq": device}
            if self.crossing(level):
                peer["col"] = 1 - lax.axis_index("col")
            slot = pick if self.crossing(level) else pick - 1
            self.start(held.at[pl.ds(part * size, size)], self.landings[level].at[slot], peer)

    def add(self, level):
        held = self.source if level == 0 else self.landings[level - 1].at[0]
        masks, (got, size) = self.stages[level], self.sizes[level]
        landing = self.landings[level]
        if self.crossing(level):
            total = widen(landing[0])
        else:
            own = toward(self.me, masks, 0)[1]
            total = widen(held[pl.ds(own * size, size)]) + widen(landing[0])
        for slot in range(1, got):
            total = total + widen(landing[slot])
        return total.astype(landing.dtype)

    def gather(self, level):
        size = self.sizes[level][1]
        region = self.total.at[pl.ds(self.place(level), size)]
        masks = self.stages[level]
        for pick in range(1, 2 ** len(masks)):
            self.start(region, region, {"seq": toward(self.me, masks, pick)[0]})

    def done(self):
        return self.at > 2 * self.levels

    def next(self):
        if self.done():
            return
        self.land()
        at, last = self.at, self.levels
        self.at += 1
        if at < last:
            if at > 0:
                self.landings[at - 1][0] = self.add(at - 1)
            self.scatter(at)
            return
        if at == last:
            self.total[pl.ds(self.place(last - 1), 1)] = self.add(last - 1)
        level = 2 * last - 1 - at
        if level >= 0:
            self.gather(level)

    def finish(self):
        for copy in self.copies:
            copy.wait_send()


def store_split(ref, value):
    rows = ref.shape[1]
    for i in range(ref.shape[0]):
        ref[i] = value[i * rows : (i + 1) * rows].astype(ref.dtype)


def advance_all(chunks):
    for chunk in chunks:
        chunk.next()


def run_out(chunks):
    while any(not chunk.done() for chunk in chunks):
        advance_all(chunks)
    for chunk in chunks:
        chunk.finish()


def small_rows(count, rank, states, selects):
    total = rank + states + selects + 8
    total += -total % (8 * count)
    return total // count


def backward_kernel(
    cotangent_ref, mixed_ref, ow_ref, owo_ref, gate_ref, mpre_ref,
    table_ref, parents_ref, lengths_ref, dl_ref, starts_ref, cum_ref,
    delta_ref, act_ref, sel_ref, pre_ref, tw_ref,
    sw_ref, skip_ref, ext_ref, cw_ref, cb_ref, hid_ref, hidt_ref, wi_ref, wio_ref, wg_ref, wgo_ref,
    tok_ref, toko_ref, gain_ref, cot_ref,
    totals, small_total, tg_ref, gg_ref,
    og_ref, igg_ref, ggrad_ref, pgrad_ref, back_ref, flow_ref,
    flows_ref, grads, c_ref, rate_ref, state_buf, b_sum, c_sum, agrad_ref, dgrad_ref,
    sel_part, sel_row, sel_low, sel_col, cig_ref, part_ref, tpart_ref,
    hid_row, tail_row, hid_low, hid_col, tail_low_ref, tail_col, tail_own, tails_ref,
    mean_out, mean_in, gain_out, gain_in, gains_ref,
    igi_ref, small_ref, og_out, ig_out, *rest,
    width,
):
    count = table_ref.shape[0]
    landings = []
    for paired in chunk_plan + (False,):
        size = len(stages_of(count, paired))
        landings.append(rest[:size])
        rest = rest[size:]
    send, recv, pair_send, pair_recv, flow_send, flow_recv, tail_send, tail_recv, gain_send, gain_recv = rest
    rows, inner = act_ref.shape
    half = rows // 2
    steps = rows // spans
    states = dl_ref.shape[0]
    rank = tw_ref.shape[0]
    selects = sw_ref.shape[1]
    me = lax.axis_index("seq")
    row = lax.axis_index("row")
    col = lax.axis_index("col")
    mine = pl.multiple_of(row * half, half)
    other = pl.multiple_of((1 - row) * half, half)
    length = lengths_ref[me]
    peers = [{"seq": lax.rem(me + j, count)} for j in range(1, count)]
    across = sorted(
        {(masks, pick) for masks in (stages_of(count, p)[-1] for p in chunk_plan) for pick in range(1, 2 ** len(masks))}
    )
    flips = sorted({sum(m for k, m in enumerate(masks) if (pick >> (len(masks) - 1 - k)) % 2) for masks, pick in across})
    crossers = []
    for flip in flips:
        masks = tuple(m for m in seq_bits(count) if (flip // m) % 2)
        crossers.append({"seq": toward(me, masks, 2 ** len(masks) - 1)[0], "col": 1 - col})
    barrier_with([row_peer(), col_peer()] + peers + crossers)

    def pair_copy(at, src, dst, peer):
        copy = remote(src, dst, pair_send.at[at], pair_recv.at[at], peer)
        copy.start()
        return copy

    def to_all(src, dst, sends, recvs):
        copies = [
            remote(src, dst.at[me], sends.at[j], recvs.at[j], peer) for j, peer in enumerate(peers)
        ]
        for copy in copies:
            copy.start()
        dst[me] = src[...]
        return copies

    def small_slabs():
        slab = small_ref.shape[1] // 8
        return lambda at: (at // slab, slice((at % slab) * 8, (at % slab) * 8 + 8))

    place_of = small_slabs()

    def small_store(first, value):
        for j in range(value.shape[0] // 8):
            a, b = place_of(first // 8 + j)
            small_ref[a, b, :] = value[j * 8 : (j + 1) * 8]

    split = inner // 2
    sources = [og_ref.at[0], og_ref.at[1], igg_ref.at[0], igg_ref.at[1]]
    targets = [totals.at[i] for i in range(4)]
    for part in range(2):
        for h in range(2):
            sources.append(igi_ref.at[h, :, :, pl.ds(part * split, split)])
            targets.append(totals.at[4 + h, :, :, pl.ds(part * split, split)])
    chunks = [
        Chunk(
            source, targets[i], landings[i], send.at[i], recv.at[i],
            stages_of(count, chunk_plan[i]), i % 2 == 1,
        )
        for i, source in enumerate(sources)
    ]
    small_chunk = Chunk(
        small_ref, small_total, landings[-1], send.at[len(sources)], recv.at[len(sources)],
        stages_of(count, False), False,
    )

    drive = og_out.at[0:rows]
    dg_ref = og_out.at[rows : 2 * rows]

    def b_at(n, step):
        return ig_out[pl.ds(pl.multiple_of(n * rows + step * spans, spans), spans), :]

    c0, c1, c2, c3 = chunks[:4]
    inners = chunks[4:]
    late = {
        1: (c1, c3, c0), 2: tuple(inners[:2]), 3: tuple(inners[2:]) + (c2,), 4: tuple(inners[:2]) + (c1, c3),
        5: tuple(inners[2:]) + (small_chunk,), 6: tuple(inners) + (c1, c3, small_chunk),
    }
    pumps = {
        (0, 0): (c0, c1), (1, 0): (c2, c3), (2, 0): (c1,), (2, 1): (c0,), (3, 0): (c3,), (3, 1): (c2,),
    }
    from_tokens = to_steps(rows, steps)
    cot = dot(from_tokens, cotangent_ref[0]).astype(BF16)
    coto = dot(from_tokens, cotangent_ref[1]).astype(BF16)
    store_split(og_ref.at[0], dot_tn(mixed_ref[...], cot))
    store_split(og_ref.at[1], dot_tn(mixed_ref[...], coto))
    advance_all((c0, c1))
    mixed_grad = dot_nt(cot, ow_ref[...]) + dot_nt(coto, owo_ref[...])
    gate = gate_ref[...]
    sigma = sigmoid(gate)
    pre_grad = mixed_grad * (gate * sigma)
    pgrad_ref[...] = pre_grad
    gate_grad = (mixed_grad * mpre_ref[...] * slope_of(gate, sigma)).astype(BF16)
    ggrad_ref[...] = gate_grad
    store_split(igg_ref.at[0], dot_tn(hid_ref[0], gate_grad))
    store_split(igg_ref.at[1], dot_tn(hid_ref[1], gate_grad))
    advance_all((c2, c3))
    skip_sum = jnp.sum(pre_grad * act_ref[...].astype(F32), axis=0, keepdims=True)
    decay_rows(dl_ref, rate_ref, log2e)
    c_ref[...] = spread(sel_ref[:, rank + states : rank + 2 * states], states)

    for group in range(inner // lanes):
        here = slice(group * lanes, (group + 1) * lanes)

        def fall(back, carry):
            step = steps - 1 - back
            d = delta_ref[step_ds(step), here]
            p = pgrad_ref[step_ds(step), here]
            out = []
            for n in range(states):
                a = jnp.exp2(d * rate_ref[n, :, here])
                out.append(a * (c_ref[step_ds(step), n * lanes : (n + 1) * lanes] * p + carry[n]))
            return tuple(out)

        ends = lax.fori_loop(0, steps, fall, (jnp.zeros((spans, lanes), F32),) * states)
        for n in range(states):
            back_ref[n, :, here] = ends[n]

    index2 = span_index((spans, inner))
    cum = cum_ref[...]
    part = cum - jnp.where(index2 >= 1, shift_spans(cum, 1), 0.0)
    shift = 1
    while shift < spans:
        inside = index2 < spans - shift
        for n in range(states):
            own = back_ref[n]
            later = jnp.where(inside, shift_spans(own, -shift), 0.0)
            back_ref[n] = own + jnp.exp2(part * rate_ref[n]) * later
        part = part + jnp.where(inside, shift_spans(part, -shift), 0.0)
        shift *= 2
    flow_ref[...] = jnp.concatenate(
        [back_ref[n, 0:1, :] for n in range(states)], axis=0
    ).astype(BF16)

    flow_copies = to_all(flow_ref, flows_ref, flow_send, flow_recv)
    rate = -jnp.exp(dl_ref[...]) * log2e
    sel = sel_ref[...]
    drive[...] = delta_ref[...] * act_ref[...].astype(F32)
    for n in range(states):
        ig_out[n * rows : (n + 1) * rows, :] = jnp.broadcast_to(
            sel[:, rank + n : rank + n + 1], (rows, lanes)
        )
    after = cum[spans - 1 : spans, :] - cum
    inside = index2 < spans - 1
    slot = lax.broadcasted_iota(jnp.int32, (count, 1, 1), 0)

    def visit(visited, carry):
        target = count - 1 - visited
        _, total = segment_sum(table_ref, target, states)
        flow = flows_ref[target].astype(F32) + jnp.exp2(rate * total) * grads[target]
        grads[...] = grads[...] + jnp.where(slot == parents_ref[target], flow[None], 0.0)
        return carry

    groups = inner // lanes
    for group in range(groups):
        here = slice(group * lanes, (group + 1) * lanes)

        def advance(step, carry):
            d = delta_ref[step_ds(step), here]
            w = drive[step_ds(step), here]
            out = []
            for n in range(states):
                state_buf[n, step_ds(step), :] = carry[n]
                a = jnp.exp2(d * rate_ref[n, :, here])
                out.append(a * carry[n] + w * b_at(n, step))
            return tuple(out)

        advance_all(pumps.get((group, 0), ()))
        finals = lax.fori_loop(0, steps, advance, tuple(starts_ref[n, :, here] for n in range(states)))
        for n in range(states):
            state_buf[n, rows : rows + spans, :] = finals[n]
        if group == 0:
            for copy in flow_copies:
                copy.wait()
            grads[...] = jnp.zeros(grads.shape, F32)
            lax.fori_loop(0, count - 1, visit, 0)
        advance_all(pumps.get((group, 1), ()))
        end_grad = grads[me]

        later = []
        for n in range(states):
            flow = jnp.where(inside[:, here], shift_spans(back_ref[n, :, here], -1), 0.0)
            later.append(flow + jnp.exp2(after[:, here] * rate_ref[n, :, here]) * end_grad[n : n + 1, here])

        def retreat(back, carry):
            step = steps - 1 - back
            at = step_ds(step)
            d = delta_ref[at, here]
            p = pgrad_ref[at, here]
            w = drive[at, here]
            flows, sums = carry
            new_flows, new_sums = [], []
            weighted = [None, None]
            decayed = [None, None]
            for n in range(states):
                cols = slice(n * lanes, (n + 1) * lanes)
                a = jnp.exp2(d * rate_ref[n, :, here])
                adjoint = c_ref[at, cols] * p + flows[n]
                moved = a * adjoint
                growth = moved * state_buf[n, at, :]
                new_flows.append(moved)
                new_sums.append(sums[n] + growth * d)
                term = adjoint * b_at(n, step)
                weighted[n % 2] = term if weighted[n % 2] is None else weighted[n % 2] + term
                term = growth * rate_ref[n, :, here]
                decayed[n % 2] = term if decayed[n % 2] is None else decayed[n % 2] + term
                b_term = adjoint * w
                c_term = state_buf[n, step_ds(step + 1), :] * p
                if group == 0:
                    b_sum[at, cols] = b_term
                    c_sum[at, cols] = c_term
                else:
                    b_sum[at, cols] += b_term
                    c_sum[at, cols] += c_term
            bw = weighted[0] + weighted[1]
            dg_ref[at, here] = (decayed[0] + decayed[1]) * (1.0 / log2e) + act_ref[at, here].astype(F32) * bw
            agrad_ref[at, here] = bw * d
            return (tuple(new_flows), tuple(new_sums))

        zero = jnp.zeros((spans, lanes), F32)
        _, sums = lax.fori_loop(0, steps, retreat, (tuple(later), (zero,) * states))
        for n in range(states):
            dgrad_ref[n : n + 1, here] = (
                jnp.sum(sums[n], axis=0, keepdims=True) * rate[n : n + 1, here] * (1.0 / log2e)
            )

    live = (step_tokens(rows, steps) < length).astype(F32)
    step_pre_grad = dg_ref[...] * live * sigmoid(pre_ref[...])
    low = step_pre_grad.astype(BF16)
    gather = gather_matrix(states)
    sel_part[...] = jnp.concatenate(
        [
            dot_nt(low, tw_ref[...]), dot(b_sum[...].astype(BF16), gather),
            dot(c_sum[...].astype(BF16), gather), jnp.zeros((rows, sel_part.shape[1] - selects), F32),
        ],
        axis=1,
    )
    first = pair_copy(0, sel_part, sel_row, row_peer())
    advance_all((c1,))
    bias_sum = jnp.sum(step_pre_grad, axis=0, keepdims=True)
    small_store(0, dot_tn(sel[:, :rank].astype(BF16), low))
    small_store(rank, dgrad_ref[...])
    first.wait()
    pair = sel_part[...] + sel_row[...]
    sel_low[...] = pair.astype(BF16)
    second = pair_copy(1, sel_low, sel_col, col_peer())
    sel_part[...] = pair
    order = to_tokens(rows, steps)
    naturalg = dot(order, ggrad_ref[...]).astype(BF16)
    gate_parts = [dot_nt(naturalg, wg[...]) for wg in (wg_ref, wgo_ref)]
    pre = conv_pre(ext_ref, cw_ref, cb_ref, rows, inner)
    slope = slope_of(pre, sigmoid(pre))
    base_grad = agrad_ref[...] + skip_ref[0:1, :].astype(F32) * pgrad_ref[...]
    advance_all((c0, c3))
    second.wait()
    selg = (sel_part[...] + sel_col[...].astype(F32)).astype(BF16)[:, :selects]
    conv_in = (base_grad + dot_nt(selg, sw_ref[...])) * slope
    cig_ref[0:rows, :] = conv_in
    taps = cw_ref[...].astype(F32)
    tails = [jnp.zeros((5, inner), F32)]
    for i in range(3):
        line = jnp.zeros((1, inner), F32)
        for k in range(i + 1):
            line = line + taps[k : k + 1, :] * conv_in[(i - k) * spans : (i - k) * spans + 1, :]
        tails.append(line * (parents_ref[me] >= 0).astype(F32))
    tail_low = jnp.concatenate(tails, axis=0).astype(BF16)
    last_span = lax.broadcasted_iota(jnp.int32, (spans, inner), 0) == spans - 1
    for j in range(3):
        slab = jnp.roll(conv_in[j * spans : (j + 1) * spans], -1, axis=0)
        cig_ref[rows + j * spans : rows + (j + 1) * spans, :] = jnp.where(last_span, 0.0, slab)
    inner_grad = jnp.zeros((rows, inner), F32)
    for k in range(4):
        inner_grad = inner_grad + taps[k : k + 1, :] * cig_ref[(3 - k) * spans : (3 - k) * spans + rows, :]
    inner_low = inner_grad.astype(BF16)
    for h in range(2):
        store_split(igi_ref.at[h], dot_tn(hid_ref[h], inner_low) + dot_tn(hidt_ref[h], tail_low))
    advance_all(inners)
    for h, wi in enumerate((wi_ref, wio_ref)):
        tpart_ref[h] = dot_nt(tail_low, wi[...])
    tail_first = pair_copy(2, tpart_ref, tail_row, row_peer())
    advance_all(late[1])
    natural = dot(order, inner_low).astype(BF16)
    hid_copies = []
    for h, wi in ((1, wio_ref), (0, wi_ref)):
        part_ref[h] = (dot_nt(natural, wi[...]) + gate_parts[h]).astype(BF16)
        hid_copies.append(
            pair_copy(3 + h, part_ref.at[h, pl.ds(other, half), :], hid_row.at[h], row_peer())
        )
    tail_first.wait()
    tail_sum = tpart_ref[...] + tail_row[...]
    tail_low_ref[...] = tail_sum[1]
    tail_second = pair_copy(5, tail_low_ref, tail_col, col_peer())
    hid_copies[0].wait()
    hid_low[...] = (
        part_ref[1, pl.ds(mine, half), :].astype(F32) + hid_row[1].astype(F32)
    ).astype(BF16)
    hid_second = pair_copy(6, hid_low, hid_col, col_peer())
    advance_all(late[2])
    tail_second.wait()
    tail_own[...] = tail_sum[0] + tail_col[...]
    tail_copies = to_all(tail_own, tails_ref, tail_send, tail_recv)
    small_store(rank + states, dot_tn(selg, act_ref[...]))
    sums = [
        jnp.sum(conv_in * ext_ref[k * spans : k * spans + rows, :], axis=0, keepdims=True)
        for k in range(4)
    ]
    sums.append(jnp.sum(conv_in, axis=0, keepdims=True))
    sums.append(skip_sum)
    sums.append(bias_sum)
    sums.append(jnp.zeros((1, inner), F32))
    small_store(rank + states + selects, jnp.concatenate(sums, axis=0))
    for at in range((rank + states + selects + 8) // 8, small_ref.shape[0] * small_ref.shape[1] // 8):
        a, b = place_of(at)
        small_ref[a, b, :] = jnp.zeros((8, inner), F32)
    small_chunk.next()
    advance_all(late[3])
    hid_copies[1].wait()
    hidden = part_ref[0, pl.ds(mine, half), :].astype(F32) + hid_row[0].astype(F32)
    advance_all(late[4])

    tok = tok_ref[...].astype(F32)
    toko = toko_ref[...].astype(F32)
    power = jnp.sum(tok * tok, axis=1, keepdims=True) + jnp.sum(toko * toko, axis=1, keepdims=True)
    inv = lax.rsqrt(power / width + norm_epsilon)
    normed = tok * inv
    margin8 = tails_ref.shape[1]
    positions = row * half + lax.broadcasted_iota(jnp.int32, (half, margin8), 0)
    line_of = lax.broadcasted_iota(jnp.int32, (half, margin8), 1)
    place = ((positions == length - margin8 + line_of) & (line_of >= margin8 - 3)).astype(F32)
    for copy in tail_copies:
        copy.wait()
    own_tail = jnp.zeros(tails_ref.shape[1:], F32)
    for child in range(count):
        is_child = (parents_ref[child] == me).astype(F32)
        own_tail = own_tail + is_child * tails_ref[child]
    hidden = hidden + jnp.dot(place, own_tail, preferred_element_type=F32, precision=lax.Precision.HIGHEST)
    hid_second.wait()
    hidden = hidden + hid_col[...].astype(F32)
    scaled = hidden * gain_ref[0:1, :].astype(F32)
    mean = jnp.sum(scaled * normed, axis=1, keepdims=True)
    mean_out[...] = lax.dot_general(
        jnp.ones((8, lanes), F32), jnp.broadcast_to(mean / lanes, (half, lanes)), (((1,), (1,)), ((), ())),
        preferred_element_type=F32, precision=lax.Precision.HIGHEST,
    )
    mean_copy = pair_copy(7, mean_out, mean_in, col_peer())
    gain_out[...] = jnp.broadcast_to(jnp.sum(hidden * normed, axis=0, keepdims=True), gain_out.shape)
    gain_copy = pair_copy(8, gain_out, gain_in, row_peer())
    advance_all(late[5])
    gain_copy.wait()
    gain_out[...] = gain_out[...] + gain_in[...]
    gain_copies = to_all(gain_out, gains_ref, gain_send, gain_recv)
    mean_copy.wait()
    apart = lax.dot_general(
        mean_in[...], jnp.full((8, lanes), 0.125, F32), (((0,), (0,)), ((), ())),
        preferred_element_type=F32, precision=lax.Precision.HIGHEST,
    )
    mean = (mean + apart[:, 0:1]) / width
    tg_ref[...] = cot_ref[...] + inv * (scaled - normed * mean)
    advance_all(late[6])
    for copy in gain_copies:
        copy.wait()
    gain_total = gains_ref[0]
    for i in range(1, count):
        gain_total = gain_total + gains_ref[i]
    gg_ref[...] = gain_total
    run_out(chunks + [small_chunk])


def backward_call(args, count, rows, width, inner, states, rank, selects, padded):
    half = width // 2
    tile = rows // 2
    block_rows = half // count
    small = small_rows(count, rank, states, selects)
    f32, bf16 = F32, BF16
    vm = pltpu.VMEM
    scratch = [
        vm((2, count, inner // count, half), bf16), vm((2, count, block_rows, inner), bf16),
        vm((rows, inner), bf16), vm((rows, inner), f32), vm((states, spans, inner), f32), vm((states, inner), bf16),
        vm((count, states, inner), bf16), vm((count, states, inner), f32),
        vm((rows, states * lanes), f32), vm((states, spans, inner), f32),
        vm((states, rows + spans, lanes), f32),
        vm((rows, states * lanes), f32), vm((rows, states * lanes), f32),
        vm((rows, inner), f32), vm((states, inner), f32),
        vm((rows, padded), f32), vm((rows, padded), f32), vm((rows, padded), bf16), vm((rows, padded), bf16),
        vm((rows + 3 * spans, inner), f32), vm((2, rows, half), bf16), vm((2, 8, half), f32),
        vm((2, tile, half), bf16), vm((2, 8, half), f32), vm((tile, half), bf16), vm((tile, half), bf16),
        vm((8, half), f32), vm((8, half), f32), vm((8, half), f32), vm((count, 8, half), f32),
        vm((8, tile), f32), vm((8, tile), f32), vm((8, half), f32), vm((8, half), f32),
        vm((count, 8, half), f32),
        vm((2, count, block_rows, inner), bf16), vm((count, small, inner), f32),
        vm((2 * inner, half), f32), vm((half * 4 * inner // lanes, lanes), f32),
    ]
    most = 0
    for i, paired in enumerate(chunk_plan + (False,)):
        last = i == len(chunk_plan)
        sizes, copies = stage_sizes(stages_of(count, paired), count, i % 2 == 1)
        most = max(most, copies)
        scratch += [
            vm(size + ((small, inner) if last else (block_rows, inner if i < 4 else inner // 2)), f32 if last else bf16)
            for size in sizes
        ]
    dma = pltpu.SemaphoreType.DMA
    scratch += [dma((len(chunk_plan) + 1, most))] * 2 + [dma((9,))] * 2 + [dma((count,))] * 6
    return run_kernel(
        functools.partial(backward_kernel, width=width),
        (
            struct((6, count, block_rows, inner), bf16),
            struct((count, small, inner), f32),
            struct((tile, half), f32),
            struct((8, half), f32),
        ),
        args,
        "backward",
        scratch=scratch,
        flops=16e9,
        collective=4,
        grant=vmem_most,
    )


def final_kernel(
    totals, small_ref, tg_ref, gg_ref, branch_ref,
    out_out, tg_out, gain_out, ig_out, conv_out, bias_out, select_out, step_out, step_bias_out, decay_out, skip_out, og_out,
):
    count, rows, width = totals.shape[1:]
    col = lax.axis_index("col")
    tiles = width // lanes
    for side in range(2):
        place = col if side == 0 else 1 - col
        base = pl.multiple_of(place * (count * rows), count * rows)
        for i in range(count):
            og_out[pl.ds(pl.multiple_of(base + i * rows, 8), rows), :] = widen(totals[side, i])
            for which in range(2):
                value = widen(totals[(4 if which == 0 else 2) + side, i])
                for j in range(tiles):
                    first = i * rows * 4 * tiles + (place * tiles + j) * 2 + which
                    ig_out[pl.ds(first, rows, stride=4 * tiles), :] = value[:, j * lanes : (j + 1) * lanes]
    slab = small_ref.shape[1] // 8

    def read(first, size):
        parts = []
        for j in range(first // 8, (first + size) // 8):
            parts.append(small_ref[j // slab, (j % slab) * 8 : (j % slab) * 8 + 8, :])
        return jnp.concatenate(parts, axis=0) if len(parts) > 1 else parts[0]

    rank, states, selects = step_out.shape[0], decay_out.shape[0], select_out.shape[1]
    step_out[...] = read(0, rank)
    decay_out[...] = read(rank, states)
    select_out[...] = read(rank + states, selects).T
    last = read(rank + states + selects, 8)
    conv_out[...] = last[0:4]
    bias_out[...] = last[4]
    skip_out[...] = last[5]
    step_bias_out[...] = last[6]
    gain_out[...] = gg_ref[0, :]
    tg_out[...] = tg_ref[...]
    out_out[...] = branch_ref[...]


def final_call(totals, small, tg, gg, output, rank, states, selects):
    inner = totals.shape[3]
    half = tg.shape[1]
    return run_kernel(
        final_kernel,
        (
            struct(output.shape, BF16), struct(tg.shape, F32), struct((half,), F32),
            struct((half * 4 * inner // lanes, lanes), F32), struct((4, inner), F32), struct((inner,), F32),
            struct((inner, selects), F32), struct((rank, inner), F32), struct((inner,), F32),
            struct((states, inner), F32), struct((inner,), F32), struct((2 * inner, half), F32),
        ),
        (totals, small, tg, gg, output),
        "final",
    )


def on_device(
    tokens_in, teacher, norm_gain, in_weight, conv_weight, conv_bias, select_weight, step_weight,
    step_bias, decay_log, skip_gain, out_weight, parents, lengths, valid_rows,
):
    rows, width = tokens_in.shape
    half = norm_gain.shape[0]
    inner = decay_log.shape[1]
    states = decay_log.shape[0]
    rank = step_weight.shape[0]
    selects = rank + 2 * states
    padded = selects + -selects % lanes
    steps = rows // spans
    count = lax.axis_size("seq")
    row_len = rows // lax.axis_size("row")
    row = lax.axis_index("row")
    col = lax.axis_index("col")
    me = lax.axis_index("seq")
    def halves(value, axis):
        size = value.shape[axis] // 2
        own = lax.dynamic_slice_in_dim(value, col * size, size, axis)
        other = lax.dynamic_slice_in_dim(value, (1 - col) * size, size, axis)
        return own, other

    def rows8(value):
        return jnp.broadcast_to(value[None, :], (8, value.shape[0]))

    swap = [(0, 1), (1, 0)]
    tok, toko = halves(tokens_in, 1)
    tail = lax.dynamic_slice_in_dim(tokens_in, lengths[me] - 8, 8, 0)
    w_own, w_send = halves(in_weight, 2)
    wi, wg = w_own[:, 0], w_own[:, 1]
    wi_send, wg_send = w_send[:, 0], w_send[:, 1]
    ow, ow_send = halves(out_weight, 0)
    gain = rows8(norm_gain)
    skip = rows8(skip_gain)
    conv_b = rows8(conv_bias)
    step_b = rows8(step_bias)

    tails, wio, gaino = entry_exchange(tail, wi_send, gain, count)
    wg_send, wio = lax.optimization_barrier((wg_send, wio))
    wgo = lax.ppermute(wg_send, "col", swap)
    tails_own, tails_oth = halves(tails, 2)

    hid, hid_tail, ext, act, sel_part = run_kernel(
        forward_in_kernel,
        (
            struct((2, rows, half), BF16),
            struct((2, 8, half), BF16),
            struct((rows + 3 * spans, inner), F32),
            struct((rows, inner), BF16),
            struct((rows, padded), F32),
        ),
        (tok, toko, tails_own, tails_oth, gain, gaino, wi, wio, conv_weight, conv_b, select_weight, parents),
        "forward_in",
        flops=2e9,
    )
    sel = quad_sum(sel_part, 1, "select_sum")
    ow_send, sel = lax.optimization_barrier((ow_send, sel))
    owo = lax.ppermute(ow_send, "col", swap)
    delta, step_pre, reach, cum, seg_map = run_kernel(
        forward_ends_kernel,
        (
            struct((rows, inner), F32),
            struct((rows, inner), F32),
            struct((states, spans, inner), F32),
            struct((spans, inner), F32),
            struct((states + 8, inner), BF16),
        ),
        (sel, step_weight, step_b, decay_log, act, lengths),
        "forward_ends",
        scratch=[
            pltpu.VMEM((rows, inner), F32),
            pltpu.VMEM((rows, states * lanes), F32),
            pltpu.VMEM((states, spans, inner), F32),
        ],
        flops=2e9,
    )
    table = seq_gather(seg_map, count, 2, "state_gather")
    starts, mixed_pre, gate, mixed, part = run_kernel(
        functools.partial(forward_out_kernel, rank=rank),
        (
            struct((states, spans, inner), F32),
            struct((rows, inner), F32),
            struct((rows, inner), F32),
            struct((rows, inner), BF16),
            struct((2, rows, half), BF16),
        ),
        (
            table, parents, decay_log, reach, cum, delta, act, sel, hid, wg, wgo, skip, ow, owo,
        ),
        "forward_out",
        scratch=[
            pltpu.VMEM((count, states, inner), F32),
            pltpu.VMEM((rows, inner), F32),
            pltpu.VMEM((rows, states * lanes), F32),
            pltpu.VMEM((rows, states * lanes), F32),
            pltpu.VMEM((states, spans, inner), F32),
        ],
        flops=4e9,
    )
    tok_tile = lax.dynamic_slice_in_dim(tok, row * row_len, row_len, 0)
    toko_tile = lax.dynamic_slice_in_dim(toko, row * row_len, row_len, 0)
    teach_tile = lax.dynamic_slice_in_dim(teacher, row * row_len, row_len, 0)
    output, cot_tile, cot = middle_exchange(part, tok_tile, teach_tile, valid_rows)
    totals, small, tokens_grad, gain_total = backward_call(
        (
            cot, mixed, ow, owo, gate, mixed_pre,
            table, parents, lengths, decay_log, starts, cum, delta, act, sel,
            step_pre, step_weight, select_weight, skip, ext, conv_weight, conv_b, hid, hid_tail,
            wi, wio, wg, wgo, tok_tile, toko_tile, gain, cot_tile,
        ),
        count, rows, width, inner, states, rank, selects, padded,
    )
    (
        output, tokens_grad, gain_grad, in_both, conv_grad, conv_bias_grad, select_grad, step_grad,
        step_bias_grad, decay_grad, skip_grad, out_grad,
    ) = final_call(totals, small, tokens_grad, gain_total, output, rank, states, selects)
    in_grad = in_both.reshape(half, -1, 2, lanes).transpose(0, 2, 1, 3).reshape(half, 2, -1)
    return (
        output,
        tokens_grad,
        gain_grad,
        in_grad,
        conv_grad,
        conv_bias_grad,
        select_grad,
        step_grad,
        step_bias_grad,
        decay_grad,
        skip_grad,
        out_grad,
    )


def solution(mesh):
    placed = (
        P("seq", None),
        P("seq", "col"),
        P("col"),
        P("col", None, "row"),
        P(None, ("row", "col")),
        P(("row", "col")),
        P(("row", "col"), None),
        P(None, ("row", "col")),
        P(("row", "col")),
        P(None, ("row", "col")),
        P(("row", "col")),
        P("row", "col"),
        P(),
        P(),
        P(),
    )
    return jax.shard_map(
        on_device,
        mesh=mesh,
        in_specs=placed,
        out_specs=(
            P(("seq", "row"), "col"),
            P(("seq", "row"), "col"),
            P("col"),
            P("col", None, "row"),
            P(None, ("row", "col")),
            P(("row", "col")),
            P(("row", "col"), None),
            P(None, ("row", "col")),
            P(("row", "col")),
            P(None, ("row", "col")),
            P(("row", "col")),
            P("row", "col"),
        ),
        check_vma=False,
    )
```

```python
import functools

import jax
import jax.numpy as jnp
from jax import lax
from jax.experimental import pallas as pl
from jax.experimental.pallas import tpu as pltpu
from jax.sharding import PartitionSpec as P

MESH = pl.DeviceIdType.MESH
F32 = jnp.float32
BF16 = jnp.bfloat16
norm_epsilon = 1e-05
spans = 8
lanes = 128
log2e = 1.4426950408889634
vmem_bytes = 60 * 1024 * 1024
vmem_most = 67043328
chunk_plan = (False, True, False, True, False, True, False, True)


def vmem_spec():
    return pl.BlockSpec(memory_space=pltpu.VMEM)


def smem_spec():
    return pl.BlockSpec(memory_space=pltpu.SMEM)


def struct(shape, dtype):
    return jax.ShapeDtypeStruct(shape, dtype)


def dot(a, b):
    return jnp.dot(a, b, preferred_element_type=F32)


def dot_tn(a, b):
    return lax.dot_general(a, b, (((0,), (0,)), ((), ())), preferred_element_type=F32)


def dot_nt(a, b):
    return lax.dot_general(a, b, (((1,), (1,)), ((), ())), preferred_element_type=F32)


def sigmoid(v):
    return 1.0 / (1.0 + jnp.exp(-v))


def slope_of(v, sigma):
    return sigma * (1.0 + v * (1.0 - sigma))


def to_steps(rows, steps):
    place = lax.broadcasted_iota(jnp.int32, (rows, rows), 0)
    token = lax.broadcasted_iota(jnp.int32, (rows, rows), 1)
    return (token == (place % spans) * steps + place // spans).astype(F32).astype(BF16)


def to_tokens(rows, steps):
    token = lax.broadcasted_iota(jnp.int32, (rows, rows), 0)
    place = lax.broadcasted_iota(jnp.int32, (rows, rows), 1)
    return (token == (place % spans) * steps + place // spans).astype(F32).astype(BF16)


def step_tokens(rows, steps):
    place = lax.broadcasted_iota(jnp.int32, (rows, 1), 0)
    return (place % spans) * steps + place // spans


def spread_matrix(states):
    row = lax.broadcasted_iota(jnp.int32, (2 * states, states * lanes), 0)
    col = lax.broadcasted_iota(jnp.int32, (2 * states, states * lanes), 1)
    return (row % states == col // lanes).astype(F32).astype(BF16)


def gather_matrix(states):
    row = lax.broadcasted_iota(jnp.int32, (states * lanes, states), 0)
    col = lax.broadcasted_iota(jnp.int32, (states * lanes, states), 1)
    return (row // lanes == col).astype(F32).astype(BF16)


def spread(values, states):
    high = values.astype(BF16)
    rest = (values - high.astype(F32)).astype(BF16)
    return dot(jnp.concatenate([high, rest], axis=1), spread_matrix(states))


def shift_spans(values, amount):
    return jnp.roll(values, amount, axis=values.ndim - 2)


def span_index(shape):
    return lax.broadcasted_iota(jnp.int32, shape, len(shape) - 2)


def run_kernel(kernel, outs, args, name, scratch=(), flops=0, collective=None, grant=vmem_bytes):
    params = dict(vmem_limit_bytes=grant)
    if collective is not None:
        params.update(collective_id=collective, has_side_effects=True)
    return pl.pallas_call(
        kernel,
        out_shape=outs,
        in_specs=[
            smem_spec() if a.dtype == jnp.int32 else vmem_spec() for a in args
        ],
        out_specs=jax.tree.map(lambda _: vmem_spec(), outs),
        scratch_shapes=list(scratch),
        compiler_params=pltpu.CompilerParams(**params),
        cost_estimate=pl.CostEstimate(
            flops=int(flops),
            transcendentals=0,
            bytes_accessed=int(sum(a.size * a.dtype.itemsize for a in args)),
        ),
        name=name,
    )(*args)


def barrier_with(peers):
    barrier = pltpu.get_barrier_semaphore()
    for peer in peers:
        pl.semaphore_signal(barrier, inc=1, device_id=peer, device_id_type=MESH)
    pl.semaphore_wait(barrier, len(peers))


def remote(src, dst, send, recv, peer):
    return pltpu.make_async_remote_copy(
        src_ref=src, dst_ref=dst, send_sem=send, recv_sem=recv, device_id=peer, device_id_type=MESH
    )


def row_peer():
    return {"row": 1 - lax.axis_index("row")}


def col_peer():
    return {"col": 1 - lax.axis_index("col")}


def middle_kernel(
    part_ref, tok_ref, teach_ref, ints_ref,
    out_ref, cot_ref, low_ref,
    from_row, to_col, from_col, send, recv,
):
    half = tok_ref.shape[0]
    segments = ints_ref.shape[0]
    row = lax.axis_index("row")
    mine = pl.multiple_of(row * half, half)
    other = pl.multiple_of((1 - row) * half, half)
    barrier_with([row_peer(), col_peer()])
    first = [
        remote(part_ref.at[h, pl.ds(other, half), :], from_row.at[h], send.at[h], recv.at[h], row_peer())
        for h in (1, 0)
    ]
    for copy in first:
        copy.start()
    first[0].wait()
    to_col[...] = (
        part_ref[1, pl.ds(mine, half), :].astype(F32) + from_row[1].astype(F32)
    ).astype(BF16)
    second = remote(to_col, from_col, send.at[2], recv.at[2], col_peer())
    second.start()
    first[1].wait()
    tile = part_ref[0, pl.ds(mine, half), :].astype(F32) + from_row[0].astype(F32)
    tile = tile + tok_ref[...].astype(F32)
    second.wait()
    result = tile + from_col[...].astype(F32)
    out_ref[...] = result.astype(BF16)
    positions = mine + lax.broadcasted_iota(jnp.int32, (half, 1), 0)
    total = ints_ref[0]
    for i in range(1, segments):
        total = total + ints_ref[i]
    share = jnp.full((half, 1), total, jnp.int32).astype(F32)
    counted = (positions < ints_ref[lax.axis_index("seq")]).astype(F32) * ((2 * half * segments) / share)
    cot = (result - teach_ref[...].astype(F32)) * counted
    cot_ref[...] = cot
    low_ref[0, pl.ds(mine, half), :] = cot.astype(BF16)
    third = [
        remote(low_ref.at[0, pl.ds(mine, half), :], low_ref.at[1, pl.ds(mine, half), :], send.at[3], recv.at[3], col_peer()),
        remote(low_ref.at[0, pl.ds(mine, half), :], low_ref.at[0, pl.ds(mine, half), :], send.at[4], recv.at[4], row_peer()),
    ]
    for copy in third:
        copy.start()
    third[0].wait()
    fourth = remote(low_ref.at[1, pl.ds(mine, half), :], low_ref.at[1, pl.ds(mine, half), :], send.at[5], recv.at[5], row_peer())
    fourth.start()
    third[1].wait()
    fourth.wait()


def middle_exchange(part, tok_tile, teach_tile, valid_rows):
    _, rows, width = part.shape
    half = rows // 2
    return run_kernel(
        middle_kernel,
        (struct((half, width), BF16), struct((half, width), F32), struct((2, rows, width), BF16)),
        (part, tok_tile, teach_tile, valid_rows),
        "middle_exchange",
        scratch=[
            pltpu.VMEM((2, half, width), BF16),
            pltpu.VMEM((half, width), BF16),
            pltpu.VMEM((half, width), BF16),
            pltpu.SemaphoreType.DMA((6,)),
            pltpu.SemaphoreType.DMA((6,)),
        ],
        collective=3,
    )


def conv_pre(ext_ref, cw_ref, cb_ref, rows, half):
    taps = cw_ref[...].astype(F32)
    pre = jnp.broadcast_to(cb_ref[0:1, :].astype(F32), (rows, half))
    for k in range(4):
        pre = pre + taps[k : k + 1, :] * ext_ref[k * spans : k * spans + rows, :]
    return pre


def group_ds(group):
    return pl.ds(pl.multiple_of(group * lanes, lanes), lanes)


def step_ds(step):
    return pl.ds(pl.multiple_of(step * spans, spans), spans)


def decay_rows(decay_log_ref, decay_b, scale):
    states, width = decay_log_ref.shape
    rate = -jnp.exp(decay_log_ref[...]) * scale
    for n in range(states):
        decay_b[n] = jnp.broadcast_to(rate[n : n + 1, :], (spans, width))


def span_sum_kernel_part(delta_ref, steps):
    total = delta_ref[0:spans, :]
    for s in range(1, steps):
        total = total + delta_ref[s * spans : (s + 1) * spans, :]
    return total


def segment_sum(table_ref, index, states):
    block = table_ref[index].astype(F32)
    return block[:states], block[states : states + 1] + block[states + 1 : states + 2] + block[states + 2 : states + 3]


def forward_kernel(
    tail_ref, wi_send, wg_send, ow_send, gain_ref, tok_ref, toko_ref, wi_ref, wg_ref, ow_ref, cw_ref, cb_ref, sw_ref,
    tw_ref, tb_ref, dl_ref, skip_ref, parents_ref, lengths_ref,
    hid_ref, hidt_ref, ext_ref, act_ref, sel_ref, delta_ref, pre_ref, cum_ref, table_ref,
    wio_ref, wgo_ref, owo_ref, starts_ref, mpre_ref, gate_ref, mixed_ref, part_ref,
    tails_ref, gaino_ref, sel_row, sel_low, sel_col, drive, b_ref, c_ref, rate_ref, map_ref, reach_ref, finals,
    pair_send, pair_recv, tail_send, tail_recv, map_send, map_recv,
):
    count = table_ref.shape[0]
    rows, half = tok_ref.shape
    steps = rows // spans
    width = 2 * half
    states = dl_ref.shape[0]
    rank = tw_ref.shape[0]
    me = lax.axis_index("seq")
    col = lax.axis_index("col")
    peers = [{"seq": lax.rem(me + j, count)} for j in range(1, count)]
    barrier_with([row_peer(), col_peer()] + peers)

    def pair_copy(at, src, dst, peer):
        copy = remote(src, dst, pair_send.at[at], pair_recv.at[at], peer)
        copy.start()
        return copy

    def to_all(src, dst, sends, recvs):
        copies = [
            remote(src, dst.at[me], sends.at[j], recvs.at[j], peer) for j, peer in enumerate(peers)
        ]
        for copy in copies:
            copy.start()
        dst[me] = src[...]
        return copies

    gain_copy = pair_copy(0, gain_ref, gaino_ref, col_peer())
    wi_copy = pair_copy(1, wi_send, wio_ref, col_peer())
    tail_copies = to_all(tail_ref, tails_ref, tail_send, tail_recv)
    quarter = half // 2
    first_part, second_part = pl.ds(0, quarter), pl.ds(quarter, quarter)
    wg_first = pair_copy(2, wg_send.at[first_part], wgo_ref.at[first_part], col_peer())

    above = parents_ref[me]
    parent = jnp.maximum(above, 0)
    present = (above >= 0).astype(F32)

    def hidden_of(own, other):
        own = own.astype(F32)
        other = other.astype(F32)
        total = jnp.sum(own * own, axis=1, keepdims=True) + jnp.sum(other * other, axis=1, keepdims=True)
        inv = lax.rsqrt(total / width + norm_epsilon)
        gain = gain_ref[0:1, :].astype(F32)
        gaino = gaino_ref[0:1, :].astype(F32)
        return (own * inv * gain).astype(BF16), (other * inv * gaino).astype(BF16)

    gain_copy.wait()
    hid, hido = hidden_of(tok_ref[...], toko_ref[...])
    order = to_steps(rows, steps)
    hid = dot(order, hid).astype(BF16)
    hido = dot(order, hido).astype(BF16)
    hid_ref[0] = hid
    hid_ref[1] = hido
    ext_ref[3 * spans :, :] = dot(hid, wi_ref[...])
    decay_rows(dl_ref, rate_ref, log2e)
    for copy in tail_copies:
        copy.wait()
    own_at = pl.ds(pl.multiple_of(col * half, half), half)
    other_at = pl.ds(pl.multiple_of((1 - col) * half, half), half)
    tail, tailo = hidden_of(tails_ref[parent, :, own_at], tails_ref[parent, :, other_at])
    hidt_ref[0] = tail
    hidt_ref[1] = tailo
    tail_inner = dot(tail, wi_ref[...])
    wi_copy.wait()
    inner = ext_ref[3 * spans :, :] + dot(hid_ref[1], wio_ref[...])
    tail_inner = (tail_inner + dot(tailo, wio_ref[...])) * present
    last = inner[rows - 3 * spans :]
    first_span = lax.broadcasted_iota(jnp.int32, (spans, half), 0) == 0
    for j in range(3):
        block = jnp.roll(last[j * spans : (j + 1) * spans], 1, axis=0)
        ext_ref[j * spans : (j + 1) * spans, :] = jnp.where(
            first_span, jnp.broadcast_to(tail_inner[5 + j : 6 + j, :], (spans, half)), block
        )
    ext_ref[3 * spans :, :] = inner
    pre = conv_pre(ext_ref, cw_ref, cb_ref, rows, half)
    act = (pre * sigmoid(pre)).astype(BF16)
    act_ref[...] = act
    chosen = dot(act, sw_ref[...])
    sel_ref[...] = jnp.concatenate(
        [chosen, jnp.zeros((rows, sel_ref.shape[1] - chosen.shape[1]), F32)], axis=1
    )
    across = pair_copy(3, sel_ref, sel_row, row_peer())
    across.wait()
    pair = sel_ref[...] + sel_row[...]
    sel_low[...] = pair.astype(BF16)
    beside = pair_copy(4, sel_low, sel_col, col_peer())
    wg_second = pair_copy(5, wg_send.at[second_part], wgo_ref.at[second_part], col_peer())
    ow_copy = pair_copy(6, ow_send, owo_ref, col_peer())
    beside.wait()
    sel = pair + sel_col[...].astype(F32)
    sel_ref[...] = sel
    length = lengths_ref[me]
    step_pre = dot(sel[:, :rank].astype(BF16), tw_ref[...]) + tb_ref[0:1, :].astype(F32)
    pre_ref[...] = step_pre
    live = (step_tokens(rows, steps) < length).astype(F32)
    delta = (jnp.maximum(step_pre, 0.0) + jnp.log1p(jnp.exp(-jnp.abs(step_pre)))) * live
    delta_ref[...] = delta
    drive[...] = delta * act_ref[...].astype(F32)
    b_ref[...] = spread(sel[:, rank : rank + states], states)

    for group in range(half // lanes):
        here = slice(group * lanes, (group + 1) * lanes)

        def advance(step, carry):
            d = delta_ref[step_ds(step), here]
            w = drive[step_ds(step), here]
            out = []
            for n in range(states):
                a = jnp.exp2(d * rate_ref[n, :, here])
                out.append(a * carry[n] + w * b_ref[step_ds(step), n * lanes : (n + 1) * lanes])
            return tuple(out)

        ends = lax.fori_loop(0, steps, advance, (jnp.zeros((spans, lanes), F32),) * states)
        for n in range(states):
            reach_ref[n, :, here] = ends[n]

    total = span_sum_kernel_part(delta_ref, steps)
    index2 = span_index((spans, half))
    part = total
    shift = 1
    while shift < spans:
        inside = index2 >= shift
        for n in range(states):
            own = reach_ref[n]
            earlier = jnp.where(inside, shift_spans(own, shift), 0.0)
            reach_ref[n] = own + jnp.exp2(part * rate_ref[n]) * earlier
        part = part + jnp.where(inside, shift_spans(part, shift), 0.0)
        shift *= 2
    cum_ref[...] = part
    sums = part[spans - 1 : spans, :]
    high = sums.astype(BF16)
    mid = (sums - high.astype(F32)).astype(BF16)
    low = (sums - high.astype(F32) - mid.astype(F32)).astype(BF16)
    ends = jnp.concatenate([reach_ref[n, spans - 1 : spans, :] for n in range(states)], axis=0)
    extra = jnp.concatenate(
        [high.astype(F32), mid.astype(F32), low.astype(F32), jnp.zeros((5, half), F32)], axis=0
    )
    map_ref[...] = jnp.concatenate([ends, extra], axis=0).astype(BF16)
    map_copies = to_all(map_ref, table_ref, map_send, map_recv)
    for copy in (wg_first, wg_second):
        copy.wait()
    gate = dot(hid_ref[0], wg_ref[...]) + dot(hid_ref[1], wgo_ref[...])
    gate_ref[...] = gate
    c_ref[...] = spread(sel[:, rank + states : rank + 2 * states], states)
    for copy in map_copies:
        copy.wait()
    rate = -jnp.exp(dl_ref[...]) * log2e

    def start_of(target):
        higher = parents_ref[target]
        return finals[jnp.maximum(higher, 0)] * (higher >= 0).astype(F32)

    def visit(target, carry):
        end, total = segment_sum(table_ref, target, states)
        finals[target] = jnp.exp2(rate * total) * start_of(target) + end
        return carry

    finals[0] = jnp.zeros(finals.shape[1:], F32)
    lax.fori_loop(0, count, visit, 0)
    start = start_of(me)
    before = jnp.where(index2 >= 1, shift_spans(cum_ref[...], 1), 0.0)
    for n in range(states):
        earlier = jnp.where(index2 >= 1, shift_spans(reach_ref[n], 1), 0.0)
        starts_ref[n] = jnp.exp2(before * rate_ref[n]) * start[n : n + 1, :] + earlier

    for group in range(half // lanes):
        here = slice(group * lanes, (group + 1) * lanes)

        def advance(step, carry):
            d = delta_ref[step_ds(step), here]
            w = drive[step_ds(step), here]
            out = []
            reads = [None] * 4
            for n in range(states):
                a = jnp.exp2(d * rate_ref[n, :, here])
                now = a * carry[n] + w * b_ref[step_ds(step), n * lanes : (n + 1) * lanes]
                out.append(now)
                term = c_ref[step_ds(step), n * lanes : (n + 1) * lanes] * now
                reads[n % 4] = term if reads[n % 4] is None else reads[n % 4] + term
            mpre_ref[step_ds(step), here] = (reads[0] + reads[1]) + (reads[2] + reads[3])
            return tuple(out)

        lax.fori_loop(0, steps, advance, tuple(starts_ref[n, :, here] for n in range(states)))

    mixed_pre = mpre_ref[...] + skip_ref[0:1, :].astype(F32) * act_ref[...].astype(F32)
    mpre_ref[...] = mixed_pre
    gate = gate_ref[...]
    mixed = (mixed_pre * (gate * sigmoid(gate))).astype(BF16)
    mixed_ref[...] = mixed
    natural = dot(to_tokens(rows, steps), mixed).astype(BF16)
    part_ref[0] = dot(natural, ow_ref[...]).astype(BF16)
    ow_copy.wait()
    part_ref[1] = dot(natural, owo_ref[...]).astype(BF16)


def seq_bits(count):
    bits = []
    mask = 1
    while mask < count:
        bits.append(mask)
        mask *= 2
    return bits


def stages_of(count, first_pair):
    bits = seq_bits(count)
    if len(bits) < 3:
        return [(mask,) for mask in bits]
    if first_pair:
        return [(bits[1],), (bits[0],)] + [(mask,) for mask in bits[2:]]
    return [(bits[0],), (bits[1], bits[2])] + [(mask,) for mask in bits[3:]]


def stage_sizes(stages, count, crossed):
    sizes, copies = [], 0
    for i, masks in enumerate(stages):
        radix = 2 ** len(masks)
        count //= radix
        got = radix if crossed and i == len(stages) - 1 else radix - 1
        sizes.append((got, count))
        copies += got + radix - 1
    return sizes, copies


def bit_of(me, mask):
    return (me // mask) % 2


def toward(me, masks, pick):
    device, part = me, 0
    for k, mask in enumerate(masks):
        bit = bit_of(me, mask)
        weight = 2 ** (len(masks) - 1 - k)
        if (pick // weight) % 2:
            device = device + mask - 2 * mask * bit
            bit = 1 - bit
        part = part + weight * bit
    return device, part


def widen(values):
    return values.astype(F32)


class Chunk:
    def __init__(self, source, total, landings, send, recv, stages, crossed):
        self.source, self.total, self.landings = source, total, landings
        self.send, self.recv, self.stages, self.crossed = send, recv, stages, crossed
        self.count = source.shape[0]
        self.me = lax.axis_index("seq")
        self.copies = []
        self.flying = []
        self.at = 0
        self.levels = len(stages)
        self.sizes = stage_sizes(stages, self.count, crossed)[0]

    def start(self, src, dst, peer):
        at = len(self.copies)
        copy = remote(src, dst, self.send.at[at], self.recv.at[at], peer)
        copy.start()
        self.copies.append(copy)
        self.flying.append(copy)

    def land(self):
        for copy in self.flying:
            copy.wait_recv()
        self.flying = []

    def place(self, level):
        start = 0
        for j in range(level + 1):
            start = start + toward(self.me, self.stages[j], 0)[1] * self.sizes[j][1]
        return start

    def crossing(self, level):
        return self.crossed and level == self.levels - 1

    def scatter(self, level):
        held = self.source if level == 0 else self.landings[level - 1].at[0]
        masks, (_, size) = self.stages[level], self.sizes[level]
        for pick in range(0 if self.crossing(level) else 1, 2 ** len(masks)):
            device, part = toward(self.me, masks, pick)
            peer = {"seq": device}
            if self.crossing(level):
                peer["col"] = 1 - lax.axis_index("col")
            slot = pick if self.crossing(level) else pick - 1
            self.start(held.at[pl.ds(part * size, size)], self.landings[level].at[slot], peer)

    def add(self, level):
        held = self.source if level == 0 else self.landings[level - 1].at[0]
        masks, (got, size) = self.stages[level], self.sizes[level]
        landing = self.landings[level]
        if self.crossing(level):
            total = widen(landing[0])
        else:
            own = toward(self.me, masks, 0)[1]
            total = widen(held[pl.ds(own * size, size)]) + widen(landing[0])
        for slot in range(1, got):
            total = total + widen(landing[slot])
        return total.astype(landing.dtype)

    def gather(self, level):
        size = self.sizes[level][1]
        region = self.total.at[pl.ds(self.place(level), size)]
        masks = self.stages[level]
        for pick in range(1, 2 ** len(masks)):
            self.start(region, region, {"seq": toward(self.me, masks, pick)[0]})

    def done(self):
        return self.at > 2 * self.levels

    def next(self):
        if self.done():
            return
        self.land()
        at, last = self.at, self.levels
        self.at += 1
        if at < last:
            if at > 0:
                self.landings[at - 1][0] = self.add(at - 1)
            self.scatter(at)
            return
        if at == last:
            self.total[pl.ds(self.place(last - 1), 1)] = self.add(last - 1)
        level = 2 * last - 1 - at
        if level >= 0:
            self.gather(level)

    def finish(self):
        for copy in self.copies:
            copy.wait_send()


def store_split(ref, value):
    rows = ref.shape[1]
    for i in range(ref.shape[0]):
        ref[i] = value[i * rows : (i + 1) * rows].astype(ref.dtype)


def advance_all(chunks):
    for chunk in chunks:
        chunk.next()


def run_out(chunks):
    while any(not chunk.done() for chunk in chunks):
        advance_all(chunks)
    for chunk in chunks:
        chunk.finish()


def small_rows(count, rank, states, selects):
    total = rank + states + selects + 8
    total += -total % (8 * count)
    return total // count


def backward_kernel(
    cotangent_ref, mixed_ref, ow_ref, owo_ref, gate_ref, mpre_ref,
    table_ref, parents_ref, lengths_ref, dl_ref, starts_ref, cum_ref,
    delta_ref, act_ref, sel_ref, pre_ref, tw_ref,
    sw_ref, skip_ref, ext_ref, cw_ref, cb_ref, hid_ref, hidt_ref, wi_ref, wio_ref, wg_ref, wgo_ref,
    tok_ref, toko_ref, gain_ref, cot_ref,
    totals, small_total, tg_ref, gg_ref,
    og_ref, igg_ref, ggrad_ref, pgrad_ref, back_ref, flow_ref,
    flows_ref, grads, c_ref, rate_ref, state_buf, b_sum, c_sum, agrad_ref, dgrad_ref,
    sel_part, sel_row, sel_low, sel_col, cig_ref, part_ref, tpart_ref,
    hid_row, tail_row, hid_low, hid_col, tail_low_ref, tail_col, tail_own, tails_ref,
    mean_out, mean_in, gain_out, gain_in, gains_ref,
    igi_ref, small_ref, og_out, ig_out, *rest,
    width,
):
    count = table_ref.shape[0]
    landings = []
    for paired in chunk_plan + (False,):
        size = len(stages_of(count, paired))
        landings.append(rest[:size])
        rest = rest[size:]
    send, recv, pair_send, pair_recv, flow_send, flow_recv, tail_send, tail_recv, gain_send, gain_recv = rest
    rows, inner = act_ref.shape
    half = rows // 2
    steps = rows // spans
    states = dl_ref.shape[0]
    rank = tw_ref.shape[0]
    selects = sw_ref.shape[1]
    me = lax.axis_index("seq")
    row = lax.axis_index("row")
    col = lax.axis_index("col")
    mine = pl.multiple_of(row * half, half)
    other = pl.multiple_of((1 - row) * half, half)
    length = lengths_ref[me]
    peers = [{"seq": lax.rem(me + j, count)} for j in range(1, count)]
    across = sorted(
        {(masks, pick) for masks in (stages_of(count, p)[-1] for p in chunk_plan) for pick in range(1, 2 ** len(masks))}
    )
    flips = sorted({sum(m for k, m in enumerate(masks) if (pick >> (len(masks) - 1 - k)) % 2) for masks, pick in across})
    crossers = []
    for flip in flips:
        masks = tuple(m for m in seq_bits(count) if (flip // m) % 2)
        crossers.append({"seq": toward(me, masks, 2 ** len(masks) - 1)[0], "col": 1 - col})
    barrier_with([row_peer(), col_peer()] + peers + crossers)

    def pair_copy(at, src, dst, peer):
        copy = remote(src, dst, pair_send.at[at], pair_recv.at[at], peer)
        copy.start()
        return copy

    def to_all(src, dst, sends, recvs):
        copies = [
            remote(src, dst.at[me], sends.at[j], recvs.at[j], peer) for j, peer in enumerate(peers)
        ]
        for copy in copies:
            copy.start()
        dst[me] = src[...]
        return copies

    def small_slabs():
        slab = small_ref.shape[1] // 8
        return lambda at: (at // slab, slice((at % slab) * 8, (at % slab) * 8 + 8))

    place_of = small_slabs()

    def small_store(first, value):
        for j in range(value.shape[0] // 8):
            a, b = place_of(first // 8 + j)
            small_ref[a, b, :] = value[j * 8 : (j + 1) * 8]

    split = inner // 2
    sources = [og_ref.at[0], og_ref.at[1], igg_ref.at[0], igg_ref.at[1]]
    targets = [totals.at[i] for i in range(4)]
    for part in range(2):
        for h in range(2):
            sources.append(igi_ref.at[h, :, :, pl.ds(part * split, split)])
            targets.append(totals.at[4 + h, :, :, pl.ds(part * split, split)])
    chunks = [
        Chunk(
            source, targets[i], landings[i], send.at[i], recv.at[i],
            stages_of(count, chunk_plan[i]), i % 2 == 1,
        )
        for i, source in enumerate(sources)
    ]
    small_chunk = Chunk(
        small_ref, small_total, landings[-1], send.at[len(sources)], recv.at[len(sources)],
        stages_of(count, False), False,
    )

    drive = og_out.at[0:rows]
    dg_ref = og_out.at[rows : 2 * rows]

    def b_at(n, step):
        return ig_out[pl.ds(pl.multiple_of(n * rows + step * spans, spans), spans), :]

    c0, c1, c2, c3 = chunks[:4]
    inners = chunks[4:]
    late = {
        1: (c1, c3, c0), 2: tuple(inners[:2]), 3: tuple(inners[2:]) + (c2,), 4: tuple(inners[:2]) + (c1, c3),
        5: tuple(inners[2:]) + (small_chunk,), 6: tuple(inners) + (c1, c3, small_chunk),
    }
    pumps = {
        (0, 0): (c0, c1), (1, 0): (c2, c3), (2, 0): (c1,), (2, 1): (c0,), (3, 0): (c3,), (3, 1): (c2,),
    }
    from_tokens = to_steps(rows, steps)
    cot = dot(from_tokens, cotangent_ref[0]).astype(BF16)
    coto = dot(from_tokens, cotangent_ref[1]).astype(BF16)
    store_split(og_ref.at[0], dot_tn(mixed_ref[...], cot))
    store_split(og_ref.at[1], dot_tn(mixed_ref[...], coto))
    advance_all((c0, c1))
    mixed_grad = dot_nt(cot, ow_ref[...]) + dot_nt(coto, owo_ref[...])
    gate = gate_ref[...]
    sigma = sigmoid(gate)
    pre_grad = mixed_grad * (gate * sigma)
    pgrad_ref[...] = pre_grad
    gate_grad = (mixed_grad * mpre_ref[...] * slope_of(gate, sigma)).astype(BF16)
    ggrad_ref[...] = gate_grad
    store_split(igg_ref.at[0], dot_tn(hid_ref[0], gate_grad))
    store_split(igg_ref.at[1], dot_tn(hid_ref[1], gate_grad))
    advance_all((c2, c3))
    skip_sum = jnp.sum(pre_grad * act_ref[...].astype(F32), axis=0, keepdims=True)
    decay_rows(dl_ref, rate_ref, log2e)
    c_ref[...] = spread(sel_ref[:, rank + states : rank + 2 * states], states)

    for group in range(inner // lanes):
        here = slice(group * lanes, (group + 1) * lanes)

        def fall(back, carry):
            step = steps - 1 - back
            d = delta_ref[step_ds(step), here]
            p = pgrad_ref[step_ds(step), here]
            out = []
            for n in range(states):
                a = jnp.exp2(d * rate_ref[n, :, here])
                out.append(a * (c_ref[step_ds(step), n * lanes : (n + 1) * lanes] * p + carry[n]))
            return tuple(out)

        ends = lax.fori_loop(0, steps, fall, (jnp.zeros((spans, lanes), F32),) * states)
        for n in range(states):
            back_ref[n, :, here] = ends[n]

    index2 = span_index((spans, inner))
    cum = cum_ref[...]
    part = cum - jnp.where(index2 >= 1, shift_spans(cum, 1), 0.0)
    shift = 1
    while shift < spans:
        inside = index2 < spans - shift
        for n in range(states):
            own = back_ref[n]
            later = jnp.where(inside, shift_spans(own, -shift), 0.0)
            back_ref[n] = own + jnp.exp2(part * rate_ref[n]) * later
        part = part + jnp.where(inside, shift_spans(part, -shift), 0.0)
        shift *= 2
    flow_ref[...] = jnp.concatenate(
        [back_ref[n, 0:1, :] for n in range(states)], axis=0
    ).astype(BF16)

    flow_copies = to_all(flow_ref, flows_ref, flow_send, flow_recv)
    rate = -jnp.exp(dl_ref[...]) * log2e
    sel = sel_ref[...]
    drive[...] = delta_ref[...] * act_ref[...].astype(F32)
    for n in range(states):
        ig_out[n * rows : (n + 1) * rows, :] = jnp.broadcast_to(
            sel[:, rank + n : rank + n + 1], (rows, lanes)
        )
    after = cum[spans - 1 : spans, :] - cum
    inside = index2 < spans - 1
    slot = lax.broadcasted_iota(jnp.int32, (count, 1, 1), 0)

    def visit(visited, carry):
        target = count - 1 - visited
        _, total = segment_sum(table_ref, target, states)
        flow = flows_ref[target].astype(F32) + jnp.exp2(rate * total) * grads[target]
        grads[...] = grads[...] + jnp.where(slot == parents_ref[target], flow[None], 0.0)
        return carry

    groups = inner // lanes
    for group in range(groups):
        here = slice(group * lanes, (group + 1) * lanes)

        def advance(step, carry):
            d = delta_ref[step_ds(step), here]
            w = drive[step_ds(step), here]
            out = []
            for n in range(states):
                state_buf[n, step_ds(step), :] = carry[n]
                a = jnp.exp2(d * rate_ref[n, :, here])
                out.append(a * carry[n] + w * b_at(n, step))
            return tuple(out)

        advance_all(pumps.get((group, 0), ()))
        finals = lax.fori_loop(0, steps, advance, tuple(starts_ref[n, :, here] for n in range(states)))
        for n in range(states):
            state_buf[n, rows : rows + spans, :] = finals[n]
        if group == 0:
            for copy in flow_copies:
                copy.wait()
            grads[...] = jnp.zeros(grads.shape, F32)
            lax.fori_loop(0, count - 1, visit, 0)
        advance_all(pumps.get((group, 1), ()))
        end_grad = grads[me]

        later = []
        for n in range(states):
            flow = jnp.where(inside[:, here], shift_spans(back_ref[n, :, here], -1), 0.0)
            later.append(flow + jnp.exp2(after[:, here] * rate_ref[n, :, here]) * end_grad[n : n + 1, here])

        def retreat(back, carry):
            step = steps - 1 - back
            at = step_ds(step)
            d = delta_ref[at, here]
            p = pgrad_ref[at, here]
            w = drive[at, here]
            flows, sums = carry
            new_flows, new_sums = [], []
            weighted = [None, None]
            decayed = [None, None]
            for n in range(states):
                cols = slice(n * lanes, (n + 1) * lanes)
                a = jnp.exp2(d * rate_ref[n, :, here])
                adjoint = c_ref[at, cols] * p + flows[n]
                moved = a * adjoint
                growth = moved * state_buf[n, at, :]
                new_flows.append(moved)
                new_sums.append(sums[n] + growth * d)
                term = adjoint * b_at(n, step)
                weighted[n % 2] = term if weighted[n % 2] is None else weighted[n % 2] + term
                term = growth * rate_ref[n, :, here]
                decayed[n % 2] = term if decayed[n % 2] is None else decayed[n % 2] + term
                b_term = adjoint * w
                c_term = state_buf[n, step_ds(step + 1), :] * p
                if group == 0:
                    b_sum[at, cols] = b_term
                    c_sum[at, cols] = c_term
                else:
                    b_sum[at, cols] += b_term
                    c_sum[at, cols] += c_term
            bw = weighted[0] + weighted[1]
            dg_ref[at, here] = (decayed[0] + decayed[1]) * (1.0 / log2e) + act_ref[at, here].astype(F32) * bw
            agrad_ref[at, here] = bw * d
            return (tuple(new_flows), tuple(new_sums))

        zero = jnp.zeros((spans, lanes), F32)
        _, sums = lax.fori_loop(0, steps, retreat, (tuple(later), (zero,) * states))
        for n in range(states):
            dgrad_ref[n : n + 1, here] = (
                jnp.sum(sums[n], axis=0, keepdims=True) * rate[n : n + 1, here] * (1.0 / log2e)
            )

    live = (step_tokens(rows, steps) < length).astype(F32)
    step_pre_grad = dg_ref[...] * live * sigmoid(pre_ref[...])
    low = step_pre_grad.astype(BF16)
    gather = gather_matrix(states)
    sel_part[...] = jnp.concatenate(
        [
            dot_nt(low, tw_ref[...]), dot(b_sum[...].astype(BF16), gather),
            dot(c_sum[...].astype(BF16), gather), jnp.zeros((rows, sel_part.shape[1] - selects), F32),
        ],
        axis=1,
    )
    first = pair_copy(0, sel_part, sel_row, row_peer())
    advance_all((c1,))
    bias_sum = jnp.sum(step_pre_grad, axis=0, keepdims=True)
    small_store(0, dot_tn(sel[:, :rank].astype(BF16), low))
    small_store(rank, dgrad_ref[...])
    first.wait()
    pair = sel_part[...] + sel_row[...]
    sel_low[...] = pair.astype(BF16)
    second = pair_copy(1, sel_low, sel_col, col_peer())
    sel_part[...] = pair
    order = to_tokens(rows, steps)
    naturalg = dot(order, ggrad_ref[...]).astype(BF16)
    gate_parts = [dot_nt(naturalg, wg[...]) for wg in (wg_ref, wgo_ref)]
    pre = conv_pre(ext_ref, cw_ref, cb_ref, rows, inner)
    slope = slope_of(pre, sigmoid(pre))
    base_grad = agrad_ref[...] + skip_ref[0:1, :].astype(F32) * pgrad_ref[...]
    advance_all((c0, c3))
    second.wait()
    selg = (sel_part[...] + sel_col[...].astype(F32)).astype(BF16)[:, :selects]
    conv_in = (base_grad + dot_nt(selg, sw_ref[...])) * slope
    cig_ref[0:rows, :] = conv_in
    taps = cw_ref[...].astype(F32)
    tails = [jnp.zeros((5, inner), F32)]
    for i in range(3):
        line = jnp.zeros((1, inner), F32)
        for k in range(i + 1):
            line = line + taps[k : k + 1, :] * conv_in[(i - k) * spans : (i - k) * spans + 1, :]
        tails.append(line * (parents_ref[me] >= 0).astype(F32))
    tail_low = jnp.concatenate(tails, axis=0).astype(BF16)
    last_span = lax.broadcasted_iota(jnp.int32, (spans, inner), 0) == spans - 1
    for j in range(3):
        slab = jnp.roll(conv_in[j * spans : (j + 1) * spans], -1, axis=0)
        cig_ref[rows + j * spans : rows + (j + 1) * spans, :] = jnp.where(last_span, 0.0, slab)
    inner_grad = jnp.zeros((rows, inner), F32)
    for k in range(4):
        inner_grad = inner_grad + taps[k : k + 1, :] * cig_ref[(3 - k) * spans : (3 - k) * spans + rows, :]
    inner_low = inner_grad.astype(BF16)
    for h in range(2):
        store_split(igi_ref.at[h], dot_tn(hid_ref[h], inner_low) + dot_tn(hidt_ref[h], tail_low))
    advance_all(inners)
    for h, wi in enumerate((wi_ref, wio_ref)):
        tpart_ref[h] = dot_nt(tail_low, wi[...])
    tail_first = pair_copy(2, tpart_ref, tail_row, row_peer())
    advance_all(late[1])
    natural = dot(order, inner_low).astype(BF16)
    hid_copies = []
    for h, wi in ((1, wio_ref), (0, wi_ref)):
        part_ref[h] = (dot_nt(natural, wi[...]) + gate_parts[h]).astype(BF16)
        hid_copies.append(
            pair_copy(3 + h, part_ref.at[h, pl.ds(other, half), :], hid_row.at[h], row_peer())
        )
    tail_first.wait()
    tail_sum = tpart_ref[...] + tail_row[...]
    tail_low_ref[...] = tail_sum[1]
    tail_second = pair_copy(5, tail_low_ref, tail_col, col_peer())
    hid_copies[0].wait()
    hid_low[...] = (
        part_ref[1, pl.ds(mine, half), :].astype(F32) + hid_row[1].astype(F32)
    ).astype(BF16)
    hid_second = pair_copy(6, hid_low, hid_col, col_peer())
    advance_all(late[2])
    tail_second.wait()
    tail_own[...] = tail_sum[0] + tail_col[...]
    tail_copies = to_all(tail_own, tails_ref, tail_send, tail_recv)
    small_store(rank + states, dot_tn(selg, act_ref[...]))
    sums = [
        jnp.sum(conv_in * ext_ref[k * spans : k * spans + rows, :], axis=0, keepdims=True)
        for k in range(4)
    ]
    sums.append(jnp.sum(conv_in, axis=0, keepdims=True))
    sums.append(skip_sum)
    sums.append(bias_sum)
    sums.append(jnp.zeros((1, inner), F32))
    small_store(rank + states + selects, jnp.concatenate(sums, axis=0))
    for at in range((rank + states + selects + 8) // 8, small_ref.shape[0] * small_ref.shape[1] // 8):
        a, b = place_of(at)
        small_ref[a, b, :] = jnp.zeros((8, inner), F32)
    small_chunk.next()
    advance_all(late[3])
    hid_copies[1].wait()
    hidden = part_ref[0, pl.ds(mine, half), :].astype(F32) + hid_row[0].astype(F32)
    advance_all(late[4])

    tok = tok_ref[...].astype(F32)
    toko = toko_ref[...].astype(F32)
    power = jnp.sum(tok * tok, axis=1, keepdims=True) + jnp.sum(toko * toko, axis=1, keepdims=True)
    inv = lax.rsqrt(power / width + norm_epsilon)
    normed = tok * inv
    margin8 = tails_ref.shape[1]
    positions = row * half + lax.broadcasted_iota(jnp.int32, (half, margin8), 0)
    line_of = lax.broadcasted_iota(jnp.int32, (half, margin8), 1)
    place = ((positions == length - margin8 + line_of) & (line_of >= margin8 - 3)).astype(F32)
    for copy in tail_copies:
        copy.wait()
    own_tail = jnp.zeros(tails_ref.shape[1:], F32)
    for child in range(count):
        is_child = (parents_ref[child] == me).astype(F32)
        own_tail = own_tail + is_child * tails_ref[child]
    hidden = hidden + jnp.dot(place, own_tail, preferred_element_type=F32, precision=lax.Precision.HIGHEST)
    hid_second.wait()
    hidden = hidden + hid_col[...].astype(F32)
    scaled = hidden * gain_ref[0:1, :].astype(F32)
    mean = jnp.sum(scaled * normed, axis=1, keepdims=True)
    mean_out[...] = lax.dot_general(
        jnp.ones((8, lanes), F32), jnp.broadcast_to(mean / lanes, (half, lanes)), (((1,), (1,)), ((), ())),
        preferred_element_type=F32, precision=lax.Precision.HIGHEST,
    )
    mean_copy = pair_copy(7, mean_out, mean_in, col_peer())
    gain_out[...] = jnp.broadcast_to(jnp.sum(hidden * normed, axis=0, keepdims=True), gain_out.shape)
    gain_copy = pair_copy(8, gain_out, gain_in, row_peer())
    advance_all(late[5])
    gain_copy.wait()
    gain_out[...] = gain_out[...] + gain_in[...]
    gain_copies = to_all(gain_out, gains_ref, gain_send, gain_recv)
    mean_copy.wait()
    apart = lax.dot_general(
        mean_in[...], jnp.full((8, lanes), 0.125, F32), (((0,), (0,)), ((), ())),
        preferred_element_type=F32, precision=lax.Precision.HIGHEST,
    )
    mean = (mean + apart[:, 0:1]) / width
    tg_ref[...] = cot_ref[...] + inv * (scaled - normed * mean)
    advance_all(late[6])
    for copy in gain_copies:
        copy.wait()
    gain_total = gains_ref[0]
    for i in range(1, count):
        gain_total = gain_total + gains_ref[i]
    gg_ref[...] = gain_total
    run_out(chunks + [small_chunk])


def backward_call(args, count, rows, width, inner, states, rank, selects, padded):
    half = width // 2
    tile = rows // 2
    block_rows = half // count
    small = small_rows(count, rank, states, selects)
    f32, bf16 = F32, BF16
    vm = pltpu.VMEM
    scratch = [
        vm((2, count, inner // count, half), bf16), vm((2, count, block_rows, inner), bf16),
        vm((rows, inner), bf16), vm((rows, inner), f32), vm((states, spans, inner), f32), vm((states, inner), bf16),
        vm((count, states, inner), bf16), vm((count, states, inner), f32),
        vm((rows, states * lanes), f32), vm((states, spans, inner), f32),
        vm((states, rows + spans, lanes), f32),
        vm((rows, states * lanes), f32), vm((rows, states * lanes), f32),
        vm((rows, inner), f32), vm((states, inner), f32),
        vm((rows, padded), f32), vm((rows, padded), f32), vm((rows, padded), bf16), vm((rows, padded), bf16),
        vm((rows + 3 * spans, inner), f32), vm((2, rows, half), bf16), vm((2, 8, half), f32),
        vm((2, tile, half), bf16), vm((2, 8, half), f32), vm((tile, half), bf16), vm((tile, half), bf16),
        vm((8, half), f32), vm((8, half), f32), vm((8, half), f32), vm((count, 8, half), f32),
        vm((8, tile), f32), vm((8, tile), f32), vm((8, half), f32), vm((8, half), f32),
        vm((count, 8, half), f32),
        vm((2, count, block_rows, inner), bf16), vm((count, small, inner), f32),
        vm((2 * inner, half), f32), vm((half * 4 * inner // lanes, lanes), f32),
    ]
    most = 0
    for i, paired in enumerate(chunk_plan + (False,)):
        last = i == len(chunk_plan)
        sizes, copies = stage_sizes(stages_of(count, paired), count, i % 2 == 1)
        most = max(most, copies)
        scratch += [
            vm(size + ((small, inner) if last else (block_rows, inner if i < 4 else inner // 2)), f32 if last else bf16)
            for size in sizes
        ]
    dma = pltpu.SemaphoreType.DMA
    scratch += [dma((len(chunk_plan) + 1, most))] * 2 + [dma((9,))] * 2 + [dma((count,))] * 6
    return run_kernel(
        functools.partial(backward_kernel, width=width),
        (
            struct((6, count, block_rows, inner), bf16),
            struct((count, small, inner), f32),
            struct((tile, half), f32),
            struct((8, half), f32),
        ),
        args,
        "backward",
        scratch=scratch,
        flops=16e9,
        collective=4,
        grant=vmem_most,
    )


def final_kernel(
    totals, small_ref, tg_ref, gg_ref, branch_ref,
    out_out, tg_out, gain_out, ig_out, conv_out, bias_out, select_out, step_out, step_bias_out, decay_out, skip_out, og_out,
):
    count, rows, width = totals.shape[1:]
    col = lax.axis_index("col")
    tiles = width // lanes
    for side in range(2):
        place = col if side == 0 else 1 - col
        base = pl.multiple_of(place * (count * rows), count * rows)
        for i in range(count):
            og_out[pl.ds(pl.multiple_of(base + i * rows, 8), rows), :] = widen(totals[side, i])
            for which in range(2):
                value = widen(totals[(4 if which == 0 else 2) + side, i])
                for j in range(tiles):
                    first = i * rows * 4 * tiles + (place * tiles + j) * 2 + which
                    ig_out[pl.ds(first, rows, stride=4 * tiles), :] = value[:, j * lanes : (j + 1) * lanes]
    slab = small_ref.shape[1] // 8

    def read(first, size):
        parts = []
        for j in range(first // 8, (first + size) // 8):
            parts.append(small_ref[j // slab, (j % slab) * 8 : (j % slab) * 8 + 8, :])
        return jnp.concatenate(parts, axis=0) if len(parts) > 1 else parts[0]

    rank, states, selects = step_out.shape[0], decay_out.shape[0], select_out.shape[1]
    step_out[...] = read(0, rank)
    decay_out[...] = read(rank, states)
    select_out[...] = read(rank + states, selects).T
    last = read(rank + states + selects, 8)
    conv_out[...] = last[0:4]
    bias_out[...] = last[4]
    skip_out[...] = last[5]
    step_bias_out[...] = last[6]
    gain_out[...] = gg_ref[0, :]
    tg_out[...] = tg_ref[...]
    out_out[...] = branch_ref[...]


def final_call(totals, small, tg, gg, output, rank, states, selects):
    inner = totals.shape[3]
    half = tg.shape[1]
    return run_kernel(
        final_kernel,
        (
            struct(output.shape, BF16), struct(tg.shape, F32), struct((half,), F32),
            struct((half * 4 * inner // lanes, lanes), F32), struct((4, inner), F32), struct((inner,), F32),
            struct((inner, selects), F32), struct((rank, inner), F32), struct((inner,), F32),
            struct((states, inner), F32), struct((inner,), F32), struct((2 * inner, half), F32),
        ),
        (totals, small, tg, gg, output),
        "final",
    )


def on_device(
    tokens_in, teacher, norm_gain, in_weight, conv_weight, conv_bias, select_weight, step_weight,
    step_bias, decay_log, skip_gain, out_weight, parents, lengths, valid_rows,
):
    rows, width = tokens_in.shape
    half = norm_gain.shape[0]
    inner = decay_log.shape[1]
    states = decay_log.shape[0]
    rank = step_weight.shape[0]
    selects = rank + 2 * states
    padded = selects + -selects % lanes
    steps = rows // spans
    count = lax.axis_size("seq")
    row_len = rows // lax.axis_size("row")
    row = lax.axis_index("row")
    col = lax.axis_index("col")
    me = lax.axis_index("seq")

    def halves(value, axis):
        size = value.shape[axis] // 2
        own = lax.dynamic_slice_in_dim(value, col * size, size, axis)
        other = lax.dynamic_slice_in_dim(value, (1 - col) * size, size, axis)
        return own, other

    def rows8(value):
        return jnp.broadcast_to(value[None, :], (8, value.shape[0]))

    tok, toko = halves(tokens_in, 1)
    tail = lax.dynamic_slice_in_dim(tokens_in, lengths[me] - 8, 8, 0)
    w_own, w_send = halves(in_weight, 2)
    wi, wg = w_own[:, 0], w_own[:, 1]
    wi_send, wg_send = w_send[:, 0], w_send[:, 1]
    ow, ow_send = halves(out_weight, 0)
    gain = rows8(norm_gain)
    skip = rows8(skip_gain)
    conv_b = rows8(conv_bias)
    step_b = rows8(step_bias)

    dma = pltpu.SemaphoreType.DMA
    (
        hid, hid_tail, ext, act, sel, delta, step_pre, cum, table, wio, wgo, owo,
        starts, mixed_pre, gate, mixed, part,
    ) = run_kernel(
        forward_kernel,
        (
            struct((2, rows, half), BF16),
            struct((2, 8, half), BF16),
            struct((rows + 3 * spans, inner), F32),
            struct((rows, inner), BF16),
            struct((rows, padded), F32),
            struct((rows, inner), F32),
            struct((rows, inner), F32),
            struct((spans, inner), F32),
            struct((count, states + 8, inner), BF16),
            struct(wi_send.shape, BF16),
            struct(wg_send.shape, BF16),
            struct(ow_send.shape, BF16),
            struct((states, spans, inner), F32),
            struct((rows, inner), F32),
            struct((rows, inner), F32),
            struct((rows, inner), BF16),
            struct((2, rows, half), BF16),
        ),
        (
            tail, wi_send, wg_send, ow_send, gain, tok, toko, wi, wg, ow, conv_weight, conv_b, select_weight,
            step_weight, step_b, decay_log, skip, parents, lengths,
        ),
        "forward",
        scratch=[
            pltpu.VMEM((count,) + tail.shape, BF16),
            pltpu.VMEM(gain.shape, BF16),
            pltpu.VMEM((rows, padded), F32),
            pltpu.VMEM((rows, padded), BF16),
            pltpu.VMEM((rows, padded), BF16),
            pltpu.VMEM((rows, inner), F32),
            pltpu.VMEM((rows, states * lanes), F32),
            pltpu.VMEM((rows, states * lanes), F32),
            pltpu.VMEM((states, spans, inner), F32),
            pltpu.VMEM((states + 8, inner), BF16),
            pltpu.VMEM((states, spans, inner), F32),
            pltpu.VMEM((count, states, inner), F32),
            dma((7,)), dma((7,)), dma((count,)), dma((count,)), dma((count,)), dma((count,)),
        ],
        flops=6e9,
        collective=0,
    )
    tok_tile = lax.dynamic_slice_in_dim(tok, row * row_len, row_len, 0)
    toko_tile = lax.dynamic_slice_in_dim(toko, row * row_len, row_len, 0)
    teach_tile = lax.dynamic_slice_in_dim(teacher, row * row_len, row_len, 0)
    output, cot_tile, cot = middle_exchange(part, tok_tile, teach_tile, valid_rows)
    totals, small, tokens_grad, gain_total = backward_call(
        (
            cot, mixed, ow, owo, gate, mixed_pre,
            table, parents, lengths, decay_log, starts, cum, delta, act, sel,
            step_pre, step_weight, select_weight, skip, ext, conv_weight, conv_b, hid, hid_tail,
            wi, wio, wg, wgo, tok_tile, toko_tile, gain, cot_tile,
        ),
        count, rows, width, inner, states, rank, selects, padded,
    )
    (
        output, tokens_grad, gain_grad, in_both, conv_grad, conv_bias_grad, select_grad, step_grad,
        step_bias_grad, decay_grad, skip_grad, out_grad,
    ) = final_call(totals, small, tokens_grad, gain_total, output, rank, states, selects)
    in_grad = in_both.reshape(half, -1, 2, lanes).transpose(0, 2, 1, 3).reshape(half, 2, -1)
    return (
        output,
        tokens_grad,
        gain_grad,
        in_grad,
        conv_grad,
        conv_bias_grad,
        select_grad,
        step_grad,
        step_bias_grad,
        decay_grad,
        skip_grad,
        out_grad,
    )


def solution(mesh):
    placed = (
        P("seq", None),
        P("seq", "col"),
        P("col"),
        P("col", None, "row"),
        P(None, ("row", "col")),
        P(("row", "col")),
        P(("row", "col"), None),
        P(None, ("row", "col")),
        P(("row", "col")),
        P(None, ("row", "col")),
        P(("row", "col")),
        P("row", "col"),
        P(),
        P(),
        P(),
    )
    return jax.shard_map(
        on_device,
        mesh=mesh,
        in_specs=placed,
        out_specs=(
            P(("seq", "row"), "col"),
            P(("seq", "row"), "col"),
            P("col"),
            P("col", None, "row"),
            P(None, ("row", "col")),
            P(("row", "col")),
            P(("row", "col"), None),
            P(None, ("row", "col")),
            P(("row", "col")),
            P(None, ("row", "col")),
            P(("row", "col")),
            P("row", "col"),
        ),
        check_vma=False,
    )
```

```python
import functools

import jax
import jax.numpy as jnp
from jax import lax
from jax.experimental import pallas as pl
from jax.experimental.pallas import tpu as pltpu
from jax.sharding import PartitionSpec as P

MESH = pl.DeviceIdType.MESH
F32 = jnp.float32
BF16 = jnp.bfloat16
norm_epsilon = 1e-05
spans = 8
lanes = 128
log2e = 1.4426950408889634
vmem_bytes = 60 * 1024 * 1024
vmem_most = 67043328
chunk_plan = (False, True, False, True, False, True, False, True)


def vmem_spec():
    return pl.BlockSpec(memory_space=pltpu.VMEM)


def smem_spec():
    return pl.BlockSpec(memory_space=pltpu.SMEM)


def struct(shape, dtype):
    return jax.ShapeDtypeStruct(shape, dtype)


def dot(a, b):
    return jnp.dot(a, b, preferred_element_type=F32)


def dot_tn(a, b):
    return lax.dot_general(a, b, (((0,), (0,)), ((), ())), preferred_element_type=F32)


def dot_nt(a, b):
    return lax.dot_general(a, b, (((1,), (1,)), ((), ())), preferred_element_type=F32)


def sigmoid(v):
    return 1.0 / (1.0 + jnp.exp(-v))


def slope_of(v, sigma):
    return sigma * (1.0 + v * (1.0 - sigma))


def to_steps(rows, steps):
    place = lax.broadcasted_iota(jnp.int32, (rows, rows), 0)
    token = lax.broadcasted_iota(jnp.int32, (rows, rows), 1)
    return (token == (place % spans) * steps + place // spans).astype(F32).astype(BF16)


def to_tokens(rows, steps):
    token = lax.broadcasted_iota(jnp.int32, (rows, rows), 0)
    place = lax.broadcasted_iota(jnp.int32, (rows, rows), 1)
    return (token == (place % spans) * steps + place // spans).astype(F32).astype(BF16)


def step_tokens(rows, steps):
    place = lax.broadcasted_iota(jnp.int32, (rows, 1), 0)
    return (place % spans) * steps + place // spans


def spread_matrix(states):
    row = lax.broadcasted_iota(jnp.int32, (2 * states, states * lanes), 0)
    col = lax.broadcasted_iota(jnp.int32, (2 * states, states * lanes), 1)
    return (row % states == col // lanes).astype(F32).astype(BF16)


def gather_matrix(states):
    row = lax.broadcasted_iota(jnp.int32, (states * lanes, states), 0)
    col = lax.broadcasted_iota(jnp.int32, (states * lanes, states), 1)
    return (row // lanes == col).astype(F32).astype(BF16)


def spread(values, states):
    high = values.astype(BF16)
    rest = (values - high.astype(F32)).astype(BF16)
    return dot(jnp.concatenate([high, rest], axis=1), spread_matrix(states))


def shift_spans(values, amount):
    return jnp.roll(values, amount, axis=values.ndim - 2)


def span_index(shape):
    return lax.broadcasted_iota(jnp.int32, shape, len(shape) - 2)


def run_kernel(kernel, outs, args, name, scratch=(), flops=0, collective=None, grant=vmem_bytes):
    params = dict(vmem_limit_bytes=grant)
    if collective is not None:
        params.update(collective_id=collective, has_side_effects=True)
    return pl.pallas_call(
        kernel,
        out_shape=outs,
        in_specs=[
            smem_spec() if a.dtype == jnp.int32 else vmem_spec() for a in args
        ],
        out_specs=jax.tree.map(lambda _: vmem_spec(), outs),
        scratch_shapes=list(scratch),
        compiler_params=pltpu.CompilerParams(**params),
        cost_estimate=pl.CostEstimate(
            flops=int(flops),
            transcendentals=0,
            bytes_accessed=int(sum(a.size * a.dtype.itemsize for a in args)),
        ),
        name=name,
    )(*args)


def barrier_with(peers):
    barrier = pltpu.get_barrier_semaphore()
    for peer in peers:
        pl.semaphore_signal(barrier, inc=1, device_id=peer, device_id_type=MESH)
    pl.semaphore_wait(barrier, len(peers))


def remote(src, dst, send, recv, peer):
    return pltpu.make_async_remote_copy(
        src_ref=src, dst_ref=dst, send_sem=send, recv_sem=recv, device_id=peer, device_id_type=MESH
    )


def row_peer():
    return {"row": 1 - lax.axis_index("row")}


def col_peer():
    return {"col": 1 - lax.axis_index("col")}


def middle_kernel(
    part_ref, tok_ref, teach_ref, ints_ref,
    out_ref, cot_ref, low_ref,
    from_row, to_col, from_col, send, recv,
):
    half = tok_ref.shape[0]
    segments = ints_ref.shape[0]
    row = lax.axis_index("row")
    mine = pl.multiple_of(row * half, half)
    other = pl.multiple_of((1 - row) * half, half)
    barrier_with([row_peer(), col_peer()])
    first = [
        remote(part_ref.at[h, pl.ds(other, half), :], from_row.at[h], send.at[h], recv.at[h], row_peer())
        for h in (1, 0)
    ]
    for copy in first:
        copy.start()
    first[0].wait()
    to_col[...] = (
        part_ref[1, pl.ds(mine, half), :].astype(F32) + from_row[1].astype(F32)
    ).astype(BF16)
    second = remote(to_col, from_col, send.at[2], recv.at[2], col_peer())
    second.start()
    first[1].wait()
    tile = part_ref[0, pl.ds(mine, half), :].astype(F32) + from_row[0].astype(F32)
    tile = tile + tok_ref[...].astype(F32)
    second.wait()
    result = tile + from_col[...].astype(F32)
    out_ref[...] = result.astype(BF16)
    positions = mine + lax.broadcasted_iota(jnp.int32, (half, 1), 0)
    total = ints_ref[0]
    for i in range(1, segments):
        total = total + ints_ref[i]
    share = jnp.full((half, 1), total, jnp.int32).astype(F32)
    counted = (positions < ints_ref[lax.axis_index("seq")]).astype(F32) * ((2 * half * segments) / share)
    cot = (result - teach_ref[...].astype(F32)) * counted
    cot_ref[...] = cot
    low_ref[0, pl.ds(mine, half), :] = cot.astype(BF16)
    third = [
        remote(low_ref.at[0, pl.ds(mine, half), :], low_ref.at[1, pl.ds(mine, half), :], send.at[3], recv.at[3], col_peer()),
        remote(low_ref.at[0, pl.ds(mine, half), :], low_ref.at[0, pl.ds(mine, half), :], send.at[4], recv.at[4], row_peer()),
    ]
    for copy in third:
        copy.start()
    third[0].wait()
    fourth = remote(low_ref.at[1, pl.ds(mine, half), :], low_ref.at[1, pl.ds(mine, half), :], send.at[5], recv.at[5], row_peer())
    fourth.start()
    third[1].wait()
    fourth.wait()


def middle_exchange(part, tok_tile, teach_tile, valid_rows):
    _, rows, width = part.shape
    half = rows // 2
    return run_kernel(
        middle_kernel,
        (struct((half, width), BF16), struct((half, width), F32), struct((2, rows, width), BF16)),
        (part, tok_tile, teach_tile, valid_rows),
        "middle_exchange",
        scratch=[
            pltpu.VMEM((2, half, width), BF16),
            pltpu.VMEM((half, width), BF16),
            pltpu.VMEM((half, width), BF16),
            pltpu.SemaphoreType.DMA((6,)),
            pltpu.SemaphoreType.DMA((6,)),
        ],
        collective=3,
    )


def conv_pre(ext_ref, cw_ref, cb_ref, rows, half):
    taps = cw_ref[...].astype(F32)
    pre = jnp.broadcast_to(cb_ref[0:1, :].astype(F32), (rows, half))
    for k in range(4):
        pre = pre + taps[k : k + 1, :] * ext_ref[k * spans : k * spans + rows, :]
    return pre


def group_ds(group):
    return pl.ds(pl.multiple_of(group * lanes, lanes), lanes)


def step_ds(step):
    return pl.ds(pl.multiple_of(step * spans, spans), spans)


def decay_rows(decay_log_ref, decay_b, scale):
    states, width = decay_log_ref.shape
    rate = -jnp.exp(decay_log_ref[...]) * scale
    for n in range(states):
        decay_b[n] = jnp.broadcast_to(rate[n : n + 1, :], (spans, width))


def span_sum_kernel_part(delta_ref, steps):
    total = delta_ref[0:spans, :]
    for s in range(1, steps):
        total = total + delta_ref[s * spans : (s + 1) * spans, :]
    return total


def segment_sum(table_ref, index, states):
    block = table_ref[index].astype(F32)
    return block[:states], block[states : states + 1] + block[states + 1 : states + 2] + block[states + 2 : states + 3]


def forward_kernel(
    tail_ref, wi_send, wg_send, ow_send, gain_ref, tok_ref, toko_ref, wi_ref, wg_ref, ow_ref, cw_ref, cb_ref, sw_ref,
    tw_ref, tb_ref, dl_ref, skip_ref, parents_ref, lengths_ref,
    hid_ref, hidt_ref, ext_ref, act_ref, sel_ref, delta_ref, pre_ref, cum_ref, table_ref,
    wio_ref, wgo_ref, owo_ref, starts_ref, mpre_ref, gate_ref, mixed_ref, part_ref,
    tails_ref, gaino_ref, sel_row, sel_low, sel_col, drive, b_ref, c_ref, rate_ref, map_ref, reach_ref, finals,
    pair_send, pair_recv, tail_send, tail_recv, map_send, map_recv,
):
    count = table_ref.shape[0]
    rows, half = tok_ref.shape
    steps = rows // spans
    width = 2 * half
    states = dl_ref.shape[0]
    rank = tw_ref.shape[0]
    me = lax.axis_index("seq")
    col = lax.axis_index("col")
    peers = [{"seq": lax.rem(me + j, count)} for j in range(1, count)]
    barrier_with([row_peer(), col_peer()] + peers)

    def pair_copy(at, src, dst, peer):
        copy = remote(src, dst, pair_send.at[at], pair_recv.at[at], peer)
        copy.start()
        return copy

    def to_all(src, dst, sends, recvs):
        copies = [
            remote(src, dst.at[me], sends.at[j], recvs.at[j], peer) for j, peer in enumerate(peers)
        ]
        for copy in copies:
            copy.start()
        dst[me] = src[...]
        return copies

    gain_copy = pair_copy(0, gain_ref, gaino_ref, col_peer())
    wi_copy = pair_copy(1, wi_send, wio_ref, col_peer())
    tail_copies = to_all(tail_ref, tails_ref, tail_send, tail_recv)
    quarter = half // 2
    first_part, second_part = pl.ds(0, quarter), pl.ds(quarter, quarter)
    wg_first = pair_copy(2, wg_send.at[first_part], wgo_ref.at[first_part], col_peer())

    above = parents_ref[me]
    parent = jnp.maximum(above, 0)
    present = (above >= 0).astype(F32)

    def hidden_of(own, other):
        own = own.astype(F32)
        other = other.astype(F32)
        total = jnp.sum(own * own, axis=1, keepdims=True) + jnp.sum(other * other, axis=1, keepdims=True)
        inv = lax.rsqrt(total / width + norm_epsilon)
        gain = gain_ref[0:1, :].astype(F32)
        gaino = gaino_ref[0:1, :].astype(F32)
        return (own * inv * gain).astype(BF16), (other * inv * gaino).astype(BF16)

    gain_copy.wait()
    hid, hido = hidden_of(tok_ref[...], toko_ref[...])
    order = to_steps(rows, steps)
    hid = dot(order, hid).astype(BF16)
    hido = dot(order, hido).astype(BF16)
    hid_ref[0] = hid
    hid_ref[1] = hido
    ext_ref[3 * spans :, :] = dot(hid, wi_ref[...])
    decay_rows(dl_ref, rate_ref, log2e)
    for copy in tail_copies:
        copy.wait()
    own_at = pl.ds(pl.multiple_of(col * half, half), half)
    other_at = pl.ds(pl.multiple_of((1 - col) * half, half), half)
    tail, tailo = hidden_of(tails_ref[parent, :, own_at], tails_ref[parent, :, other_at])
    hidt_ref[0] = tail
    hidt_ref[1] = tailo
    tail_inner = dot(tail, wi_ref[...])
    wi_copy.wait()
    inner = ext_ref[3 * spans :, :] + dot(hid_ref[1], wio_ref[...])
    tail_inner = (tail_inner + dot(tailo, wio_ref[...])) * present
    last = inner[rows - 3 * spans :]
    first_span = lax.broadcasted_iota(jnp.int32, (spans, half), 0) == 0
    for j in range(3):
        block = jnp.roll(last[j * spans : (j + 1) * spans], 1, axis=0)
        ext_ref[j * spans : (j + 1) * spans, :] = jnp.where(
            first_span, jnp.broadcast_to(tail_inner[5 + j : 6 + j, :], (spans, half)), block
        )
    ext_ref[3 * spans :, :] = inner
    pre = conv_pre(ext_ref, cw_ref, cb_ref, rows, half)
    act = (pre * sigmoid(pre)).astype(BF16)
    act_ref[...] = act
    chosen = dot(act, sw_ref[...])
    sel_ref[...] = jnp.concatenate(
        [chosen, jnp.zeros((rows, sel_ref.shape[1] - chosen.shape[1]), F32)], axis=1
    )
    across = pair_copy(3, sel_ref, sel_row, row_peer())
    across.wait()
    pair = sel_ref[...] + sel_row[...]
    sel_low[...] = pair.astype(BF16)
    beside = pair_copy(4, sel_low, sel_col, col_peer())
    wg_second = pair_copy(5, wg_send.at[second_part], wgo_ref.at[second_part], col_peer())
    ow_copy = pair_copy(6, ow_send, owo_ref, col_peer())
    beside.wait()
    sel = pair + sel_col[...].astype(F32)
    sel_ref[...] = sel
    length = lengths_ref[me]
    step_pre = dot(sel[:, :rank].astype(BF16), tw_ref[...]) + tb_ref[0:1, :].astype(F32)
    pre_ref[...] = step_pre
    live = (step_tokens(rows, steps) < length).astype(F32)
    delta = (jnp.maximum(step_pre, 0.0) + jnp.log1p(jnp.exp(-jnp.abs(step_pre)))) * live
    delta_ref[...] = delta
    drive[...] = delta * act_ref[...].astype(F32)
    b_ref[...] = spread(sel[:, rank : rank + states], states)

    for group in range(half // lanes):
        here = slice(group * lanes, (group + 1) * lanes)

        def advance(step, carry):
            d = delta_ref[step_ds(step), here]
            w = drive[step_ds(step), here]
            out = []
            for n in range(states):
                a = jnp.exp2(d * rate_ref[n, :, here])
                out.append(a * carry[n] + w * b_ref[step_ds(step), n * lanes : (n + 1) * lanes])
            return tuple(out)

        ends = lax.fori_loop(0, steps, advance, (jnp.zeros((spans, lanes), F32),) * states)
        for n in range(states):
            reach_ref[n, :, here] = ends[n]

    total = span_sum_kernel_part(delta_ref, steps)
    index2 = span_index((spans, half))
    part = total
    shift = 1
    while shift < spans:
        inside = index2 >= shift
        for n in range(states):
            own = reach_ref[n]
            earlier = jnp.where(inside, shift_spans(own, shift), 0.0)
            reach_ref[n] = own + jnp.exp2(part * rate_ref[n]) * earlier
        part = part + jnp.where(inside, shift_spans(part, shift), 0.0)
        shift *= 2
    cum_ref[...] = part
    sums = part[spans - 1 : spans, :]
    high = sums.astype(BF16)
    mid = (sums - high.astype(F32)).astype(BF16)
    low = (sums - high.astype(F32) - mid.astype(F32)).astype(BF16)
    ends = jnp.concatenate([reach_ref[n, spans - 1 : spans, :] for n in range(states)], axis=0)
    extra = jnp.concatenate(
        [high.astype(F32), mid.astype(F32), low.astype(F32), jnp.zeros((5, half), F32)], axis=0
    )
    map_ref[...] = jnp.concatenate([ends, extra], axis=0).astype(BF16)
    map_copies = to_all(map_ref, table_ref, map_send, map_recv)
    for copy in (wg_first, wg_second):
        copy.wait()
    gate = dot(hid_ref[0], wg_ref[...]) + dot(hid_ref[1], wgo_ref[...])
    gate_ref[...] = gate
    c_ref[...] = spread(sel[:, rank + states : rank + 2 * states], states)
    for copy in map_copies:
        copy.wait()
    rate = -jnp.exp(dl_ref[...]) * log2e

    def start_of(target):
        higher = parents_ref[target]
        return finals[jnp.maximum(higher, 0)] * (higher >= 0).astype(F32)

    def visit(target, carry):
        end, total = segment_sum(table_ref, target, states)
        finals[target] = jnp.exp2(rate * total) * start_of(target) + end
        return carry

    finals[0] = jnp.zeros(finals.shape[1:], F32)
    lax.fori_loop(0, count, visit, 0)
    start = start_of(me)
    before = jnp.where(index2 >= 1, shift_spans(cum_ref[...], 1), 0.0)
    for n in range(states):
        earlier = jnp.where(index2 >= 1, shift_spans(reach_ref[n], 1), 0.0)
        starts_ref[n] = jnp.exp2(before * rate_ref[n]) * start[n : n + 1, :] + earlier

    for group in range(half // lanes):
        here = slice(group * lanes, (group + 1) * lanes)

        def advance(step, carry):
            d = delta_ref[step_ds(step), here]
            w = drive[step_ds(step), here]
            out = []
            reads = [None] * 4
            for n in range(states):
                a = jnp.exp2(d * rate_ref[n, :, here])
                now = a * carry[n] + w * b_ref[step_ds(step), n * lanes : (n + 1) * lanes]
                out.append(now)
                term = c_ref[step_ds(step), n * lanes : (n + 1) * lanes] * now
                reads[n % 4] = term if reads[n % 4] is None else reads[n % 4] + term
            mpre_ref[step_ds(step), here] = (reads[0] + reads[1]) + (reads[2] + reads[3])
            return tuple(out)

        lax.fori_loop(0, steps, advance, tuple(starts_ref[n, :, here] for n in range(states)))

    mixed_pre = mpre_ref[...] + skip_ref[0:1, :].astype(F32) * act_ref[...].astype(F32)
    mpre_ref[...] = mixed_pre
    gate = gate_ref[...]
    mixed = (mixed_pre * (gate * sigmoid(gate))).astype(BF16)
    mixed_ref[...] = mixed
    natural = dot(to_tokens(rows, steps), mixed).astype(BF16)
    part_ref[0] = dot(natural, ow_ref[...]).astype(BF16)
    ow_copy.wait()
    part_ref[1] = dot(natural, owo_ref[...]).astype(BF16)


def seq_bits(count):
    bits = []
    mask = 1
    while mask < count:
        bits.append(mask)
        mask *= 2
    return bits


def stages_of(count, first_pair):
    bits = seq_bits(count)
    if len(bits) < 3:
        return [(mask,) for mask in bits]
    if first_pair:
        return [(bits[1],), (bits[0],)] + [(mask,) for mask in bits[2:]]
    return [(bits[0],), (bits[1], bits[2])] + [(mask,) for mask in bits[3:]]


def stage_sizes(stages, count, crossed):
    sizes, copies = [], 0
    for i, masks in enumerate(stages):
        radix = 2 ** len(masks)
        count //= radix
        got = radix if crossed and i == len(stages) - 1 else radix - 1
        sizes.append((got, count))
        copies += got + radix - 1
    return sizes, copies


def bit_of(me, mask):
    return (me // mask) % 2


def toward(me, masks, pick):
    device, part = me, 0
    for k, mask in enumerate(masks):
        bit = bit_of(me, mask)
        weight = 2 ** (len(masks) - 1 - k)
        if (pick // weight) % 2:
            device = device + mask - 2 * mask * bit
            bit = 1 - bit
        part = part + weight * bit
    return device, part


def widen(values):
    return values.astype(F32)


class Chunk:
    def __init__(self, source, total, landings, send, recv, stages, crossed):
        self.source, self.total, self.landings = source, total, landings
        self.send, self.recv, self.stages, self.crossed = send, recv, stages, crossed
        self.count = source.shape[0]
        self.me = lax.axis_index("seq")
        self.copies = []
        self.flying = []
        self.at = 0
        self.levels = len(stages)
        self.sizes = stage_sizes(stages, self.count, crossed)[0]

    def start(self, src, dst, peer):
        at = len(self.copies)
        copy = remote(src, dst, self.send.at[at], self.recv.at[at], peer)
        copy.start()
        self.copies.append(copy)
        self.flying.append(copy)

    def land(self):
        for copy in self.flying:
            copy.wait_recv()
        self.flying = []

    def place(self, level):
        start = 0
        for j in range(level + 1):
            start = start + toward(self.me, self.stages[j], 0)[1] * self.sizes[j][1]
        return start

    def crossing(self, level):
        return self.crossed and level == self.levels - 1

    def scatter(self, level):
        held = self.source if level == 0 else self.landings[level - 1].at[0]
        masks, (_, size) = self.stages[level], self.sizes[level]
        for pick in range(0 if self.crossing(level) else 1, 2 ** len(masks)):
            device, part = toward(self.me, masks, pick)
            peer = {"seq": device}
            if self.crossing(level):
                peer["col"] = 1 - lax.axis_index("col")
            slot = pick if self.crossing(level) else pick - 1
            self.start(held.at[pl.ds(part * size, size)], self.landings[level].at[slot], peer)

    def add(self, level):
        held = self.source if level == 0 else self.landings[level - 1].at[0]
        masks, (got, size) = self.stages[level], self.sizes[level]
        landing = self.landings[level]
        if self.crossing(level):
            total = widen(landing[0])
        else:
            own = toward(self.me, masks, 0)[1]
            total = widen(held[pl.ds(own * size, size)]) + widen(landing[0])
        for slot in range(1, got):
            total = total + widen(landing[slot])
        return total.astype(landing.dtype)

    def gather(self, level):
        size = self.sizes[level][1]
        region = self.total.at[pl.ds(self.place(level), size)]
        masks = self.stages[level]
        for pick in range(1, 2 ** len(masks)):
            self.start(region, region, {"seq": toward(self.me, masks, pick)[0]})

    def done(self):
        return self.at > 2 * self.levels

    def next(self):
        if self.done():
            return
        self.land()
        at, last = self.at, self.levels
        self.at += 1
        if at < last:
            if at > 0:
                self.landings[at - 1][0] = self.add(at - 1)
            self.scatter(at)
            return
        if at == last:
            self.total[pl.ds(self.place(last - 1), 1)] = self.add(last - 1)
        level = 2 * last - 1 - at
        if level >= 0:
            self.gather(level)

    def finish(self):
        for copy in self.copies:
            copy.wait_send()


def store_split(ref, value):
    rows = ref.shape[1]
    for i in range(ref.shape[0]):
        ref[i] = value[i * rows : (i + 1) * rows].astype(ref.dtype)


def advance_all(chunks):
    for chunk in chunks:
        chunk.next()


def run_out(chunks):
    while any(not chunk.done() for chunk in chunks):
        advance_all(chunks)
    for chunk in chunks:
        chunk.finish()


def small_rows(count, rank, states, selects):
    total = rank + states + selects + 8
    total += -total % (8 * count)
    return total // count


def backward_kernel(
    cotangent_ref, mixed_ref, ow_ref, owo_ref, gate_ref, mpre_ref,
    table_ref, parents_ref, lengths_ref, dl_ref, starts_ref, cum_ref,
    delta_ref, act_ref, sel_ref, pre_ref, tw_ref,
    sw_ref, skip_ref, ext_ref, cw_ref, cb_ref, hid_ref, hidt_ref, wi_ref, wio_ref, wg_ref, wgo_ref,
    tok_ref, toko_ref, gain_ref, cot_ref,
    totals, small_total, tg_ref, gg_ref,
    og_ref, igg_ref, ggrad_ref, pgrad_ref, back_ref, flow_ref,
    flows_ref, grads, c_ref, rate_ref, state_buf, b_sum, c_sum, agrad_ref, dgrad_ref,
    sel_part, sel_row, sel_low, sel_col, cig_ref, part_ref, tpart_ref,
    hid_row, tail_row, hid_low, hid_col, tail_low_ref, tail_col, tail_own, tails_ref,
    mean_out, mean_in, gain_out, gain_in, gains_ref,
    igi_ref, small_ref, og_out, ig_out, *rest,
    width,
):
    count = table_ref.shape[0]
    landings = []
    for paired in chunk_plan + (False,):
        size = len(stages_of(count, paired))
        landings.append(rest[:size])
        rest = rest[size:]
    send, recv, pair_send, pair_recv, flow_send, flow_recv, tail_send, tail_recv, gain_send, gain_recv = rest
    rows, inner = act_ref.shape
    half = rows // 2
    steps = rows // spans
    states = dl_ref.shape[0]
    rank = tw_ref.shape[0]
    selects = sw_ref.shape[1]
    me = lax.axis_index("seq")
    row = lax.axis_index("row")
    col = lax.axis_index("col")
    mine = pl.multiple_of(row * half, half)
    other = pl.multiple_of((1 - row) * half, half)
    length = lengths_ref[me]
    peers = [{"seq": lax.rem(me + j, count)} for j in range(1, count)]
    across = sorted(
        {(masks, pick) for masks in (stages_of(count, p)[-1] for p in chunk_plan) for pick in range(1, 2 ** len(masks))}
    )
    flips = sorted({sum(m for k, m in enumerate(masks) if (pick >> (len(masks) - 1 - k)) % 2) for masks, pick in across})
    crossers = []
    for flip in flips:
        masks = tuple(m for m in seq_bits(count) if (flip // m) % 2)
        crossers.append({"seq": toward(me, masks, 2 ** len(masks) - 1)[0], "col": 1 - col})
    barrier_with([row_peer(), col_peer()] + peers + crossers)

    def pair_copy(at, src, dst, peer):
        copy = remote(src, dst, pair_send.at[at], pair_recv.at[at], peer)
        copy.start()
        return copy

    def to_all(src, dst, sends, recvs):
        copies = [
            remote(src, dst.at[me], sends.at[j], recvs.at[j], peer) for j, peer in enumerate(peers)
        ]
        for copy in copies:
            copy.start()
        dst[me] = src[...]
        return copies

    def small_slabs():
        slab = small_ref.shape[1] // 8
        return lambda at: (at // slab, slice((at % slab) * 8, (at % slab) * 8 + 8))

    place_of = small_slabs()

    def small_store(first, value):
        for j in range(value.shape[0] // 8):
            a, b = place_of(first // 8 + j)
            small_ref[a, b, :] = value[j * 8 : (j + 1) * 8]

    split = inner // 2
    sources = [og_ref.at[0], og_ref.at[1], igg_ref.at[0], igg_ref.at[1]]
    targets = [totals.at[i] for i in range(4)]
    for part in range(2):
        for h in range(2):
            sources.append(igi_ref.at[h, :, :, pl.ds(part * split, split)])
            targets.append(totals.at[4 + h, :, :, pl.ds(part * split, split)])
    chunks = [
        Chunk(
            source, targets[i], landings[i], send.at[i], recv.at[i],
            stages_of(count, chunk_plan[i]), i % 2 == 1,
        )
        for i, source in enumerate(sources)
    ]
    small_chunk = Chunk(
        small_ref, small_total, landings[-1], send.at[len(sources)], recv.at[len(sources)],
        stages_of(count, False), False,
    )

    drive = og_out.at[0:rows]
    dg_ref = og_out.at[rows : 2 * rows]

    def b_at(n, step):
        return ig_out[pl.ds(pl.multiple_of(n * rows + step * spans, spans), spans), :]

    c0, c1, c2, c3 = chunks[:4]
    inners = chunks[4:]
    late = {
        1: (c1, c3, c0), 2: tuple(inners[:2]), 3: tuple(inners[2:]) + (c2,), 4: tuple(inners[:2]) + (c1, c3),
        5: tuple(inners[2:]) + (small_chunk,), 6: tuple(inners) + (c1, c3, small_chunk),
    }
    pumps = {
        (0, 0): (c0, c1), (1, 0): (c2, c3), (2, 0): (c1,), (2, 1): (c0,), (3, 0): (c3,), (3, 1): (c2,),
    }
    from_tokens = to_steps(rows, steps)
    cot = dot(from_tokens, cotangent_ref[0]).astype(BF16)
    coto = dot(from_tokens, cotangent_ref[1]).astype(BF16)
    store_split(og_ref.at[0], dot_tn(mixed_ref[...], cot))
    store_split(og_ref.at[1], dot_tn(mixed_ref[...], coto))
    advance_all((c0, c1))
    mixed_grad = dot_nt(cot, ow_ref[...]) + dot_nt(coto, owo_ref[...])
    gate = gate_ref[...]
    sigma = sigmoid(gate)
    pre_grad = mixed_grad * (gate * sigma)
    pgrad_ref[...] = pre_grad
    gate_grad = (mixed_grad * mpre_ref[...] * slope_of(gate, sigma)).astype(BF16)
    ggrad_ref[...] = gate_grad
    store_split(igg_ref.at[0], dot_tn(hid_ref[0], gate_grad))
    store_split(igg_ref.at[1], dot_tn(hid_ref[1], gate_grad))
    advance_all((c2, c3))
    skip_sum = jnp.sum(pre_grad * act_ref[...].astype(F32), axis=0, keepdims=True)
    decay_rows(dl_ref, rate_ref, log2e)
    c_ref[...] = spread(sel_ref[:, rank + states : rank + 2 * states], states)

    for group in range(inner // lanes):
        here = slice(group * lanes, (group + 1) * lanes)

        def fall(back, carry):
            step = steps - 1 - back
            d = delta_ref[step_ds(step), here]
            p = pgrad_ref[step_ds(step), here]
            out = []
            for n in range(states):
                a = jnp.exp2(d * rate_ref[n, :, here])
                out.append(a * (c_ref[step_ds(step), n * lanes : (n + 1) * lanes] * p + carry[n]))
            return tuple(out)

        ends = lax.fori_loop(0, steps, fall, (jnp.zeros((spans, lanes), F32),) * states)
        for n in range(states):
            back_ref[n, :, here] = ends[n]

    index2 = span_index((spans, inner))
    cum = cum_ref[...]
    part = cum - jnp.where(index2 >= 1, shift_spans(cum, 1), 0.0)
    shift = 1
    while shift < spans:
        inside = index2 < spans - shift
        for n in range(states):
            own = back_ref[n]
            later = jnp.where(inside, shift_spans(own, -shift), 0.0)
            back_ref[n] = own + jnp.exp2(part * rate_ref[n]) * later
        part = part + jnp.where(inside, shift_spans(part, -shift), 0.0)
        shift *= 2
    flow_ref[...] = jnp.concatenate(
        [back_ref[n, 0:1, :] for n in range(states)], axis=0
    ).astype(BF16)

    flow_copies = to_all(flow_ref, flows_ref, flow_send, flow_recv)
    rate = -jnp.exp(dl_ref[...]) * log2e
    sel = sel_ref[...]
    drive[...] = delta_ref[...] * act_ref[...].astype(F32)
    for n in range(states):
        ig_out[n * rows : (n + 1) * rows, :] = jnp.broadcast_to(
            sel[:, rank + n : rank + n + 1], (rows, lanes)
        )
    after = cum[spans - 1 : spans, :] - cum
    inside = index2 < spans - 1
    slot = lax.broadcasted_iota(jnp.int32, (count, 1, 1), 0)

    def visit(visited, carry):
        target = count - 1 - visited
        _, total = segment_sum(table_ref, target, states)
        flow = flows_ref[target].astype(F32) + jnp.exp2(rate * total) * grads[target]
        grads[...] = grads[...] + jnp.where(slot == parents_ref[target], flow[None], 0.0)
        return carry

    groups = inner // lanes
    for group in range(groups):
        here = slice(group * lanes, (group + 1) * lanes)

        def advance(step, carry):
            d = delta_ref[step_ds(step), here]
            w = drive[step_ds(step), here]
            out = []
            for n in range(states):
                state_buf[n, step_ds(step), :] = carry[n]
                a = jnp.exp2(d * rate_ref[n, :, here])
                out.append(a * carry[n] + w * b_at(n, step))
            return tuple(out)

        advance_all(pumps.get((group, 0), ()))
        finals = lax.fori_loop(0, steps, advance, tuple(starts_ref[n, :, here] for n in range(states)))
        for n in range(states):
            state_buf[n, rows : rows + spans, :] = finals[n]
        if group == 0:
            for copy in flow_copies:
                copy.wait()
            grads[...] = jnp.zeros(grads.shape, F32)
            lax.fori_loop(0, count - 1, visit, 0)
        advance_all(pumps.get((group, 1), ()))
        end_grad = grads[me]

        later = []
        for n in range(states):
            flow = jnp.where(inside[:, here], shift_spans(back_ref[n, :, here], -1), 0.0)
            later.append(flow + jnp.exp2(after[:, here] * rate_ref[n, :, here]) * end_grad[n : n + 1, here])

        def retreat(back, carry):
            step = steps - 1 - back
            at = step_ds(step)
            d = delta_ref[at, here]
            p = pgrad_ref[at, here]
            w = drive[at, here]
            flows, sums = carry
            new_flows, new_sums = [], []
            weighted = [None, None]
            decayed = [None, None]
            for n in range(states):
                cols = slice(n * lanes, (n + 1) * lanes)
                a = jnp.exp2(d * rate_ref[n, :, here])
                adjoint = c_ref[at, cols] * p + flows[n]
                moved = a * adjoint
                growth = moved * state_buf[n, at, :]
                new_flows.append(moved)
                new_sums.append(sums[n] + growth * d)
                term = adjoint * b_at(n, step)
                weighted[n % 2] = term if weighted[n % 2] is None else weighted[n % 2] + term
                term = growth * rate_ref[n, :, here]
                decayed[n % 2] = term if decayed[n % 2] is None else decayed[n % 2] + term
                b_term = adjoint * w
                c_term = state_buf[n, step_ds(step + 1), :] * p
                if group == 0:
                    b_sum[at, cols] = b_term
                    c_sum[at, cols] = c_term
                else:
                    b_sum[at, cols] += b_term
                    c_sum[at, cols] += c_term
            bw = weighted[0] + weighted[1]
            dg_ref[at, here] = (decayed[0] + decayed[1]) * (1.0 / log2e) + act_ref[at, here].astype(F32) * bw
            agrad_ref[at, here] = bw * d
            return (tuple(new_flows), tuple(new_sums))

        zero = jnp.zeros((spans, lanes), F32)
        _, sums = lax.fori_loop(0, steps, retreat, (tuple(later), (zero,) * states))
        for n in range(states):
            dgrad_ref[n : n + 1, here] = (
                jnp.sum(sums[n], axis=0, keepdims=True) * rate[n : n + 1, here] * (1.0 / log2e)
            )

    live = (step_tokens(rows, steps) < length).astype(F32)
    step_pre_grad = dg_ref[...] * live * sigmoid(pre_ref[...])
    low = step_pre_grad.astype(BF16)
    gather = gather_matrix(states)
    sel_part[...] = jnp.concatenate(
        [
            dot_nt(low, tw_ref[...]), dot(b_sum[...].astype(BF16), gather),
            dot(c_sum[...].astype(BF16), gather), jnp.zeros((rows, sel_part.shape[1] - selects), F32),
        ],
        axis=1,
    )
    first = pair_copy(0, sel_part, sel_row, row_peer())
    advance_all((c1,))
    bias_sum = jnp.sum(step_pre_grad, axis=0, keepdims=True)
    small_store(0, dot_tn(sel[:, :rank].astype(BF16), low))
    small_store(rank, dgrad_ref[...])
    first.wait()
    pair = sel_part[...] + sel_row[...]
    sel_low[...] = pair.astype(BF16)
    second = pair_copy(1, sel_low, sel_col, col_peer())
    sel_part[...] = pair
    order = to_tokens(rows, steps)
    naturalg = dot(order, ggrad_ref[...]).astype(BF16)
    gate_parts = [dot_nt(naturalg, wg[...]) for wg in (wg_ref, wgo_ref)]
    pre = conv_pre(ext_ref, cw_ref, cb_ref, rows, inner)
    slope = slope_of(pre, sigmoid(pre))
    base_grad = agrad_ref[...] + skip_ref[0:1, :].astype(F32) * pgrad_ref[...]
    advance_all((c0, c3))
    second.wait()
    selg = (sel_part[...] + sel_col[...].astype(F32)).astype(BF16)[:, :selects]
    conv_in = (base_grad + dot_nt(selg, sw_ref[...])) * slope
    cig_ref[0:rows, :] = conv_in
    taps = cw_ref[...].astype(F32)
    tails = [jnp.zeros((5, inner), F32)]
    for i in range(3):
        line = jnp.zeros((1, inner), F32)
        for k in range(i + 1):
            line = line + taps[k : k + 1, :] * conv_in[(i - k) * spans : (i - k) * spans + 1, :]
        tails.append(line * (parents_ref[me] >= 0).astype(F32))
    tail_low = jnp.concatenate(tails, axis=0).astype(BF16)
    last_span = lax.broadcasted_iota(jnp.int32, (spans, inner), 0) == spans - 1
    for j in range(3):
        slab = jnp.roll(conv_in[j * spans : (j + 1) * spans], -1, axis=0)
        cig_ref[rows + j * spans : rows + (j + 1) * spans, :] = jnp.where(last_span, 0.0, slab)
    inner_grad = jnp.zeros((rows, inner), F32)
    for k in range(4):
        inner_grad = inner_grad + taps[k : k + 1, :] * cig_ref[(3 - k) * spans : (3 - k) * spans + rows, :]
    inner_low = inner_grad.astype(BF16)
    for h in range(2):
        store_split(igi_ref.at[h], dot_tn(hid_ref[h], inner_low) + dot_tn(hidt_ref[h], tail_low))
    advance_all(inners)
    for h, wi in enumerate((wi_ref, wio_ref)):
        tpart_ref[h] = dot_nt(tail_low, wi[...])
    tail_first = pair_copy(2, tpart_ref, tail_row, row_peer())
    advance_all(late[1])
    natural = dot(order, inner_low).astype(BF16)
    hid_copies = []
    for h, wi in ((1, wio_ref), (0, wi_ref)):
        part_ref[h] = (dot_nt(natural, wi[...]) + gate_parts[h]).astype(BF16)
        hid_copies.append(
            pair_copy(3 + h, part_ref.at[h, pl.ds(other, half), :], hid_row.at[h], row_peer())
        )
    tail_first.wait()
    tail_sum = tpart_ref[...] + tail_row[...]
    tail_low_ref[...] = tail_sum[1]
    tail_second = pair_copy(5, tail_low_ref, tail_col, col_peer())
    hid_copies[0].wait()
    hid_low[...] = (
        part_ref[1, pl.ds(mine, half), :].astype(F32) + hid_row[1].astype(F32)
    ).astype(BF16)
    hid_second = pair_copy(6, hid_low, hid_col, col_peer())
    advance_all(late[2])
    tail_second.wait()
    tail_own[...] = tail_sum[0] + tail_col[...]
    tail_copies = to_all(tail_own, tails_ref, tail_send, tail_recv)
    small_store(rank + states, dot_tn(selg, act_ref[...]))
    sums = [
        jnp.sum(conv_in * ext_ref[k * spans : k * spans + rows, :], axis=0, keepdims=True)
        for k in range(4)
    ]
    sums.append(jnp.sum(conv_in, axis=0, keepdims=True))
    sums.append(skip_sum)
    sums.append(bias_sum)
    sums.append(jnp.zeros((1, inner), F32))
    small_store(rank + states + selects, jnp.concatenate(sums, axis=0))
    for at in range((rank + states + selects + 8) // 8, small_ref.shape[0] * small_ref.shape[1] // 8):
        a, b = place_of(at)
        small_ref[a, b, :] = jnp.zeros((8, inner), F32)
    small_chunk.next()
    advance_all(late[3])
    hid_copies[1].wait()
    hidden = part_ref[0, pl.ds(mine, half), :].astype(F32) + hid_row[0].astype(F32)
    advance_all(late[4])

    tok = tok_ref[...].astype(F32)
    toko = toko_ref[...].astype(F32)
    power = jnp.sum(tok * tok, axis=1, keepdims=True) + jnp.sum(toko * toko, axis=1, keepdims=True)
    inv = lax.rsqrt(power / width + norm_epsilon)
    normed = tok * inv
    margin8 = tails_ref.shape[1]
    positions = row * half + lax.broadcasted_iota(jnp.int32, (half, margin8), 0)
    line_of = lax.broadcasted_iota(jnp.int32, (half, margin8), 1)
    place = ((positions == length - margin8 + line_of) & (line_of >= margin8 - 3)).astype(F32)
    for copy in tail_copies:
        copy.wait()
    own_tail = jnp.zeros(tails_ref.shape[1:], F32)
    for child in range(count):
        is_child = (parents_ref[child] == me).astype(F32)
        own_tail = own_tail + is_child * tails_ref[child]
    hidden = hidden + jnp.dot(place, own_tail, preferred_element_type=F32, precision=lax.Precision.HIGHEST)
    hid_second.wait()
    hidden = hidden + hid_col[...].astype(F32)
    scaled = hidden * gain_ref[0:1, :].astype(F32)
    mean = jnp.sum(scaled * normed, axis=1, keepdims=True)
    mean_out[...] = lax.dot_general(
        jnp.ones((8, lanes), F32), jnp.broadcast_to(mean / lanes, (half, lanes)), (((1,), (1,)), ((), ())),
        preferred_element_type=F32, precision=lax.Precision.HIGHEST,
    )
    mean_copy = pair_copy(7, mean_out, mean_in, col_peer())
    gain_out[...] = jnp.broadcast_to(jnp.sum(hidden * normed, axis=0, keepdims=True), gain_out.shape)
    gain_copy = pair_copy(8, gain_out, gain_in, row_peer())
    advance_all(late[5])
    gain_copy.wait()
    gain_out[...] = gain_out[...] + gain_in[...]
    gain_copies = to_all(gain_out, gains_ref, gain_send, gain_recv)
    mean_copy.wait()
    apart = lax.dot_general(
        mean_in[...], jnp.full((8, lanes), 0.125, F32), (((0,), (0,)), ((), ())),
        preferred_element_type=F32, precision=lax.Precision.HIGHEST,
    )
    mean = (mean + apart[:, 0:1]) / width
    tg_ref[...] = cot_ref[...] + inv * (scaled - normed * mean)
    advance_all(late[6])
    for copy in gain_copies:
        copy.wait()
    gain_total = gains_ref[0]
    for i in range(1, count):
        gain_total = gain_total + gains_ref[i]
    gg_ref[...] = gain_total
    run_out(chunks + [small_chunk])


def backward_call(args, count, rows, width, inner, states, rank, selects, padded):
    half = width // 2
    tile = rows // 2
    block_rows = half // count
    small = small_rows(count, rank, states, selects)
    f32, bf16 = F32, BF16
    vm = pltpu.VMEM
    scratch = [
        vm((2, count, inner // count, half), bf16), vm((2, count, block_rows, inner), bf16),
        vm((rows, inner), bf16), vm((rows, inner), f32), vm((states, spans, inner), f32), vm((states, inner), bf16),
        vm((count, states, inner), bf16), vm((count, states, inner), f32),
        vm((rows, states * lanes), f32), vm((states, spans, inner), f32),
        vm((states, rows + spans, lanes), f32),
        vm((rows, states * lanes), f32), vm((rows, states * lanes), f32),
        vm((rows, inner), f32), vm((states, inner), f32),
        vm((rows, padded), f32), vm((rows, padded), f32), vm((rows, padded), bf16), vm((rows, padded), bf16),
        vm((rows + 3 * spans, inner), f32), vm((2, rows, half), bf16), vm((2, 8, half), f32),
        vm((2, tile, half), bf16), vm((2, 8, half), f32), vm((tile, half), bf16), vm((tile, half), bf16),
        vm((8, half), f32), vm((8, half), f32), vm((8, half), f32), vm((count, 8, half), f32),
        vm((8, tile), f32), vm((8, tile), f32), vm((8, half), f32), vm((8, half), f32),
        vm((count, 8, half), f32),
        vm((2, count, block_rows, inner), bf16), vm((count, small, inner), f32),
        vm((2 * inner, half), f32), vm((half * 4 * inner // lanes, lanes), f32),
    ]
    most = 0
    for i, paired in enumerate(chunk_plan + (False,)):
        last = i == len(chunk_plan)
        sizes, copies = stage_sizes(stages_of(count, paired), count, i % 2 == 1)
        most = max(most, copies)
        scratch += [
            vm(size + ((small, inner) if last else (block_rows, inner if i < 4 else inner // 2)), f32 if last else bf16)
            for size in sizes
        ]
    dma = pltpu.SemaphoreType.DMA
    scratch += [dma((len(chunk_plan) + 1, most))] * 2 + [dma((9,))] * 2 + [dma((count,))] * 6
    return run_kernel(
        functools.partial(backward_kernel, width=width),
        (
            struct((6, count, block_rows, inner), bf16),
            struct((count, small, inner), f32),
            struct((tile, half), f32),
            struct((8, half), f32),
        ),
        args,
        "backward",
        scratch=scratch,
        flops=16e9,
        collective=4,
        grant=vmem_most,
    )


def final_kernel(
    totals, small_ref, tg_ref, gg_ref, branch_ref,
    out_out, tg_out, gain_out, ig_out, conv_out, bias_out, select_out, step_out, step_bias_out, decay_out, skip_out, og_out,
):
    count, rows, width = totals.shape[1:]
    col = lax.axis_index("col")
    tiles = width // lanes
    for side in range(2):
        place = col if side == 0 else 1 - col
        base = pl.multiple_of(place * (count * rows), count * rows)
        for i in range(count):
            og_out[pl.ds(pl.multiple_of(base + i * rows, 8), rows), :] = widen(totals[side, i])
            for which in range(2):
                value = widen(totals[(4 if which == 0 else 2) + side, i])
                for j in range(tiles):
                    first = i * rows * 4 * tiles + (place * tiles + j) * 2 + which
                    ig_out[pl.ds(first, rows, stride=4 * tiles), :] = value[:, j * lanes : (j + 1) * lanes]
    slab = small_ref.shape[1] // 8

    def read(first, size):
        parts = []
        for j in range(first // 8, (first + size) // 8):
            parts.append(small_ref[j // slab, (j % slab) * 8 : (j % slab) * 8 + 8, :])
        return jnp.concatenate(parts, axis=0) if len(parts) > 1 else parts[0]

    rank, states, selects = step_out.shape[0], decay_out.shape[0], select_out.shape[1]
    step_out[...] = read(0, rank)
    decay_out[...] = read(rank, states)
    select_out[...] = read(rank + states, selects).T
    last = read(rank + states + selects, 8)
    conv_out[...] = last[0:4]
    bias_out[...] = last[4]
    skip_out[...] = last[5]
    step_bias_out[...] = last[6]
    gain_out[...] = gg_ref[0, :]
    tg_out[...] = tg_ref[...]
    out_out[...] = branch_ref[...]


def final_call(totals, small, tg, gg, output, rank, states, selects):
    inner = totals.shape[3]
    half = tg.shape[1]
    return run_kernel(
        final_kernel,
        (
            struct(output.shape, BF16), struct(tg.shape, F32), struct((half,), F32),
            struct((half * 4 * inner // lanes, lanes), F32), struct((4, inner), F32), struct((inner,), F32),
            struct((inner, selects), F32), struct((rank, inner), F32), struct((inner,), F32),
            struct((states, inner), F32), struct((inner,), F32), struct((2 * inner, half), F32),
        ),
        (totals, small, tg, gg, output),
        "final",
    )


def on_device(
    tokens_in, teacher, norm_gain, in_weight, conv_weight, conv_bias, select_weight, step_weight,
    step_bias, decay_log, skip_gain, out_weight, parents, lengths, valid_rows,
):
    rows, width = tokens_in.shape
    half = norm_gain.shape[0]
    inner = decay_log.shape[1]
    states = decay_log.shape[0]
    rank = step_weight.shape[0]
    selects = rank + 2 * states
    padded = selects + -selects % lanes
    steps = rows // spans
    count = lax.axis_size("seq")
    row_len = rows // lax.axis_size("row")
    row = lax.axis_index("row")
    col = lax.axis_index("col")
    me = lax.axis_index("seq")

    def halves(value, axis):
        size = value.shape[axis] // 2
        own = lax.dynamic_slice_in_dim(value, col * size, size, axis)
        other = lax.dynamic_slice_in_dim(value, (1 - col) * size, size, axis)
        return own, other

    def one_row(value):
        return value[None, :]

    tok, toko = halves(tokens_in, 1)
    tail = lax.dynamic_slice_in_dim(tokens_in, lengths[me] - 8, 8, 0)
    w_own, w_send = halves(in_weight, 2)
    wi, wg = w_own[:, 0], w_own[:, 1]
    wi_send, wg_send = w_send[:, 0], w_send[:, 1]
    ow, ow_send = halves(out_weight, 0)
    gain = one_row(norm_gain)
    skip = one_row(skip_gain)
    conv_b = one_row(conv_bias)
    step_b = one_row(step_bias)

    dma = pltpu.SemaphoreType.DMA
    (
        hid, hid_tail, ext, act, sel, delta, step_pre, cum, table, wio, wgo, owo,
        starts, mixed_pre, gate, mixed, part,
    ) = run_kernel(
        forward_kernel,
        (
            struct((2, rows, half), BF16),
            struct((2, 8, half), BF16),
            struct((rows + 3 * spans, inner), F32),
            struct((rows, inner), BF16),
            struct((rows, padded), F32),
            struct((rows, inner), F32),
            struct((rows, inner), F32),
            struct((spans, inner), F32),
            struct((count, states + 8, inner), BF16),
            struct(wi_send.shape, BF16),
            struct(wg_send.shape, BF16),
            struct(ow_send.shape, BF16),
            struct((states, spans, inner), F32),
            struct((rows, inner), F32),
            struct((rows, inner), F32),
            struct((rows, inner), BF16),
            struct((2, rows, half), BF16),
        ),
        (
            tail, wi_send, wg_send, ow_send, gain, tok, toko, wi, wg, ow, conv_weight, conv_b, select_weight,
            step_weight, step_b, decay_log, skip, parents, lengths,
        ),
        "forward",
        scratch=[
            pltpu.VMEM((count,) + tail.shape, BF16),
            pltpu.VMEM(gain.shape, BF16),
            pltpu.VMEM((rows, padded), F32),
            pltpu.VMEM((rows, padded), BF16),
            pltpu.VMEM((rows, padded), BF16),
            pltpu.VMEM((rows, inner), F32),
            pltpu.VMEM((rows, states * lanes), F32),
            pltpu.VMEM((rows, states * lanes), F32),
            pltpu.VMEM((states, spans, inner), F32),
            pltpu.VMEM((states + 8, inner), BF16),
            pltpu.VMEM((states, spans, inner), F32),
            pltpu.VMEM((count, states, inner), F32),
            dma((7,)), dma((7,)), dma((count,)), dma((count,)), dma((count,)), dma((count,)),
        ],
        flops=6e9,
        collective=0,
    )
    tok_tile = lax.dynamic_slice_in_dim(tok, row * row_len, row_len, 0)
    toko_tile = lax.dynamic_slice_in_dim(toko, row * row_len, row_len, 0)
    teach_tile = lax.dynamic_slice_in_dim(teacher, row * row_len, row_len, 0)
    output, cot_tile, cot = middle_exchange(part, tok_tile, teach_tile, valid_rows)
    totals, small, tokens_grad, gain_total = backward_call(
        (
            cot, mixed, ow, owo, gate, mixed_pre,
            table, parents, lengths, decay_log, starts, cum, delta, act, sel,
            step_pre, step_weight, select_weight, skip, ext, conv_weight, conv_b, hid, hid_tail,
            wi, wio, wg, wgo, tok_tile, toko_tile, gain, cot_tile,
        ),
        count, rows, width, inner, states, rank, selects, padded,
    )
    (
        output, tokens_grad, gain_grad, in_both, conv_grad, conv_bias_grad, select_grad, step_grad,
        step_bias_grad, decay_grad, skip_grad, out_grad,
    ) = final_call(totals, small, tokens_grad, gain_total, output, rank, states, selects)
    in_grad = in_both.reshape(half, -1, 2, lanes).transpose(0, 2, 1, 3).reshape(half, 2, -1)
    return (
        output,
        tokens_grad,
        gain_grad,
        in_grad,
        conv_grad,
        conv_bias_grad,
        select_grad,
        step_grad,
        step_bias_grad,
        decay_grad,
        skip_grad,
        out_grad,
    )


def solution(mesh):
    placed = (
        P("seq", None),
        P("seq", "col"),
        P("col"),
        P("col", None, "row"),
        P(None, ("row", "col")),
        P(("row", "col")),
        P(("row", "col"), None),
        P(None, ("row", "col")),
        P(("row", "col")),
        P(None, ("row", "col")),
        P(("row", "col")),
        P("row", "col"),
        P(),
        P(),
        P(),
    )
    return jax.shard_map(
        on_device,
        mesh=mesh,
        in_specs=placed,
        out_specs=(
            P(("seq", "row"), "col"),
            P(("seq", "row"), "col"),
            P("col"),
            P("col", None, "row"),
            P(None, ("row", "col")),
            P(("row", "col")),
            P(("row", "col"), None),
            P(None, ("row", "col")),
            P(("row", "col")),
            P(None, ("row", "col")),
            P(("row", "col")),
            P("row", "col"),
        ),
        check_vma=False,
    )
```
